32 devices in a mesh: clips: 16 (over z, x, core), mlp: 2 (over y).
Axes of the slice: x: 2, y: 2, z: 4, core: 2. Of those that a mesh axis runs over, the one named last changes fastest.
Arguments:
- flat_params: bfloat16 [3804160], replicated
- w_fc1: bfloat16 [768, 3072], P(None, 'mlp'), may hold values from -0.21875 to 0.21875
- w_fc2: bfloat16 [3072, 768], P('mlp'), may hold values from -0.15625 to 0.15625
- w_up: bfloat16 [512, 2048], P(None, 'mlp'), may hold values from -0.25 to 0.25
- w_down: bfloat16 [2048, 512], P('mlp'), may hold values from -0.21875 to 0.21875
- patches: bfloat16 [9984, 768], P(('clips', 'mlp')), may hold values from -6 to 6
- clip_ids: int32 [49152], P(('clips', 'mlp')), may hold values from 0 to 2, as said below
- visible_index: int32 [9984], P(('clips', 'mlp')), may hold values from 0 to 1535, as said below
- cotangent: bfloat16 [49152, 512], P(('clips', 'mlp')), may hold values from -6 to 6
Outputs:
- decoded: bfloat16 [49152, 512], P(('clips', 'mlp'))
- input_grad: float32 [9984, 768], P(('clips', 'mlp'))
- param_grad: float32 [3804160], P('mlp')
- fc1_grad: float32 [768, 3072], P(None, 'mlp')
- fc2_grad: float32 [3072, 768], P('mlp')
- up_grad: float32 [512, 2048], P(None, 'mlp')
- down_grad: float32 [2048, 512], P('mlp')
The draws below stay inside these ranges and needn't reach their ends.
Inputs may be any that keep to these rules, and one draw needn't show every extreme that they name: `clip_ids`: each buffer of 1536 patches is either one clip of 192 x 8 patches, all with id 0, or three clips of 512 patches with ids 0, 1, 2 in order; a clip's patch (t, f) is row t * 8 + f of it. Both kinds occur in every draw. `visible_index`: the 312 entries of a buffer are distinct and increasing positions within that buffer; a three-clip buffer has 104 of them in each clip.
All inputs are finite; a program needn't handle non-finite values.
Results may differ from the reference program's by a relative error of at most 0.028.
Values may be sent and summed in bfloat16 or wider, within the bound.
No kernel may reach another device: no remote copies, remote signals or barrier semaphores. Data moves between devices by JAX's collectives and lax.ppermute only.
A program may use at most 384 MiB of HBM per device.

```python
import math
import jax
import jax.numpy as jnp
from jax import lax

D = 768
HEADS = 12
FF = 3072
DD = 512
DHEADS = 16
DFF = 2048
HD = 64
FREQ = 8
WIN = 4
VIS_SHORT = 104
LONG_FRAMES = 192
SHORT_PATCHES = 512
ROWS = 1536
VIS = 312
BUF_ALL = 32
ROWS_ALL = 49152
VIS_ALL = 9984
PARAMS_PAD = 3804160


def buffer_layout(key):

    def one_buffer(index):
        seeded = jax.random.fold_in(key, index)
        coin = jax.random.randint(jax.random.fold_in(seeded, 1), (), 0, 11)
        single = jnp.where(index == 0, False, jnp.where(index == 1, True, coin < 2))
        positions = jnp.arange(ROWS, dtype=jnp.int32)
        ids_short = (positions // SHORT_PATCHES).astype(jnp.int32)
        ids_long = jnp.zeros((ROWS,), jnp.int32)
        buffer_ids = jnp.where(single, ids_long, ids_short)
        long_pick = jnp.sort(jax.random.permutation(jax.random.fold_in(seeded, 2), ROWS)[:VIS]).astype(jnp.int32)
        short_parts = []
        for clip_number in range(3):
            picked = jax.random.permutation(jax.random.fold_in(seeded, 3 + clip_number), SHORT_PATCHES)[:VIS_SHORT]
            short_parts.append(jnp.sort(picked).astype(jnp.int32) + clip_number * SHORT_PATCHES)
        short_pick = jnp.concatenate(short_parts)
        visible = jnp.where(single, long_pick, short_pick).astype(jnp.int32)
        return (buffer_ids, visible)
    all_ids, all_visible = jax.vmap(one_buffer)(jnp.arange(BUF_ALL, dtype=jnp.int32))
    return (all_ids.reshape(-1), all_visible.reshape(-1))


def draw_clip_ids(key, part):
    return buffer_layout(jax.random.fold_in(key, 7))[0]


def draw_visible_index(key, part):
    return buffer_layout(jax.random.fold_in(key, 7))[1]


def draw_flat_params(key, part):
    layout = ((3 * D * D, 1.4 / math.sqrt(D), 0.0), (D * D, 4.0 / math.sqrt(D), 0.0), (D, 0.1, 1.0), (D, 0.1, 1.0), (D * DD, 1.0 / math.sqrt(D), 0.0), (DD, 1.0, 0.0), (3 * DD * DD, 1.4 / math.sqrt(DD), 0.0), (DD * DD, 2.5 / math.sqrt(DD), 0.0), (DD, 0.1, 1.0), (DD, 0.1, 1.0))
    position = jnp.arange(PARAMS_PAD, dtype=jnp.int32)
    spread = jnp.zeros((PARAMS_PAD,), jnp.float32) + 1.0 / math.sqrt(D)
    centre = jnp.zeros((PARAMS_PAD,), jnp.float32)
    offset = 0
    for length, std_dev, middle in layout:
        inside = (position >= offset) & (position < offset + length)
        spread = jnp.where(inside, std_dev, spread)
        centre = jnp.where(inside, middle, centre)
        offset = offset + length
    noise = jnp.clip(jax.random.normal(key, (PARAMS_PAD,), jnp.float32), -5.0, 5.0)
    return (centre + spread * noise).astype(jnp.bfloat16)


def shard_levels(stream_key, extent, shards, smallest, high):
    def one(dim, parts):
        steps = jax.random.uniform(jax.random.fold_in(jax.random.fold_in(stream_key, 6), dim), (parts,), jnp.float32, smallest / len(shards), high / len(shards))
        return jnp.repeat(jnp.exp(steps), extent[dim] // parts).reshape((-1,) + (1,) * (len(extent) - dim - 1))

    gain = one(*shards[0])
    for cut in shards[1:]:
        gain = gain * one(*cut)
    return gain


def gaussian(stream_key, dims, width, bound, cuts=(), held_as=jnp.bfloat16):
    values = width * jax.random.normal(stream_key, dims, jnp.float32)
    if cuts:
        values = values * shard_levels(stream_key, dims, cuts, -0.22, 0.18)
    return jnp.clip(values, -bound, bound).astype(held_as)


def setup_inputs(seed: int = 0) -> dict:
    seeds = jax.random.split(jax.random.key(seed), 10)
    flat_params = draw_flat_params(jax.random.fold_in(seeds[9], 71), 0)
    w_fc1 = gaussian(seeds[1], (D, FF), D ** -0.5, 0.21875, ((1, 2),))
    w_fc2 = gaussian(seeds[2], (FF, D), (FF * 2 // 5) ** -0.5, 0.15625, ((0, 2),))
    w_up = gaussian(seeds[3], (DD, DFF), DD ** -0.5, 0.25, ((1, 2),))
    w_down = gaussian(seeds[4], (DFF, DD), (DFF * 2 // 5) ** -0.5, 0.21875, ((0, 2),))
    patches = gaussian(seeds[5], (VIS_ALL, D), 1.0, 6.0, ((0, 32),))
    clip_ids = draw_clip_ids(jax.random.fold_in(seeds[9], 71), 0)
    visible_index = draw_visible_index(jax.random.fold_in(seeds[9], 71), 0)
    cotangent = gaussian(seeds[8], (ROWS_ALL, DD), 1.0, 6.0, ((0, 32),))
    return dict(flat_params=flat_params, w_fc1=w_fc1, w_fc2=w_fc2, w_up=w_up, w_down=w_down, patches=patches, clip_ids=clip_ids, visible_index=visible_index, cotangent=cotangent)


EPSILON = 1e-06
PRECISE = lax.Precision.HIGHEST

@jax.custom_vjp
def low(v):
    return lax.optimization_barrier(v.astype(jnp.bfloat16)).astype(jnp.float32)

@jax.custom_vjp
def low_back(v):
    return v

def low_keep(v):
    return (low(v), None)

def low_pass(kept, grad):
    return (grad,)

def back_keep(v):
    return (v, None)

def back_low(kept, grad):
    return (low(grad),)
low.defvjp(low_keep, low_pass)
low_back.defvjp(back_keep, back_low)

def matmul(left, right):
    return jnp.dot(left, right, precision=PRECISE, preferred_element_type=jnp.float32)

def layer_norm(inputs, weight_gain):
    row_mean = lax.optimization_barrier(jnp.mean(inputs, axis=-1, keepdims=True))
    centred = inputs - row_mean
    variance = lax.optimization_barrier(jnp.mean(centred * centred, axis=-1, keepdims=True))
    return centred * lax.rsqrt(variance + EPSILON) * weight_gain

def unpack(flat):
    layout = ((D, 3 * D), (D, D), (D,), (D,), (D, DD), (DD,), (DD, 3 * DD), (DD, DD), (DD,), (DD,))
    members = []
    offset = 0
    for dims_of in layout:
        length = math.prod(dims_of)
        members.append(flat[offset:offset + length].reshape(dims_of))
        offset = offset + length
    return members

def to_windows(source, head_count):
    head_size = source.shape[-1] // head_count
    blocks = source.reshape(-1, LONG_FRAMES // WIN, WIN, FREQ // WIN, WIN, head_count, head_size)
    blocks = blocks.transpose(0, 1, 3, 2, 4, 5, 6)
    return blocks.reshape(-1, WIN * WIN, head_count, head_size)

def from_windows(source, buffers):
    blocks = source.reshape(buffers, LONG_FRAMES // WIN, FREQ // WIN, WIN, WIN, -1)
    blocks = blocks.transpose(0, 1, 3, 2, 4, 5)
    return blocks.reshape(buffers * ROWS, -1)

def attend(queries, key_rows, val_rows, allowed):
    factor = 1.0 / math.sqrt(queries.shape[-1])
    products = jnp.einsum('bqhd,bkhd->bhqk', queries, key_rows, precision=PRECISE)
    scores = low_back(products * factor)
    if allowed is not None:
        scores = jnp.where(allowed, scores, -1e+30)
    attn_probs = low(jax.nn.softmax(scores, axis=-1))
    return jnp.einsum('bhqk,bkhd->bqhd', attn_probs, val_rows, precision=PRECISE)

def forward(flat, fc_one, fc_two, up_proj, down_proj, patch_rows, segment, visible):
    w_qkv, w_proj, g_one, g_two, w_embed, mask_token, w_dqkv, w_dproj, gd_one, gd_two = unpack(flat)
    enc_norm = low(layer_norm(patch_rows, g_one))
    enc_qkv = low(low_back(matmul(enc_norm, w_qkv))).reshape(1, VIS, 3, HEADS, HD)
    allowed = (segment[:, None] == segment[None, :])[None, None]
    enc_mix = attend(enc_qkv[:, :, 0], enc_qkv[:, :, 1], enc_qkv[:, :, 2], allowed)
    enc_mix = low(low_back(enc_mix.reshape(VIS, D)))
    first = patch_rows + low_back(matmul(enc_mix, w_proj))
    enc_in2 = low(layer_norm(first, g_two))
    enc_hidden = low(jax.nn.gelu(low_back(matmul(enc_in2, fc_one)), approximate=False))
    second = first + low_back(matmul(enc_hidden, fc_two))
    embedded = low(low_back(matmul(low(second), w_embed)))
    matches = visible[None, :] == jnp.arange(ROWS, dtype=jnp.int32)[:, None]
    filled = matmul(matches.astype(embedded.dtype), embedded)
    masked_rows = 1.0 - jnp.any(matches, axis=1).astype(embedded.dtype)
    start = filled + masked_rows[:, None] * mask_token[None, :]
    dec_norm = low(layer_norm(start, gd_one))
    dec_qkv = low(low_back(matmul(dec_norm, w_dqkv)))
    dec_mix = attend(to_windows(dec_qkv[:, :DD], DHEADS), to_windows(dec_qkv[:, DD:2 * DD], DHEADS), to_windows(dec_qkv[:, 2 * DD:], DHEADS), None)
    dec_mix = low(low_back(from_windows(dec_mix, 1)))
    middle = start + low_back(matmul(dec_mix, w_dproj))
    dec_in2 = low(layer_norm(middle, gd_two))
    dec_hidden = low(jax.nn.gelu(low_back(matmul(dec_in2, up_proj)), approximate=False))
    return middle + matmul(dec_hidden, down_proj)

def reference(flat_params, w_fc1, w_fc2, w_up, w_down, patches, clip_ids, visible_index, cotangent):
    flat = flat_params.astype(jnp.float32)
    fc_one = w_fc1.astype(jnp.float32)
    fc_two = w_fc2.astype(jnp.float32)
    up_proj = w_up.astype(jnp.float32)
    down_proj = w_down.astype(jnp.float32)
    inputs = (patches.astype(jnp.float32).reshape(BUF_ALL, VIS, D), clip_ids.reshape(BUF_ALL, ROWS), visible_index.reshape(BUF_ALL, VIS), cotangent.astype(jnp.float32).reshape(BUF_ALL, ROWS, DD))

    def one_buffer(totals, slices):
        patch_rows, buffer_ids, visible, upstream = slices
        segment = jnp.take(buffer_ids, visible)

        def run_block(flat_in, fc_one_in, fc_two_in, up_in, down_in, rows_in):
            return forward(flat_in, fc_one_in, fc_two_in, up_in, down_in, rows_in, segment, visible)
        result, pullback = jax.vjp(run_block, flat, fc_one, fc_two, up_proj, down_proj, patch_rows)
        grad_flat, grad_fc_one, grad_fc_two, grad_up, grad_down, grad_rows = pullback(upstream)
        totals = (totals[0] + grad_flat, totals[1] + grad_fc_one, totals[2] + grad_fc_two, totals[3] + grad_up, totals[4] + grad_down)
        return (totals, (result.astype(jnp.bfloat16), grad_rows))
    starting = (jnp.zeros_like(flat), jnp.zeros_like(fc_one), jnp.zeros_like(fc_two), jnp.zeros_like(up_proj), jnp.zeros_like(down_proj))
    totals, (decoded, input_grad) = lax.scan(one_buffer, starting, inputs)
    return (decoded.reshape(ROWS_ALL, DD), input_grad.reshape(VIS_ALL, D), totals[0], totals[1], totals[2], totals[3], totals[4])
```

```python
import math

import jax
import jax.numpy as jnp
from jax import lax
from jax.experimental import pallas as pl
from jax.experimental.pallas import tpu as pltpu
from jax.sharding import PartitionSpec as P

D = 768
HEADS = 12
DD = 512
DHEADS = 16
FREQ = 8
WIN = 4
ROWS = 1536
VIS = 312
PAD = 320
SHORT_PATCHES = 512
PARAMS = 3804160
EPSILON = 1e-06
BLOCK = 256
GROUP = WIN * FREQ
HALF = DD // 2
ENC_SCALE = 1.0 / math.sqrt(D // HEADS)
DEC_SCALE = 1.0 / math.sqrt(DD // DHEADS)
LOWEST = -1e30
CORES = 2
bf16 = jnp.bfloat16
f32 = jnp.float32


def mm(left, right):
    return jnp.dot(left, right, preferred_element_type=f32)


def mm_nt(left, right):
    return lax.dot_general(left, right, (((1,), (1,)), ((), ())), preferred_element_type=f32)


def mm_tn(left, right):
    return lax.dot_general(left, right, (((0,), (0,)), ((), ())), preferred_element_type=f32)


def normalize(rows):
    centred = rows - jnp.mean(rows, axis=-1, keepdims=True)
    scale = lax.rsqrt(jnp.mean(centred * centred, axis=-1, keepdims=True) + EPSILON)
    return centred * scale, scale


def norm_back(grad, normed, scale, gain):
    weighted = grad * gain
    return scale * (
        weighted
        - jnp.mean(weighted, axis=-1, keepdims=True)
        - normed * jnp.mean(weighted * normed, axis=-1, keepdims=True)
    )


def gelu_parts(pre):
    cdf = 0.5 * (1.0 + lax.erf(pre * math.sqrt(0.5)))
    return pre * cdf, cdf + pre * jnp.exp(-0.5 * pre * pre) * (1.0 / math.sqrt(2.0 * math.pi))


def gained(grad, normed):
    return jnp.sum(grad * normed, axis=0, keepdims=True)


SMEM = pl.BlockSpec(memory_space=pltpu.SMEM)
VMEM = pl.BlockSpec(memory_space=pltpu.VMEM)


def call(body, outs, *args, **more):
    return pl.pallas_call(
        body,
        out_shape=[jax.ShapeDtypeStruct(shape, dtype) for shape, dtype in outs],
        compiler_params=pltpu.CompilerParams(vmem_limit_bytes=56 * 2**20),
        **more,
    )(*args)


TILES = {"wqkv": 18, "wproj": 6, "wemb": 4, "wdqkv": 12, "wdproj": 4}
G1_AT = (D * 3 * D + D * D) // 128
WEMB_AT = G1_AT + 12
MASK_AT = WEMB_AT + D * 4
WDQKV_AT = MASK_AT + 4
WDPROJ_AT = WDQKV_AT + DD * 12
GD1_AT = WDPROJ_AT + DD * 4
FLAT_ROWS = PARAMS // 128
DEC_ROWS = FLAT_ROWS - WEMB_AT
PREP = 64


def widen(flat_ref, first, out_ref, tiles):
    for t in range(tiles):
        out_ref[:, t * 128 : t * 128 + 128] = flat_ref[
            pl.ds(first + t, out_ref.shape[0], stride=tiles), :
        ].astype(bf16)


def vector(flat_ref, first, count):
    return jnp.concatenate([flat_ref[first + i : first + i + 1, :] for i in range(count)], axis=1)


def flatten(flat_ref, first, value, tiles):
    for t in range(tiles):
        flat_ref[pl.ds(first + t, value.shape[0], stride=tiles), :] = value[:, t * 128 : t * 128 + 128]


def enc_prep_kernel(qkv_ref, proj_ref, gains_ref, wqkv_ref, wproj_ref, g1_ref, g2_ref, qkv_flat, proj_flat, gains_flat):
    qkv_flat[...] = qkv_ref[...].astype(f32)
    proj_flat[...] = proj_ref[...].astype(f32)
    widen(qkv_flat, 0, wqkv_ref, 18)
    widen(proj_flat, 0, wproj_ref, 6)

    @pl.when(pl.program_id(0) == 0)
    def _():
        gains_flat[...] = gains_ref[...].astype(f32)
        g1_ref[...] = vector(gains_flat, 0, 6)
        g2_ref[...] = vector(gains_flat, 6, 6)


def enc_prep(flat):
    whole = lambda *shape: pl.BlockSpec(shape, lambda i: (0,) * len(shape))
    return pl.pallas_call(
        enc_prep_kernel,
        grid=(D // PREP,),
        in_specs=[
            pl.BlockSpec((PREP * 18, 128), lambda i: (i, 0)),
            pl.BlockSpec((PREP * 6, 128), lambda i: (D * 18 // (PREP * 6) + i, 0)),
            pl.BlockSpec((16, 128), lambda i: (G1_AT // 16, 0)),
        ],
        out_specs=[
            pl.BlockSpec((PREP, 3 * D), lambda i: (i, 0)),
            pl.BlockSpec((PREP, D), lambda i: (i, 0)),
            whole(1, D),
            whole(1, D),
        ],
        out_shape=[
            jax.ShapeDtypeStruct((D, 3 * D), bf16),
            jax.ShapeDtypeStruct((D, D), bf16),
            jax.ShapeDtypeStruct((1, D), f32),
            jax.ShapeDtypeStruct((1, D), f32),
        ],
        scratch_shapes=[
            pltpu.VMEM((PREP * 18, 128), f32), pltpu.VMEM((PREP * 6, 128), f32), pltpu.VMEM((16, 128), f32),
        ],
    )(flat, flat, flat)


def dec_prep_kernel(
    flat_ref, _, wemb_ref, mask_ref, wdqkv_ref, wdproj_ref, gd1_ref, gd2_ref, low, wide, sem,
):
    copy = pltpu.make_async_copy(flat_ref.at[pl.ds(G1_AT, FLAT_ROWS - G1_AT), :], low, sem)
    copy.start()
    copy.wait()
    wide[...] = low[...].astype(f32)
    widen(wide, WEMB_AT - G1_AT, wemb_ref, 4)
    widen(wide, WDQKV_AT - G1_AT, wdqkv_ref, 12)
    widen(wide, WDPROJ_AT - G1_AT, wdproj_ref, 4)
    mask_ref[...] = vector(wide, MASK_AT - G1_AT, 4)
    gd1_ref[...] = vector(wide, GD1_AT - G1_AT, 4)
    gd2_ref[...] = vector(wide, GD1_AT - G1_AT + 4, 4)


def dec_prep(flat, after):
    hbm = pl.BlockSpec(memory_space=pl.ANY)
    return call(
        dec_prep_kernel,
        [((D, DD), bf16), ((1, DD), f32), ((DD, 3 * DD), bf16), ((DD, DD), bf16), ((1, DD), f32), ((1, DD), f32)],
        flat, after,
        in_specs=[hbm, hbm],
        scratch_shapes=[
            pltpu.VMEM((FLAT_ROWS - G1_AT, 128), bf16), pltpu.VMEM((FLAT_ROWS - G1_AT, 128), f32),
            pltpu.SemaphoreType.DMA,
        ],
    )


def enc_attend_kernel(
    x_ref, wqkv_ref, wproj_ref, g1_ref, g2_ref, segr_ref, segc_ref,
    qkv_ref, probs_ref, mix_ref, first_ref, in2_ref,
):
    x = x_ref[...].astype(f32)
    normed, _ = normalize(x)
    qkv_ref[...] = mm((normed * g1_ref[...]).astype(bf16), wqkv_ref[...]).astype(bf16)
    allowed = segr_ref[...] == segc_ref[...]
    low_lanes = lax.broadcasted_iota(jnp.int32, (PAD, 128), 1) < 64
    for pair in range(HEADS // 2):
        at = slice(pair * 128, pair * 128 + 128)
        query = qkv_ref[:, at]
        key = qkv_ref[:, D + pair * 128 : D + pair * 128 + 128]
        value = qkv_ref[:, 2 * D + pair * 128 : 2 * D + pair * 128 + 128]
        mixed = []
        for side in range(2):
            mine = low_lanes if side == 0 else jnp.logical_not(low_lanes)
            own = jnp.where(mine, query.astype(f32), 0.0).astype(bf16)
            scores = jnp.where(allowed, mm_nt(own, key) * ENC_SCALE, LOWEST)
            top = jnp.max(scores, axis=-1, keepdims=True)
            raised = jnp.exp(scores - top)
            probs = (raised / jnp.sum(raised, axis=-1, keepdims=True)).astype(bf16)
            probs_ref[2 * pair + side] = probs
            mixed.append(mm(probs, value))
        mix_ref[:, at] = jnp.where(low_lanes, mixed[0], mixed[1]).astype(bf16)
    first = x + mm(mix_ref[...], wproj_ref[...])
    first_ref[...] = first
    normed2, _ = normalize(first)
    in2_ref[...] = (normed2 * g2_ref[...]).astype(bf16)


def enc_ffn_kernel(in2_ref, fc1_ref, fc2_ref, part_ref, hidden_ref, slope_ref):
    act, slope = gelu_parts(mm(in2_ref[...], fc1_ref[...]))
    hidden = act.astype(bf16)
    hidden_ref[...] = hidden
    slope_ref[...] = slope.astype(bf16)
    part_ref[...] = mm(hidden, fc2_ref[...]).astype(part_ref.dtype)


def enc_ffn_back_kernel(out_grad_ref, slope_ref, fc1_ref, fc2_ref, pre_grad_ref, part_ref):
    grad = mm_nt(out_grad_ref[...], fc2_ref[...]) * slope_ref[...].astype(f32)
    pre_grad = grad.astype(bf16)
    pre_grad_ref[...] = pre_grad
    part_ref[...] = mm_nt(pre_grad, fc1_ref[...]).astype(part_ref.dtype)


def halve(core, value, keep_ref, send_ref):
    half = value.shape[0] // 2
    low, high = value[:half].astype(bf16), value[half:].astype(bf16)

    @pl.when(core == 0)
    def _():
        keep_ref[...] = low.reshape(keep_ref.shape)
        send_ref[...] = high.reshape(send_ref.shape)

    @pl.when(core != 0)
    def _():
        keep_ref[...] = high.reshape(keep_ref.shape)
        send_ref[...] = low.reshape(send_ref.shape)


def enc_weights_kernel(count):
    def body(core_ref, *refs):
        in2s, pre_grads, hiddens, out_grads = (refs[i * count : (i + 1) * count] for i in range(4))
        one_keep, one_send, two_keep, two_send = refs[4 * count :]
        one = mm_tn(in2s[0][...], pre_grads[0][...])
        for i in range(1, count):
            one = one + mm_tn(in2s[i][...], pre_grads[i][...])
        halve(core_ref[0], one, one_keep, one_send)
        two = mm_tn(hiddens[0][...], out_grads[0][...])
        for i in range(1, count):
            two = two + mm_tn(hiddens[i][...], out_grads[i][...])
        halve(core_ref[0], two, two_keep, two_send)

    return body


def embed_kernel(count):
    def body(first_ref, own_ref, *refs):
        parts = refs[: count - 1]
        wemb_ref, mask_ref, gd1_ref, wdqkv_ref, second_ref, table_ref, norm_ref = refs[count - 1 :]
        second = first_ref[...] + own_ref[...]
        for part in parts:
            second += part[...].astype(f32)
        low = second.astype(bf16)
        second_ref[...] = low
        embedded = mm(low, wemb_ref[...]).astype(bf16).astype(f32)
        row = lax.broadcasted_iota(jnp.int32, (PAD, DD), 0)
        start = jnp.where(row == VIS, mask_ref[...], embedded)
        normed, _ = normalize(start)
        dec_norm = (normed * gd1_ref[...]).astype(bf16)
        norm_ref[...] = dec_norm
        table_ref[:, : 3 * DD] = mm(dec_norm, wdqkv_ref[...]).astype(bf16)
        table_ref[:, 3 * DD :] = start.astype(bf16)

    return body


def spread(rows, same):
    left = jnp.concatenate([rows[:, :128]] * 4, axis=0) * same
    right = jnp.concatenate([rows[:, 128:]] * 4, axis=0) * same
    none = jnp.zeros_like(left)
    return jnp.concatenate(
        [jnp.concatenate([left, none], axis=1), jnp.concatenate([none, right], axis=1)], axis=0
    )


def segment_max(rows):
    tiles = []
    lane = lax.broadcasted_iota(jnp.int32, (rows.shape[0], 128), 1)
    for t in range(rows.shape[1] // 128):
        tile = rows[:, t * 128 : t * 128 + 128]
        for step in (1, 2, 8, 16):
            other = jnp.where(
                lane & step == 0, pltpu.roll(tile, 128 - step, 1), pltpu.roll(tile, step, 1)
            )
            tile = jnp.maximum(tile, other)
        tiles.append(tile)
    return jnp.concatenate(tiles, axis=1)


def decoder_kernel(chunks):
    def body(
        vis_ref, table_ref, cot_ref, wdproj_ref, gd2_ref, up_ref, down_ref,
        decoded_ref, up_grad_ref, down_grad_ref, proj_grad_ref, gd2_grad_ref, packed_ref,
        qkv_ref, mix_ref, s_ref, p_ref, l_ref, dmix_ref, ds_ref, d_ref, back_ref, same_ref, ones_ref,
        up_acc, down_acc, proj_acc, gd2_acc, packed_acc,
    ):
        step = pl.program_id(0)

        @pl.when(step == 0)
        def _():
            up_acc[...] = jnp.zeros_like(up_acc)
            down_acc[...] = jnp.zeros_like(down_acc)
            proj_acc[...] = jnp.zeros_like(proj_acc)
            gd2_acc[...] = jnp.zeros_like(gd2_acc)
            packed_acc[...] = jnp.zeros_like(packed_acc)
            head_row = lax.broadcasted_iota(jnp.int32, (HALF, HALF), 0) // GROUP
            head_lane = lax.broadcasted_iota(jnp.int32, (HALF, HALF), 1) // GROUP
            ones = (head_row == head_lane).astype(f32).astype(bf16)
            ones_ref[...] = ones
            same_ref[...] = ones[:128, :128]

        row = lax.broadcasted_iota(jnp.int32, (BLOCK, PAD), 0) + step * BLOCK
        named = row == vis_ref[...]
        col = lax.broadcasted_iota(jnp.int32, (BLOCK, PAD), 1)
        hit = jnp.max(jnp.where(named, 1.0, 0.0), axis=1, keepdims=True)
        one_hot = jnp.where(named, 1.0, jnp.where(col == VIS, 1.0 - hit, 0.0)).astype(bf16)
        qkv_ref[...] = mm(one_hot, table_ref[:, : 3 * DD]).astype(bf16)
        start = mm(one_hot, table_ref[:, 3 * DD :])

        lane = lax.broadcasted_iota(jnp.int32, (BLOCK, DD), 1)
        line = lax.broadcasted_iota(jnp.int32, (BLOCK, DD), 0)
        window = (lane % FREQ) // WIN == (line % FREQ) // WIN
        n_groups = BLOCK // GROUP

        def parts(group, half):
            at = pl.ds(pl.multiple_of(group * GROUP, GROUP), GROUP)
            return at, slice(half * HALF, (half + 1) * HALF)

        def scores(group, _):
            same = same_ref[...]
            for half in range(2):
                at, cols = parts(group, half)
                key = qkv_ref[at, DD + half * HALF : DD + (half + 1) * HALF]
                s_ref[at, cols] = mm_nt(qkv_ref[at, cols], spread(key, same))
            return 0

        lax.fori_loop(0, n_groups, scores, 0, unroll=4)
        raw = s_ref[...] * DEC_SCALE
        top = segment_max(raw)
        raised = jnp.where(window, jnp.exp(raw - top), 0.0)
        p_low = raised.astype(bf16)
        total = jnp.concatenate(
            [mm(p_low[:, :HALF], ones_ref[...]), mm(p_low[:, HALF:], ones_ref[...])], axis=1
        )
        l_ref[...] = top + jnp.log(total)
        p_ref[...] = (raised / total).astype(bf16)

        def mixes(group, _):
            same = same_ref[...]
            for half in range(2):
                at, cols = parts(group, half)
                value = qkv_ref[at, 2 * DD + half * HALF : 2 * DD + (half + 1) * HALF]
                mix_ref[at, cols] = mm(p_ref[at, cols], spread(value, same)).astype(bf16)
            return 0

        lax.fori_loop(0, n_groups, mixes, 0, unroll=4)

        middle = start + mm(mix_ref[...], wdproj_ref[...])
        normed, scale = normalize(middle)
        in2 = (normed * gd2_ref[...]).astype(bf16)
        cot = cot_ref[...]
        out = jnp.zeros_like(middle)
        in2_grad = jnp.zeros_like(middle)
        for c in range(chunks):
            act, slope = gelu_parts(mm(in2, up_ref[c]))
            hidden = act.astype(bf16)
            out += mm(hidden, down_ref[c])
            pre_grad = (mm_nt(cot, down_ref[c]) * slope).astype(bf16)
            in2_grad += mm_nt(pre_grad, up_ref[c])
            down_acc[c] += mm_tn(hidden, cot)
            up_acc[c] += mm_tn(in2, pre_grad)
        decoded_ref[...] = (middle + out).astype(bf16)

        gd2_acc[...] += gained(in2_grad, normed)
        middle_grad = cot.astype(f32) + norm_back(in2_grad, normed, scale, gd2_ref[...])
        branch = middle_grad.astype(bf16)
        back_ref[:, 3 * DD :] = branch
        proj_acc[...] += mm_tn(mix_ref[...], branch)
        dmix_ref[...] = mm_nt(branch, wdproj_ref[...]).astype(bf16)

        def prob_grads(group, _):
            same = same_ref[...]
            for half in range(2):
                at, cols = parts(group, half)
                value = qkv_ref[at, 2 * DD + half * HALF : 2 * DD + (half + 1) * HALF]
                s_ref[at, cols] = mm_nt(dmix_ref[at, cols], spread(value, same))
            return 0

        lax.fori_loop(0, n_groups, prob_grads, 0, unroll=4)
        probs = p_ref[...].astype(f32)
        prob_grad = s_ref[...]
        weighed = (probs * prob_grad).astype(bf16)
        row_sum = jnp.concatenate(
            [mm(weighed[:, :HALF], ones_ref[...]), mm(weighed[:, HALF:], ones_ref[...])], axis=1
        )
        d_ref[...] = row_sum
        ds_ref[...] = (probs * (prob_grad - row_sum)).astype(bf16)

        small_lane = lax.broadcasted_iota(jnp.int32, (GROUP, HALF), 1)
        small_line = lax.broadcasted_iota(jnp.int32, (GROUP, HALF), 0)
        pick = small_lane % GROUP == small_line
        small_window = (small_lane % FREQ) // WIN == (small_line % FREQ) // WIN

        def qkv_grads(group, _):
            same = same_ref[...]
            for half in range(2):
                at, cols = parts(group, half)
                key_cols = slice(DD + half * HALF, DD + (half + 1) * HALF)
                value_cols = slice(2 * DD + half * HALF, 2 * DD + (half + 1) * HALF)
                key = qkv_ref[at, key_cols]
                wide_query = spread(qkv_ref[at, cols], same)
                wide_mix_grad = spread(dmix_ref[at, cols], same)
                back_ref[at, cols] = (mm(ds_ref[at, cols], spread(key, same)) * DEC_SCALE).astype(bf16)
                log_total = jnp.sum(jnp.where(pick, l_ref[at, cols], 0.0), axis=0, keepdims=True)
                turned_sum = jnp.sum(jnp.where(pick, d_ref[at, cols], 0.0), axis=0, keepdims=True)
                turned = mm_nt(key, wide_query) * DEC_SCALE
                turned = jnp.where(small_window, jnp.exp(turned - log_total), 0.0)
                turned_grad = mm_nt(qkv_ref[at, value_cols], wide_mix_grad)
                score_grad = (turned * (turned_grad - turned_sum)).astype(bf16)
                back_ref[at, key_cols] = (mm(score_grad, wide_query) * DEC_SCALE).astype(bf16)
                back_ref[at, value_cols] = mm(turned.astype(bf16), wide_mix_grad).astype(bf16)
            return 0

        lax.fori_loop(0, n_groups, qkv_grads, 0, unroll=2)
        packed_acc[...] += mm_tn(one_hot, back_ref[...])

        @pl.when(step == pl.num_programs(0) - 1)
        def _():
            up_grad_ref[...] = up_acc[...].astype(bf16)
            down_grad_ref[...] = down_acc[...].astype(bf16)
            proj_grad_ref[...] = proj_acc[...].astype(bf16)
            gd2_grad_ref[...] = gd2_acc[...]
            packed_ref[...] = packed_acc[...]

    return body


def decoder(vis_row, table, cotangent, w_dproj, gd_two, up, down):
    chunks, _, width = up.shape
    rows = cotangent.shape[0]
    kept = lambda *shape: pl.BlockSpec(shape, lambda i: (0,) * len(shape), pipeline_mode=pl.Buffered(1))
    by_rows = pl.BlockSpec((BLOCK, DD), lambda i: (i, 0))
    outs = [
        ((rows, DD), bf16, by_rows),
        ((chunks, DD, width), bf16, kept(chunks, DD, width)),
        ((chunks, width, DD), bf16, kept(chunks, width, DD)),
        ((DD, DD), bf16, kept(DD, DD)),
        ((1, DD), f32, kept(1, DD)),
        ((PAD, 4 * DD), f32, kept(PAD, 4 * DD)),
    ]
    return pl.pallas_call(
        decoder_kernel(chunks),
        grid=(rows // BLOCK,),
        in_specs=[
            kept(1, PAD), kept(PAD, 4 * DD), by_rows, kept(DD, DD), kept(1, DD),
            kept(chunks, DD, width), kept(chunks, width, DD),
        ],
        out_specs=[spec for _, _, spec in outs],
        out_shape=[jax.ShapeDtypeStruct(shape, dtype) for shape, dtype, _ in outs],
        scratch_shapes=[
            pltpu.VMEM((BLOCK, 3 * DD), bf16),
            pltpu.VMEM((BLOCK, DD), bf16),
            pltpu.VMEM((BLOCK, DD), f32),
            pltpu.VMEM((BLOCK, DD), bf16),
            pltpu.VMEM((BLOCK, DD), f32),
            pltpu.VMEM((BLOCK, DD), bf16),
            pltpu.VMEM((BLOCK, DD), bf16),
            pltpu.VMEM((BLOCK, DD), f32),
            pltpu.VMEM((BLOCK, 4 * DD), bf16),
            pltpu.VMEM((128, 128), bf16),
            pltpu.VMEM((HALF, HALF), bf16),
            pltpu.VMEM((chunks, DD, width), f32),
            pltpu.VMEM((chunks, width, DD), f32),
            pltpu.VMEM((DD, DD), f32),
            pltpu.VMEM((1, DD), f32),
            pltpu.VMEM((PAD, 4 * DD), f32),
        ],
        compiler_params=pltpu.CompilerParams(vmem_limit_bytes=56 * 2**20),
    )(vis_row, table, cotangent, w_dproj, gd_two, up, down)


def embed_back_kernel(
    packed_ref, table_ref, norm_ref, second_ref, gd1_ref, wdqkv_ref, wemb_ref,
    second_grad_ref, out_grad_ref, qkv_grad_ref, embed_grad_ref, gd1_grad_ref, mask_grad_ref,
):
    qkv_grad = packed_ref[:, : 3 * DD].astype(bf16)
    qkv_grad_ref[...] = qkv_grad
    grad = mm_nt(qkv_grad, wdqkv_ref[...])
    normed, scale = normalize(table_ref[:, 3 * DD :].astype(f32))
    gd1_grad_ref[...] = gained(grad, normed)
    start_grad = packed_ref[:, 3 * DD :] + norm_back(grad, normed, scale, gd1_ref[...])
    mask_grad_ref[...] = start_grad[VIS : VIS + 1]
    row = lax.broadcasted_iota(jnp.int32, (PAD, DD), 0)
    embed_grad = jnp.where(row < VIS, start_grad, 0.0).astype(bf16)
    embed_grad_ref[...] = embed_grad
    second_grad = mm_nt(embed_grad, wemb_ref[...])
    second_grad_ref[...] = second_grad
    out_grad_ref[...] = second_grad.astype(bf16)


def dec_flat_kernel(
    norm_ref, qkv_grad_ref, second_ref, embed_grad_ref, proj_grad_ref, mask_grad_ref, gd1_grad_ref, gd2_grad_ref,
    flat_ref, wide,
):
    flatten(wide, 0, mm_tn(second_ref[...], embed_grad_ref[...]), 4)
    flatten(wide, MASK_AT - WEMB_AT, mask_grad_ref[...], 4)
    flatten(wide, WDQKV_AT - WEMB_AT, mm_tn(norm_ref[...], qkv_grad_ref[...]), 12)
    flatten(wide, WDPROJ_AT - WEMB_AT, proj_grad_ref[...].astype(f32), 4)
    flatten(wide, GD1_AT - WEMB_AT, gd1_grad_ref[...], 4)
    flatten(wide, GD1_AT + 4 - WEMB_AT, gd2_grad_ref[...], 4)
    flat_ref[...] = wide[...].astype(bf16)


def enc_back_kernel(count, ring):
    def body(core_ref, own_ref, *refs):
        parts = refs[: count - 1]
        (
            second_grad_ref, first_ref, x_ref, qkv_ref, probs_ref, mix_ref, wqkv_ref, wproj_ref, g1_ref, g2_ref,
            dec_flat_ref, input_grad_ref, keep_ref, send_ref, qkv_grad_ref, wide,
        ) = refs[count - 1 :]
        in2_grad = own_ref[...]
        for part in parts:
            in2_grad += part[...].astype(f32)
        normed2, scale2 = normalize(first_ref[...])
        flatten(wide, G1_AT + 6, gained(in2_grad, normed2), 6)
        first_grad = second_grad_ref[...] + norm_back(in2_grad, normed2, scale2, g2_ref[...])
        branch = first_grad.astype(bf16)
        flatten(wide, D * 18, mm_tn(mix_ref[...], branch), 6)
        wide[WEMB_AT:, :] = dec_flat_ref[...].astype(f32)
        mix_grad = mm_nt(branch, wproj_ref[...]).astype(bf16)
        low_lanes = lax.broadcasted_iota(jnp.int32, (PAD, 128), 1) < 64
        for pair in range(HEADS // 2):
            at = slice(pair * 128, pair * 128 + 128)
            query = qkv_ref[:, at]
            key = qkv_ref[:, D + pair * 128 : D + pair * 128 + 128]
            value = qkv_ref[:, 2 * D + pair * 128 : 2 * D + pair * 128 + 128]
            upstream = mix_grad[:, at]
            found = []
            for side in range(2):
                mine = low_lanes if side == 0 else jnp.logical_not(low_lanes)
                own = jnp.where(mine, upstream.astype(f32), 0.0).astype(bf16)
                low_probs = probs_ref[2 * pair + side]
                probs = low_probs.astype(f32)
                prob_grad = mm_nt(own, value)
                row_sum = jnp.sum(probs * prob_grad, axis=-1, keepdims=True)
                score_grad = (probs * (prob_grad - row_sum)).astype(bf16)
                found.append((mm(score_grad, key), mm_tn(score_grad, query), mm_tn(low_probs, upstream)))
            for part, factor in enumerate((ENC_SCALE, ENC_SCALE, 1.0)):
                merged = jnp.where(low_lanes, found[0][part], found[1][part]) * factor
                qkv_grad_ref[:, part * D + pair * 128 : part * D + pair * 128 + 128] = merged.astype(bf16)
        normed, scale = normalize(x_ref[...].astype(f32))
        flatten(wide, 0, mm_tn((normed * g1_ref[...]).astype(bf16), qkv_grad_ref[...]), 18)
        grad = mm_nt(qkv_grad_ref[...], wqkv_ref[...])
        flatten(wide, G1_AT, gained(grad, normed), 6)
        input_grad_ref[...] = (first_grad + norm_back(grad, normed, scale, g1_ref[...]))[:VIS]

        part = FLAT_ROWS // ring.group
        height = keep_ref.shape[3]

        def split(target, half):
            for way in range(2):
                for chip in range(ring.chips):
                    first = ((half * 2 + way) * ring.chips + chip) * height
                    for y in range(ring.group):
                        count = min(height, part - first)
                        if count > 0:
                            target[way, chip, y, :count] = wide[y * part + first : y * part + first + count, :].astype(bf16)
                        if count < height:
                            target[way, chip, y, max(count, 0) :] = jnp.zeros((height - max(count, 0), 128), bf16)

        for half in range(CORES):
            @pl.when(core_ref[0] == half)
            def _(half=half):
                split(keep_ref, half)
                split(send_ref, 1 - half)

    return body


class Ring:
    def __init__(self, clips, group):
        self.chips = clips // CORES
        self.group = group
        chips = self.chips
        if chips == 8:
            order = [4 * z // 2 for z in range(4)] + [4 * z // 2 + 1 for z in reversed(range(4))]
        else:
            order = list(range(chips))
        place = [0] * chips
        for at, chip in enumerate(order):
            place[chip] = at
        clip = lax.axis_index("clips")
        self.core = clip % CORES
        chip = clip // CORES
        if chips == 8:
            self.at = jnp.where(chip % 2 == 0, chip // 2, 7 - chip // 2)
        else:
            self.at = chip
        self.lane = lax.axis_index("mlp")
        step = lambda way: [
            (order[i] * CORES + c, order[(i + way) % chips] * CORES + c) for i in range(chips) for c in range(CORES)
        ]
        self.ways = (step(1), step(-1))
        self.swap = [(i, i ^ 1) for i in range(clips)]
        self.clips = clips

    def clip_of(self, side, slot):
        chip = jnp.where(slot < 4, 2 * slot, 15 - 2 * slot) if self.chips == 8 else slot
        return chip * CORES + side


    def fetch(self, block):
        half = block.shape[0] // CORES
        mine = lax.dynamic_slice_in_dim(block, self.core * half, half, 0)
        blocks = [block]
        for k in range(1, self.group):
            near = lax.ppermute(mine, "mlp", [(j, (j - k) % self.group) for j in range(self.group)])
            far = self.swapped(near)
            low, high = (jnp.where(self.core == side, near, far) for side in range(CORES))
            blocks.append(jnp.concatenate([low, high]))
        stacked = jnp.stack(blocks)
        if self.group == 2:
            return jnp.where(self.lane == 0, stacked, stacked[::-1])
        return jnp.roll(stacked, self.lane, axis=0)

    def halves(self, rows, width):
        return ((2, self.chips, rows // (2 * CORES * self.chips), width), bf16)

    def swapped(self, value):
        return lax.ppermute(value, "clips", self.swap)

    def block(self, half, way, back):
        sign = 1 if way == 0 else -1
        return lax.dynamic_index_in_dim(half[way], (self.at - sign * back) % self.chips, 0, False)

    def scattered(self, grads):
        group, rows, width = grads.shape
        blocks = grads.reshape(group, self.clips, rows // self.clips, width).transpose(1, 0, 2, 3)
        flat = blocks.reshape(-1, width)
        return lax.psum_scatter(flat, "clips", scatter_dimension=0, tiled=True).reshape(group, -1, width)

    def scattered_trip(self, block):
        group, rows, width = block.shape
        ways = block.reshape(group, 2, rows // 2, width)
        held = yield self.over_group([ways[:, 0], ways[:, 1]])
        return (yield from self.spread(held))

    def scattered_row(self, rows):
        height = rows // (self.clips * 2)
        return lambda side, way, slot: (self.clip_of(side, slot) * 2 + way) * height

    def start(self, keep, send):
        return keep + self.swapped(send)

    def round_trip(self, half):
        held = [self.block(half, way, 0) for way in range(2)]
        for step in range(1, self.chips):
            came = [lax.ppermute(held[way], "clips", self.ways[way]) for way in range(2)]
            held = yield [came[way] + self.block(half, way, step) for way in range(2)]
        if half.ndim == 5:
            held = yield self.over_group(held)
        return (yield from self.spread(held))

    def over_group(self, held):
        both = jnp.stack(held, axis=1)
        total = lax.dynamic_index_in_dim(both, self.lane, 0, False)
        for k in range(1, self.group):
            away = lax.dynamic_index_in_dim(both, (self.lane + k) % self.group, 0, False)
            total = total + lax.ppermute(away, "mlp", [(j, (j + k) % self.group) for j in range(self.group)])
        return [total[0], total[1]]

    def spread(self, held):
        found = [[held[0]], [held[1]]]
        cut = self.chips - 2
        early = None
        for step in range(1, self.chips):
            came = yield [lax.ppermute(found[way][-1], "clips", self.ways[way]) for way in range(2)]
            for way in range(2):
                found[way].append(came[way])
            if step == cut - 1:
                early = self.swapped(jnp.stack(found[0] + found[1]))
        late = self.swapped(jnp.stack(found[0][cut:] + found[1][cut:]))
        return found[0] + found[1], early, late


def in_step(*trips):
    done = [None] * len(trips)
    kept = [None] * len(trips)
    round_at = 0
    while any(one is None for one in done):
        live = []
        for i, (trip, first) in enumerate(trips):
            if done[i] is None and round_at >= first:
                try:
                    kept[i] = next(trip) if kept[i] is None else trip.send(kept[i])
                    live.append(i)
                except StopIteration as end:
                    done[i] = end.value
        if live:
            tied = lax.optimization_barrier([kept[i] for i in live])
            for i, value in zip(live, tied):
                kept[i] = value
        round_at += 1
    return done


def place_kernel(chips, height, total, row_of, lead):
    cut = chips - 2

    def body(where_ref, *refs):
        mine, early, late, out = refs[: 2 * chips], refs[2 * chips], refs[2 * chips + 1], refs[2 * chips + 2]
        core, at = where_ref[0], where_ref[1]

        def put(side, way, slot, value):
            row = row_of(side, way, slot)
            if total % height == 0:
                out[pl.ds(pl.multiple_of(row, 8) if height % 8 == 0 else row, height), :] = value
            else:
                short = total % height

                @pl.when(row + height <= total)
                def _():
                    out[pl.ds(pl.multiple_of(row, 8), height), :] = value

                @pl.when(row + height > total)
                def _():
                    out[total - short :, :] = value[:short]

        for way in range(2):
            sign = 1 if way == 0 else -1
            for step in range(chips):
                slot = lax.rem(at + sign * (lead - step) + chips, chips)
                put(core, way, slot, mine[way * chips + step][...].astype(f32))
                other = early[way * cut + step] if step < cut else late[way * 2 + step - cut]
                put(1 - core, way, slot, other.astype(f32))

    return body


def place_rows(ring, found, total, row_of, lead):
    mine, early, late = found
    cut = ring.chips - 2
    out = jnp.zeros((total, mine[0].shape[1]), f32)
    for way in range(2):
        for step in range(ring.chips):
            slot = (ring.at + (1 if way == 0 else -1) * (lead - step)) % ring.chips
            other = early[way * cut + step] if step < cut else late[way * 2 + step - cut]
            for side, value in ((ring.core, mine[way * ring.chips + step]), (1 - ring.core, other)):
                out = lax.dynamic_update_slice_in_dim(out, value.astype(f32), row_of(side, way, slot), 0)
    return out


def place(ring, where, found, total, row_of=None, lead=1):
    mine, early, late = found
    height, width = mine[0].shape
    if row_of is None:
        row_of = lambda side, way, slot: ((side * 2 + way) * ring.chips + slot) * height
    if height % 8:
        return place_rows(ring, found, total, row_of, lead)
    return call(
        place_kernel(ring.chips, height, total, row_of, lead),
        [((total, width), f32)],
        where, *mine, early, late,
        in_specs=[SMEM] + [VMEM] * (len(mine) + 2),
    )[0]


def after(value, *others):
    return lax.optimization_barrier((value,) + others)[0]


def shards(clips, group, flat_params, w_fc1, w_fc2, w_up, w_down, patches, clip_ids, visible_index, cotangent):
    width = w_fc1.shape[1]
    ring = Ring(clips, group)
    core = ring.core.astype(jnp.int32).reshape(1)
    turns = [[(i, (i + k) % group) for i in range(group)] for k in range(1, group)]
    back_turns = [[(i, (i - k) % group) for i in range(group)] for k in range(1, group)]

    up_all = ring.fetch(w_up)
    down_all = ring.fetch(w_down)

    flat = flat_params.reshape(FLAT_ROWS, 128)
    w_qkv, w_proj, g_one, g_two = enc_prep(flat)
    x = jnp.pad(patches, ((0, PAD - VIS), (0, 0)))
    vis = jnp.pad(visible_index, (0, PAD - VIS), constant_values=-1)
    segment = jnp.where(vis < 0, -1, jnp.minimum(vis // SHORT_PATCHES, clip_ids[ROWS - 1]))
    qkv, probs, mix, first, in2 = call(
        enc_attend_kernel,
        [((PAD, 3 * D), bf16), ((HEADS, PAD, PAD), bf16), ((PAD, D), bf16), ((PAD, D), f32), ((PAD, D), bf16)],
        x, w_qkv, w_proj, g_one, g_two, segment[None, :], segment[:, None],
    )

    in2s, hiddens, slopes, parts = [in2], [], [], []
    for i in range(group):
        if i > 0:
            in2s.append(after(lax.ppermute(in2, "mlp", turns[i - 1]), parts[0]))
        part, hidden, slope = call(
            enc_ffn_kernel,
            [((PAD, D), f32 if i == 0 else bf16), ((PAD, width), bf16), ((PAD, width), bf16)],
            in2s[i], w_fc1, w_fc2,
        )
        hiddens.append(hidden)
        slopes.append(slope)
        parts.append(part if i == 0 else lax.ppermute(part, "mlp", back_turns[i - 1]))
    w_embed, mask_token, w_dqkv, w_dproj, gd_one, gd_two = dec_prep(flat, part)

    second_low, table, dec_norm = call(
        embed_kernel(group),
        [((PAD, D), bf16), ((PAD, 4 * DD), bf16), ((PAD, DD), bf16)],
        first, *parts, w_embed, mask_token, gd_one, w_dqkv,
    )
    decoded, up_part, down_part, wdproj_grad, gd_two_grad, packed = decoder(
        vis[None, :], table, cotangent, w_dproj, gd_two, up_all, down_all
    )
    up_mine = ring.scattered(up_part)
    down_mine = ring.scattered(down_part)
    second_grad, out_grad, dec_qkv_grad, embed_grad, gd_one_grad, mask_grad = call(
        embed_back_kernel,
        [
            ((PAD, D), f32), ((PAD, D), bf16), ((PAD, 3 * DD), bf16), ((PAD, DD), bf16), ((1, DD), f32), ((1, DD), f32),
        ],
        packed, table, dec_norm, second_low, gd_one, w_dqkv, w_embed,
    )
    dec_flat = call(
        dec_flat_kernel,
        [((DEC_ROWS, 128), bf16)],
        dec_norm, dec_qkv_grad, second_low, embed_grad, wdproj_grad, mask_grad, gd_one_grad, gd_two_grad,
        scratch_shapes=[pltpu.VMEM((DEC_ROWS, 128), f32)],
    )[0]

    out_grads, pre_grads, parts = [out_grad], [], []
    for i in range(group):
        if i > 0:
            out_grads.append(after(lax.ppermute(out_grad, "mlp", turns[i - 1]), parts[0], dec_flat))
        pre_grad, part = call(
            enc_ffn_back_kernel,
            [((PAD, width), bf16), ((PAD, D), f32 if i == 0 else bf16)],
            out_grads[i], slopes[i], w_fc1, w_fc2,
        )
        pre_grads.append(pre_grad)
        parts.append(part if i == 0 else lax.ppermute(part, "mlp", back_turns[i - 1]))
    fc1_halves = ring.halves(D, width)
    fc2_halves = ring.halves(width, D)
    fc1_keep, fc1_send, fc2_keep, fc2_send = call(
        enc_weights_kernel(group), [fc1_halves, fc1_halves, fc2_halves, fc2_halves],
        core, *in2s, *pre_grads, *hiddens, *out_grads,
        in_specs=[SMEM] + [VMEM] * (4 * group),
    )
    parts[1:] = [after(part, fc1_keep) for part in parts[1:]]
    height = -(-FLAT_ROWS // group // (CORES * 2 * ring.chips) // 8) * 8
    flat_halves = ((2, ring.chips, group, height, 128), bf16)
    input_grad, flat_keep, flat_send = call(
        enc_back_kernel(group, ring),
        [((VIS, D), f32), flat_halves, flat_halves],
        core, *parts, second_grad, first, x, qkv, probs, mix, w_qkv, w_proj, g_one, g_two, dec_flat,
        in_specs=[SMEM] + [VMEM] * (group + 11),
        scratch_shapes=[pltpu.VMEM((PAD, 3 * D), bf16), pltpu.VMEM((FLAT_ROWS, 128), f32)],
    )
    fc1_found, fc2_found, flat_found, up_found, down_found = in_step(
        (ring.round_trip(ring.start(fc1_keep, fc1_send)), 0),
        (ring.round_trip(ring.start(fc2_keep, fc2_send)), 0),
        (ring.round_trip(ring.start(flat_keep, flat_send)), 2),
        (ring.scattered_trip(up_mine), ring.chips + 2),
        (ring.scattered_trip(down_mine), ring.chips + 2),
    )
    where = jnp.stack([ring.core, ring.at]).astype(jnp.int32)
    return (
        decoded,
        input_grad,
        place(ring, where, flat_found, FLAT_ROWS // group).reshape(-1),
        place(ring, where, fc1_found, D),
        place(ring, where, fc2_found, width),
        place(ring, where, up_found, DD, ring.scattered_row(DD), 0),
        place(ring, where, down_found, w_down.shape[0], ring.scattered_row(w_down.shape[0]), 0),
    )


def solution(mesh):
    placed = (
        P(),
        P(None, "mlp"),
        P("mlp", None),
        P(None, "mlp"),
        P("mlp", None),
        P(("clips", "mlp"), None),
        P(("clips", "mlp")),
        P(("clips", "mlp")),
        P(("clips", "mlp"), None),
    )
    group = mesh.shape["mlp"]

    def body(*args):
        return shards(mesh.shape["clips"], group, *args)

    return jax.shard_map(
        body,
        mesh=mesh,
        in_specs=placed,
        out_specs=(
            P(("clips", "mlp"), None),
            P(("clips", "mlp"), None),
            P("mlp"),
            P(None, "mlp"),
            P("mlp", None),
            P(None, "mlp"),
            P("mlp", None),
        ),
        check_vma=False,
    )
```

```python
import math

import jax
import jax.numpy as jnp
from jax import lax
from jax.experimental import pallas as pl
from jax.experimental.pallas import tpu as pltpu
from jax.sharding import PartitionSpec as P

D = 768
HEADS = 12
DD = 512
DHEADS = 16
FREQ = 8
WIN = 4
ROWS = 1536
VIS = 312
PAD = 320
SHORT_PATCHES = 512
PARAMS = 3804160
EPSILON = 1e-06
BLOCK = 256
GROUP = WIN * FREQ
HALF = DD // 2
ENC_SCALE = 1.0 / math.sqrt(D // HEADS)
DEC_SCALE = 1.0 / math.sqrt(DD // DHEADS)
LOWEST = -1e30
CORES = 2
bf16 = jnp.bfloat16
f32 = jnp.float32


def mm(left, right):
    return jnp.dot(left, right, preferred_element_type=f32)


def mm_nt(left, right):
    return lax.dot_general(left, right, (((1,), (1,)), ((), ())), preferred_element_type=f32)


def mm_tn(left, right):
    return lax.dot_general(left, right, (((0,), (0,)), ((), ())), preferred_element_type=f32)


def normalize(rows):
    centred = rows - jnp.mean(rows, axis=-1, keepdims=True)
    scale = lax.rsqrt(jnp.mean(centred * centred, axis=-1, keepdims=True) + EPSILON)
    return centred * scale, scale


def norm_back(grad, normed, scale, gain):
    weighted = grad * gain
    return scale * (
        weighted
        - jnp.mean(weighted, axis=-1, keepdims=True)
        - normed * jnp.mean(weighted * normed, axis=-1, keepdims=True)
    )


def gelu_parts(pre):
    cdf = 0.5 * (1.0 + lax.erf(pre * math.sqrt(0.5)))
    return pre * cdf, cdf + pre * jnp.exp(-0.5 * pre * pre) * (1.0 / math.sqrt(2.0 * math.pi))


def gained(grad, normed):
    return jnp.sum(grad * normed, axis=0, keepdims=True)


SMEM = pl.BlockSpec(memory_space=pltpu.SMEM)
VMEM = pl.BlockSpec(memory_space=pltpu.VMEM)


def hint(us):
    return pl.CostEstimate(flops=int(us * 8e8), transcendentals=0, bytes_accessed=int(us * 1e6))


def call(body, outs, *args, us=5, **more):
    return pl.pallas_call(
        body,
        cost_estimate=hint(us),
        out_shape=[jax.ShapeDtypeStruct(shape, dtype) for shape, dtype in outs],
        compiler_params=pltpu.CompilerParams(vmem_limit_bytes=56 * 2**20),
        **more,
    )(*args)


TILES = {"wqkv": 18, "wproj": 6, "wemb": 4, "wdqkv": 12, "wdproj": 4}
G1_AT = (D * 3 * D + D * D) // 128
WEMB_AT = G1_AT + 12
MASK_AT = WEMB_AT + D * 4
WDQKV_AT = MASK_AT + 4
WDPROJ_AT = WDQKV_AT + DD * 12
GD1_AT = WDPROJ_AT + DD * 4
FLAT_ROWS = PARAMS // 128
DEC_ROWS = FLAT_ROWS - WEMB_AT
PREP = 64


def widen(flat_ref, first, out_ref, tiles):
    for t in range(tiles):
        out_ref[:, t * 128 : t * 128 + 128] = flat_ref[
            pl.ds(first + t, out_ref.shape[0], stride=tiles), :
        ].astype(bf16)


def vector(flat_ref, first, count):
    return jnp.concatenate([flat_ref[first + i : first + i + 1, :] for i in range(count)], axis=1)


def flatten(flat_ref, first, value, tiles):
    for t in range(tiles):
        flat_ref[pl.ds(first + t, value.shape[0], stride=tiles), :] = value[:, t * 128 : t * 128 + 128]


def enc_prep_kernel(qkv_ref, proj_ref, gains_ref, wqkv_ref, wproj_ref, g1_ref, g2_ref, qkv_flat, proj_flat, gains_flat):
    qkv_flat[...] = qkv_ref[...].astype(f32)
    proj_flat[...] = proj_ref[...].astype(f32)
    widen(qkv_flat, 0, wqkv_ref, 18)
    widen(proj_flat, 0, wproj_ref, 6)

    @pl.when(pl.program_id(0) == 0)
    def _():
        gains_flat[...] = gains_ref[...].astype(f32)
        g1_ref[...] = vector(gains_flat, 0, 6)
        g2_ref[...] = vector(gains_flat, 6, 6)


def enc_prep(flat):
    whole = lambda *shape: pl.BlockSpec(shape, lambda i: (0,) * len(shape))
    return pl.pallas_call(
        enc_prep_kernel,
        grid=(D // PREP,),
        in_specs=[
            pl.BlockSpec((PREP * 18, 128), lambda i: (i, 0)),
            pl.BlockSpec((PREP * 6, 128), lambda i: (D * 18 // (PREP * 6) + i, 0)),
            pl.BlockSpec((16, 128), lambda i: (G1_AT // 16, 0)),
        ],
        out_specs=[
            pl.BlockSpec((PREP, 3 * D), lambda i: (i, 0)),
            pl.BlockSpec((PREP, D), lambda i: (i, 0)),
            whole(1, D),
            whole(1, D),
        ],
        out_shape=[
            jax.ShapeDtypeStruct((D, 3 * D), bf16),
            jax.ShapeDtypeStruct((D, D), bf16),
            jax.ShapeDtypeStruct((1, D), f32),
            jax.ShapeDtypeStruct((1, D), f32),
        ],
        scratch_shapes=[
            pltpu.VMEM((PREP * 18, 128), f32), pltpu.VMEM((PREP * 6, 128), f32), pltpu.VMEM((16, 128), f32),
        ],
    )(flat, flat, flat)


def dec_prep_kernel(
    flat_ref, _, wemb_ref, mask_ref, wdqkv_ref, wdproj_ref, gd1_ref, gd2_ref, low, wide, sem,
):
    copy = pltpu.make_async_copy(flat_ref.at[pl.ds(G1_AT, FLAT_ROWS - G1_AT), :], low, sem)
    copy.start()
    copy.wait()
    wide[...] = low[...].astype(f32)
    widen(wide, WEMB_AT - G1_AT, wemb_ref, 4)
    widen(wide, WDQKV_AT - G1_AT, wdqkv_ref, 12)
    widen(wide, WDPROJ_AT - G1_AT, wdproj_ref, 4)
    mask_ref[...] = vector(wide, MASK_AT - G1_AT, 4)
    gd1_ref[...] = vector(wide, GD1_AT - G1_AT, 4)
    gd2_ref[...] = vector(wide, GD1_AT - G1_AT + 4, 4)


def dec_prep(flat, after):
    hbm = pl.BlockSpec(memory_space=pl.ANY)
    return call(
        dec_prep_kernel,
        [((D, DD), bf16), ((1, DD), f32), ((DD, 3 * DD), bf16), ((DD, DD), bf16), ((1, DD), f32), ((1, DD), f32)],
        flat, after,
        in_specs=[hbm, hbm],
        scratch_shapes=[
            pltpu.VMEM((FLAT_ROWS - G1_AT, 128), bf16), pltpu.VMEM((FLAT_ROWS - G1_AT, 128), f32),
            pltpu.SemaphoreType.DMA,
        ],
    )


def enc_attend_kernel(
    x_ref, wqkv_ref, wproj_ref, g1_ref, g2_ref, segr_ref, segc_ref,
    qkv_ref, probs_ref, mix_ref, first_ref, in2_ref,
):
    x = x_ref[...].astype(f32)
    normed, _ = normalize(x)
    qkv_ref[...] = mm((normed * g1_ref[...]).astype(bf16), wqkv_ref[...]).astype(bf16)
    allowed = segr_ref[...] == segc_ref[...]
    low_lanes = lax.broadcasted_iota(jnp.int32, (PAD, 128), 1) < 64
    for pair in range(HEADS // 2):
        at = slice(pair * 128, pair * 128 + 128)
        query = qkv_ref[:, at]
        key = qkv_ref[:, D + pair * 128 : D + pair * 128 + 128]
        value = qkv_ref[:, 2 * D + pair * 128 : 2 * D + pair * 128 + 128]
        mixed = []
        for side in range(2):
            mine = low_lanes if side == 0 else jnp.logical_not(low_lanes)
            own = jnp.where(mine, query.astype(f32), 0.0).astype(bf16)
            scores = jnp.where(allowed, mm_nt(own, key) * ENC_SCALE, LOWEST)
            top = jnp.max(scores, axis=-1, keepdims=True)
            raised = jnp.exp(scores - top)
            probs = (raised / jnp.sum(raised, axis=-1, keepdims=True)).astype(bf16)
            probs_ref[2 * pair + side] = probs
            mixed.append(mm(probs, value))
        mix_ref[:, at] = jnp.where(low_lanes, mixed[0], mixed[1]).astype(bf16)
    first = x + mm(mix_ref[...], wproj_ref[...])
    first_ref[...] = first
    normed2, _ = normalize(first)
    in2_ref[...] = (normed2 * g2_ref[...]).astype(bf16)


def enc_ffn_kernel(in2_ref, fc1_ref, fc2_ref, part_ref, hidden_ref, slope_ref):
    act, slope = gelu_parts(mm(in2_ref[...], fc1_ref[...]))
    hidden = act.astype(bf16)
    hidden_ref[...] = hidden
    slope_ref[...] = slope.astype(bf16)
    part_ref[...] = mm(hidden, fc2_ref[...]).astype(part_ref.dtype)


def enc_ffn_back_kernel(out_grad_ref, slope_ref, fc1_ref, fc2_ref, pre_grad_ref, part_ref):
    grad = mm_nt(out_grad_ref[...], fc2_ref[...]) * slope_ref[...].astype(f32)
    pre_grad = grad.astype(bf16)
    pre_grad_ref[...] = pre_grad
    part_ref[...] = mm_nt(pre_grad, fc1_ref[...]).astype(part_ref.dtype)


def slabs(rows):
    return jnp.concatenate([rows[:, t * 128 : t * 128 + 128] for t in range(rows.shape[1] // 128)], axis=0)


def enc_weights_kernel(count, chips):
    def body(core_ref, *refs):
        in2s, pre_grads, hiddens, out_grads = (refs[i * count : (i + 1) * count] for i in range(4))
        keep_ref, send_ref = refs[4 * count : 4 * count + 2]
        at = 0
        for lefts, rights in ((in2s, pre_grads), (hiddens, out_grads)):
            total = mm_tn(lefts[0][...], rights[0][...])
            for i in range(1, count):
                total = total + mm_tn(lefts[i][...], rights[i][...])
            height = total.shape[0] // (CORES * 2 * chips)
            rows = height * total.shape[1] // 128

            def split(target, half, total=total, height=height, rows=rows, at=at):
                for way in range(2):
                    for chip in range(chips):
                        first = ((half * 2 + way) * chips + chip) * height
                        target[way, chip, at : at + rows, :] = slabs(total[first : first + height].astype(bf16))

            for half in range(CORES):
                @pl.when(core_ref[0] == half)
                def _(half=half, split=split):
                    split(keep_ref, half)
                    split(send_ref, 1 - half)

            at += rows

    return body


def embed_kernel(count):
    def body(first_ref, own_ref, *refs):
        parts = refs[: count - 1]
        wemb_ref, mask_ref, gd1_ref, wdqkv_ref, second_ref, table_ref, norm_ref = refs[count - 1 :]
        second = first_ref[...] + own_ref[...]
        for part in parts:
            second += part[...].astype(f32)
        low = second.astype(bf16)
        second_ref[...] = low
        embedded = mm(low, wemb_ref[...]).astype(bf16).astype(f32)
        row = lax.broadcasted_iota(jnp.int32, (PAD, DD), 0)
        start = jnp.where(row == VIS, mask_ref[...], embedded)
        normed, _ = normalize(start)
        dec_norm = (normed * gd1_ref[...]).astype(bf16)
        norm_ref[...] = dec_norm
        table_ref[:, : 3 * DD] = mm(dec_norm, wdqkv_ref[...]).astype(bf16)
        table_ref[:, 3 * DD :] = start.astype(bf16)

    return body


def spread(rows, same):
    left = jnp.concatenate([rows[:, :128]] * 4, axis=0) * same
    right = jnp.concatenate([rows[:, 128:]] * 4, axis=0) * same
    none = jnp.zeros_like(left)
    return jnp.concatenate(
        [jnp.concatenate([left, none], axis=1), jnp.concatenate([none, right], axis=1)], axis=0
    )


def segment_max(rows):
    tiles = []
    lane = lax.broadcasted_iota(jnp.int32, (rows.shape[0], 128), 1)
    for t in range(rows.shape[1] // 128):
        tile = rows[:, t * 128 : t * 128 + 128]
        for step in (1, 2, 8, 16):
            other = jnp.where(
                lane & step == 0, pltpu.roll(tile, 128 - step, 1), pltpu.roll(tile, step, 1)
            )
            tile = jnp.maximum(tile, other)
        tiles.append(tile)
    return jnp.concatenate(tiles, axis=1)


def decoder_kernel(chunks, ring):
    def body(
        vis_ref, table_ref, cot_ref, wdproj_ref, gd2_ref, up_ref, down_ref,
        decoded_ref, ends_ref, proj_grad_ref, gd2_grad_ref, packed_ref,
        qkv_ref, mix_ref, s_ref, p_ref, l_ref, dmix_ref, ds_ref, d_ref, back_ref, same_ref, ones_ref,
        up_acc, down_acc, proj_acc, gd2_acc, packed_acc,
    ):
        step = pl.program_id(0)

        @pl.when(step == 0)
        def _():
            up_acc[...] = jnp.zeros_like(up_acc)
            down_acc[...] = jnp.zeros_like(down_acc)
            proj_acc[...] = jnp.zeros_like(proj_acc)
            gd2_acc[...] = jnp.zeros_like(gd2_acc)
            packed_acc[...] = jnp.zeros_like(packed_acc)
            head_row = lax.broadcasted_iota(jnp.int32, (HALF, HALF), 0) // GROUP
            head_lane = lax.broadcasted_iota(jnp.int32, (HALF, HALF), 1) // GROUP
            ones = (head_row == head_lane).astype(f32).astype(bf16)
            ones_ref[...] = ones
            same_ref[...] = ones[:128, :128]

        row = lax.broadcasted_iota(jnp.int32, (BLOCK, PAD), 0) + step * BLOCK
        named = row == vis_ref[...]
        col = lax.broadcasted_iota(jnp.int32, (BLOCK, PAD), 1)
        hit = jnp.max(jnp.where(named, 1.0, 0.0), axis=1, keepdims=True)
        one_hot = jnp.where(named, 1.0, jnp.where(col == VIS, 1.0 - hit, 0.0)).astype(bf16)
        qkv_ref[...] = mm(one_hot, table_ref[:, : 3 * DD]).astype(bf16)
        start = mm(one_hot, table_ref[:, 3 * DD :])

        lane = lax.broadcasted_iota(jnp.int32, (BLOCK, DD), 1)
        line = lax.broadcasted_iota(jnp.int32, (BLOCK, DD), 0)
        window = (lane % FREQ) // WIN == (line % FREQ) // WIN
        n_groups = BLOCK // GROUP

        def parts(group, half):
            at = pl.ds(pl.multiple_of(group * GROUP, GROUP), GROUP)
            return at, slice(half * HALF, (half + 1) * HALF)

        def scores(group, _):
            same = same_ref[...]
            for half in range(2):
                at, cols = parts(group, half)
                key = qkv_ref[at, DD + half * HALF : DD + (half + 1) * HALF]
                s_ref[at, cols] = mm_nt(qkv_ref[at, cols], spread(key, same))
            return 0

        lax.fori_loop(0, n_groups, scores, 0, unroll=4)
        raw = s_ref[...] * DEC_SCALE
        top = segment_max(raw)
        raised = jnp.where(window, jnp.exp(raw - top), 0.0)
        p_low = raised.astype(bf16)
        total = jnp.concatenate(
            [mm(p_low[:, :HALF], ones_ref[...]), mm(p_low[:, HALF:], ones_ref[...])], axis=1
        )
        l_ref[...] = top + jnp.log(total)
        p_ref[...] = (raised / total).astype(bf16)

        def mixes(group, _):
            same = same_ref[...]
            for half in range(2):
                at, cols = parts(group, half)
                value = qkv_ref[at, 2 * DD + half * HALF : 2 * DD + (half + 1) * HALF]
                mix_ref[at, cols] = mm(p_ref[at, cols], spread(value, same)).astype(bf16)
            return 0

        lax.fori_loop(0, n_groups, mixes, 0, unroll=4)

        middle = start + mm(mix_ref[...], wdproj_ref[...])
        normed, scale = normalize(middle)
        in2 = (normed * gd2_ref[...]).astype(bf16)
        cot = cot_ref[...]
        out = jnp.zeros_like(middle)
        in2_grad = jnp.zeros_like(middle)
        for c in range(chunks):
            act, slope = gelu_parts(mm(in2, up_ref[c]))
            hidden = act.astype(bf16)
            out += mm(hidden, down_ref[c])
            pre_grad = (mm_nt(cot, down_ref[c]) * slope).astype(bf16)
            in2_grad += mm_nt(pre_grad, up_ref[c])
            down_acc[c] += mm_tn(hidden, cot)
            up_acc[c] += mm_tn(in2, pre_grad)
        decoded_ref[...] = (middle + out).astype(bf16)

        gd2_acc[...] += gained(in2_grad, normed)
        middle_grad = cot.astype(f32) + norm_back(in2_grad, normed, scale, gd2_ref[...])
        branch = middle_grad.astype(bf16)
        back_ref[:, 3 * DD :] = branch
        proj_acc[...] += mm_tn(mix_ref[...], branch)
        dmix_ref[...] = mm_nt(branch, wdproj_ref[...]).astype(bf16)

        def prob_grads(group, _):
            same = same_ref[...]
            for half in range(2):
                at, cols = parts(group, half)
                value = qkv_ref[at, 2 * DD + half * HALF : 2 * DD + (half + 1) * HALF]
                s_ref[at, cols] = mm_nt(dmix_ref[at, cols], spread(value, same))
            return 0

        lax.fori_loop(0, n_groups, prob_grads, 0, unroll=4)
        probs = p_ref[...].astype(f32)
        prob_grad = s_ref[...]
        weighed = (probs * prob_grad).astype(bf16)
        row_sum = jnp.concatenate(
            [mm(weighed[:, :HALF], ones_ref[...]), mm(weighed[:, HALF:], ones_ref[...])], axis=1
        )
        d_ref[...] = row_sum
        ds_ref[...] = (probs * (prob_grad - row_sum)).astype(bf16)

        small_lane = lax.broadcasted_iota(jnp.int32, (GROUP, HALF), 1)
        small_line = lax.broadcasted_iota(jnp.int32, (GROUP, HALF), 0)
        pick = small_lane % GROUP == small_line
        small_window = (small_lane % FREQ) // WIN == (small_line % FREQ) // WIN

        def qkv_grads(group, _):
            same = same_ref[...]
            for half in range(2):
                at, cols = parts(group, half)
                key_cols = slice(DD + half * HALF, DD + (half + 1) * HALF)
                value_cols = slice(2 * DD + half * HALF, 2 * DD + (half + 1) * HALF)
                key = qkv_ref[at, key_cols]
                wide_query = spread(qkv_ref[at, cols], same)
                wide_mix_grad = spread(dmix_ref[at, cols], same)
                back_ref[at, cols] = (mm(ds_ref[at, cols], spread(key, same)) * DEC_SCALE).astype(bf16)
                log_total = jnp.sum(jnp.where(pick, l_ref[at, cols], 0.0), axis=0, keepdims=True)
                turned_sum = jnp.sum(jnp.where(pick, d_ref[at, cols], 0.0), axis=0, keepdims=True)
                turned = mm_nt(key, wide_query) * DEC_SCALE
                turned = jnp.where(small_window, jnp.exp(turned - log_total), 0.0)
                turned_grad = mm_nt(qkv_ref[at, value_cols], wide_mix_grad)
                score_grad = (turned * (turned_grad - turned_sum)).astype(bf16)
                back_ref[at, key_cols] = (mm(score_grad, wide_query) * DEC_SCALE).astype(bf16)
                back_ref[at, value_cols] = mm(turned.astype(bf16), wide_mix_grad).astype(bf16)
            return 0

        lax.fori_loop(0, n_groups, qkv_grads, 0, unroll=2)
        packed_acc[...] += mm_tn(one_hot, back_ref[...])

        @pl.when(step == pl.num_programs(0) - 1)
        def _():
            tall, low = DD // (CORES * 2 * ring.chips), up_acc.shape[2] // (CORES * 2 * ring.chips)
            cut = tall * up_acc.shape[2] // 128
            for clip in range(ring.clips):
                for way in range(2):
                    chip = (ring.places[clip // CORES] + (1 if way == 0 else -1)) % ring.chips
                    block = (clip % CORES * 2 + way) * ring.chips + chip
                    for y in range(chunks):
                        ends_ref[clip, y, way, :cut] = slabs(up_acc[y, block * tall : (block + 1) * tall].astype(bf16))
                        ends_ref[clip, y, way, cut:] = slabs(down_acc[y, block * low : (block + 1) * low].astype(bf16))
            proj_grad_ref[...] = proj_acc[...].astype(bf16)
            gd2_grad_ref[...] = gd2_acc[...]
            packed_ref[...] = packed_acc[...]

    return body


def decoder(ring, vis_row, table, cotangent, w_dproj, gd_two, up, down):
    chunks, _, width = up.shape
    rows = cotangent.shape[0]
    kept = lambda *shape: pl.BlockSpec(shape, lambda i: (0,) * len(shape), pipeline_mode=pl.Buffered(1))
    by_rows = pl.BlockSpec((BLOCK, DD), lambda i: (i, 0))
    ends = (ring.clips, chunks, 2, DD * width // (128 * ring.clips), 128)
    outs = [
        ((rows, DD), bf16, by_rows),
        (ends, bf16, kept(*ends)),
        ((DD, DD), bf16, kept(DD, DD)),
        ((1, DD), f32, kept(1, DD)),
        ((PAD, 4 * DD), f32, kept(PAD, 4 * DD)),
    ]
    return pl.pallas_call(
        decoder_kernel(chunks, ring),
        cost_estimate=hint(80),
        grid=(rows // BLOCK,),
        in_specs=[
            kept(1, PAD), kept(PAD, 4 * DD), by_rows, kept(DD, DD), kept(1, DD),
            kept(chunks, DD, width), kept(chunks, width, DD),
        ],
        out_specs=[spec for _, _, spec in outs],
        out_shape=[jax.ShapeDtypeStruct(shape, dtype) for shape, dtype, _ in outs],
        scratch_shapes=[
            pltpu.VMEM((BLOCK, 3 * DD), bf16),
            pltpu.VMEM((BLOCK, DD), bf16),
            pltpu.VMEM((BLOCK, DD), f32),
            pltpu.VMEM((BLOCK, DD), bf16),
            pltpu.VMEM((BLOCK, DD), f32),
            pltpu.VMEM((BLOCK, DD), bf16),
            pltpu.VMEM((BLOCK, DD), bf16),
            pltpu.VMEM((BLOCK, DD), f32),
            pltpu.VMEM((BLOCK, 4 * DD), bf16),
            pltpu.VMEM((128, 128), bf16),
            pltpu.VMEM((HALF, HALF), bf16),
            pltpu.VMEM((chunks, DD, width), f32),
            pltpu.VMEM((chunks, width, DD), f32),
            pltpu.VMEM((DD, DD), f32),
            pltpu.VMEM((1, DD), f32),
            pltpu.VMEM((PAD, 4 * DD), f32),
        ],
        compiler_params=pltpu.CompilerParams(vmem_limit_bytes=56 * 2**20),
    )(vis_row, table, cotangent, w_dproj, gd_two, up, down)


def embed_back_kernel(
    packed_ref, table_ref, norm_ref, second_ref, gd1_ref, wdqkv_ref, wemb_ref,
    second_grad_ref, out_grad_ref, qkv_grad_ref, embed_grad_ref, gd1_grad_ref, mask_grad_ref,
):
    qkv_grad = packed_ref[:, : 3 * DD].astype(bf16)
    qkv_grad_ref[...] = qkv_grad
    grad = mm_nt(qkv_grad, wdqkv_ref[...])
    normed, scale = normalize(table_ref[:, 3 * DD :].astype(f32))
    gd1_grad_ref[...] = gained(grad, normed)
    start_grad = packed_ref[:, 3 * DD :] + norm_back(grad, normed, scale, gd1_ref[...])
    mask_grad_ref[...] = start_grad[VIS : VIS + 1]
    row = lax.broadcasted_iota(jnp.int32, (PAD, DD), 0)
    embed_grad = jnp.where(row < VIS, start_grad, 0.0).astype(bf16)
    embed_grad_ref[...] = embed_grad
    second_grad = mm_nt(embed_grad, wemb_ref[...])
    second_grad_ref[...] = second_grad
    out_grad_ref[...] = second_grad.astype(bf16)


def dec_flat_kernel(
    norm_ref, qkv_grad_ref, second_ref, embed_grad_ref, proj_grad_ref, mask_grad_ref, gd1_grad_ref, gd2_grad_ref,
    flat_ref, wide,
):
    flatten(wide, 0, mm_tn(second_ref[...], embed_grad_ref[...]), 4)
    flatten(wide, MASK_AT - WEMB_AT, mask_grad_ref[...], 4)
    flatten(wide, WDQKV_AT - WEMB_AT, mm_tn(norm_ref[...], qkv_grad_ref[...]), 12)
    flatten(wide, WDPROJ_AT - WEMB_AT, proj_grad_ref[...].astype(f32), 4)
    flatten(wide, GD1_AT - WEMB_AT, gd1_grad_ref[...], 4)
    flatten(wide, GD1_AT + 4 - WEMB_AT, gd2_grad_ref[...], 4)
    flat_ref[...] = wide[...].astype(bf16)


def enc_back_kernel(count, ring):
    def body(core_ref, own_ref, *refs):
        parts = refs[: count - 1]
        (
            second_grad_ref, first_ref, x_ref, qkv_ref, probs_ref, mix_ref, wqkv_ref, wproj_ref, g1_ref, g2_ref,
            dec_flat_ref, input_grad_ref, keep_ref, send_ref, qkv_grad_ref, wide,
        ) = refs[count - 1 :]
        in2_grad = own_ref[...]
        for part in parts:
            in2_grad += part[...].astype(f32)
        normed2, scale2 = normalize(first_ref[...])
        flatten(wide, G1_AT + 6, gained(in2_grad, normed2), 6)
        first_grad = second_grad_ref[...] + norm_back(in2_grad, normed2, scale2, g2_ref[...])
        branch = first_grad.astype(bf16)
        flatten(wide, D * 18, mm_tn(mix_ref[...], branch), 6)
        wide[WEMB_AT:, :] = dec_flat_ref[...].astype(f32)
        mix_grad = mm_nt(branch, wproj_ref[...]).astype(bf16)
        low_lanes = lax.broadcasted_iota(jnp.int32, (PAD, 128), 1) < 64
        for pair in range(HEADS // 2):
            at = slice(pair * 128, pair * 128 + 128)
            query = qkv_ref[:, at]
            key = qkv_ref[:, D + pair * 128 : D + pair * 128 + 128]
            value = qkv_ref[:, 2 * D + pair * 128 : 2 * D + pair * 128 + 128]
            upstream = mix_grad[:, at]
            found = []
            for side in range(2):
                mine = low_lanes if side == 0 else jnp.logical_not(low_lanes)
                own = jnp.where(mine, upstream.astype(f32), 0.0).astype(bf16)
                low_probs = probs_ref[2 * pair + side]
                probs = low_probs.astype(f32)
                prob_grad = mm_nt(own, value)
                row_sum = jnp.sum(probs * prob_grad, axis=-1, keepdims=True)
                score_grad = (probs * (prob_grad - row_sum)).astype(bf16)
                found.append((mm(score_grad, key), mm_tn(score_grad, query), mm_tn(low_probs, upstream)))
            for part, factor in enumerate((ENC_SCALE, ENC_SCALE, 1.0)):
                merged = jnp.where(low_lanes, found[0][part], found[1][part]) * factor
                qkv_grad_ref[:, part * D + pair * 128 : part * D + pair * 128 + 128] = merged.astype(bf16)
        normed, scale = normalize(x_ref[...].astype(f32))
        flatten(wide, 0, mm_tn((normed * g1_ref[...]).astype(bf16), qkv_grad_ref[...]), 18)
        grad = mm_nt(qkv_grad_ref[...], wqkv_ref[...])
        flatten(wide, G1_AT, gained(grad, normed), 6)
        input_grad_ref[...] = (first_grad + norm_back(grad, normed, scale, g1_ref[...]))[:VIS]

        part = FLAT_ROWS // ring.group
        height = keep_ref.shape[3]

        def split(target, half):
            for way in range(2):
                for chip in range(ring.chips):
                    first = ((half * 2 + way) * ring.chips + chip) * height
                    for y in range(ring.group):
                        count = min(height, part - first)
                        if count > 0:
                            target[way, chip, y, :count] = wide[y * part + first : y * part + first + count, :].astype(bf16)
                        if count < height:
                            target[way, chip, y, max(count, 0) :] = jnp.zeros((height - max(count, 0), 128), bf16)

        for half in range(CORES):
            @pl.when(core_ref[0] == half)
            def _(half=half):
                split(keep_ref, half)
                split(send_ref, 1 - half)

    return body


class Ring:
    def __init__(self, clips, group):
        self.chips = clips // CORES
        self.group = group
        chips = self.chips
        if chips == 8:
            order = [4 * z // 2 for z in range(4)] + [4 * z // 2 + 1 for z in reversed(range(4))]
        else:
            order = list(range(chips))
        place = [0] * chips
        for at, chip in enumerate(order):
            place[chip] = at
        clip = lax.axis_index("clips")
        self.places = place
        self.core = clip % CORES
        chip = clip // CORES
        if chips == 8:
            self.at = jnp.where(chip % 2 == 0, chip // 2, 7 - chip // 2)
        else:
            self.at = chip
        self.lane = lax.axis_index("mlp")
        step = lambda way: [
            (order[i] * CORES + c, order[(i + way) % chips] * CORES + c) for i in range(chips) for c in range(CORES)
        ]
        self.ways = (step(1), step(-1))
        self.swap = [(i, i ^ 1) for i in range(clips)]
        self.clips = clips

    def clip_of(self, side, slot):
        chip = jnp.where(slot < 4, 2 * slot, 15 - 2 * slot) if self.chips == 8 else slot
        return chip * CORES + side


    def fetch(self, block):
        half = block.shape[0] // CORES
        mine = lax.dynamic_slice_in_dim(block, self.core * half, half, 0)
        blocks = [block]
        for k in range(1, self.group):
            near = lax.ppermute(mine, "mlp", [(j, (j - k) % self.group) for j in range(self.group)])
            far = self.swapped(near)
            low, high = (jnp.where(self.core == side, near, far) for side in range(CORES))
            blocks.append(jnp.concatenate([low, high]))
        stacked = jnp.stack(blocks)
        if self.group == 2:
            return jnp.where(self.lane == 0, stacked, stacked[::-1])
        return jnp.roll(stacked, self.lane, axis=0)

    def swapped(self, value):
        return lax.ppermute(value, "clips", self.swap)

    def block(self, half, way, back):
        sign = 1 if way == 0 else -1
        return lax.dynamic_index_in_dim(half[way], (self.at - sign * back) % self.chips, 0, False)

    def start(self, keep, send):
        return keep + self.swapped(send)

    def round_trip(self, half, ends=None):
        held = [self.block(half, way, 0) for way in range(2)]
        for step in range(1, self.chips):
            came = [lax.ppermute(held[way], "clips", self.ways[way]) for way in range(2)]
            held = yield [came[way] + self.block(half, way, step) for way in range(2)]
        if ends is not None:
            both = [jnp.concatenate([held[way], ends[way]], axis=1) for way in range(2)]
            held = self.over_group(both)
        return (yield from self.spread(held))

    def over_group(self, held):
        both = jnp.stack(held, axis=1)
        total = lax.dynamic_index_in_dim(both, self.lane, 0, False)
        for k in range(1, self.group):
            away = lax.dynamic_index_in_dim(both, (self.lane + k) % self.group, 0, False)
            total = total + lax.ppermute(away, "mlp", [(j, (j + k) % self.group) for j in range(self.group)])
        return [total[0], total[1]]

    def spread(self, held):
        found = [[held[0]], [held[1]]]
        cut = self.chips - 2
        early = None
        for step in range(1, self.chips):
            came = yield [lax.ppermute(found[way][-1], "clips", self.ways[way]) for way in range(2)]
            for way in range(2):
                found[way].append(came[way])
            if step == cut - 1:
                early = self.swapped(jnp.stack(found[0] + found[1]))
        late = self.swapped(jnp.stack(found[0][cut:] + found[1][cut:]))
        return found[0] + found[1], early, late


def side_by_side(one, two, lead):
    trips, done = (one, two), [None, None]
    kept = [None, None]

    def advance(i):
        try:
            value = next(trips[i]) if kept[i] is None else trips[i].send(kept[i])
        except StopIteration as end:
            done[i] = end.value
            return
        other = kept[1 - i]
        kept[i] = value if other is None else lax.optimization_barrier((value, other))[0]

    for _ in range(lead):
        advance(0)
    while done[0] is None or done[1] is None:
        for i in range(2):
            if done[i] is None:
                advance(i)
    return done


def place_kernel(chips, parts):
    cut = chips - 2

    def body(where_ref, *refs):
        mine, early, late, outs = refs[: 2 * chips], refs[2 * chips], refs[2 * chips + 1], refs[2 * chips + 2 :]
        core, at = where_ref[0], where_ref[1]

        def put(out, height, row, value):
            total = out.shape[0]
            short = total % height
            if short == 0:
                out[pl.ds(pl.multiple_of(row, 8), height), :] = value
                return

            @pl.when(row + height <= total)
            def _():
                out[pl.ds(pl.multiple_of(row, 8), height), :] = value

            @pl.when(row + height > total)
            def _():
                out[total - short :, :] = value[:short]

        def put_all(side, way, slot, value):
            first = 0
            for out, (_, columns, height) in zip(outs, parts):
                tiles = columns // 128
                row = ((side * 2 + way) * chips + slot) * height
                wide = [value[first + t * height : first + (t + 1) * height] for t in range(tiles)]
                put(out, height, row, jnp.concatenate(wide, axis=1) if tiles > 1 else wide[0])
                first += tiles * height

        for way in range(2):
            sign = 1 if way == 0 else -1
            for step in range(chips):
                slot = lax.rem(at + sign * (1 - step) + chips, chips)
                put_all(core, way, slot, mine[way * chips + step][...].astype(f32))
                other = early[way * cut + step] if step < cut else late[way * 2 + step - cut]
                put_all(1 - core, way, slot, other.astype(f32))

    return body


def place_rows(ring, found, parts):
    mine, early, late = found
    chips, cut = ring.chips, ring.chips - 2
    outs = []
    first = 0
    for total, columns, height in parts:
        tiles = columns // 128
        out = jnp.zeros((CORES * 2 * chips * height, columns), f32)
        for way in range(2):
            for step in range(chips):
                slot = (ring.at + (1 if way == 0 else -1) * (1 - step)) % chips
                other = early[way * cut + step] if step < cut else late[way * 2 + step - cut]
                for side, value in ((ring.core, mine[way * chips + step]), (1 - ring.core, other)):
                    value = value[first : first + tiles * height].reshape(tiles, height, 128)
                    value = value.transpose(1, 0, 2).reshape(height, columns).astype(f32)
                    row = ((side * 2 + way) * chips + slot) * height
                    out = lax.dynamic_update_slice_in_dim(out, value, row, 0)
        outs.append(out[:total])
        first += tiles * height
    return outs


def place(ring, where, found, shapes):
    mine, early, late = found
    blocks = CORES * 2 * ring.chips
    parts = [(total, columns, height or total // blocks) for total, columns, height in shapes]
    if any(height % 8 for _, _, height in parts):
        return place_rows(ring, found, parts)
    return call(
        place_kernel(ring.chips, parts),
        [((total, columns), f32) for total, columns, _ in parts],
        where, *mine, early, late,
        in_specs=[SMEM] + [VMEM] * (len(mine) + 2),
    )


def after(value, *others):
    return lax.optimization_barrier((value,) + others)[0]


def shards(clips, group, flat_params, w_fc1, w_fc2, w_up, w_down, patches, clip_ids, visible_index, cotangent):
    width = w_fc1.shape[1]
    ring = Ring(clips, group)
    core = ring.core.astype(jnp.int32).reshape(1)
    turns = [[(i, (i + k) % group) for i in range(group)] for k in range(1, group)]
    back_turns = [[(i, (i - k) % group) for i in range(group)] for k in range(1, group)]

    up_all = ring.fetch(w_up)
    down_all = ring.fetch(w_down)

    flat = flat_params.reshape(FLAT_ROWS, 128)
    w_qkv, w_proj, g_one, g_two = enc_prep(flat)
    x = jnp.pad(patches, ((0, PAD - VIS), (0, 0)))
    vis = jnp.pad(visible_index, (0, PAD - VIS), constant_values=-1)
    segment = jnp.where(vis < 0, -1, jnp.minimum(vis // SHORT_PATCHES, clip_ids[ROWS - 1]))
    qkv, probs, mix, first, in2 = call(
        enc_attend_kernel,
        [((PAD, 3 * D), bf16), ((HEADS, PAD, PAD), bf16), ((PAD, D), bf16), ((PAD, D), f32), ((PAD, D), bf16)],
        x, w_qkv, w_proj, g_one, g_two, segment[None, :], segment[:, None],
    )

    in2s, hiddens, slopes, parts = [in2], [], [], []
    for i in range(group):
        if i > 0:
            in2s.append(after(lax.ppermute(in2, "mlp", turns[i - 1]), parts[0]))
        part, hidden, slope = call(
            enc_ffn_kernel,
            [((PAD, D), f32 if i == 0 else bf16), ((PAD, width), bf16), ((PAD, width), bf16)],
            in2s[i], w_fc1, w_fc2,
        )
        hiddens.append(hidden)
        slopes.append(slope)
        parts.append(part if i == 0 else lax.ppermute(part, "mlp", back_turns[i - 1]))
    w_embed, mask_token, w_dqkv, w_dproj, gd_one, gd_two = dec_prep(flat, part)

    second_low, table, dec_norm = call(
        embed_kernel(group),
        [((PAD, D), bf16), ((PAD, 4 * DD), bf16), ((PAD, DD), bf16)],
        first, *parts, w_embed, mask_token, gd_one, w_dqkv,
    )
    decoded, ends, wdproj_grad, gd_two_grad, packed = decoder(
        ring, vis[None, :], table, cotangent, w_dproj, gd_two, up_all, down_all
    )
    ends = lax.psum_scatter(ends.reshape(-1, 128), "clips", scatter_dimension=0, tiled=True)
    ends = ends.reshape(group, 2, -1, 128)
    second_grad, out_grad, dec_qkv_grad, embed_grad, gd_one_grad, mask_grad = call(
        embed_back_kernel,
        [
            ((PAD, D), f32), ((PAD, D), bf16), ((PAD, 3 * DD), bf16), ((PAD, DD), bf16), ((1, DD), f32), ((1, DD), f32),
        ],
        packed, table, dec_norm, second_low, gd_one, w_dqkv, w_embed,
    )
    dec_flat = call(
        dec_flat_kernel,
        [((DEC_ROWS, 128), bf16)],
        dec_norm, dec_qkv_grad, second_low, embed_grad, wdproj_grad, mask_grad, gd_one_grad, gd_two_grad,
        scratch_shapes=[pltpu.VMEM((DEC_ROWS, 128), f32)],
    )[0]

    out_grads, pre_grads, parts = [out_grad], [], []
    for i in range(group):
        if i > 0:
            out_grads.append(after(lax.ppermute(out_grad, "mlp", turns[i - 1]), parts[0], dec_flat))
        pre_grad, part = call(
            enc_ffn_back_kernel,
            [((PAD, width), bf16), ((PAD, D), f32 if i == 0 else bf16)],
            out_grads[i], slopes[i], w_fc1, w_fc2,
        )
        pre_grads.append(pre_grad)
        parts.append(part if i == 0 else lax.ppermute(part, "mlp", back_turns[i - 1]))
    fc_halves = ((2, ring.chips, 2 * D * width // (CORES * 2 * ring.chips * 128), 128), bf16)
    fc_keep, fc_send = call(
        enc_weights_kernel(group, ring.chips), [fc_halves, fc_halves],
        core, *in2s, *pre_grads, *hiddens, *out_grads,
        in_specs=[SMEM] + [VMEM] * (4 * group),
        us=10,
    )
    parts[1:] = [after(part, fc_keep) for part in parts[1:]]
    height = -(-FLAT_ROWS // group // (CORES * 2 * ring.chips) // 8) * 8
    flat_halves = ((2, ring.chips, group, height, 128), bf16)
    input_grad, flat_keep, flat_send = call(
        enc_back_kernel(group, ring),
        [((VIS, D), f32), flat_halves, flat_halves],
        core, *parts, second_grad, first, x, qkv, probs, mix, w_qkv, w_proj, g_one, g_two, dec_flat,
        in_specs=[SMEM] + [VMEM] * (group + 11),
        scratch_shapes=[pltpu.VMEM((PAD, 3 * D), bf16), pltpu.VMEM((FLAT_ROWS, 128), f32)],
        us=20,
    )
    fc_found, flat_found = side_by_side(
        ring.round_trip(ring.start(fc_keep, fc_send)),
        ring.round_trip(ring.start(flat_keep, flat_send), [ends[:, 0], ends[:, 1]]),
        2,
    )
    where = jnp.stack([ring.core, ring.at]).astype(jnp.int32)
    fc1_grad, fc2_grad = place(ring, where, fc_found, [(D, width, 0), (width, D, 0)])
    param_grad, up_grad, down_grad = place(
        ring, where, flat_found,
        [(FLAT_ROWS // group, 128, height), (DD, w_up.shape[1], 0), (w_up.shape[1], DD, 0)],
    )
    return decoded, input_grad, param_grad.reshape(-1), fc1_grad, fc2_grad, up_grad, down_grad


def solution(mesh):
    placed = (
        P(),
        P(None, "mlp"),
        P("mlp", None),
        P(None, "mlp"),
        P("mlp", None),
        P(("clips", "mlp"), None),
        P(("clips", "mlp")),
        P(("clips", "mlp")),
        P(("clips", "mlp"), None),
    )
    group = mesh.shape["mlp"]

    def body(*args):
        return shards(mesh.shape["clips"], group, *args)

    return jax.shard_map(
        body,
        mesh=mesh,
        in_specs=placed,
        out_specs=(
            P(("clips", "mlp"), None),
            P(("clips", "mlp"), None),
            P("mlp"),
            P(None, "mlp"),
            P("mlp", None),
            P(None, "mlp"),
            P("mlp", None),
        ),
        check_vma=False,
    )
```

```python
import math

import jax
import jax.numpy as jnp
from jax import lax
from jax.experimental import pallas as pl
from jax.experimental.pallas import tpu as pltpu
from jax.sharding import PartitionSpec as P

D = 768
HEADS = 12
DD = 512
DHEADS = 16
FREQ = 8
WIN = 4
ROWS = 1536
VIS = 312
PAD = 320
SHORT_PATCHES = 512
PARAMS = 3804160
EPSILON = 1e-06
BLOCK = 256
GROUP = WIN * FREQ
HALF = DD // 2
ENC_SCALE = 1.0 / math.sqrt(D // HEADS)
DEC_SCALE = 1.0 / math.sqrt(DD // DHEADS)
LOWEST = -1e30
CORES = 2
bf16 = jnp.bfloat16
f32 = jnp.float32


def mm(left, right):
    return jnp.dot(left, right, preferred_element_type=f32)


def mm_nt(left, right):
    return lax.dot_general(left, right, (((1,), (1,)), ((), ())), preferred_element_type=f32)


def mm_tn(left, right):
    return lax.dot_general(left, right, (((0,), (0,)), ((), ())), preferred_element_type=f32)


def normalize(rows):
    centred = rows - jnp.mean(rows, axis=-1, keepdims=True)
    scale = lax.rsqrt(jnp.mean(centred * centred, axis=-1, keepdims=True) + EPSILON)
    return centred * scale, scale


def norm_back(grad, normed, scale, gain):
    weighted = grad * gain
    return scale * (
        weighted
        - jnp.mean(weighted, axis=-1, keepdims=True)
        - normed * jnp.mean(weighted * normed, axis=-1, keepdims=True)
    )


def gelu_parts(pre):
    cdf = 0.5 * (1.0 + lax.erf(pre * math.sqrt(0.5)))
    return pre * cdf, cdf + pre * jnp.exp(-0.5 * pre * pre) * (1.0 / math.sqrt(2.0 * math.pi))


def gained(grad, normed):
    return jnp.sum(grad * normed, axis=0, keepdims=True)


SMEM = pl.BlockSpec(memory_space=pltpu.SMEM)
VMEM = pl.BlockSpec(memory_space=pltpu.VMEM)


def hint(us):
    return pl.CostEstimate(flops=int(us * 8e8), transcendentals=0, bytes_accessed=int(us * 1e6))


def call(body, outs, *args, us=5, **more):
    return pl.pallas_call(
        body,
        cost_estimate=hint(us),
        out_shape=[jax.ShapeDtypeStruct(shape, dtype) for shape, dtype in outs],
        compiler_params=pltpu.CompilerParams(vmem_limit_bytes=56 * 2**20),
        **more,
    )(*args)


TILES = {"wqkv": 18, "wproj": 6, "wemb": 4, "wdqkv": 12, "wdproj": 4}
G1_AT = (D * 3 * D + D * D) // 128
WEMB_AT = G1_AT + 12
MASK_AT = WEMB_AT + D * 4
WDQKV_AT = MASK_AT + 4
WDPROJ_AT = WDQKV_AT + DD * 12
GD1_AT = WDPROJ_AT + DD * 4
FLAT_ROWS = PARAMS // 128
DEC_ROWS = FLAT_ROWS - WEMB_AT
PREP = 64


def widen(flat_ref, first, out_ref, tiles):
    for t in range(tiles):
        out_ref[:, t * 128 : t * 128 + 128] = flat_ref[
            pl.ds(first + t, out_ref.shape[0], stride=tiles), :
        ].astype(bf16)


def vector(flat_ref, first, count):
    return jnp.concatenate([flat_ref[first + i : first + i + 1, :] for i in range(count)], axis=1)


def flatten(flat_ref, first, value, tiles):
    for t in range(tiles):
        flat_ref[pl.ds(first + t, value.shape[0], stride=tiles), :] = value[:, t * 128 : t * 128 + 128]


def enc_prep_kernel(qkv_ref, proj_ref, gains_ref, wqkv_ref, wproj_ref, g1_ref, g2_ref, qkv_flat, proj_flat, gains_flat):
    qkv_flat[...] = qkv_ref[...].astype(f32)
    proj_flat[...] = proj_ref[...].astype(f32)
    widen(qkv_flat, 0, wqkv_ref, 18)
    widen(proj_flat, 0, wproj_ref, 6)

    @pl.when(pl.program_id(0) == 0)
    def _():
        gains_flat[...] = gains_ref[...].astype(f32)
        g1_ref[...] = vector(gains_flat, 0, 6)
        g2_ref[...] = vector(gains_flat, 6, 6)


def enc_prep(flat):
    whole = lambda *shape: pl.BlockSpec(shape, lambda i: (0,) * len(shape))
    return pl.pallas_call(
        enc_prep_kernel,
        grid=(D // PREP,),
        in_specs=[
            pl.BlockSpec((PREP * 18, 128), lambda i: (i, 0)),
            pl.BlockSpec((PREP * 6, 128), lambda i: (D * 18 // (PREP * 6) + i, 0)),
            pl.BlockSpec((16, 128), lambda i: (G1_AT // 16, 0)),
        ],
        out_specs=[
            pl.BlockSpec((PREP, 3 * D), lambda i: (i, 0)),
            pl.BlockSpec((PREP, D), lambda i: (i, 0)),
            whole(1, D),
            whole(1, D),
        ],
        out_shape=[
            jax.ShapeDtypeStruct((D, 3 * D), bf16),
            jax.ShapeDtypeStruct((D, D), bf16),
            jax.ShapeDtypeStruct((1, D), f32),
            jax.ShapeDtypeStruct((1, D), f32),
        ],
        scratch_shapes=[
            pltpu.VMEM((PREP * 18, 128), f32), pltpu.VMEM((PREP * 6, 128), f32), pltpu.VMEM((16, 128), f32),
        ],
    )(flat, flat, flat)


def dec_prep_kernel(count):
    def body(where_ref, flat_ref, _, *refs):
        ups, downs = refs[: 2 * count - 1], refs[2 * count - 1 : 4 * count - 2]
        (
            wemb_ref, mask_ref, wdqkv_ref, wdproj_ref, gd1_ref, gd2_ref, up_ref, down_ref, low, wide, sem,
        ) = refs[4 * count - 2 :]
        copy = pltpu.make_async_copy(flat_ref.at[pl.ds(G1_AT, FLAT_ROWS - G1_AT), :], low, sem)
        copy.start()
        core, lane = where_ref[0], where_ref[1]
        for pieces, whole in ((ups, up_ref), (downs, down_ref)):
            half = whole.shape[1] // CORES
            whole[lane] = pieces[0][...]
            for k in range(1, count):
                at = lax.rem(lane + k, count)
                near = pl.multiple_of(core * half, 8)
                far = pl.multiple_of((1 - core) * half, 8)
                whole[at, pl.ds(near, half), :] = pieces[2 * k - 1][...]
                whole[at, pl.ds(far, half), :] = pieces[2 * k][...]
        copy.wait()
        wide[...] = low[...].astype(f32)
        widen(wide, WEMB_AT - G1_AT, wemb_ref, 4)
        widen(wide, WDQKV_AT - G1_AT, wdqkv_ref, 12)
        widen(wide, WDPROJ_AT - G1_AT, wdproj_ref, 4)
        mask_ref[...] = vector(wide, MASK_AT - G1_AT, 4)
        gd1_ref[...] = vector(wide, GD1_AT - G1_AT, 4)
        gd2_ref[...] = vector(wide, GD1_AT - G1_AT + 4, 4)

    return body


def dec_prep(ring, flat, ups, downs, later):
    hbm = pl.BlockSpec(memory_space=pl.ANY)
    whole = lambda block: ((ring.group,) + block.shape, bf16)
    return call(
        dec_prep_kernel(ring.group),
        [
            ((D, DD), bf16), ((1, DD), f32), ((DD, 3 * DD), bf16), ((DD, DD), bf16), ((1, DD), f32), ((1, DD), f32),
            whole(ups[0]), whole(downs[0]),
        ],
        jnp.stack([ring.core, ring.lane]).astype(jnp.int32), flat, later, *ups, *downs,
        in_specs=[SMEM, hbm, hbm] + [VMEM] * (len(ups) + len(downs)),
        scratch_shapes=[
            pltpu.VMEM((FLAT_ROWS - G1_AT, 128), bf16), pltpu.VMEM((FLAT_ROWS - G1_AT, 128), f32),
            pltpu.SemaphoreType.DMA,
        ],
    )


def enc_attend_kernel(
    patches_ref, visible_ref, ids_ref, wqkv_ref, wproj_ref, g1_ref, g2_ref,
    x_ref, vis_ref, qkv_ref, probs_ref, mix_ref, first_ref, in2_ref, wide_vis,
):
    x_ref[...] = jnp.concatenate(
        [patches_ref[...].astype(f32), jnp.zeros((PAD - VIS, D), f32)], axis=0
    ).astype(bf16)
    wide_vis[...] = jnp.full(wide_vis.shape, -1, jnp.int32)
    wide_vis[:, :VIS] = visible_ref[...]
    vis = wide_vis[:, :PAD]
    vis_ref[...] = vis
    last = jnp.max(ids_ref[...].astype(f32))
    clip = jnp.where(vis < 0, -1.0, jnp.minimum((vis // SHORT_PATCHES).astype(f32), last))
    square = (PAD, PAD)
    across = jnp.broadcast_to(clip, square)
    diagonal = lax.broadcasted_iota(jnp.int32, square, 0) == lax.broadcasted_iota(jnp.int32, square, 1)
    allowed = across == jnp.sum(jnp.where(diagonal, across, 0.0), axis=1, keepdims=True)
    x = x_ref[...].astype(f32)
    normed, _ = normalize(x)
    qkv_ref[...] = mm((normed * g1_ref[...]).astype(bf16), wqkv_ref[...]).astype(bf16)
    low_lanes = lax.broadcasted_iota(jnp.int32, (PAD, 128), 1) < 64
    for pair in range(HEADS // 2):
        at = slice(pair * 128, pair * 128 + 128)
        query = qkv_ref[:, at]
        key = qkv_ref[:, D + pair * 128 : D + pair * 128 + 128]
        value = qkv_ref[:, 2 * D + pair * 128 : 2 * D + pair * 128 + 128]
        mixed = []
        for side in range(2):
            mine = low_lanes if side == 0 else jnp.logical_not(low_lanes)
            own = jnp.where(mine, query.astype(f32), 0.0).astype(bf16)
            scores = jnp.where(allowed, mm_nt(own, key) * ENC_SCALE, LOWEST)
            top = jnp.max(scores, axis=-1, keepdims=True)
            raised = jnp.exp(scores - top)
            probs = (raised / jnp.sum(raised, axis=-1, keepdims=True)).astype(bf16)
            probs_ref[2 * pair + side] = probs
            mixed.append(mm(probs, value))
        mix_ref[:, at] = jnp.where(low_lanes, mixed[0], mixed[1]).astype(bf16)
    first = x + mm(mix_ref[...], wproj_ref[...])
    first_ref[...] = first
    normed2, _ = normalize(first)
    in2_ref[...] = (normed2 * g2_ref[...]).astype(bf16)


def enc_ffn_kernel(in2_ref, fc1_ref, fc2_ref, part_ref, hidden_ref, slope_ref):
    act, slope = gelu_parts(mm(in2_ref[...], fc1_ref[...]))
    hidden = act.astype(bf16)
    hidden_ref[...] = hidden
    slope_ref[...] = slope.astype(bf16)
    part_ref[...] = mm(hidden, fc2_ref[...]).astype(part_ref.dtype)


def enc_ffn_back_kernel(out_grad_ref, slope_ref, fc1_ref, fc2_ref, pre_grad_ref, part_ref):
    grad = mm_nt(out_grad_ref[...], fc2_ref[...]) * slope_ref[...].astype(f32)
    pre_grad = grad.astype(bf16)
    pre_grad_ref[...] = pre_grad
    part_ref[...] = mm_nt(pre_grad, fc1_ref[...]).astype(part_ref.dtype)


def slabs(rows):
    return jnp.concatenate([rows[:, t * 128 : t * 128 + 128] for t in range(rows.shape[1] // 128)], axis=0)


def enc_weights_kernel(count, chips):
    def body(core_ref, *refs):
        in2s, pre_grads, hiddens, out_grads = (refs[i * count : (i + 1) * count] for i in range(4))
        keep_ref, send_ref = refs[4 * count : 4 * count + 2]
        at = 0
        for lefts, rights in ((in2s, pre_grads), (hiddens, out_grads)):
            total = mm_tn(lefts[0][...], rights[0][...])
            for i in range(1, count):
                total = total + mm_tn(lefts[i][...], rights[i][...])
            height = total.shape[0] // (CORES * 2 * chips)
            rows = height * total.shape[1] // 128

            def split(target, half, total=total, height=height, rows=rows, at=at):
                for way in range(2):
                    for chip in range(chips):
                        first = ((half * 2 + way) * chips + chip) * height
                        target[way, chip, at : at + rows, :] = slabs(total[first : first + height].astype(bf16))

            for half in range(CORES):
                @pl.when(core_ref[0] == half)
                def _(half=half, split=split):
                    split(keep_ref, half)
                    split(send_ref, 1 - half)

            at += rows

    return body


def embed_kernel(count):
    def body(first_ref, own_ref, *refs):
        parts = refs[: count - 1]
        wemb_ref, mask_ref, gd1_ref, wdqkv_ref, second_ref, table_ref, norm_ref = refs[count - 1 :]
        second = first_ref[...] + own_ref[...]
        for part in parts:
            second += part[...].astype(f32)
        low = second.astype(bf16)
        second_ref[...] = low
        embedded = mm(low, wemb_ref[...]).astype(bf16).astype(f32)
        row = lax.broadcasted_iota(jnp.int32, (PAD, DD), 0)
        start = jnp.where(row == VIS, mask_ref[...], embedded)
        normed, _ = normalize(start)
        dec_norm = (normed * gd1_ref[...]).astype(bf16)
        norm_ref[...] = dec_norm
        table_ref[:, : 3 * DD] = mm(dec_norm, wdqkv_ref[...]).astype(bf16)
        table_ref[:, 3 * DD :] = start.astype(bf16)

    return body


def spread(rows, same):
    left = jnp.concatenate([rows[:, :128]] * 4, axis=0) * same
    right = jnp.concatenate([rows[:, 128:]] * 4, axis=0) * same
    none = jnp.zeros_like(left)
    return jnp.concatenate(
        [jnp.concatenate([left, none], axis=1), jnp.concatenate([none, right], axis=1)], axis=0
    )


def segment_max(rows):
    tiles = []
    lane = lax.broadcasted_iota(jnp.int32, (rows.shape[0], 128), 1)
    for t in range(rows.shape[1] // 128):
        tile = rows[:, t * 128 : t * 128 + 128]
        for step in (1, 2, 8, 16):
            other = jnp.where(
                lane & step == 0, pltpu.roll(tile, 128 - step, 1), pltpu.roll(tile, step, 1)
            )
            tile = jnp.maximum(tile, other)
        tiles.append(tile)
    return jnp.concatenate(tiles, axis=1)


def decoder_kernel(chunks, ring):
    def body(
        vis_ref, table_ref, cot_ref, wdproj_ref, gd2_ref, up_ref, down_ref,
        decoded_ref, ends_ref, proj_grad_ref, gd2_grad_ref, packed_ref,
        qkv_ref, mix_ref, s_ref, p_ref, l_ref, dmix_ref, ds_ref, d_ref, back_ref, same_ref, ones_ref,
        up_acc, down_acc, proj_acc, gd2_acc, packed_acc,
    ):
        step = pl.program_id(0)

        @pl.when(step == 0)
        def _():
            up_acc[...] = jnp.zeros_like(up_acc)
            down_acc[...] = jnp.zeros_like(down_acc)
            proj_acc[...] = jnp.zeros_like(proj_acc)
            gd2_acc[...] = jnp.zeros_like(gd2_acc)
            packed_acc[...] = jnp.zeros_like(packed_acc)
            head_row = lax.broadcasted_iota(jnp.int32, (HALF, HALF), 0) // GROUP
            head_lane = lax.broadcasted_iota(jnp.int32, (HALF, HALF), 1) // GROUP
            ones = (head_row == head_lane).astype(f32).astype(bf16)
            ones_ref[...] = ones
            same_ref[...] = ones[:128, :128]

        row = lax.broadcasted_iota(jnp.int32, (BLOCK, PAD), 0) + step * BLOCK
        named = row == vis_ref[...]
        col = lax.broadcasted_iota(jnp.int32, (BLOCK, PAD), 1)
        hit = jnp.max(jnp.where(named, 1.0, 0.0), axis=1, keepdims=True)
        one_hot = jnp.where(named, 1.0, jnp.where(col == VIS, 1.0 - hit, 0.0)).astype(bf16)
        qkv_ref[...] = mm(one_hot, table_ref[:, : 3 * DD]).astype(bf16)
        start = mm(one_hot, table_ref[:, 3 * DD :])

        lane = lax.broadcasted_iota(jnp.int32, (BLOCK, DD), 1)
        line = lax.broadcasted_iota(jnp.int32, (BLOCK, DD), 0)
        window = (lane % FREQ) // WIN == (line % FREQ) // WIN
        n_groups = BLOCK // GROUP

        def parts(group, half):
            at = pl.ds(pl.multiple_of(group * GROUP, GROUP), GROUP)
            return at, slice(half * HALF, (half + 1) * HALF)

        def scores(group, _):
            same = same_ref[...]
            for half in range(2):
                at, cols = parts(group, half)
                key = qkv_ref[at, DD + half * HALF : DD + (half + 1) * HALF]
                s_ref[at, cols] = mm_nt(qkv_ref[at, cols], spread(key, same))
            return 0

        lax.fori_loop(0, n_groups, scores, 0, unroll=8)
        raw = s_ref[...] * DEC_SCALE
        top = segment_max(raw)
        raised = jnp.where(window, jnp.exp(raw - top), 0.0)
        p_low = raised.astype(bf16)
        total = jnp.concatenate(
            [mm(p_low[:, :HALF], ones_ref[...]), mm(p_low[:, HALF:], ones_ref[...])], axis=1
        )
        l_ref[...] = top + jnp.log(total)
        p_ref[...] = (raised / total).astype(bf16)

        def mixes(group, _):
            same = same_ref[...]
            for half in range(2):
                at, cols = parts(group, half)
                value = qkv_ref[at, 2 * DD + half * HALF : 2 * DD + (half + 1) * HALF]
                mix_ref[at, cols] = mm(p_ref[at, cols], spread(value, same)).astype(bf16)
            return 0

        lax.fori_loop(0, n_groups, mixes, 0, unroll=8)

        middle = start + mm(mix_ref[...], wdproj_ref[...])
        normed, scale = normalize(middle)
        in2 = (normed * gd2_ref[...]).astype(bf16)
        cot = cot_ref[...]
        out = jnp.zeros_like(middle)
        in2_grad = jnp.zeros_like(middle)
        for c in range(chunks):
            act, slope = gelu_parts(mm(in2, up_ref[c]))
            hidden = act.astype(bf16)
            out += mm(hidden, down_ref[c])
            pre_grad = (mm_nt(cot, down_ref[c]) * slope).astype(bf16)
            in2_grad += mm_nt(pre_grad, up_ref[c])
            down_acc[c] += mm_tn(hidden, cot)
            up_acc[c] += mm_tn(in2, pre_grad)
        decoded_ref[...] = (middle + out).astype(bf16)

        gd2_acc[...] += gained(in2_grad, normed)
        middle_grad = cot.astype(f32) + norm_back(in2_grad, normed, scale, gd2_ref[...])
        branch = middle_grad.astype(bf16)
        back_ref[:, 3 * DD :] = branch
        proj_acc[...] += mm_tn(mix_ref[...], branch)
        dmix_ref[...] = mm_nt(branch, wdproj_ref[...]).astype(bf16)

        def prob_grads(group, _):
            same = same_ref[...]
            for half in range(2):
                at, cols = parts(group, half)
                value = qkv_ref[at, 2 * DD + half * HALF : 2 * DD + (half + 1) * HALF]
                s_ref[at, cols] = mm_nt(dmix_ref[at, cols], spread(value, same))
            return 0

        lax.fori_loop(0, n_groups, prob_grads, 0, unroll=8)
        probs = p_ref[...].astype(f32)
        prob_grad = s_ref[...]
        weighed = (probs * prob_grad).astype(bf16)
        row_sum = jnp.concatenate(
            [mm(weighed[:, :HALF], ones_ref[...]), mm(weighed[:, HALF:], ones_ref[...])], axis=1
        )
        d_ref[...] = row_sum
        ds_ref[...] = (probs * (prob_grad - row_sum)).astype(bf16)

        small_lane = lax.broadcasted_iota(jnp.int32, (GROUP, HALF), 1)
        small_line = lax.broadcasted_iota(jnp.int32, (GROUP, HALF), 0)
        pick = small_lane % GROUP == small_line
        small_window = (small_lane % FREQ) // WIN == (small_line % FREQ) // WIN

        def qkv_grads(group, _):
            same = same_ref[...]
            for half in range(2):
                at, cols = parts(group, half)
                key_cols = slice(DD + half * HALF, DD + (half + 1) * HALF)
                value_cols = slice(2 * DD + half * HALF, 2 * DD + (half + 1) * HALF)
                key = qkv_ref[at, key_cols]
                wide_query = spread(qkv_ref[at, cols], same)
                wide_mix_grad = spread(dmix_ref[at, cols], same)
                back_ref[at, cols] = (mm(ds_ref[at, cols], spread(key, same)) * DEC_SCALE).astype(bf16)
                log_total = jnp.sum(jnp.where(pick, l_ref[at, cols], 0.0), axis=0, keepdims=True)
                turned_sum = jnp.sum(jnp.where(pick, d_ref[at, cols], 0.0), axis=0, keepdims=True)
                turned = mm_nt(key, wide_query) * DEC_SCALE
                turned = jnp.where(small_window, jnp.exp(turned - log_total), 0.0)
                turned_grad = mm_nt(qkv_ref[at, value_cols], wide_mix_grad)
                score_grad = (turned * (turned_grad - turned_sum)).astype(bf16)
                back_ref[at, key_cols] = (mm(score_grad, wide_query) * DEC_SCALE).astype(bf16)
                back_ref[at, value_cols] = mm(turned.astype(bf16), wide_mix_grad).astype(bf16)
            return 0

        lax.fori_loop(0, n_groups, qkv_grads, 0, unroll=8)
        packed_acc[...] += mm_tn(one_hot, back_ref[...])

        @pl.when(step == pl.num_programs(0) - 1)
        def _():
            tall, low = DD // (CORES * 2 * ring.chips), up_acc.shape[2] // (CORES * 2 * ring.chips)
            cut = tall * up_acc.shape[2] // 128
            for clip in range(ring.clips):
                for way in range(2):
                    chip = (ring.places[clip // CORES] + (1 if way == 0 else -1)) % ring.chips
                    block = (clip % CORES * 2 + way) * ring.chips + chip
                    for y in range(chunks):
                        ends_ref[clip, y, way, :cut] = slabs(up_acc[y, block * tall : (block + 1) * tall].astype(bf16))
                        ends_ref[clip, y, way, cut:] = slabs(down_acc[y, block * low : (block + 1) * low].astype(bf16))
            proj_grad_ref[...] = proj_acc[...].astype(bf16)
            gd2_grad_ref[...] = gd2_acc[...]
            packed_ref[...] = packed_acc[...]

    return body


def decoder(ring, vis_row, table, cotangent, w_dproj, gd_two, up, down):
    chunks, _, width = up.shape
    rows = cotangent.shape[0]
    kept = lambda *shape: pl.BlockSpec(shape, lambda i: (0,) * len(shape), pipeline_mode=pl.Buffered(1))
    by_rows = pl.BlockSpec((BLOCK, DD), lambda i: (i, 0))
    ends = (ring.clips, chunks, 2, DD * width // (128 * ring.clips), 128)
    outs = [
        ((rows, DD), bf16, by_rows),
        (ends, bf16, kept(*ends)),
        ((DD, DD), bf16, kept(DD, DD)),
        ((1, DD), f32, kept(1, DD)),
        ((PAD, 4 * DD), f32, kept(PAD, 4 * DD)),
    ]
    return pl.pallas_call(
        decoder_kernel(chunks, ring),
        cost_estimate=hint(80),
        grid=(rows // BLOCK,),
        in_specs=[
            kept(1, PAD), kept(PAD, 4 * DD), by_rows, kept(DD, DD), kept(1, DD),
            kept(chunks, DD, width), kept(chunks, width, DD),
        ],
        out_specs=[spec for _, _, spec in outs],
        out_shape=[jax.ShapeDtypeStruct(shape, dtype) for shape, dtype, _ in outs],
        scratch_shapes=[
            pltpu.VMEM((BLOCK, 3 * DD), bf16),
            pltpu.VMEM((BLOCK, DD), bf16),
            pltpu.VMEM((BLOCK, DD), f32),
            pltpu.VMEM((BLOCK, DD), bf16),
            pltpu.VMEM((BLOCK, DD), f32),
            pltpu.VMEM((BLOCK, DD), bf16),
            pltpu.VMEM((BLOCK, DD), bf16),
            pltpu.VMEM((BLOCK, DD), f32),
            pltpu.VMEM((BLOCK, 4 * DD), bf16),
            pltpu.VMEM((128, 128), bf16),
            pltpu.VMEM((HALF, HALF), bf16),
            pltpu.VMEM((chunks, DD, width), f32),
            pltpu.VMEM((chunks, width, DD), f32),
            pltpu.VMEM((DD, DD), f32),
            pltpu.VMEM((1, DD), f32),
            pltpu.VMEM((PAD, 4 * DD), f32),
        ],
        compiler_params=pltpu.CompilerParams(vmem_limit_bytes=56 * 2**20),
    )(vis_row, table, cotangent, w_dproj, gd_two, up, down)


def embed_back_kernel(
    packed_ref, table_ref, norm_ref, second_ref, gd1_ref, wdqkv_ref, wemb_ref,
    second_grad_ref, out_grad_ref, qkv_grad_ref, embed_grad_ref, gd1_grad_ref, mask_grad_ref,
):
    qkv_grad = packed_ref[:, : 3 * DD].astype(bf16)
    qkv_grad_ref[...] = qkv_grad
    grad = mm_nt(qkv_grad, wdqkv_ref[...])
    normed, scale = normalize(table_ref[:, 3 * DD :].astype(f32))
    gd1_grad_ref[...] = gained(grad, normed)
    start_grad = packed_ref[:, 3 * DD :] + norm_back(grad, normed, scale, gd1_ref[...])
    mask_grad_ref[...] = start_grad[VIS : VIS + 1]
    row = lax.broadcasted_iota(jnp.int32, (PAD, DD), 0)
    embed_grad = jnp.where(row < VIS, start_grad, 0.0).astype(bf16)
    embed_grad_ref[...] = embed_grad
    second_grad = mm_nt(embed_grad, wemb_ref[...])
    second_grad_ref[...] = second_grad
    out_grad_ref[...] = second_grad.astype(bf16)


def dec_flat_kernel(
    norm_ref, qkv_grad_ref, second_ref, embed_grad_ref, proj_grad_ref, mask_grad_ref, gd1_grad_ref, gd2_grad_ref,
    flat_ref, wide,
):
    flatten(wide, 0, mm_tn(second_ref[...], embed_grad_ref[...]), 4)
    flatten(wide, MASK_AT - WEMB_AT, mask_grad_ref[...], 4)
    flatten(wide, WDQKV_AT - WEMB_AT, mm_tn(norm_ref[...], qkv_grad_ref[...]), 12)
    flatten(wide, WDPROJ_AT - WEMB_AT, proj_grad_ref[...].astype(f32), 4)
    flatten(wide, GD1_AT - WEMB_AT, gd1_grad_ref[...], 4)
    flatten(wide, GD1_AT + 4 - WEMB_AT, gd2_grad_ref[...], 4)
    flat_ref[...] = wide[...].astype(bf16)


def enc_back_kernel(count, ring):
    def body(core_ref, own_ref, *refs):
        parts = refs[: count - 1]
        (
            second_grad_ref, first_ref, x_ref, qkv_ref, probs_ref, mix_ref, wqkv_ref, wproj_ref, g1_ref, g2_ref,
            dec_flat_ref, input_grad_ref, keep_ref, send_ref, qkv_grad_ref, wide,
        ) = refs[count - 1 :]
        in2_grad = own_ref[...]
        for part in parts:
            in2_grad += part[...].astype(f32)
        normed2, scale2 = normalize(first_ref[...])
        flatten(wide, G1_AT + 6, gained(in2_grad, normed2), 6)
        first_grad = second_grad_ref[...] + norm_back(in2_grad, normed2, scale2, g2_ref[...])
        branch = first_grad.astype(bf16)
        flatten(wide, D * 18, mm_tn(mix_ref[...], branch), 6)
        wide[WEMB_AT:, :] = dec_flat_ref[...].astype(f32)
        mix_grad = mm_nt(branch, wproj_ref[...]).astype(bf16)
        low_lanes = lax.broadcasted_iota(jnp.int32, (PAD, 128), 1) < 64
        for pair in range(HEADS // 2):
            at = slice(pair * 128, pair * 128 + 128)
            query = qkv_ref[:, at]
            key = qkv_ref[:, D + pair * 128 : D + pair * 128 + 128]
            value = qkv_ref[:, 2 * D + pair * 128 : 2 * D + pair * 128 + 128]
            upstream = mix_grad[:, at]
            found = []
            for side in range(2):
                mine = low_lanes if side == 0 else jnp.logical_not(low_lanes)
                own = jnp.where(mine, upstream.astype(f32), 0.0).astype(bf16)
                low_probs = probs_ref[2 * pair + side]
                probs = low_probs.astype(f32)
                prob_grad = mm_nt(own, value)
                row_sum = jnp.sum(probs * prob_grad, axis=-1, keepdims=True)
                score_grad = (probs * (prob_grad - row_sum)).astype(bf16)
                found.append((mm(score_grad, key), mm_tn(score_grad, query), mm_tn(low_probs, upstream)))
            for part, factor in enumerate((ENC_SCALE, ENC_SCALE, 1.0)):
                merged = jnp.where(low_lanes, found[0][part], found[1][part]) * factor
                qkv_grad_ref[:, part * D + pair * 128 : part * D + pair * 128 + 128] = merged.astype(bf16)
        normed, scale = normalize(x_ref[...].astype(f32))
        flatten(wide, 0, mm_tn((normed * g1_ref[...]).astype(bf16), qkv_grad_ref[...]), 18)
        grad = mm_nt(qkv_grad_ref[...], wqkv_ref[...])
        flatten(wide, G1_AT, gained(grad, normed), 6)
        input_grad_ref[...] = (first_grad + norm_back(grad, normed, scale, g1_ref[...]))[:VIS]

        part = FLAT_ROWS // ring.group
        height = keep_ref.shape[3]

        def split(target, half):
            for way in range(2):
                for chip in range(ring.chips):
                    first = ((half * 2 + way) * ring.chips + chip) * height
                    for y in range(ring.group):
                        count = min(height, part - first)
                        if count > 0:
                            target[way, chip, y, :count] = wide[y * part + first : y * part + first + count, :].astype(bf16)
                        if count < height:
                            target[way, chip, y, max(count, 0) :] = jnp.zeros((height - max(count, 0), 128), bf16)

        for half in range(CORES):
            @pl.when(core_ref[0] == half)
            def _(half=half):
                split(keep_ref, half)
                split(send_ref, 1 - half)

    return body


class Ring:
    def __init__(self, clips, group):
        self.chips = clips // CORES
        self.group = group
        chips = self.chips
        if chips == 8:
            order = [4 * z // 2 for z in range(4)] + [4 * z // 2 + 1 for z in reversed(range(4))]
        else:
            order = list(range(chips))
        place = [0] * chips
        for at, chip in enumerate(order):
            place[chip] = at
        clip = lax.axis_index("clips")
        self.places = place
        self.core = clip % CORES
        chip = clip // CORES
        if chips == 8:
            self.at = jnp.where(chip % 2 == 0, chip // 2, 7 - chip // 2)
        else:
            self.at = chip
        self.lane = lax.axis_index("mlp")
        step = lambda way: [
            (order[i] * CORES + c, order[(i + way) % chips] * CORES + c) for i in range(chips) for c in range(CORES)
        ]
        self.ways = (step(1), step(-1))
        self.swap = [(i, i ^ 1) for i in range(clips)]
        self.clips = clips

    def clip_of(self, side, slot):
        chip = jnp.where(slot < 4, 2 * slot, 15 - 2 * slot) if self.chips == 8 else slot
        return chip * CORES + side


    def fetch(self, block):
        half = block.shape[0] // CORES
        mine = lax.dynamic_slice_in_dim(block, self.core * half, half, 0)
        pieces = [block]
        for k in range(1, self.group):
            near = lax.ppermute(mine, "mlp", [(j, (j - k) % self.group) for j in range(self.group)])
            pieces += [near, self.swapped(near)]
        return pieces

    def swapped(self, value):
        return lax.ppermute(value, "clips", self.swap)

    def block(self, half, way, back):
        sign = 1 if way == 0 else -1
        return lax.dynamic_index_in_dim(half[way], (self.at - sign * back) % self.chips, 0, False)

    def start(self, keep, send):
        return keep + self.swapped(send)

    def round_trip(self, half, ends=None):
        held = [self.block(half, way, 0) for way in range(2)]
        for step in range(1, self.chips):
            came = [lax.ppermute(held[way], "clips", self.ways[way]) for way in range(2)]
            held = [came[way] + self.block(half, way, step) for way in range(2)]
            if ends is not None and step == 2:
                held, ends = lax.optimization_barrier((held, ends))
            held = yield held
        if ends is not None:
            both = [jnp.concatenate([held[way], ends[way]], axis=1) for way in range(2)]
            held = self.over_group(both)
        return (yield from self.spread(held))

    def over_group(self, held):
        both = jnp.stack(held, axis=1)
        total = lax.dynamic_index_in_dim(both, self.lane, 0, False)
        for k in range(1, self.group):
            away = lax.dynamic_index_in_dim(both, (self.lane + k) % self.group, 0, False)
            total = total + lax.ppermute(away, "mlp", [(j, (j + k) % self.group) for j in range(self.group)])
        return [total[0], total[1]]

    def spread(self, held):
        found = [[held[0]], [held[1]]]
        cut = self.chips - 2
        early = None
        for step in range(1, self.chips):
            came = yield [lax.ppermute(found[way][-1], "clips", self.ways[way]) for way in range(2)]
            for way in range(2):
                found[way].append(came[way])
            if step == cut - 1:
                early = self.swapped(jnp.stack(found[0] + found[1]))
        late = self.swapped(jnp.stack(found[0][cut:] + found[1][cut:]))
        return found[0] + found[1], early, late


def side_by_side(one, two, lead):
    trips, done = (one, two), [None, None]
    kept = [None, None]

    def advance(i):
        try:
            value = next(trips[i]) if kept[i] is None else trips[i].send(kept[i])
        except StopIteration as end:
            done[i] = end.value
            return
        other = kept[1 - i]
        kept[i] = value if other is None else lax.optimization_barrier((value, other))[0]

    for _ in range(lead):
        advance(0)
    while done[0] is None or done[1] is None:
        for i in range(2):
            if done[i] is None:
                advance(i)
    return done


def place_kernel(chips, parts):
    cut = chips - 2

    def body(where_ref, *refs):
        mine, early, late, outs = refs[: 2 * chips], refs[2 * chips], refs[2 * chips + 1], refs[2 * chips + 2 :]
        core, at = where_ref[0], where_ref[1]

        def put(out, height, row, value):
            total = out.shape[0]
            short = total % height
            if short == 0:
                out[pl.ds(pl.multiple_of(row, 8), height), :] = value
                return

            @pl.when(row + height <= total)
            def _():
                out[pl.ds(pl.multiple_of(row, 8), height), :] = value

            @pl.when(row + height > total)
            def _():
                out[total - short :, :] = value[:short]

        def put_all(side, way, slot, value):
            first = 0
            for out, (_, columns, height) in zip(outs, parts):
                tiles = columns // 128
                row = ((side * 2 + way) * chips + slot) * height
                wide = [value[first + t * height : first + (t + 1) * height] for t in range(tiles)]
                put(out, height, row, jnp.concatenate(wide, axis=1) if tiles > 1 else wide[0])
                first += tiles * height

        for way in range(2):
            sign = 1 if way == 0 else -1
            for step in range(chips):
                slot = lax.rem(at + sign * (1 - step) + chips, chips)
                put_all(core, way, slot, mine[way * chips + step][...].astype(f32))
                other = early[way * cut + step] if step < cut else late[way * 2 + step - cut]
                put_all(1 - core, way, slot, other.astype(f32))

    return body


def place_rows(ring, found, parts):
    mine, early, late = found
    chips, cut = ring.chips, ring.chips - 2
    outs = []
    first = 0
    for total, columns, height in parts:
        tiles = columns // 128
        out = jnp.zeros((CORES * 2 * chips * height, columns), f32)
        for way in range(2):
            for step in range(chips):
                slot = (ring.at + (1 if way == 0 else -1) * (1 - step)) % chips
                other = early[way * cut + step] if step < cut else late[way * 2 + step - cut]
                for side, value in ((ring.core, mine[way * chips + step]), (1 - ring.core, other)):
                    value = value[first : first + tiles * height].reshape(tiles, height, 128)
                    value = value.transpose(1, 0, 2).reshape(height, columns).astype(f32)
                    row = ((side * 2 + way) * chips + slot) * height
                    out = lax.dynamic_update_slice_in_dim(out, value, row, 0)
        outs.append(out[:total])
        first += tiles * height
    return outs


def place(ring, where, found, shapes):
    mine, early, late = found
    blocks = CORES * 2 * ring.chips
    parts = [(total, columns, height or total // blocks) for total, columns, height in shapes]
    if any(height % 8 for _, _, height in parts):
        return place_rows(ring, found, parts)
    return call(
        place_kernel(ring.chips, parts),
        [((total, columns), f32) for total, columns, _ in parts],
        where, *mine, early, late,
        in_specs=[SMEM] + [VMEM] * (len(mine) + 2),
    )


def after(value, *others):
    return lax.optimization_barrier((value,) + others)[0]


def shards(clips, group, flat_params, w_fc1, w_fc2, w_up, w_down, patches, clip_ids, visible_index, cotangent):
    width = w_fc1.shape[1]
    ring = Ring(clips, group)
    core = ring.core.astype(jnp.int32).reshape(1)
    turns = [[(i, (i + k) % group) for i in range(group)] for k in range(1, group)]
    back_turns = [[(i, (i - k) % group) for i in range(group)] for k in range(1, group)]

    ups = ring.fetch(w_up)
    downs = ring.fetch(w_down)

    flat = flat_params.reshape(FLAT_ROWS, 128)
    w_qkv, w_proj, g_one, g_two = enc_prep(flat)
    x, vis, qkv, probs, mix, first, in2 = call(
        enc_attend_kernel,
        [
            ((PAD, D), bf16), ((1, PAD), jnp.int32), ((PAD, 3 * D), bf16), ((HEADS, PAD, PAD), bf16), ((PAD, D), bf16),
            ((PAD, D), f32), ((PAD, D), bf16),
        ],
        patches, visible_index[None, :], clip_ids.reshape(-1, 128), w_qkv, w_proj, g_one, g_two,
        scratch_shapes=[pltpu.VMEM((1, 384), jnp.int32)],
        us=11,
    )

    in2s, hiddens, slopes, parts = [in2], [], [], []
    for i in range(group):
        if i > 0:
            in2s.append(after(lax.ppermute(in2, "mlp", turns[i - 1]), parts[0]))
        part, hidden, slope = call(
            enc_ffn_kernel,
            [((PAD, D), f32 if i == 0 else bf16), ((PAD, width), bf16), ((PAD, width), bf16)],
            in2s[i], w_fc1, w_fc2,
        )
        hiddens.append(hidden)
        slopes.append(slope)
        parts.append(part if i == 0 else lax.ppermute(part, "mlp", back_turns[i - 1]))
    w_embed, mask_token, w_dqkv, w_dproj, gd_one, gd_two, up_all, down_all = dec_prep(ring, flat, ups, downs, part)

    second_low, table, dec_norm = call(
        embed_kernel(group),
        [((PAD, D), bf16), ((PAD, 4 * DD), bf16), ((PAD, DD), bf16)],
        first, *parts, w_embed, mask_token, gd_one, w_dqkv,
    )
    decoded, ends, wdproj_grad, gd_two_grad, packed = decoder(
        ring, vis, table, cotangent, w_dproj, gd_two, up_all, down_all
    )
    ends = lax.psum_scatter(ends.reshape(-1, 128), "clips", scatter_dimension=0, tiled=True)
    ends = ends.reshape(group, 2, -1, 128)
    second_grad, out_grad, dec_qkv_grad, embed_grad, gd_one_grad, mask_grad = call(
        embed_back_kernel,
        [
            ((PAD, D), f32), ((PAD, D), bf16), ((PAD, 3 * DD), bf16), ((PAD, DD), bf16), ((1, DD), f32), ((1, DD), f32),
        ],
        packed, table, dec_norm, second_low, gd_one, w_dqkv, w_embed,
    )
    dec_flat = call(
        dec_flat_kernel,
        [((DEC_ROWS, 128), bf16)],
        dec_norm, dec_qkv_grad, second_low, embed_grad, wdproj_grad, mask_grad, gd_one_grad, gd_two_grad,
        scratch_shapes=[pltpu.VMEM((DEC_ROWS, 128), f32)],
    )[0]

    out_grads, pre_grads, parts = [out_grad], [], []
    for i in range(group):
        if i > 0:
            out_grads.append(after(lax.ppermute(out_grad, "mlp", turns[i - 1]), parts[0], dec_flat))
        pre_grad, part = call(
            enc_ffn_back_kernel,
            [((PAD, width), bf16), ((PAD, D), f32 if i == 0 else bf16)],
            out_grads[i], slopes[i], w_fc1, w_fc2,
        )
        pre_grads.append(pre_grad)
        parts.append(part if i == 0 else lax.ppermute(part, "mlp", back_turns[i - 1]))
    fc_halves = ((2, ring.chips, 2 * D * width // (CORES * 2 * ring.chips * 128), 128), bf16)
    fc_keep, fc_send = call(
        enc_weights_kernel(group, ring.chips), [fc_halves, fc_halves],
        core, *in2s, *pre_grads, *hiddens, *out_grads,
        in_specs=[SMEM] + [VMEM] * (4 * group),
        us=10,
    )
    parts[1:] = [after(part, fc_keep) for part in parts[1:]]
    height = -(-FLAT_ROWS // group // (CORES * 2 * ring.chips) // 8) * 8
    flat_halves = ((2, ring.chips, group, height, 128), bf16)
    input_grad, flat_keep, flat_send = call(
        enc_back_kernel(group, ring),
        [((VIS, D), f32), flat_halves, flat_halves],
        core, *parts, second_grad, first, x, qkv, probs, mix, w_qkv, w_proj, g_one, g_two, dec_flat,
        in_specs=[SMEM] + [VMEM] * (group + 11),
        scratch_shapes=[pltpu.VMEM((PAD, 3 * D), bf16), pltpu.VMEM((FLAT_ROWS, 128), f32)],
        us=20,
    )
    fc_found, flat_found = side_by_side(
        ring.round_trip(ring.start(fc_keep, fc_send)),
        ring.round_trip(ring.start(flat_keep, flat_send), [ends[:, 0], ends[:, 1]]),
        2,
    )
    where = jnp.stack([ring.core, ring.at]).astype(jnp.int32)
    fc1_grad, fc2_grad = place(ring, where, fc_found, [(D, width, 0), (width, D, 0)])
    param_grad, up_grad, down_grad = place(
        ring, where, flat_found,
        [(FLAT_ROWS // group, 128, height), (DD, w_up.shape[1], 0), (w_up.shape[1], DD, 0)],
    )
    return decoded, input_grad, param_grad.reshape(-1), fc1_grad, fc2_grad, up_grad, down_grad


def solution(mesh):
    placed = (
        P(),
        P(None, "mlp"),
        P("mlp", None),
        P(None, "mlp"),
        P("mlp", None),
        P(("clips", "mlp"), None),
        P(("clips", "mlp")),
        P(("clips", "mlp")),
        P(("clips", "mlp"), None),
    )
    group = mesh.shape["mlp"]

    def body(*args):
        return shards(mesh.shape["clips"], group, *args)

    return jax.shard_map(
        body,
        mesh=mesh,
        in_specs=placed,
        out_specs=(
            P(("clips", "mlp"), None),
            P(("clips", "mlp"), None),
            P("mlp"),
            P(None, "mlp"),
            P("mlp", None),
            P(None, "mlp"),
            P("mlp", None),
        ),
        check_vma=False,
    )
```

```python
import math

import jax
import jax.numpy as jnp
from jax import lax
from jax.experimental import pallas as pl
from jax.experimental.pallas import tpu as pltpu
from jax.sharding import PartitionSpec as P

D = 768
HEADS = 12
DD = 512
DHEADS = 16
FREQ = 8
WIN = 4
ROWS = 1536
VIS = 312
PAD = 320
SHORT_PATCHES = 512
PARAMS = 3804160
EPSILON = 1e-06
BLOCK = 256
GROUP = WIN * FREQ
HALF = DD // 2
ENC_SCALE = 1.0 / math.sqrt(D // HEADS)
DEC_SCALE = 1.0 / math.sqrt(DD // DHEADS)
LOWEST = -1e30
CORES = 2
bf16 = jnp.bfloat16
f32 = jnp.float32


def mm(left, right):
    return jnp.dot(left, right, preferred_element_type=f32)


def mm_nt(left, right):
    return lax.dot_general(left, right, (((1,), (1,)), ((), ())), preferred_element_type=f32)


def mm_tn(left, right):
    return lax.dot_general(left, right, (((0,), (0,)), ((), ())), preferred_element_type=f32)


def normalize(rows):
    centred = rows - jnp.mean(rows, axis=-1, keepdims=True)
    scale = lax.rsqrt(jnp.mean(centred * centred, axis=-1, keepdims=True) + EPSILON)
    return centred * scale, scale


def norm_back(grad, normed, scale, gain):
    weighted = grad * gain
    return scale * (
        weighted
        - jnp.mean(weighted, axis=-1, keepdims=True)
        - normed * jnp.mean(weighted * normed, axis=-1, keepdims=True)
    )


def gelu_parts(pre):
    cdf = 0.5 * (1.0 + lax.erf(pre * math.sqrt(0.5)))
    return pre * cdf, cdf + pre * jnp.exp(-0.5 * pre * pre) * (1.0 / math.sqrt(2.0 * math.pi))


def gained(grad, normed):
    return jnp.sum(grad * normed, axis=0, keepdims=True)


SMEM = pl.BlockSpec(memory_space=pltpu.SMEM)
VMEM = pl.BlockSpec(memory_space=pltpu.VMEM)


def hint(us):
    return pl.CostEstimate(flops=int(us * 8e8), transcendentals=0, bytes_accessed=int(us * 1e6))


def call(body, outs, *args, us=5, **more):
    return pl.pallas_call(
        body,
        cost_estimate=hint(us),
        out_shape=[jax.ShapeDtypeStruct(shape, dtype) for shape, dtype in outs],
        compiler_params=pltpu.CompilerParams(vmem_limit_bytes=56 * 2**20),
        **more,
    )(*args)


TILES = {"wqkv": 18, "wproj": 6, "wemb": 4, "wdqkv": 12, "wdproj": 4}
G1_AT = (D * 3 * D + D * D) // 128
WEMB_AT = G1_AT + 12
MASK_AT = WEMB_AT + D * 4
WDQKV_AT = MASK_AT + 4
WDPROJ_AT = WDQKV_AT + DD * 12
GD1_AT = WDPROJ_AT + DD * 4
FLAT_ROWS = PARAMS // 128
DEC_ROWS = FLAT_ROWS - WEMB_AT
PREP = 64


def widen(flat_ref, first, out_ref, tiles):
    for t in range(tiles):
        out_ref[:, t * 128 : t * 128 + 128] = flat_ref[
            pl.ds(first + t, out_ref.shape[0], stride=tiles), :
        ].astype(bf16)


def vector(flat_ref, first, count):
    return jnp.concatenate([flat_ref[first + i : first + i + 1, :] for i in range(count)], axis=1)


def flatten(flat_ref, first, value, tiles):
    for t in range(tiles):
        flat_ref[pl.ds(first + t, value.shape[0], stride=tiles), :] = value[:, t * 128 : t * 128 + 128]


def enc_prep_kernel(qkv_ref, proj_ref, gains_ref, wqkv_ref, wproj_ref, g1_ref, g2_ref, qkv_flat, proj_flat, gains_flat):
    qkv_flat[...] = qkv_ref[...].astype(f32)
    proj_flat[...] = proj_ref[...].astype(f32)
    widen(qkv_flat, 0, wqkv_ref, 18)
    widen(proj_flat, 0, wproj_ref, 6)

    @pl.when(pl.program_id(0) == 0)
    def _():
        gains_flat[...] = gains_ref[...].astype(f32)
        g1_ref[...] = vector(gains_flat, 0, 6)
        g2_ref[...] = vector(gains_flat, 6, 6)


def enc_prep(flat):
    whole = lambda *shape: pl.BlockSpec(shape, lambda i: (0,) * len(shape))
    return pl.pallas_call(
        enc_prep_kernel,
        grid=(D // PREP,),
        in_specs=[
            pl.BlockSpec((PREP * 18, 128), lambda i: (i, 0)),
            pl.BlockSpec((PREP * 6, 128), lambda i: (D * 18 // (PREP * 6) + i, 0)),
            pl.BlockSpec((16, 128), lambda i: (G1_AT // 16, 0)),
        ],
        out_specs=[
            pl.BlockSpec((PREP, 3 * D), lambda i: (i, 0)),
            pl.BlockSpec((PREP, D), lambda i: (i, 0)),
            whole(1, D),
            whole(1, D),
        ],
        out_shape=[
            jax.ShapeDtypeStruct((D, 3 * D), bf16),
            jax.ShapeDtypeStruct((D, D), bf16),
            jax.ShapeDtypeStruct((1, D), f32),
            jax.ShapeDtypeStruct((1, D), f32),
        ],
        scratch_shapes=[
            pltpu.VMEM((PREP * 18, 128), f32), pltpu.VMEM((PREP * 6, 128), f32), pltpu.VMEM((16, 128), f32),
        ],
    )(flat, flat, flat)


def dec_prep_kernel(count):
    def body(where_ref, flat_ref, _, *refs):
        ups, downs = refs[: 2 * count - 1], refs[2 * count - 1 : 4 * count - 2]
        (
            wemb_ref, mask_ref, wdqkv_ref, wdproj_ref, gd1_ref, gd2_ref, up_ref, down_ref, low, wide, sem,
        ) = refs[4 * count - 2 :]
        copy = pltpu.make_async_copy(flat_ref.at[pl.ds(G1_AT, FLAT_ROWS - G1_AT), :], low, sem)
        copy.start()
        core, lane = where_ref[0], where_ref[1]
        for pieces, whole in ((ups, up_ref), (downs, down_ref)):
            half = whole.shape[1] // CORES
            whole[lane] = pieces[0][...]
            for k in range(1, count):
                at = lax.rem(lane + k, count)
                near = pl.multiple_of(core * half, 8)
                far = pl.multiple_of((1 - core) * half, 8)
                whole[at, pl.ds(near, half), :] = pieces[2 * k - 1][...]
                whole[at, pl.ds(far, half), :] = pieces[2 * k][...]
        copy.wait()
        wide[...] = low[...].astype(f32)
        widen(wide, WEMB_AT - G1_AT, wemb_ref, 4)
        widen(wide, WDQKV_AT - G1_AT, wdqkv_ref, 12)
        widen(wide, WDPROJ_AT - G1_AT, wdproj_ref, 4)
        mask_ref[...] = vector(wide, MASK_AT - G1_AT, 4)
        gd1_ref[...] = vector(wide, GD1_AT - G1_AT, 4)
        gd2_ref[...] = vector(wide, GD1_AT - G1_AT + 4, 4)

    return body


def dec_prep(ring, flat, ups, downs, later):
    hbm = pl.BlockSpec(memory_space=pl.ANY)
    whole = lambda block: ((ring.group,) + block.shape, bf16)
    return call(
        dec_prep_kernel(ring.group),
        [
            ((D, DD), bf16), ((1, DD), f32), ((DD, 3 * DD), bf16), ((DD, DD), bf16), ((1, DD), f32), ((1, DD), f32),
            whole(ups[0]), whole(downs[0]),
        ],
        jnp.stack([ring.core, ring.lane]).astype(jnp.int32), flat, later, *ups, *downs,
        in_specs=[SMEM, hbm, hbm] + [VMEM] * (len(ups) + len(downs)),
        scratch_shapes=[
            pltpu.VMEM((FLAT_ROWS - G1_AT, 128), bf16), pltpu.VMEM((FLAT_ROWS - G1_AT, 128), f32),
            pltpu.SemaphoreType.DMA,
        ],
    )


def enc_attend_kernel(
    patches_ref, visible_ref, ids_ref, wqkv_ref, wproj_ref, g1_ref, g2_ref,
    x_ref, vis_ref, qkv_ref, probs_ref, mix_ref, first_ref, in2_ref, wide_vis,
):
    x_ref[...] = jnp.concatenate(
        [patches_ref[...].astype(f32), jnp.zeros((PAD - VIS, D), f32)], axis=0
    ).astype(bf16)
    wide_vis[...] = jnp.full(wide_vis.shape, -1, jnp.int32)
    wide_vis[:, :VIS] = visible_ref[...]
    vis = wide_vis[:, :PAD]
    vis_ref[...] = vis
    last = jnp.max(ids_ref[...].astype(f32))
    clip = jnp.where(vis < 0, -1.0, jnp.minimum((vis // SHORT_PATCHES).astype(f32), last))
    square = (PAD, PAD)
    across = jnp.broadcast_to(clip, square)
    diagonal = lax.broadcasted_iota(jnp.int32, square, 0) == lax.broadcasted_iota(jnp.int32, square, 1)
    allowed = across == jnp.sum(jnp.where(diagonal, across, 0.0), axis=1, keepdims=True)
    x = x_ref[...].astype(f32)
    normed, _ = normalize(x)
    qkv_ref[...] = mm((normed * g1_ref[...]).astype(bf16), wqkv_ref[...]).astype(bf16)
    low_lanes = lax.broadcasted_iota(jnp.int32, (PAD, 128), 1) < 64
    for pair in range(HEADS // 2):
        at = slice(pair * 128, pair * 128 + 128)
        query = qkv_ref[:, at]
        key = qkv_ref[:, D + pair * 128 : D + pair * 128 + 128]
        value = qkv_ref[:, 2 * D + pair * 128 : 2 * D + pair * 128 + 128]
        mixed = []
        for side in range(2):
            mine = low_lanes if side == 0 else jnp.logical_not(low_lanes)
            own = jnp.where(mine, query.astype(f32), 0.0).astype(bf16)
            scores = jnp.where(allowed, mm_nt(own, key) * ENC_SCALE, LOWEST)
            top = jnp.max(scores, axis=-1, keepdims=True)
            raised = jnp.exp(scores - top)
            probs = (raised / jnp.sum(raised, axis=-1, keepdims=True)).astype(bf16)
            probs_ref[2 * pair + side] = probs
            mixed.append(mm(probs, value))
        mix_ref[:, at] = jnp.where(low_lanes, mixed[0], mixed[1]).astype(bf16)
    first = x + mm(mix_ref[...], wproj_ref[...])
    first_ref[...] = first
    normed2, _ = normalize(first)
    in2_ref[...] = (normed2 * g2_ref[...]).astype(bf16)


def enc_ffn_kernel(in2_ref, fc1_ref, fc2_ref, part_ref, hidden_ref, slope_ref):
    act, slope = gelu_parts(mm(in2_ref[...], fc1_ref[...]))
    hidden = act.astype(bf16)
    hidden_ref[...] = hidden
    slope_ref[...] = slope.astype(bf16)
    part_ref[...] = mm(hidden, fc2_ref[...]).astype(part_ref.dtype)


def enc_ffn_back_kernel(out_grad_ref, slope_ref, fc1_ref, fc2_ref, pre_grad_ref, part_ref):
    grad = mm_nt(out_grad_ref[...], fc2_ref[...]) * slope_ref[...].astype(f32)
    pre_grad = grad.astype(bf16)
    pre_grad_ref[...] = pre_grad
    part_ref[...] = mm_nt(pre_grad, fc1_ref[...]).astype(part_ref.dtype)


def slabs(rows):
    return jnp.concatenate([rows[:, t * 128 : t * 128 + 128] for t in range(rows.shape[1] // 128)], axis=0)


def enc_weights_kernel(count, chips):
    def body(core_ref, *refs):
        in2s, pre_grads, hiddens, out_grads = (refs[i * count : (i + 1) * count] for i in range(4))
        keep_ref, send_ref = refs[4 * count : 4 * count + 2]
        at = 0
        for lefts, rights in ((in2s, pre_grads), (hiddens, out_grads)):
            total = mm_tn(lefts[0][...], rights[0][...])
            for i in range(1, count):
                total = total + mm_tn(lefts[i][...], rights[i][...])
            height = total.shape[0] // (CORES * 2 * chips)
            rows = height * total.shape[1] // 128

            def split(target, half, total=total, height=height, rows=rows, at=at):
                for way in range(2):
                    for chip in range(chips):
                        first = ((half * 2 + way) * chips + chip) * height
                        target[way, chip, at : at + rows, :] = slabs(total[first : first + height].astype(bf16))

            for half in range(CORES):
                @pl.when(core_ref[0] == half)
                def _(half=half, split=split):
                    split(keep_ref, half)
                    split(send_ref, 1 - half)

            at += rows

    return body


def embed_kernel(count):
    def body(first_ref, own_ref, *refs):
        parts = refs[: count - 1]
        wemb_ref, mask_ref, gd1_ref, wdqkv_ref, second_ref, table_ref, norm_ref = refs[count - 1 :]
        second = first_ref[...] + own_ref[...]
        for part in parts:
            second += part[...].astype(f32)
        low = second.astype(bf16)
        second_ref[...] = low
        embedded = mm(low, wemb_ref[...]).astype(bf16).astype(f32)
        row = lax.broadcasted_iota(jnp.int32, (PAD, DD), 0)
        start = jnp.where(row == VIS, mask_ref[...], embedded)
        normed, _ = normalize(start)
        dec_norm = (normed * gd1_ref[...]).astype(bf16)
        norm_ref[...] = dec_norm
        table_ref[:, : 3 * DD] = mm(dec_norm, wdqkv_ref[...]).astype(bf16)
        table_ref[:, 3 * DD :] = start.astype(bf16)

    return body


def spread(rows, same):
    left = jnp.concatenate([rows[:, :128]] * 4, axis=0) * same
    right = jnp.concatenate([rows[:, 128:]] * 4, axis=0) * same
    none = jnp.zeros_like(left)
    return jnp.concatenate(
        [jnp.concatenate([left, none], axis=1), jnp.concatenate([none, right], axis=1)], axis=0
    )


def segment_max(rows):
    tiles = []
    lane = lax.broadcasted_iota(jnp.int32, (rows.shape[0], 128), 1)
    for t in range(rows.shape[1] // 128):
        tile = rows[:, t * 128 : t * 128 + 128]
        for step in (1, 2, 8, 16):
            other = jnp.where(
                lane & step == 0, pltpu.roll(tile, 128 - step, 1), pltpu.roll(tile, step, 1)
            )
            tile = jnp.maximum(tile, other)
        tiles.append(tile)
    return jnp.concatenate(tiles, axis=1)


def decoder_kernel(chunks, ring):
    def body(
        vis_ref, table_ref, cot_ref, wdproj_ref, gd2_ref, up_ref, down_ref,
        decoded_ref, ends_ref, proj_grad_ref, gd2_grad_ref, packed_ref,
        qkv_ref, mix_ref, s_ref, p_ref, l_ref, dmix_ref, ds_ref, d_ref, back_ref, same_ref, ones_ref,
        up_acc, down_acc, proj_acc, gd2_acc, packed_acc,
    ):
        step = pl.program_id(0)

        @pl.when(step == 0)
        def _():
            up_acc[...] = jnp.zeros_like(up_acc)
            down_acc[...] = jnp.zeros_like(down_acc)
            proj_acc[...] = jnp.zeros_like(proj_acc)
            gd2_acc[...] = jnp.zeros_like(gd2_acc)
            packed_acc[...] = jnp.zeros_like(packed_acc)
            head_row = lax.broadcasted_iota(jnp.int32, (HALF, HALF), 0) // GROUP
            head_lane = lax.broadcasted_iota(jnp.int32, (HALF, HALF), 1) // GROUP
            ones = (head_row == head_lane).astype(f32).astype(bf16)
            ones_ref[...] = ones
            same_ref[...] = ones[:128, :128]

        row = lax.broadcasted_iota(jnp.int32, (BLOCK, PAD), 0) + step * BLOCK
        named = row == vis_ref[...]
        col = lax.broadcasted_iota(jnp.int32, (BLOCK, PAD), 1)
        hit = jnp.max(jnp.where(named, 1.0, 0.0), axis=1, keepdims=True)
        one_hot = jnp.where(named, 1.0, jnp.where(col == VIS, 1.0 - hit, 0.0)).astype(bf16)
        qkv_ref[...] = mm(one_hot, table_ref[:, : 3 * DD]).astype(bf16)
        start = mm(one_hot, table_ref[:, 3 * DD :])

        lane = lax.broadcasted_iota(jnp.int32, (BLOCK, DD), 1)
        line = lax.broadcasted_iota(jnp.int32, (BLOCK, DD), 0)
        window = (lane % FREQ) // WIN == (line % FREQ) // WIN
        n_groups = BLOCK // GROUP

        def parts(group, half):
            at = pl.ds(pl.multiple_of(group * GROUP, GROUP), GROUP)
            return at, slice(half * HALF, (half + 1) * HALF)

        def scores(group, _):
            same = same_ref[...]
            for half in range(2):
                at, cols = parts(group, half)
                key = qkv_ref[at, DD + half * HALF : DD + (half + 1) * HALF]
                s_ref[at, cols] = mm_nt(qkv_ref[at, cols], spread(key, same))
            return 0

        lax.fori_loop(0, n_groups, scores, 0, unroll=8)
        raw = s_ref[...] * DEC_SCALE
        top = segment_max(raw)
        raised = jnp.where(window, jnp.exp(raw - top), 0.0)
        p_low = raised.astype(bf16)
        total = jnp.concatenate(
            [mm(p_low[:, :HALF], ones_ref[...]), mm(p_low[:, HALF:], ones_ref[...])], axis=1
        )
        l_ref[...] = top + jnp.log(total)
        p_ref[...] = (raised / total).astype(bf16)

        def mixes(group, _):
            same = same_ref[...]
            for half in range(2):
                at, cols = parts(group, half)
                value = qkv_ref[at, 2 * DD + half * HALF : 2 * DD + (half + 1) * HALF]
                mix_ref[at, cols] = mm(p_ref[at, cols], spread(value, same)).astype(bf16)
            return 0

        lax.fori_loop(0, n_groups, mixes, 0, unroll=8)

        middle = start + mm(mix_ref[...], wdproj_ref[...])
        normed, scale = normalize(middle)
        in2 = (normed * gd2_ref[...]).astype(bf16)
        cot = cot_ref[...]
        out = jnp.zeros_like(middle)
        in2_grad = jnp.zeros_like(middle)
        for c in range(chunks):
            act, slope = gelu_parts(mm(in2, up_ref[c]))
            hidden = act.astype(bf16)
            out += mm(hidden, down_ref[c])
            pre_grad = (mm_nt(cot, down_ref[c]) * slope).astype(bf16)
            in2_grad += mm_nt(pre_grad, up_ref[c])
            down_acc[c] += mm_tn(hidden, cot)
            up_acc[c] += mm_tn(in2, pre_grad)
        decoded_ref[...] = (middle + out).astype(bf16)

        gd2_acc[...] += gained(in2_grad, normed)
        middle_grad = cot.astype(f32) + norm_back(in2_grad, normed, scale, gd2_ref[...])
        branch = middle_grad.astype(bf16)
        back_ref[:, 3 * DD :] = branch
        proj_acc[...] += mm_tn(mix_ref[...], branch)
        dmix_ref[...] = mm_nt(branch, wdproj_ref[...]).astype(bf16)

        def prob_grads(group, _):
            same = same_ref[...]
            for half in range(2):
                at, cols = parts(group, half)
                value = qkv_ref[at, 2 * DD + half * HALF : 2 * DD + (half + 1) * HALF]
                s_ref[at, cols] = mm_nt(dmix_ref[at, cols], spread(value, same))
            return 0

        lax.fori_loop(0, n_groups, prob_grads, 0, unroll=8)
        probs = p_ref[...].astype(f32)
        prob_grad = s_ref[...]
        weighed = (probs * prob_grad).astype(bf16)
        row_sum = jnp.concatenate(
            [mm(weighed[:, :HALF], ones_ref[...]), mm(weighed[:, HALF:], ones_ref[...])], axis=1
        )
        d_ref[...] = row_sum
        ds_ref[...] = (probs * (prob_grad - row_sum)).astype(bf16)

        small_lane = lax.broadcasted_iota(jnp.int32, (GROUP, HALF), 1)
        small_line = lax.broadcasted_iota(jnp.int32, (GROUP, HALF), 0)
        pick = small_lane % GROUP == small_line
        small_window = (small_lane % FREQ) // WIN == (small_line % FREQ) // WIN

        def qkv_grads(group, _):
            same = same_ref[...]
            for half in range(2):
                at, cols = parts(group, half)
                key_cols = slice(DD + half * HALF, DD + (half + 1) * HALF)
                value_cols = slice(2 * DD + half * HALF, 2 * DD + (half + 1) * HALF)
                key = qkv_ref[at, key_cols]
                wide_query = spread(qkv_ref[at, cols], same)
                wide_mix_grad = spread(dmix_ref[at, cols], same)
                back_ref[at, cols] = (mm(ds_ref[at, cols], spread(key, same)) * DEC_SCALE).astype(bf16)
                log_total = jnp.sum(jnp.where(pick, l_ref[at, cols], 0.0), axis=0, keepdims=True)
                turned_sum = jnp.sum(jnp.where(pick, d_ref[at, cols], 0.0), axis=0, keepdims=True)
                turned = mm_nt(key, wide_query) * DEC_SCALE
                turned = jnp.where(small_window, jnp.exp(turned - log_total), 0.0)
                turned_grad = mm_nt(qkv_ref[at, value_cols], wide_mix_grad)
                score_grad = (turned * (turned_grad - turned_sum)).astype(bf16)
                back_ref[at, key_cols] = (mm(score_grad, wide_query) * DEC_SCALE).astype(bf16)
                back_ref[at, value_cols] = mm(turned.astype(bf16), wide_mix_grad).astype(bf16)
            return 0

        lax.fori_loop(0, n_groups, qkv_grads, 0, unroll=8)
        packed_acc[...] += mm_tn(one_hot, back_ref[...])

        @pl.when(step == pl.num_programs(0) - 1)
        def _():
            tall, low = DD // (CORES * 2 * ring.chips), up_acc.shape[2] // (CORES * 2 * ring.chips)
            cut = tall * up_acc.shape[2] // 128
            for clip in range(ring.clips):
                for way in range(2):
                    block = ring.ahead(clip, way)
                    for y in range(chunks):
                        ends_ref[clip, y, way, :cut] = slabs(up_acc[y, block * tall : (block + 1) * tall].astype(bf16))
                        ends_ref[clip, y, way, cut:] = slabs(down_acc[y, block * low : (block + 1) * low].astype(bf16))
            proj_grad_ref[...] = proj_acc[...].astype(bf16)
            gd2_grad_ref[...] = gd2_acc[...]
            packed_ref[...] = packed_acc[...]

    return body


def decoder(ring, vis_row, table, cotangent, w_dproj, gd_two, up, down):
    chunks, _, width = up.shape
    rows = cotangent.shape[0]
    kept = lambda *shape: pl.BlockSpec(shape, lambda i: (0,) * len(shape), pipeline_mode=pl.Buffered(1))
    by_rows = pl.BlockSpec((BLOCK, DD), lambda i: (i, 0))
    ends = (ring.clips, chunks, 2, DD * width // (128 * ring.clips), 128)
    outs = [
        ((rows, DD), bf16, by_rows),
        (ends, bf16, kept(*ends)),
        ((DD, DD), bf16, kept(DD, DD)),
        ((1, DD), f32, kept(1, DD)),
        ((PAD, 4 * DD), f32, kept(PAD, 4 * DD)),
    ]
    return pl.pallas_call(
        decoder_kernel(chunks, ring),
        cost_estimate=hint(80),
        grid=(rows // BLOCK,),
        in_specs=[
            kept(1, PAD), kept(PAD, 4 * DD), by_rows, kept(DD, DD), kept(1, DD),
            kept(chunks, DD, width), kept(chunks, width, DD),
        ],
        out_specs=[spec for _, _, spec in outs],
        out_shape=[jax.ShapeDtypeStruct(shape, dtype) for shape, dtype, _ in outs],
        scratch_shapes=[
            pltpu.VMEM((BLOCK, 3 * DD), bf16),
            pltpu.VMEM((BLOCK, DD), bf16),
            pltpu.VMEM((BLOCK, DD), f32),
            pltpu.VMEM((BLOCK, DD), bf16),
            pltpu.VMEM((BLOCK, DD), f32),
            pltpu.VMEM((BLOCK, DD), bf16),
            pltpu.VMEM((BLOCK, DD), bf16),
            pltpu.VMEM((BLOCK, DD), f32),
            pltpu.VMEM((BLOCK, 4 * DD), bf16),
            pltpu.VMEM((128, 128), bf16),
            pltpu.VMEM((HALF, HALF), bf16),
            pltpu.VMEM((chunks, DD, width), f32),
            pltpu.VMEM((chunks, width, DD), f32),
            pltpu.VMEM((DD, DD), f32),
            pltpu.VMEM((1, DD), f32),
            pltpu.VMEM((PAD, 4 * DD), f32),
        ],
        compiler_params=pltpu.CompilerParams(vmem_limit_bytes=56 * 2**20),
    )(vis_row, table, cotangent, w_dproj, gd_two, up, down)


def embed_back_kernel(
    packed_ref, table_ref, norm_ref, second_ref, gd1_ref, wdqkv_ref, wemb_ref,
    second_grad_ref, out_grad_ref, qkv_grad_ref, embed_grad_ref, gd1_grad_ref, mask_grad_ref,
):
    qkv_grad = packed_ref[:, : 3 * DD].astype(bf16)
    qkv_grad_ref[...] = qkv_grad
    grad = mm_nt(qkv_grad, wdqkv_ref[...])
    normed, scale = normalize(table_ref[:, 3 * DD :].astype(f32))
    gd1_grad_ref[...] = gained(grad, normed)
    start_grad = packed_ref[:, 3 * DD :] + norm_back(grad, normed, scale, gd1_ref[...])
    mask_grad_ref[...] = start_grad[VIS : VIS + 1]
    row = lax.broadcasted_iota(jnp.int32, (PAD, DD), 0)
    embed_grad = jnp.where(row < VIS, start_grad, 0.0).astype(bf16)
    embed_grad_ref[...] = embed_grad
    second_grad = mm_nt(embed_grad, wemb_ref[...])
    second_grad_ref[...] = second_grad
    out_grad_ref[...] = second_grad.astype(bf16)


def dec_flat_kernel(ring):
    def body(
        norm_ref, qkv_grad_ref, second_ref, embed_grad_ref, proj_grad_ref, mask_grad_ref, gd1_grad_ref, gd2_grad_ref,
        flat_ref, wide,
    ):
        flatten(wide, 0, mm_tn(second_ref[...], embed_grad_ref[...]), 4)
        flatten(wide, MASK_AT - WEMB_AT, mask_grad_ref[...], 4)
        flatten(wide, WDQKV_AT - WEMB_AT, mm_tn(norm_ref[...], qkv_grad_ref[...]), 12)
        flatten(wide, WDPROJ_AT - WEMB_AT, proj_grad_ref[...].astype(f32), 4)
        flatten(wide, GD1_AT - WEMB_AT, gd1_grad_ref[...], 4)
        flatten(wide, GD1_AT + 4 - WEMB_AT, gd2_grad_ref[...], 4)
        if not ring.apart:
            flat_ref[...] = wide[...].astype(bf16)
            return
        wide[DEC_ROWS:, :] = jnp.zeros((wide.shape[0] - DEC_ROWS, 128), f32)
        for clip in range(ring.clips):
            for way in range(2):
                block = ring.ahead(clip, way)
                flat_ref[clip, way] = wide[block * ring.dec_rows : (block + 1) * ring.dec_rows, :].astype(bf16)

    return body


def enc_back_kernel(count, ring):
    def body(core_ref, own_ref, *refs):
        parts = refs[: count - 1]
        (
            second_grad_ref, first_ref, x_ref, qkv_ref, probs_ref, mix_ref, wqkv_ref, wproj_ref, g1_ref, g2_ref,
        ) = refs[count - 1 : count + 9]
        input_grad_ref, keep_ref, send_ref, qkv_grad_ref, wide = refs[-5:]
        in2_grad = own_ref[...]
        for part in parts:
            in2_grad += part[...].astype(f32)
        normed2, scale2 = normalize(first_ref[...])
        flatten(wide, G1_AT + 6, gained(in2_grad, normed2), 6)
        first_grad = second_grad_ref[...] + norm_back(in2_grad, normed2, scale2, g2_ref[...])
        branch = first_grad.astype(bf16)
        flatten(wide, D * 18, mm_tn(mix_ref[...], branch), 6)
        if not ring.apart:
            wide[WEMB_AT:FLAT_ROWS, :] = refs[-6][...].astype(f32)
        mix_grad = mm_nt(branch, wproj_ref[...]).astype(bf16)
        low_lanes = lax.broadcasted_iota(jnp.int32, (PAD, 128), 1) < 64
        for pair in range(HEADS // 2):
            at = slice(pair * 128, pair * 128 + 128)
            query = qkv_ref[:, at]
            key = qkv_ref[:, D + pair * 128 : D + pair * 128 + 128]
            value = qkv_ref[:, 2 * D + pair * 128 : 2 * D + pair * 128 + 128]
            upstream = mix_grad[:, at]
            found = []
            for side in range(2):
                mine = low_lanes if side == 0 else jnp.logical_not(low_lanes)
                own = jnp.where(mine, upstream.astype(f32), 0.0).astype(bf16)
                low_probs = probs_ref[2 * pair + side]
                probs = low_probs.astype(f32)
                prob_grad = mm_nt(own, value)
                row_sum = jnp.sum(probs * prob_grad, axis=-1, keepdims=True)
                score_grad = (probs * (prob_grad - row_sum)).astype(bf16)
                found.append((mm(score_grad, key), mm_tn(score_grad, query), mm_tn(low_probs, upstream)))
            for part, factor in enumerate((ENC_SCALE, ENC_SCALE, 1.0)):
                merged = jnp.where(low_lanes, found[0][part], found[1][part]) * factor
                qkv_grad_ref[:, part * D + pair * 128 : part * D + pair * 128 + 128] = merged.astype(bf16)
        normed, scale = normalize(x_ref[...].astype(f32))
        flatten(wide, 0, mm_tn((normed * g1_ref[...]).astype(bf16), qkv_grad_ref[...]), 18)
        grad = mm_nt(qkv_grad_ref[...], wqkv_ref[...])
        flatten(wide, G1_AT, gained(grad, normed), 6)
        input_grad_ref[...] = (first_grad + norm_back(grad, normed, scale, g1_ref[...]))[:VIS]

        def split(target, half):
            for way in range(2):
                for chip in range(ring.chips):
                    block = (half * 2 + way) * ring.chips + chip
                    at = 0
                    for y in range(ring.group):
                        height = ring.rows[y]
                        first = y * ring.part + block * height
                        count = max(0, min(height, ring.counts[y] - block * height))
                        if count > 0:
                            target[way, chip, at : at + count] = wide[first : first + count, :].astype(bf16)
                        if count < height:
                            target[way, chip, at + count : at + height] = jnp.zeros((height - count, 128), bf16)
                        at += height

        for half in range(CORES):
            @pl.when(core_ref[0] == half)
            def _(half=half):
                split(keep_ref, half)
                split(send_ref, 1 - half)

    return body


class Ring:
    def __init__(self, clips, group):
        self.chips = clips // CORES
        self.group = group
        chips = self.chips
        if chips == 8:
            order = [4 * z // 2 for z in range(4)] + [4 * z // 2 + 1 for z in reversed(range(4))]
        else:
            order = list(range(chips))
        place = [0] * chips
        for at, chip in enumerate(order):
            place[chip] = at
        clip = lax.axis_index("clips")
        self.places = place
        self.core = clip % CORES
        chip = clip // CORES
        if chips == 8:
            self.at = jnp.where(chip % 2 == 0, chip // 2, 7 - chip // 2)
        else:
            self.at = chip
        self.lane = lax.axis_index("mlp")
        step = lambda way: [
            (order[i] * CORES + c, order[(i + way) % chips] * CORES + c) for i in range(chips) for c in range(CORES)
        ]
        self.ways = (step(1), step(-1))
        self.swap = [(i, i ^ 1) for i in range(clips)]
        self.clips = clips
        self.cut = max(1, chips - 3)
        blocks = CORES * 2 * chips
        self.part = FLAT_ROWS // group
        whole = -(-(-(-self.part // blocks)) // 8) * 8
        self.apart = group == 2
        if self.apart:
            self.counts = [self.part, WEMB_AT - self.part]
            second = -(-(-(-self.counts[1] // blocks)) // 8) * 8
            self.rows = [whole, second]
            self.dec_rows = whole - second
        else:
            self.counts = [self.part] * group
            self.rows = [whole] * group
            self.dec_rows = 0

    def ahead(self, clip, way):
        chip = (self.places[clip // CORES] + (1 if way == 0 else -1)) % self.chips
        return (clip % CORES * 2 + way) * self.chips + chip

    def fetch(self, block):
        half = block.shape[0] // CORES
        mine = lax.dynamic_slice_in_dim(block, self.core * half, half, 0)
        pieces = [block]
        for k in range(1, self.group):
            near = lax.ppermute(mine, "mlp", [(j, (j - k) % self.group) for j in range(self.group)])
            pieces += [near, self.swapped(near)]
        return pieces

    def swapped(self, value):
        return lax.ppermute(value, "clips", self.swap)

    def block(self, half, way, back):
        sign = 1 if way == 0 else -1
        return lax.dynamic_index_in_dim(half[way], (self.at - sign * back) % self.chips, 0, False)

    def start(self, keep, send):
        return keep + self.swapped(send)

    def round_trip(self, half, early, ends=None):
        held = [self.block(half, way, 0) for way in range(2)]
        for step in range(1, self.chips):
            came = [lax.ppermute(held[way], "clips", self.ways[way]) for way in range(2)]
            held = [came[way] + self.block(half, way, step) for way in range(2)]
            if ends is not None and step == 2:
                held, ends[0] = lax.optimization_barrier((held, ends[0]))
            if ends is not None and step == 5:
                held, ends[1:] = lax.optimization_barrier((held, ends[1:]))
            held = yield held
        if ends is not None:
            both = []
            for way in range(2):
                parts = []
                at = 0
                for y in range(self.group):
                    rows = [held[way][at : at + self.rows[y]]]
                    at += self.rows[y]
                    if self.apart and y == 1:
                        rows.append(ends[1][way])
                    parts.append(jnp.concatenate(rows + [ends[0][y, way]]))
                both.append(jnp.stack(parts))
            held = self.over_group(both)
        return (yield from self.spread(held, early))

    def over_group(self, held):
        both = jnp.stack(held, axis=1)
        total = lax.dynamic_index_in_dim(both, self.lane, 0, False)
        for k in range(1, self.group):
            away = lax.dynamic_index_in_dim(both, (self.lane + k) % self.group, 0, False)
            total = total + lax.ppermute(away, "mlp", [(j, (j + k) % self.group) for j in range(self.group)])
        return [total[0], total[1]]

    def spread(self, held, early):
        found = [[held[0]], [held[1]]]
        cut = self.cut
        placed = None
        for step in range(1, self.chips):
            came = [lax.ppermute(found[way][-1], "clips", self.ways[way]) for way in range(2)]
            if step == self.chips - 2:
                came, placed = lax.optimization_barrier((came, placed))
            came = yield came
            for way in range(2):
                found[way].append(came[way])
            if step == cut - 1:
                first = found[0] + found[1]
                placed = early(first, self.swapped(jnp.stack(first)))
        last = found[0][cut:] + found[1][cut:]
        return placed, last, self.swapped(jnp.stack(last))


def side_by_side(one, two, lead):
    trips, done = (one, two), [None, None]
    kept = [None, None]

    def advance(i):
        try:
            value = next(trips[i]) if kept[i] is None else trips[i].send(kept[i])
        except StopIteration as end:
            done[i] = end.value
            return
        other = kept[1 - i]
        kept[i] = value if other is None else lax.optimization_barrier((value, other))[0]

    for _ in range(lead):
        advance(0)
    while done[0] is None or done[1] is None:
        for i in range(2):
            if done[i] is None:
                advance(i)
    return done


def place_kernel(ring, shares, steps, aliased):
    n_outs = len(shares)
    count = len(steps)
    last_block = CORES * 2 * ring.chips - 1

    def body(where_ref, *refs):
        mine, other = refs[: 2 * count], refs[2 * count]
        rest = refs[2 * count + 1 + (n_outs if aliased else 0) :]
        outs, buffers, sems = rest[:n_outs], rest[n_outs : 2 * n_outs], rest[2 * n_outs]
        core, at, lane = where_ref[0], where_ref[1], where_ref[2]
        copies = []
        for way in range(2):
            sign = 1 if way == 0 else -1
            for i, step in enumerate(steps):
                slot = lax.rem(at + sign * (1 - step) + ring.chips, ring.chips)
                for near in (True, False):
                    value = mine[way * count + i][...] if near else other[way * count + i]
                    value = value.astype(f32)
                    side = core if near else 1 - core
                    block = (side * 2 + way) * ring.chips + slot
                    index = (way * count + i) * 2 + (0 if near else 1)
                    first = 0
                    for out, buffer, (total, columns, pieces) in zip(outs, buffers, shares):
                        tiles = columns // 128
                        high = sum(height for height, _, _ in pieces)
                        wide = [value[first + t * high : first + (t + 1) * high] for t in range(tiles)]
                        buffer[index] = jnp.concatenate(wide, axis=1) if tiles > 1 else wide[0]
                        first += tiles * high
                        start = 0
                        for height, row_of, short in pieces:
                            row = pl.multiple_of(row_of(block, lane), 8)
                            cases = [(height, None)] if short == height else [(height, False), (short, True)]
                            for rows, at_end in cases:
                                if rows == 0:
                                    continue
                                copy = pltpu.make_async_copy(
                                    buffer.at[index, pl.ds(start, rows), :], out.at[pl.ds(row, rows), :], sems.at[len(copies)]
                                )
                                copies.append((copy, None if at_end is None else (block == last_block) == at_end))
                                run(copy.start, copies[-1][1])
                            start += height
        for copy, condition in copies:
            run(copy.wait, condition)

    return body


def run(action, condition):
    if condition is None:
        action()
    else:
        pl.when(condition)(action)


def place(ring, where, shares, steps, mine, other, earlier=()):
    hbm = pl.BlockSpec(memory_space=pl.ANY)
    count = len(steps)
    copies = 4 * count * sum(1 if s == h else 2 for _, _, pieces in shares for h, _, s in pieces)
    return call(
        place_kernel(ring, shares, steps, bool(earlier)),
        [((total, columns), f32) for total, columns, _ in shares],
        where, *mine, other, *earlier,
        in_specs=[SMEM] + [VMEM] * (len(mine) + 1) + [hbm] * len(earlier),
        out_specs=[hbm] * len(shares),
        input_output_aliases={len(mine) + 2 + i: i for i in range(len(earlier))},
        scratch_shapes=[
            pltpu.VMEM((4 * count, sum(h for h, _, _ in pieces), columns), f32) for _, columns, pieces in shares
        ] + [pltpu.SemaphoreType.DMA((copies,))],
        us=6,
    )


def place_rows(ring, shares, steps, mine, other, earlier):
    count = len(steps)
    outs = list(earlier)
    first = 0
    for k, (total, columns, pieces) in enumerate(shares):
        tiles = columns // 128
        (height, _, _) = pieces[0]
        padded = CORES * 2 * ring.chips * height
        out = outs[k] if earlier else jnp.zeros((padded, columns), f32)
        for way in range(2):
            for i, step in enumerate(steps):
                slot = (ring.at + (1 if way == 0 else -1) * (1 - step)) % ring.chips
                for side, value in ((ring.core, mine[way * count + i]), (1 - ring.core, other[way * count + i])):
                    value = value[first : first + tiles * height].reshape(tiles, height, 128)
                    value = value.transpose(1, 0, 2).reshape(height, columns).astype(f32)
                    row = ((side * 2 + way) * ring.chips + slot) * height
                    out = lax.dynamic_update_slice_in_dim(out, value, row, 0)
        if earlier:
            outs[k] = out
        else:
            outs.append(out)
        first += tiles * height
    return outs


class Placer:
    def __init__(self, ring, where, totals):
        self.ring, self.where = ring, where
        blocks = CORES * 2 * ring.chips
        self.shares = []
        for total, columns in totals:
            flat = columns == 128
            if flat and ring.apart:
                whole, second = ring.rows
                cut = max(0, total - (blocks - 1) * whole)
                pieces = [
                    (second, lambda b, lane: jnp.where(lane == 0, b * whole, b * second), min(second, cut)),
                    (
                        whole - second,
                        lambda b, lane: jnp.where(
                            lane == 0, b * whole + second, ring.counts[1] + b * (whole - second)
                        ),
                        max(0, cut - second),
                    ),
                ]
            else:
                height = ring.rows[0] if flat else total // blocks
                pieces = [(height, lambda b, lane, height=height: b * height, total - (blocks - 1) * height)]
            self.shares.append((total, columns, pieces))
        self.plain = any(h % 8 for _, _, pieces in self.shares for h, _, _ in pieces) or not ring.apart

    def early(self, mine, other):
        return self.put(range(self.ring.cut), mine, other, [])

    def late(self, found):
        placed, mine, other = found
        outs = self.put(range(self.ring.cut, self.ring.chips), mine, other, placed)
        return [out[:total] for out, (total, _, _) in zip(outs, self.shares)]

    def put(self, steps, mine, other, earlier):
        steps = list(steps)
        if self.plain:
            return place_rows(self.ring, self.shares, steps, mine, other, earlier)
        return place(self.ring, self.where, self.shares, steps, mine, other, earlier)


def after(value, *others):
    return lax.optimization_barrier((value,) + others)[0]


def shards(clips, group, flat_params, w_fc1, w_fc2, w_up, w_down, patches, clip_ids, visible_index, cotangent):
    width = w_fc1.shape[1]
    ring = Ring(clips, group)
    core = ring.core.astype(jnp.int32).reshape(1)
    turns = [[(i, (i + k) % group) for i in range(group)] for k in range(1, group)]
    back_turns = [[(i, (i - k) % group) for i in range(group)] for k in range(1, group)]

    ups = ring.fetch(w_up)
    downs = ring.fetch(w_down)

    flat = flat_params.reshape(FLAT_ROWS, 128)
    w_qkv, w_proj, g_one, g_two = enc_prep(flat)
    x, vis, qkv, probs, mix, first, in2 = call(
        enc_attend_kernel,
        [
            ((PAD, D), bf16), ((1, PAD), jnp.int32), ((PAD, 3 * D), bf16), ((HEADS, PAD, PAD), bf16), ((PAD, D), bf16),
            ((PAD, D), f32), ((PAD, D), bf16),
        ],
        patches, visible_index[None, :], clip_ids.reshape(-1, 128), w_qkv, w_proj, g_one, g_two,
        scratch_shapes=[pltpu.VMEM((1, 384), jnp.int32)],
        us=11,
    )

    in2s, hiddens, slopes, parts = [in2], [], [], []
    for i in range(group):
        if i > 0:
            in2s.append(after(lax.ppermute(in2, "mlp", turns[i - 1]), parts[0]))
        part, hidden, slope = call(
            enc_ffn_kernel,
            [((PAD, D), f32 if i == 0 else bf16), ((PAD, width), bf16), ((PAD, width), bf16)],
            in2s[i], w_fc1, w_fc2,
        )
        hiddens.append(hidden)
        slopes.append(slope)
        parts.append(part if i == 0 else lax.ppermute(part, "mlp", back_turns[i - 1]))
    w_embed, mask_token, w_dqkv, w_dproj, gd_one, gd_two, up_all, down_all = dec_prep(ring, flat, ups, downs, part)

    second_low, table, dec_norm = call(
        embed_kernel(group),
        [((PAD, D), bf16), ((PAD, 4 * DD), bf16), ((PAD, DD), bf16)],
        first, *parts, w_embed, mask_token, gd_one, w_dqkv,
    )
    decoded, ends, wdproj_grad, gd_two_grad, packed = decoder(
        ring, vis, table, cotangent, w_dproj, gd_two, up_all, down_all
    )
    ends = lax.psum_scatter(ends.reshape(-1, 128), "clips", scatter_dimension=0, tiled=True)
    ends = ends.reshape(group, 2, -1, 128)
    second_grad, out_grad, dec_qkv_grad, embed_grad, gd_one_grad, mask_grad = call(
        embed_back_kernel,
        [
            ((PAD, D), f32), ((PAD, D), bf16), ((PAD, 3 * DD), bf16), ((PAD, DD), bf16), ((1, DD), f32), ((1, DD), f32),
        ],
        packed, table, dec_norm, second_low, gd_one, w_dqkv, w_embed,
    )
    dec_wide = CORES * 2 * ring.chips * ring.dec_rows if ring.apart else DEC_ROWS
    dec_flat = call(
        dec_flat_kernel(ring),
        [((clips, 2, ring.dec_rows, 128) if ring.apart else (DEC_ROWS, 128), bf16)],
        dec_norm, dec_qkv_grad, second_low, embed_grad, wdproj_grad, mask_grad, gd_one_grad, gd_two_grad,
        scratch_shapes=[pltpu.VMEM((dec_wide, 128), f32)],
    )[0]
    dec_ends = []
    if ring.apart:
        dec_ends = lax.psum_scatter(dec_flat.reshape(-1, 128), "clips", scatter_dimension=0, tiled=True)
        dec_ends = [dec_ends.reshape(2, -1, 128)]

    out_grads, pre_grads, parts = [out_grad], [], []
    for i in range(group):
        if i > 0:
            out_grads.append(after(lax.ppermute(out_grad, "mlp", turns[i - 1]), parts[0], dec_flat))
        pre_grad, part = call(
            enc_ffn_back_kernel,
            [((PAD, width), bf16), ((PAD, D), f32 if i == 0 else bf16)],
            out_grads[i], slopes[i], w_fc1, w_fc2,
        )
        pre_grads.append(pre_grad)
        parts.append(part if i == 0 else lax.ppermute(part, "mlp", back_turns[i - 1]))
    fc_halves = ((2, ring.chips, 2 * D * width // (CORES * 2 * ring.chips * 128), 128), bf16)
    fc_keep, fc_send = call(
        enc_weights_kernel(group, ring.chips), [fc_halves, fc_halves],
        core, *in2s, *pre_grads, *hiddens, *out_grads,
        in_specs=[SMEM] + [VMEM] * (4 * group),
        us=10,
    )
    parts[1:] = [after(part, fc_keep) for part in parts[1:]]
    flat_halves = ((2, ring.chips, sum(ring.rows), 128), bf16)
    input_grad, flat_keep, flat_send = call(
        enc_back_kernel(group, ring),
        [((VIS, D), f32), flat_halves, flat_halves],
        core, *parts, second_grad, first, x, qkv, probs, mix, w_qkv, w_proj, g_one, g_two, *([] if ring.apart else [dec_flat]),
        in_specs=[SMEM] + [VMEM] * (group + (10 if ring.apart else 11)),
        scratch_shapes=[
            pltpu.VMEM((PAD, 3 * D), bf16), pltpu.VMEM((WEMB_AT + 4 if ring.apart else FLAT_ROWS, 128), f32),
        ],
        us=20,
    )
    where = jnp.stack([ring.core, ring.at, ring.lane]).astype(jnp.int32)
    fc_placer = Placer(ring, where, [(D, width), (width, D)])
    flat_placer = Placer(ring, where, [(ring.part, 128), (DD, w_up.shape[1]), (w_up.shape[1], DD)])
    fc_found, flat_found = side_by_side(
        ring.round_trip(ring.start(fc_keep, fc_send), fc_placer.early),
        ring.round_trip(ring.start(flat_keep, flat_send), flat_placer.early, [ends] + dec_ends),
        2,
    )
    fc1_grad, fc2_grad = fc_placer.late(fc_found)
    param_grad, up_grad, down_grad = flat_placer.late(flat_found)
    return decoded, input_grad, param_grad.reshape(-1), fc1_grad, fc2_grad, up_grad, down_grad


def solution(mesh):
    placed = (
        P(),
        P(None, "mlp"),
        P("mlp", None),
        P(None, "mlp"),
        P("mlp", None),
        P(("clips", "mlp"), None),
        P(("clips", "mlp")),
        P(("clips", "mlp")),
        P(("clips", "mlp"), None),
    )
    group = mesh.shape["mlp"]

    def body(*args):
        return shards(mesh.shape["clips"], group, *args)

    return jax.shard_map(
        body,
        mesh=mesh,
        in_specs=placed,
        out_specs=(
            P(("clips", "mlp"), None),
            P(("clips", "mlp"), None),
            P("mlp"),
            P(None, "mlp"),
            P("mlp", None),
            P(None, "mlp"),
            P("mlp", None),
        ),
        check_vma=False,
    )
```

```python
import math

import jax
import jax.numpy as jnp
from jax import lax
from jax.experimental import pallas as pl
from jax.experimental.pallas import tpu as pltpu
from jax.sharding import PartitionSpec as P

D = 768
HEADS = 12
DD = 512
DHEADS = 16
FREQ = 8
WIN = 4
ROWS = 1536
VIS = 312
PAD = 320
SHORT_PATCHES = 512
PARAMS = 3804160
EPSILON = 1e-06
BLOCK = 256
GROUP = WIN * FREQ
HALF = DD // 2
ENC_SCALE = 1.0 / math.sqrt(D // HEADS)
DEC_SCALE = 1.0 / math.sqrt(DD // DHEADS)
LOWEST = -1e30
CORES = 2
bf16 = jnp.bfloat16
f32 = jnp.float32


def mm(left, right):
    return jnp.dot(left, right, preferred_element_type=f32)


def mm_nt(left, right):
    return lax.dot_general(left, right, (((1,), (1,)), ((), ())), preferred_element_type=f32)


def mm_tn(left, right):
    return lax.dot_general(left, right, (((0,), (0,)), ((), ())), preferred_element_type=f32)


def normalize(rows):
    centred = rows - jnp.mean(rows, axis=-1, keepdims=True)
    scale = lax.rsqrt(jnp.mean(centred * centred, axis=-1, keepdims=True) + EPSILON)
    return centred * scale, scale


def norm_back(grad, normed, scale, gain):
    weighted = grad * gain
    return scale * (
        weighted
        - jnp.mean(weighted, axis=-1, keepdims=True)
        - normed * jnp.mean(weighted * normed, axis=-1, keepdims=True)
    )


def gelu_parts(pre):
    cdf = 0.5 * (1.0 + lax.erf(pre * math.sqrt(0.5)))
    return pre * cdf, cdf + pre * jnp.exp(-0.5 * pre * pre) * (1.0 / math.sqrt(2.0 * math.pi))


def gained(grad, normed):
    return jnp.sum(grad * normed, axis=0, keepdims=True)


SMEM = pl.BlockSpec(memory_space=pltpu.SMEM)
VMEM = pl.BlockSpec(memory_space=pltpu.VMEM)


def hint(us):
    return pl.CostEstimate(flops=int(us * 8e8), transcendentals=0, bytes_accessed=int(us * 1e6))


def call(body, outs, *args, us=5, **more):
    return pl.pallas_call(
        body,
        cost_estimate=hint(us),
        out_shape=[jax.ShapeDtypeStruct(shape, dtype) for shape, dtype in outs],
        compiler_params=pltpu.CompilerParams(vmem_limit_bytes=56 * 2**20),
        **more,
    )(*args)


TILES = {"wqkv": 18, "wproj": 6, "wemb": 4, "wdqkv": 12, "wdproj": 4}
G1_AT = (D * 3 * D + D * D) // 128
WEMB_AT = G1_AT + 12
MASK_AT = WEMB_AT + D * 4
WDQKV_AT = MASK_AT + 4
WDPROJ_AT = WDQKV_AT + DD * 12
GD1_AT = WDPROJ_AT + DD * 4
FLAT_ROWS = PARAMS // 128
DEC_ROWS = FLAT_ROWS - WEMB_AT
PREP = 64


def widen(flat_ref, first, out_ref, tiles):
    for t in range(tiles):
        out_ref[:, t * 128 : t * 128 + 128] = flat_ref[
            pl.ds(first + t, out_ref.shape[0], stride=tiles), :
        ].astype(bf16)


def vector(flat_ref, first, count):
    return jnp.concatenate([flat_ref[first + i : first + i + 1, :] for i in range(count)], axis=1)


def flatten(flat_ref, first, value, tiles):
    for t in range(tiles):
        flat_ref[pl.ds(first + t, value.shape[0], stride=tiles), :] = value[:, t * 128 : t * 128 + 128]


def enc_prep_kernel(qkv_ref, proj_ref, gains_ref, wqkv_ref, wproj_ref, g1_ref, g2_ref, qkv_flat, proj_flat, gains_flat):
    qkv_flat[...] = qkv_ref[...].astype(f32)
    proj_flat[...] = proj_ref[...].astype(f32)
    widen(qkv_flat, 0, wqkv_ref, 18)
    widen(proj_flat, 0, wproj_ref, 6)

    @pl.when(pl.program_id(0) == 0)
    def _():
        gains_flat[...] = gains_ref[...].astype(f32)
        g1_ref[...] = vector(gains_flat, 0, 6)
        g2_ref[...] = vector(gains_flat, 6, 6)


def enc_prep(flat):
    whole = lambda *shape: pl.BlockSpec(shape, lambda i: (0,) * len(shape))
    return pl.pallas_call(
        enc_prep_kernel,
        grid=(D // PREP,),
        in_specs=[
            pl.BlockSpec((PREP * 18, 128), lambda i: (i, 0)),
            pl.BlockSpec((PREP * 6, 128), lambda i: (D * 18 // (PREP * 6) + i, 0)),
            pl.BlockSpec((16, 128), lambda i: (G1_AT // 16, 0)),
        ],
        out_specs=[
            pl.BlockSpec((PREP, 3 * D), lambda i: (i, 0)),
            pl.BlockSpec((PREP, D), lambda i: (i, 0)),
            whole(1, D),
            whole(1, D),
        ],
        out_shape=[
            jax.ShapeDtypeStruct((D, 3 * D), bf16),
            jax.ShapeDtypeStruct((D, D), bf16),
            jax.ShapeDtypeStruct((1, D), f32),
            jax.ShapeDtypeStruct((1, D), f32),
        ],
        scratch_shapes=[
            pltpu.VMEM((PREP * 18, 128), f32), pltpu.VMEM((PREP * 6, 128), f32), pltpu.VMEM((16, 128), f32),
        ],
    )(flat, flat, flat)


def dec_prep_kernel(count):
    def body(where_ref, flat_ref, _, *refs):
        ups, downs = refs[: 2 * count - 1], refs[2 * count - 1 : 4 * count - 2]
        (
            wemb_ref, mask_ref, wdqkv_ref, wdproj_ref, gd1_ref, gd2_ref, up_ref, down_ref, low, wide, sem,
        ) = refs[4 * count - 2 :]
        copy = pltpu.make_async_copy(flat_ref.at[pl.ds(G1_AT, FLAT_ROWS - G1_AT), :], low, sem)
        copy.start()
        core, lane = where_ref[0], where_ref[1]
        for pieces, whole in ((ups, up_ref), (downs, down_ref)):
            half = whole.shape[1] // CORES
            whole[lane] = pieces[0][...]
            for k in range(1, count):
                at = lax.rem(lane + k, count)
                near = pl.multiple_of(core * half, 8)
                far = pl.multiple_of((1 - core) * half, 8)
                whole[at, pl.ds(near, half), :] = pieces[2 * k - 1][...]
                whole[at, pl.ds(far, half), :] = pieces[2 * k][...]
        copy.wait()
        wide[...] = low[...].astype(f32)
        widen(wide, WEMB_AT - G1_AT, wemb_ref, 4)
        widen(wide, WDQKV_AT - G1_AT, wdqkv_ref, 12)
        widen(wide, WDPROJ_AT - G1_AT, wdproj_ref, 4)
        mask_ref[...] = vector(wide, MASK_AT - G1_AT, 4)
        gd1_ref[...] = vector(wide, GD1_AT - G1_AT, 4)
        gd2_ref[...] = vector(wide, GD1_AT - G1_AT + 4, 4)

    return body


def dec_prep(ring, flat, ups, downs, later):
    hbm = pl.BlockSpec(memory_space=pl.ANY)
    whole = lambda block: ((ring.group,) + block.shape, bf16)
    return call(
        dec_prep_kernel(ring.group),
        [
            ((D, DD), bf16), ((1, DD), f32), ((DD, 3 * DD), bf16), ((DD, DD), bf16), ((1, DD), f32), ((1, DD), f32),
            whole(ups[0]), whole(downs[0]),
        ],
        jnp.stack([ring.core, ring.lane]).astype(jnp.int32), flat, later, *ups, *downs,
        in_specs=[SMEM, hbm, hbm] + [VMEM] * (len(ups) + len(downs)),
        scratch_shapes=[
            pltpu.VMEM((FLAT_ROWS - G1_AT, 128), bf16), pltpu.VMEM((FLAT_ROWS - G1_AT, 128), f32),
            pltpu.SemaphoreType.DMA,
        ],
    )


def enc_attend_kernel(
    patches_ref, visible_ref, ids_ref, wqkv_ref, wproj_ref, g1_ref, g2_ref,
    x_ref, vis_ref, qkv_ref, probs_ref, mix_ref, first_ref, in2_ref, wide_vis,
):
    x_ref[...] = jnp.concatenate(
        [patches_ref[...].astype(f32), jnp.zeros((PAD - VIS, D), f32)], axis=0
    ).astype(bf16)
    wide_vis[...] = jnp.full(wide_vis.shape, -1, jnp.int32)
    wide_vis[:, :VIS] = visible_ref[...]
    vis = wide_vis[:, :PAD]
    vis_ref[...] = vis
    last = jnp.max(ids_ref[...].astype(f32))
    clip = jnp.where(vis < 0, -1.0, jnp.minimum((vis // SHORT_PATCHES).astype(f32), last))
    square = (PAD, PAD)
    across = jnp.broadcast_to(clip, square)
    diagonal = lax.broadcasted_iota(jnp.int32, square, 0) == lax.broadcasted_iota(jnp.int32, square, 1)
    allowed = across == jnp.sum(jnp.where(diagonal, across, 0.0), axis=1, keepdims=True)
    x = x_ref[...].astype(f32)
    normed, _ = normalize(x)
    qkv_ref[...] = mm((normed * g1_ref[...]).astype(bf16), wqkv_ref[...]).astype(bf16)
    low_lanes = lax.broadcasted_iota(jnp.int32, (PAD, 128), 1) < 64
    for pair in range(HEADS // 2):
        at = slice(pair * 128, pair * 128 + 128)
        query = qkv_ref[:, at]
        key = qkv_ref[:, D + pair * 128 : D + pair * 128 + 128]
        value = qkv_ref[:, 2 * D + pair * 128 : 2 * D + pair * 128 + 128]
        mixed = []
        for side in range(2):
            mine = low_lanes if side == 0 else jnp.logical_not(low_lanes)
            own = jnp.where(mine, query.astype(f32), 0.0).astype(bf16)
            scores = jnp.where(allowed, mm_nt(own, key) * ENC_SCALE, LOWEST)
            top = jnp.max(scores, axis=-1, keepdims=True)
            raised = jnp.exp(scores - top)
            probs = (raised / jnp.sum(raised, axis=-1, keepdims=True)).astype(bf16)
            probs_ref[2 * pair + side] = probs
            mixed.append(mm(probs, value))
        mix_ref[:, at] = jnp.where(low_lanes, mixed[0], mixed[1]).astype(bf16)
    first = x + mm(mix_ref[...], wproj_ref[...])
    first_ref[...] = first
    normed2, _ = normalize(first)
    in2_ref[...] = (normed2 * g2_ref[...]).astype(bf16)


def enc_ffn_kernel(in2_ref, fc1_ref, fc2_ref, part_ref, hidden_ref, slope_ref):
    act, slope = gelu_parts(mm(in2_ref[...], fc1_ref[...]))
    hidden = act.astype(bf16)
    hidden_ref[...] = hidden
    slope_ref[...] = slope.astype(bf16)
    part_ref[...] = mm(hidden, fc2_ref[...]).astype(part_ref.dtype)


def enc_ffn_back_kernel(out_grad_ref, slope_ref, fc1_ref, fc2_ref, pre_grad_ref, part_ref):
    grad = mm_nt(out_grad_ref[...], fc2_ref[...]) * slope_ref[...].astype(f32)
    pre_grad = grad.astype(bf16)
    pre_grad_ref[...] = pre_grad
    part_ref[...] = mm_nt(pre_grad, fc1_ref[...]).astype(part_ref.dtype)


def slabs(rows):
    return jnp.concatenate([rows[:, t * 128 : t * 128 + 128] for t in range(rows.shape[1] // 128)], axis=0)


def enc_weights_kernel(count, chips):
    def body(core_ref, *refs):
        in2s, pre_grads, hiddens, out_grads = (refs[i * count : (i + 1) * count] for i in range(4))
        keep_ref, send_ref = refs[4 * count : 4 * count + 2]
        at = 0
        for lefts, rights in ((in2s, pre_grads), (hiddens, out_grads)):
            total = mm_tn(lefts[0][...], rights[0][...])
            for i in range(1, count):
                total = total + mm_tn(lefts[i][...], rights[i][...])
            height = total.shape[0] // (CORES * 2 * chips)
            rows = height * total.shape[1] // 128

            def split(target, half, total=total, height=height, rows=rows, at=at):
                for way in range(2):
                    for chip in range(chips):
                        first = ((half * 2 + way) * chips + chip) * height
                        target[way, chip, at : at + rows, :] = slabs(total[first : first + height].astype(bf16))

            for half in range(CORES):
                @pl.when(core_ref[0] == half)
                def _(half=half, split=split):
                    split(keep_ref, half)
                    split(send_ref, 1 - half)

            at += rows

    return body


def embed_kernel(count):
    def body(first_ref, own_ref, *refs):
        parts = refs[: count - 1]
        wemb_ref, mask_ref, gd1_ref, wdqkv_ref, second_ref, table_ref, norm_ref = refs[count - 1 :]
        second = first_ref[...] + own_ref[...]
        for part in parts:
            second += part[...].astype(f32)
        low = second.astype(bf16)
        second_ref[...] = low
        embedded = mm(low, wemb_ref[...]).astype(bf16).astype(f32)
        row = lax.broadcasted_iota(jnp.int32, (PAD, DD), 0)
        start = jnp.where(row == VIS, mask_ref[...], embedded)
        normed, _ = normalize(start)
        dec_norm = (normed * gd1_ref[...]).astype(bf16)
        norm_ref[...] = dec_norm
        table_ref[:, : 3 * DD] = mm(dec_norm, wdqkv_ref[...]).astype(bf16)
        table_ref[:, 3 * DD :] = start.astype(bf16)

    return body


def spread(rows, same):
    left = jnp.concatenate([rows[:, :128]] * 4, axis=0) * same
    right = jnp.concatenate([rows[:, 128:]] * 4, axis=0) * same
    none = jnp.zeros_like(left)
    return jnp.concatenate(
        [jnp.concatenate([left, none], axis=1), jnp.concatenate([none, right], axis=1)], axis=0
    )


def segment_max(rows):
    tiles = []
    lane = lax.broadcasted_iota(jnp.int32, (rows.shape[0], 128), 1)
    for t in range(rows.shape[1] // 128):
        tile = rows[:, t * 128 : t * 128 + 128]
        for step in (1, 2, 8, 16):
            other = jnp.where(
                lane & step == 0, pltpu.roll(tile, 128 - step, 1), pltpu.roll(tile, step, 1)
            )
            tile = jnp.maximum(tile, other)
        tiles.append(tile)
    return jnp.concatenate(tiles, axis=1)


def decoder_kernel(chunks, ring):
    def body(
        vis_ref, table_ref, cot_ref, wdproj_ref, gd2_ref, up_ref, down_ref,
        decoded_ref, ends_ref, proj_grad_ref, gd2_grad_ref, packed_ref,
        qkv_ref, mix_ref, s_ref, p_ref, l_ref, dmix_ref, ds_ref, d_ref, back_ref, same_ref, ones_ref,
        up_acc, down_acc, proj_acc, gd2_acc, packed_acc,
    ):
        step = pl.program_id(0)

        @pl.when(step == 0)
        def _():
            up_acc[...] = jnp.zeros_like(up_acc)
            down_acc[...] = jnp.zeros_like(down_acc)
            proj_acc[...] = jnp.zeros_like(proj_acc)
            gd2_acc[...] = jnp.zeros_like(gd2_acc)
            packed_acc[...] = jnp.zeros_like(packed_acc)
            head_row = lax.broadcasted_iota(jnp.int32, (HALF, HALF), 0) // GROUP
            head_lane = lax.broadcasted_iota(jnp.int32, (HALF, HALF), 1) // GROUP
            ones = (head_row == head_lane).astype(f32).astype(bf16)
            ones_ref[...] = ones
            same_ref[...] = ones[:128, :128]

        row = lax.broadcasted_iota(jnp.int32, (BLOCK, PAD), 0) + step * BLOCK
        named = row == vis_ref[...]
        col = lax.broadcasted_iota(jnp.int32, (BLOCK, PAD), 1)
        hit = jnp.max(jnp.where(named, 1.0, 0.0), axis=1, keepdims=True)
        one_hot = jnp.where(named, 1.0, jnp.where(col == VIS, 1.0 - hit, 0.0)).astype(bf16)
        qkv_ref[...] = mm(one_hot, table_ref[:, : 3 * DD]).astype(bf16)
        start = mm(one_hot, table_ref[:, 3 * DD :])

        lane = lax.broadcasted_iota(jnp.int32, (BLOCK, DD), 1)
        line = lax.broadcasted_iota(jnp.int32, (BLOCK, DD), 0)
        window = (lane % FREQ) // WIN == (line % FREQ) // WIN
        n_groups = BLOCK // GROUP

        def parts(group, half):
            at = pl.ds(pl.multiple_of(group * GROUP, GROUP), GROUP)
            return at, slice(half * HALF, (half + 1) * HALF)

        def scores(group, _):
            same = same_ref[...]
            for half in range(2):
                at, cols = parts(group, half)
                key = qkv_ref[at, DD + half * HALF : DD + (half + 1) * HALF]
                s_ref[at, cols] = mm_nt(qkv_ref[at, cols], spread(key, same))
            return 0

        lax.fori_loop(0, n_groups, scores, 0, unroll=8)
        raw = s_ref[...] * DEC_SCALE
        top = segment_max(raw)
        raised = jnp.where(window, jnp.exp(raw - top), 0.0)
        p_low = raised.astype(bf16)
        total = jnp.concatenate(
            [mm(p_low[:, :HALF], ones_ref[...]), mm(p_low[:, HALF:], ones_ref[...])], axis=1
        )
        l_ref[...] = top + jnp.log(total)
        p_ref[...] = (raised / total).astype(bf16)

        def mixes(group, _):
            same = same_ref[...]
            for half in range(2):
                at, cols = parts(group, half)
                value = qkv_ref[at, 2 * DD + half * HALF : 2 * DD + (half + 1) * HALF]
                mix_ref[at, cols] = mm(p_ref[at, cols], spread(value, same)).astype(bf16)
            return 0

        lax.fori_loop(0, n_groups, mixes, 0, unroll=8)

        middle = start + mm(mix_ref[...], wdproj_ref[...])
        normed, scale = normalize(middle)
        in2 = (normed * gd2_ref[...]).astype(bf16)
        cot = cot_ref[...]
        out = jnp.zeros_like(middle)
        in2_grad = jnp.zeros_like(middle)
        for c in range(chunks):
            act, slope = gelu_parts(mm(in2, up_ref[c]))
            hidden = act.astype(bf16)
            out += mm(hidden, down_ref[c])
            pre_grad = (mm_nt(cot, down_ref[c]) * slope).astype(bf16)
            in2_grad += mm_nt(pre_grad, up_ref[c])
            down_acc[c] += mm_tn(hidden, cot)
            up_acc[c] += mm_tn(in2, pre_grad)
        decoded_ref[...] = (middle + out).astype(bf16)

        gd2_acc[...] += gained(in2_grad, normed)
        middle_grad = cot.astype(f32) + norm_back(in2_grad, normed, scale, gd2_ref[...])
        branch = middle_grad.astype(bf16)
        back_ref[:, 3 * DD :] = branch
        proj_acc[...] += mm_tn(mix_ref[...], branch)
        dmix_ref[...] = mm_nt(branch, wdproj_ref[...]).astype(bf16)

        def prob_grads(group, _):
            same = same_ref[...]
            for half in range(2):
                at, cols = parts(group, half)
                value = qkv_ref[at, 2 * DD + half * HALF : 2 * DD + (half + 1) * HALF]
                s_ref[at, cols] = mm_nt(dmix_ref[at, cols], spread(value, same))
            return 0

        lax.fori_loop(0, n_groups, prob_grads, 0, unroll=8)
        probs = p_ref[...].astype(f32)
        prob_grad = s_ref[...]
        weighed = (probs * prob_grad).astype(bf16)
        row_sum = jnp.concatenate(
            [mm(weighed[:, :HALF], ones_ref[...]), mm(weighed[:, HALF:], ones_ref[...])], axis=1
        )
        d_ref[...] = row_sum
        ds_ref[...] = (probs * (prob_grad - row_sum)).astype(bf16)

        small_lane = lax.broadcasted_iota(jnp.int32, (GROUP, HALF), 1)
        small_line = lax.broadcasted_iota(jnp.int32, (GROUP, HALF), 0)
        pick = small_lane % GROUP == small_line
        small_window = (small_lane % FREQ) // WIN == (small_line % FREQ) // WIN

        def qkv_grads(group, _):
            same = same_ref[...]
            for half in range(2):
                at, cols = parts(group, half)
                key_cols = slice(DD + half * HALF, DD + (half + 1) * HALF)
                value_cols = slice(2 * DD + half * HALF, 2 * DD + (half + 1) * HALF)
                key = qkv_ref[at, key_cols]
                wide_query = spread(qkv_ref[at, cols], same)
                wide_mix_grad = spread(dmix_ref[at, cols], same)
                back_ref[at, cols] = (mm(ds_ref[at, cols], spread(key, same)) * DEC_SCALE).astype(bf16)
                log_total = jnp.sum(jnp.where(pick, l_ref[at, cols], 0.0), axis=0, keepdims=True)
                turned_sum = jnp.sum(jnp.where(pick, d_ref[at, cols], 0.0), axis=0, keepdims=True)
                turned = mm_nt(key, wide_query) * DEC_SCALE
                turned = jnp.where(small_window, jnp.exp(turned - log_total), 0.0)
                turned_grad = mm_nt(qkv_ref[at, value_cols], wide_mix_grad)
                score_grad = (turned * (turned_grad - turned_sum)).astype(bf16)
                back_ref[at, key_cols] = (mm(score_grad, wide_query) * DEC_SCALE).astype(bf16)
                back_ref[at, value_cols] = mm(turned.astype(bf16), wide_mix_grad).astype(bf16)
            return 0

        lax.fori_loop(0, n_groups, qkv_grads, 0, unroll=8)
        packed_acc[...] += mm_tn(one_hot, back_ref[...])

        @pl.when(step == pl.num_programs(0) - 1)
        def _():
            tall, low = DD // (CORES * 2 * ring.chips), up_acc.shape[2] // (CORES * 2 * ring.chips)
            cut = tall * up_acc.shape[2] // 128
            for clip in range(ring.clips):
                for way in range(2):
                    block = ring.ahead(clip, way)
                    for y in range(chunks):
                        first = (y * 2 + way) * 2 * cut
                        ends_ref[clip, first : first + cut] = slabs(up_acc[y, block * tall : (block + 1) * tall].astype(bf16))
                        ends_ref[clip, first + cut : first + 2 * cut] = slabs(
                            down_acc[y, block * low : (block + 1) * low].astype(bf16)
                        )
            proj_grad_ref[...] = proj_acc[...].astype(bf16)
            gd2_grad_ref[...] = gd2_acc[...]
            packed_ref[...] = packed_acc[...]

    return body


def decoder(ring, vis_row, table, cotangent, w_dproj, gd_two, up, down):
    chunks, _, width = up.shape
    rows = cotangent.shape[0]
    kept = lambda *shape: pl.BlockSpec(shape, lambda i: (0,) * len(shape), pipeline_mode=pl.Buffered(1))
    by_rows = pl.BlockSpec((BLOCK, DD), lambda i: (i, 0))
    ends = (ring.clips, ring.end_rows + 2 * ring.dec_rows, 128)
    outs = [
        ((rows, DD), bf16, by_rows),
        (ends, bf16, kept(*ends)),
        ((DD, DD), bf16, kept(DD, DD)),
        ((1, DD), f32, kept(1, DD)),
        ((PAD, 4 * DD), f32, kept(PAD, 4 * DD)),
    ]
    return pl.pallas_call(
        decoder_kernel(chunks, ring),
        cost_estimate=hint(80),
        grid=(rows // BLOCK,),
        in_specs=[
            kept(1, PAD), kept(PAD, 4 * DD), by_rows, kept(DD, DD), kept(1, DD),
            kept(chunks, DD, width), kept(chunks, width, DD),
        ],
        out_specs=[spec for _, _, spec in outs],
        out_shape=[jax.ShapeDtypeStruct(shape, dtype) for shape, dtype, _ in outs],
        scratch_shapes=[
            pltpu.VMEM((BLOCK, 3 * DD), bf16),
            pltpu.VMEM((BLOCK, DD), bf16),
            pltpu.VMEM((BLOCK, DD), f32),
            pltpu.VMEM((BLOCK, DD), bf16),
            pltpu.VMEM((BLOCK, DD), f32),
            pltpu.VMEM((BLOCK, DD), bf16),
            pltpu.VMEM((BLOCK, DD), bf16),
            pltpu.VMEM((BLOCK, DD), f32),
            pltpu.VMEM((BLOCK, 4 * DD), bf16),
            pltpu.VMEM((128, 128), bf16),
            pltpu.VMEM((HALF, HALF), bf16),
            pltpu.VMEM((chunks, DD, width), f32),
            pltpu.VMEM((chunks, width, DD), f32),
            pltpu.VMEM((DD, DD), f32),
            pltpu.VMEM((1, DD), f32),
            pltpu.VMEM((PAD, 4 * DD), f32),
        ],
        compiler_params=pltpu.CompilerParams(vmem_limit_bytes=56 * 2**20),
    )(vis_row, table, cotangent, w_dproj, gd_two, up, down)


def embed_back_kernel(
    packed_ref, table_ref, norm_ref, second_ref, gd1_ref, wdqkv_ref, wemb_ref,
    second_grad_ref, out_grad_ref, qkv_grad_ref, embed_grad_ref, gd1_grad_ref, mask_grad_ref,
):
    qkv_grad = packed_ref[:, : 3 * DD].astype(bf16)
    qkv_grad_ref[...] = qkv_grad
    grad = mm_nt(qkv_grad, wdqkv_ref[...])
    normed, scale = normalize(table_ref[:, 3 * DD :].astype(f32))
    gd1_grad_ref[...] = gained(grad, normed)
    start_grad = packed_ref[:, 3 * DD :] + norm_back(grad, normed, scale, gd1_ref[...])
    mask_grad_ref[...] = start_grad[VIS : VIS + 1]
    row = lax.broadcasted_iota(jnp.int32, (PAD, DD), 0)
    embed_grad = jnp.where(row < VIS, start_grad, 0.0).astype(bf16)
    embed_grad_ref[...] = embed_grad
    second_grad = mm_nt(embed_grad, wemb_ref[...])
    second_grad_ref[...] = second_grad
    out_grad_ref[...] = second_grad.astype(bf16)


def dec_flat_kernel(ring):
    def body(
        norm_ref, qkv_grad_ref, second_ref, embed_grad_ref, proj_grad_ref, mask_grad_ref, gd1_grad_ref, gd2_grad_ref,
        *refs,
    ):
        if ring.apart:
            _, flat_ref, wide, low, sems = refs
        else:
            flat_ref, wide = refs
        flatten(wide, 0, mm_tn(second_ref[...], embed_grad_ref[...]), 4)
        flatten(wide, MASK_AT - WEMB_AT, mask_grad_ref[...], 4)
        flatten(wide, WDQKV_AT - WEMB_AT, mm_tn(norm_ref[...], qkv_grad_ref[...]), 12)
        flatten(wide, WDPROJ_AT - WEMB_AT, proj_grad_ref[...].astype(f32), 4)
        flatten(wide, GD1_AT - WEMB_AT, gd1_grad_ref[...], 4)
        flatten(wide, GD1_AT + 4 - WEMB_AT, gd2_grad_ref[...], 4)
        if not ring.apart:
            flat_ref[...] = wide[...].astype(bf16)
            return
        wide[DEC_ROWS:, :] = jnp.zeros((wide.shape[0] - DEC_ROWS, 128), f32)
        for clip in range(ring.clips):
            for way in range(2):
                block = ring.ahead(clip, way)
                low[clip, way * ring.dec_rows : (way + 1) * ring.dec_rows] = wide[
                    block * ring.dec_rows : (block + 1) * ring.dec_rows, :
                ].astype(bf16)
        copies = [
            pltpu.make_async_copy(
                low.at[clip], flat_ref.at[clip, pl.ds(ring.end_rows, 2 * ring.dec_rows), :], sems.at[clip]
            )
            for clip in range(ring.clips)
        ]
        for copy in copies:
            copy.start()
        for copy in copies:
            copy.wait()

    return body


def enc_back_kernel(count, ring):
    def body(core_ref, own_ref, *refs):
        parts = refs[: count - 1]
        (
            second_grad_ref, first_ref, x_ref, qkv_ref, probs_ref, mix_ref, wqkv_ref, wproj_ref, g1_ref, g2_ref,
        ) = refs[count - 1 : count + 9]
        input_grad_ref, keep_ref, send_ref, qkv_grad_ref, wide = refs[-5:]
        in2_grad = own_ref[...]
        for part in parts:
            in2_grad += part[...].astype(f32)
        normed2, scale2 = normalize(first_ref[...])
        flatten(wide, G1_AT + 6, gained(in2_grad, normed2), 6)
        first_grad = second_grad_ref[...] + norm_back(in2_grad, normed2, scale2, g2_ref[...])
        branch = first_grad.astype(bf16)
        flatten(wide, D * 18, mm_tn(mix_ref[...], branch), 6)
        if not ring.apart:
            wide[WEMB_AT:FLAT_ROWS, :] = refs[-6][...].astype(f32)
        mix_grad = mm_nt(branch, wproj_ref[...]).astype(bf16)
        low_lanes = lax.broadcasted_iota(jnp.int32, (PAD, 128), 1) < 64
        for pair in range(HEADS // 2):
            at = slice(pair * 128, pair * 128 + 128)
            query = qkv_ref[:, at]
            key = qkv_ref[:, D + pair * 128 : D + pair * 128 + 128]
            value = qkv_ref[:, 2 * D + pair * 128 : 2 * D + pair * 128 + 128]
            upstream = mix_grad[:, at]
            found = []
            for side in range(2):
                mine = low_lanes if side == 0 else jnp.logical_not(low_lanes)
                own = jnp.where(mine, upstream.astype(f32), 0.0).astype(bf16)
                low_probs = probs_ref[2 * pair + side]
                probs = low_probs.astype(f32)
                prob_grad = mm_nt(own, value)
                row_sum = jnp.sum(probs * prob_grad, axis=-1, keepdims=True)
                score_grad = (probs * (prob_grad - row_sum)).astype(bf16)
                found.append((mm(score_grad, key), mm_tn(score_grad, query), mm_tn(low_probs, upstream)))
            for part, factor in enumerate((ENC_SCALE, ENC_SCALE, 1.0)):
                merged = jnp.where(low_lanes, found[0][part], found[1][part]) * factor
                qkv_grad_ref[:, part * D + pair * 128 : part * D + pair * 128 + 128] = merged.astype(bf16)
        normed, scale = normalize(x_ref[...].astype(f32))
        flatten(wide, 0, mm_tn((normed * g1_ref[...]).astype(bf16), qkv_grad_ref[...]), 18)
        grad = mm_nt(qkv_grad_ref[...], wqkv_ref[...])
        flatten(wide, G1_AT, gained(grad, normed), 6)
        input_grad_ref[...] = (first_grad + norm_back(grad, normed, scale, g1_ref[...]))[:VIS]

        def split(target, half):
            for way in range(2):
                for chip in range(ring.chips):
                    block = (half * 2 + way) * ring.chips + chip
                    at = 0
                    for y in range(ring.group):
                        height = ring.rows[y]
                        first = y * ring.part + block * height
                        count = max(0, min(height, ring.counts[y] - block * height))
                        if count > 0:
                            target[way, chip, at : at + count] = wide[first : first + count, :].astype(bf16)
                        if count < height:
                            target[way, chip, at + count : at + height] = jnp.zeros((height - count, 128), bf16)
                        at += height

        for half in range(CORES):
            @pl.when(core_ref[0] == half)
            def _(half=half):
                split(keep_ref, half)
                split(send_ref, 1 - half)

    return body


class Ring:
    def __init__(self, clips, group, hidden):
        self.chips = clips // CORES
        self.group = group
        chips = self.chips
        if chips == 8:
            order = [4 * z // 2 for z in range(4)] + [4 * z // 2 + 1 for z in reversed(range(4))]
        else:
            order = list(range(chips))
        place = [0] * chips
        for at, chip in enumerate(order):
            place[chip] = at
        clip = lax.axis_index("clips")
        self.places = place
        self.core = clip % CORES
        chip = clip // CORES
        if chips == 8:
            self.at = jnp.where(chip % 2 == 0, chip // 2, 7 - chip // 2)
        else:
            self.at = chip
        self.lane = lax.axis_index("mlp")
        step = lambda way: [
            (order[i] * CORES + c, order[(i + way) % chips] * CORES + c) for i in range(chips) for c in range(CORES)
        ]
        self.ways = (step(1), step(-1))
        self.swap = [(i, i ^ 1) for i in range(clips)]
        self.clips = clips
        self.cut = max(1, chips - 3)
        blocks = CORES * 2 * chips
        self.part = FLAT_ROWS // group
        whole = -(-(-(-self.part // blocks)) // 8) * 8
        self.apart = group == 2
        if self.apart:
            self.counts = [self.part, WEMB_AT - self.part]
            second = -(-(-(-self.counts[1] // blocks)) // 8) * 8
            self.rows = [whole, second]
            self.dec_rows = whole - second
        else:
            self.counts = [self.part] * group
            self.rows = [whole] * group
            self.dec_rows = 0
        self.end_rows = 2 * DD * hidden // (128 * clips)

    def ahead(self, clip, way):
        chip = (self.places[clip // CORES] + (1 if way == 0 else -1)) % self.chips
        return (clip % CORES * 2 + way) * self.chips + chip

    def fetch(self, block):
        half = block.shape[0] // CORES
        mine = lax.dynamic_slice_in_dim(block, self.core * half, half, 0)
        pieces = [block]
        for k in range(1, self.group):
            near = lax.ppermute(mine, "mlp", [(j, (j - k) % self.group) for j in range(self.group)])
            pieces += [near, self.swapped(near)]
        return pieces

    def swapped(self, value):
        return lax.ppermute(value, "clips", self.swap)

    def block(self, half, way, back):
        sign = 1 if way == 0 else -1
        return lax.dynamic_index_in_dim(half[way], (self.at - sign * back) % self.chips, 0, False)

    def start(self, keep, send):
        return keep + self.swapped(send)

    def round_trip(self, half, early, ends=None):
        held = [self.block(half, way, 0) for way in range(2)]
        for step in range(1, self.chips):
            came = [lax.ppermute(held[way], "clips", self.ways[way]) for way in range(2)]
            held = [came[way] + self.block(half, way, step) for way in range(2)]
            if ends is not None and step == 4:
                held, ends = lax.optimization_barrier((held, ends))
            held = yield held
        if ends is not None:
            both = []
            halves = ends[: self.end_rows].reshape(self.group, 2, -1, 128)
            for way in range(2):
                parts = []
                at = 0
                for y in range(self.group):
                    rows = [held[way][at : at + self.rows[y]]]
                    at += self.rows[y]
                    if self.apart and y == 1:
                        first = self.end_rows + way * self.dec_rows
                        rows.append(ends[first : first + self.dec_rows])
                    parts.append(jnp.concatenate(rows + [halves[y, way]]))
                both.append(jnp.stack(parts))
            held = self.over_group(both)
        return (yield from self.spread(held, early))

    def over_group(self, held):
        both = jnp.stack(held, axis=1)
        total = lax.dynamic_index_in_dim(both, self.lane, 0, False)
        for k in range(1, self.group):
            away = lax.dynamic_index_in_dim(both, (self.lane + k) % self.group, 0, False)
            total = total + lax.ppermute(away, "mlp", [(j, (j + k) % self.group) for j in range(self.group)])
        return [total[0], total[1]]

    def spread(self, held, early):
        found = [[held[0]], [held[1]]]
        cut = self.cut
        placed = None
        for step in range(1, self.chips):
            came = [lax.ppermute(found[way][-1], "clips", self.ways[way]) for way in range(2)]
            if step == self.chips - 2:
                came, placed = lax.optimization_barrier((came, placed))
            came = yield came
            for way in range(2):
                found[way].append(came[way])
            if step == cut - 1:
                first = found[0] + found[1]
                placed = early(first, self.swapped(jnp.stack(first)))
        last = found[0][cut:] + found[1][cut:]
        return placed, last, self.swapped(jnp.stack(last))


def side_by_side(one, two, lead):
    trips, done = (one, two), [None, None]
    kept = [None, None]

    def advance(i):
        try:
            value = next(trips[i]) if kept[i] is None else trips[i].send(kept[i])
        except StopIteration as end:
            done[i] = end.value
            return
        other = kept[1 - i]
        kept[i] = value if other is None else lax.optimization_barrier((value, other))[0]

    for _ in range(lead):
        advance(0)
    while done[0] is None or done[1] is None:
        for i in range(2):
            if done[i] is None:
                advance(i)
    return done


def place_kernel(ring, shares, steps, aliased):
    n_outs = len(shares)
    count = len(steps)
    last_block = CORES * 2 * ring.chips - 1

    def body(where_ref, *refs):
        mine, other = refs[: 2 * count], refs[2 * count]
        rest = refs[2 * count + 1 + (n_outs if aliased else 0) :]
        outs, buffers, sems = rest[:n_outs], rest[n_outs : 2 * n_outs], rest[2 * n_outs]
        core, at, lane = where_ref[0], where_ref[1], where_ref[2]
        copies = []
        for way in range(2):
            sign = 1 if way == 0 else -1
            for i, step in enumerate(steps):
                slot = lax.rem(at + sign * (1 - step) + ring.chips, ring.chips)
                for near in (True, False):
                    value = mine[way * count + i][...] if near else other[way * count + i]
                    value = value.astype(f32)
                    side = core if near else 1 - core
                    block = (side * 2 + way) * ring.chips + slot
                    index = (way * count + i) * 2 + (0 if near else 1)
                    first = 0
                    for out, buffer, (total, columns, pieces) in zip(outs, buffers, shares):
                        tiles = columns // 128
                        high = sum(height for height, _, _ in pieces)
                        wide = [value[first + t * high : first + (t + 1) * high] for t in range(tiles)]
                        buffer[index] = jnp.concatenate(wide, axis=1) if tiles > 1 else wide[0]
                        first += tiles * high
                        start = 0
                        for height, row_of, short in pieces:
                            row = pl.multiple_of(row_of(block, lane), 8)
                            cases = [(height, None)] if short == height else [(height, False), (short, True)]
                            for rows, at_end in cases:
                                if rows == 0:
                                    continue
                                copy = pltpu.make_async_copy(
                                    buffer.at[index, pl.ds(start, rows), :], out.at[pl.ds(row, rows), :], sems.at[len(copies)]
                                )
                                copies.append((copy, None if at_end is None else (block == last_block) == at_end))
                                run(copy.start, copies[-1][1])
                            start += height
        for copy, condition in copies:
            run(copy.wait, condition)

    return body


def run(action, condition):
    if condition is None:
        action()
    else:
        pl.when(condition)(action)


def place(ring, where, shares, steps, mine, other, earlier=()):
    hbm = pl.BlockSpec(memory_space=pl.ANY)
    count = len(steps)
    copies = 4 * count * sum(1 if s == h else 2 for _, _, pieces in shares for h, _, s in pieces)
    return call(
        place_kernel(ring, shares, steps, bool(earlier)),
        [((total, columns), f32) for total, columns, _ in shares],
        where, *mine, other, *earlier,
        in_specs=[SMEM] + [VMEM] * (len(mine) + 1) + [hbm] * len(earlier),
        out_specs=[hbm] * len(shares),
        input_output_aliases={len(mine) + 2 + i: i for i in range(len(earlier))},
        scratch_shapes=[
            pltpu.VMEM((4 * count, sum(h for h, _, _ in pieces), columns), f32) for _, columns, pieces in shares
        ] + [pltpu.SemaphoreType.DMA((copies,))],
        us=6,
    )


def place_rows(ring, shares, steps, mine, other, earlier):
    count = len(steps)
    outs = list(earlier)
    first = 0
    for k, (total, columns, pieces) in enumerate(shares):
        tiles = columns // 128
        (height, _, _) = pieces[0]
        padded = CORES * 2 * ring.chips * height
        out = outs[k] if earlier else jnp.zeros((padded, columns), f32)
        for way in range(2):
            for i, step in enumerate(steps):
                slot = (ring.at + (1 if way == 0 else -1) * (1 - step)) % ring.chips
                for side, value in ((ring.core, mine[way * count + i]), (1 - ring.core, other[way * count + i])):
                    value = value[first : first + tiles * height].reshape(tiles, height, 128)
                    value = value.transpose(1, 0, 2).reshape(height, columns).astype(f32)
                    row = ((side * 2 + way) * ring.chips + slot) * height
                    out = lax.dynamic_update_slice_in_dim(out, value, row, 0)
        if earlier:
            outs[k] = out
        else:
            outs.append(out)
        first += tiles * height
    return outs


class Placer:
    def __init__(self, ring, where, totals):
        self.ring, self.where = ring, where
        blocks = CORES * 2 * ring.chips
        self.shares = []
        for total, columns in totals:
            flat = columns == 128
            if flat and ring.apart:
                whole, second = ring.rows
                cut = max(0, total - (blocks - 1) * whole)
                pieces = [
                    (second, lambda b, lane: jnp.where(lane == 0, b * whole, b * second), min(second, cut)),
                    (
                        whole - second,
                        lambda b, lane: jnp.where(
                            lane == 0, b * whole + second, ring.counts[1] + b * (whole - second)
                        ),
                        max(0, cut - second),
                    ),
                ]
            else:
                height = ring.rows[0] if flat else total // blocks
                pieces = [(height, lambda b, lane, height=height: b * height, total - (blocks - 1) * height)]
            self.shares.append((total, columns, pieces))
        self.plain = any(h % 8 for _, _, pieces in self.shares for h, _, _ in pieces) or not ring.apart

    def early(self, mine, other):
        return self.put(range(self.ring.cut), mine, other, [])

    def late(self, found):
        placed, mine, other = found
        outs = self.put(range(self.ring.cut, self.ring.chips), mine, other, placed)
        return [out[:total] for out, (total, _, _) in zip(outs, self.shares)]

    def put(self, steps, mine, other, earlier):
        steps = list(steps)
        if self.plain:
            return place_rows(self.ring, self.shares, steps, mine, other, earlier)
        return place(self.ring, self.where, self.shares, steps, mine, other, earlier)


def after(value, *others):
    return lax.optimization_barrier((value,) + others)[0]


def shards(clips, group, flat_params, w_fc1, w_fc2, w_up, w_down, patches, clip_ids, visible_index, cotangent):
    width = w_fc1.shape[1]
    ring = Ring(clips, group, group * w_up.shape[1])
    core = ring.core.astype(jnp.int32).reshape(1)
    turns = [[(i, (i + k) % group) for i in range(group)] for k in range(1, group)]
    back_turns = [[(i, (i - k) % group) for i in range(group)] for k in range(1, group)]

    ups = ring.fetch(w_up)
    downs = ring.fetch(w_down)

    flat = flat_params.reshape(FLAT_ROWS, 128)
    w_qkv, w_proj, g_one, g_two = enc_prep(flat)
    x, vis, qkv, probs, mix, first, in2 = call(
        enc_attend_kernel,
        [
            ((PAD, D), bf16), ((1, PAD), jnp.int32), ((PAD, 3 * D), bf16), ((HEADS, PAD, PAD), bf16), ((PAD, D), bf16),
            ((PAD, D), f32), ((PAD, D), bf16),
        ],
        patches, visible_index[None, :], clip_ids.reshape(-1, 128), w_qkv, w_proj, g_one, g_two,
        scratch_shapes=[pltpu.VMEM((1, 384), jnp.int32)],
        us=11,
    )

    in2s, hiddens, slopes, parts = [in2], [], [], []
    for i in range(group):
        if i > 0:
            in2s.append(after(lax.ppermute(in2, "mlp", turns[i - 1]), parts[0]))
        part, hidden, slope = call(
            enc_ffn_kernel,
            [((PAD, D), f32 if i == 0 else bf16), ((PAD, width), bf16), ((PAD, width), bf16)],
            in2s[i], w_fc1, w_fc2,
        )
        hiddens.append(hidden)
        slopes.append(slope)
        parts.append(part if i == 0 else lax.ppermute(part, "mlp", back_turns[i - 1]))
    w_embed, mask_token, w_dqkv, w_dproj, gd_one, gd_two, up_all, down_all = dec_prep(ring, flat, ups, downs, part)

    second_low, table, dec_norm = call(
        embed_kernel(group),
        [((PAD, D), bf16), ((PAD, 4 * DD), bf16), ((PAD, DD), bf16)],
        first, *parts, w_embed, mask_token, gd_one, w_dqkv,
    )
    decoded, ends, wdproj_grad, gd_two_grad, packed = decoder(
        ring, vis, table, cotangent, w_dproj, gd_two, up_all, down_all
    )
    second_grad, out_grad, dec_qkv_grad, embed_grad, gd_one_grad, mask_grad = call(
        embed_back_kernel,
        [
            ((PAD, D), f32), ((PAD, D), bf16), ((PAD, 3 * DD), bf16), ((PAD, DD), bf16), ((1, DD), f32), ((1, DD), f32),
        ],
        packed, table, dec_norm, second_low, gd_one, w_dqkv, w_embed,
    )
    dec_parts = [dec_norm, dec_qkv_grad, second_low, embed_grad, wdproj_grad, mask_grad, gd_one_grad, gd_two_grad]
    if ring.apart:
        hbm = pl.BlockSpec(memory_space=pl.ANY)
        ends = dec_flat = call(
            dec_flat_kernel(ring),
            [(ends.shape, bf16)],
            *dec_parts, ends,
            in_specs=[VMEM] * len(dec_parts) + [hbm],
            out_specs=[hbm],
            input_output_aliases={len(dec_parts): 0},
            scratch_shapes=[
                pltpu.VMEM((CORES * 2 * ring.chips * ring.dec_rows, 128), f32),
                pltpu.VMEM((clips, 2 * ring.dec_rows, 128), bf16),
                pltpu.SemaphoreType.DMA((clips,)),
            ],
        )[0]
    else:
        dec_flat = call(
            dec_flat_kernel(ring),
            [((DEC_ROWS, 128), bf16)],
            *dec_parts,
            scratch_shapes=[pltpu.VMEM((DEC_ROWS, 128), f32)],
        )[0]
    ends = lax.psum_scatter(ends.reshape(-1, 128), "clips", scatter_dimension=0, tiled=True)

    out_grads, pre_grads, parts = [out_grad], [], []
    for i in range(group):
        if i > 0:
            out_grads.append(after(lax.ppermute(out_grad, "mlp", turns[i - 1]), parts[0], dec_flat[:8]))
        pre_grad, part = call(
            enc_ffn_back_kernel,
            [((PAD, width), bf16), ((PAD, D), f32 if i == 0 else bf16)],
            out_grads[i], slopes[i], w_fc1, w_fc2,
        )
        pre_grads.append(pre_grad)
        parts.append(part if i == 0 else lax.ppermute(part, "mlp", back_turns[i - 1]))
    fc_halves = ((2, ring.chips, 2 * D * width // (CORES * 2 * ring.chips * 128), 128), bf16)
    fc_keep, fc_send = call(
        enc_weights_kernel(group, ring.chips), [fc_halves, fc_halves],
        core, *in2s, *pre_grads, *hiddens, *out_grads,
        in_specs=[SMEM] + [VMEM] * (4 * group),
        us=10,
    )
    parts[1:] = [after(part, fc_keep) for part in parts[1:]]
    flat_halves = ((2, ring.chips, sum(ring.rows), 128), bf16)
    input_grad, flat_keep, flat_send = call(
        enc_back_kernel(group, ring),
        [((VIS, D), f32), flat_halves, flat_halves],
        core, *parts, second_grad, first, x, qkv, probs, mix, w_qkv, w_proj, g_one, g_two, *([] if ring.apart else [dec_flat]),
        in_specs=[SMEM] + [VMEM] * (group + (10 if ring.apart else 11)),
        scratch_shapes=[
            pltpu.VMEM((PAD, 3 * D), bf16), pltpu.VMEM((WEMB_AT + 4 if ring.apart else FLAT_ROWS, 128), f32),
        ],
        us=20,
    )
    where = jnp.stack([ring.core, ring.at, ring.lane]).astype(jnp.int32)
    fc_placer = Placer(ring, where, [(D, width), (width, D)])
    flat_placer = Placer(ring, where, [(ring.part, 128), (DD, w_up.shape[1]), (w_up.shape[1], DD)])
    fc_found, flat_found = side_by_side(
        ring.round_trip(ring.start(fc_keep, fc_send), fc_placer.early),
        ring.round_trip(ring.start(flat_keep, flat_send), flat_placer.early, ends),
        0,
    )
    fc1_grad, fc2_grad = fc_placer.late(fc_found)
    param_grad, up_grad, down_grad = flat_placer.late(flat_found)
    return decoded, input_grad, param_grad.reshape(-1), fc1_grad, fc2_grad, up_grad, down_grad


def solution(mesh):
    placed = (
        P(),
        P(None, "mlp"),
        P("mlp", None),
        P(None, "mlp"),
        P("mlp", None),
        P(("clips", "mlp"), None),
        P(("clips", "mlp")),
        P(("clips", "mlp")),
        P(("clips", "mlp"), None),
    )
    group = mesh.shape["mlp"]

    def body(*args):
        return shards(mesh.shape["clips"], group, *args)

    return jax.shard_map(
        body,
        mesh=mesh,
        in_specs=placed,
        out_specs=(
            P(("clips", "mlp"), None),
            P(("clips", "mlp"), None),
            P("mlp"),
            P(None, "mlp"),
            P("mlp", None),
            P(None, "mlp"),
            P("mlp", None),
        ),
        check_vma=False,
    )
```

```python
import math

import jax
import jax.numpy as jnp
from jax import lax
from jax.experimental import pallas as pl
from jax.experimental.pallas import tpu as pltpu
from jax.sharding import PartitionSpec as P

D = 768
HEADS = 12
DD = 512
DHEADS = 16
FREQ = 8
WIN = 4
ROWS = 1536
VIS = 312
PAD = 320
SHORT_PATCHES = 512
PARAMS = 3804160
EPSILON = 1e-06
BLOCK = 256
GROUP = WIN * FREQ
HALF = DD // 2
ENC_SCALE = 1.0 / math.sqrt(D // HEADS)
DEC_SCALE = 1.0 / math.sqrt(DD // DHEADS)
LOWEST = -1e30
CORES = 2
bf16 = jnp.bfloat16
f32 = jnp.float32


def mm(left, right):
    return jnp.dot(left, right, preferred_element_type=f32)


def mm_nt(left, right):
    return lax.dot_general(left, right, (((1,), (1,)), ((), ())), preferred_element_type=f32)


def mm_tn(left, right):
    return lax.dot_general(left, right, (((0,), (0,)), ((), ())), preferred_element_type=f32)


def normalize(rows):
    centred = rows - jnp.mean(rows, axis=-1, keepdims=True)
    scale = lax.rsqrt(jnp.mean(centred * centred, axis=-1, keepdims=True) + EPSILON)
    return centred * scale, scale


def norm_back(grad, normed, scale, gain):
    weighted = grad * gain
    return scale * (
        weighted
        - jnp.mean(weighted, axis=-1, keepdims=True)
        - normed * jnp.mean(weighted * normed, axis=-1, keepdims=True)
    )


def gelu_parts(pre):
    cdf = 0.5 * (1.0 + lax.erf(pre * math.sqrt(0.5)))
    return pre * cdf, cdf + pre * jnp.exp(-0.5 * pre * pre) * (1.0 / math.sqrt(2.0 * math.pi))


def gained(grad, normed):
    return jnp.sum(grad * normed, axis=0, keepdims=True)


SMEM = pl.BlockSpec(memory_space=pltpu.SMEM)
VMEM = pl.BlockSpec(memory_space=pltpu.VMEM)


def hint(us):
    return pl.CostEstimate(flops=int(us * 8e8), transcendentals=0, bytes_accessed=int(us * 1e6))


def call(body, outs, *args, us=5, **more):
    return pl.pallas_call(
        body,
        cost_estimate=hint(us),
        out_shape=[jax.ShapeDtypeStruct(shape, dtype) for shape, dtype in outs],
        compiler_params=pltpu.CompilerParams(vmem_limit_bytes=56 * 2**20),
        **more,
    )(*args)


TILES = {"wqkv": 18, "wproj": 6, "wemb": 4, "wdqkv": 12, "wdproj": 4}
G1_AT = (D * 3 * D + D * D) // 128
WEMB_AT = G1_AT + 12
MASK_AT = WEMB_AT + D * 4
WDQKV_AT = MASK_AT + 4
WDPROJ_AT = WDQKV_AT + DD * 12
GD1_AT = WDPROJ_AT + DD * 4
FLAT_ROWS = PARAMS // 128
DEC_ROWS = FLAT_ROWS - WEMB_AT
PREP = 64


def widen(flat_ref, first, out_ref, tiles):
    for t in range(tiles):
        out_ref[:, t * 128 : t * 128 + 128] = flat_ref[
            pl.ds(first + t, out_ref.shape[0], stride=tiles), :
        ].astype(bf16)


def vector(flat_ref, first, count):
    return jnp.concatenate([flat_ref[first + i : first + i + 1, :] for i in range(count)], axis=1)


def flatten(flat_ref, first, value, tiles):
    for t in range(tiles):
        flat_ref[pl.ds(first + t, value.shape[0], stride=tiles), :] = value[:, t * 128 : t * 128 + 128]


def enc_prep_kernel(qkv_ref, proj_ref, gains_ref, wqkv_ref, wproj_ref, g1_ref, g2_ref, qkv_flat, proj_flat, gains_flat):
    qkv_flat[...] = qkv_ref[...].astype(f32)
    proj_flat[...] = proj_ref[...].astype(f32)
    widen(qkv_flat, 0, wqkv_ref, 18)
    widen(proj_flat, 0, wproj_ref, 6)

    @pl.when(pl.program_id(0) == 0)
    def _():
        gains_flat[...] = gains_ref[...].astype(f32)
        g1_ref[...] = vector(gains_flat, 0, 6)
        g2_ref[...] = vector(gains_flat, 6, 6)


def enc_prep(flat):
    whole = lambda *shape: pl.BlockSpec(shape, lambda i: (0,) * len(shape))
    return pl.pallas_call(
        enc_prep_kernel,
        grid=(D // PREP,),
        in_specs=[
            pl.BlockSpec((PREP * 18, 128), lambda i: (i, 0)),
            pl.BlockSpec((PREP * 6, 128), lambda i: (D * 18 // (PREP * 6) + i, 0)),
            pl.BlockSpec((16, 128), lambda i: (G1_AT // 16, 0)),
        ],
        out_specs=[
            pl.BlockSpec((PREP, 3 * D), lambda i: (i, 0)),
            pl.BlockSpec((PREP, D), lambda i: (i, 0)),
            whole(1, D),
            whole(1, D),
        ],
        out_shape=[
            jax.ShapeDtypeStruct((D, 3 * D), bf16),
            jax.ShapeDtypeStruct((D, D), bf16),
            jax.ShapeDtypeStruct((1, D), f32),
            jax.ShapeDtypeStruct((1, D), f32),
        ],
        scratch_shapes=[
            pltpu.VMEM((PREP * 18, 128), f32), pltpu.VMEM((PREP * 6, 128), f32), pltpu.VMEM((16, 128), f32),
        ],
    )(flat, flat, flat)


def dec_prep_kernel(count):
    def body(where_ref, flat_ref, _, *refs):
        ups, downs = refs[: 2 * count - 1], refs[2 * count - 1 : 4 * count - 2]
        (
            wemb_ref, mask_ref, wdqkv_ref, wdproj_ref, gd1_ref, gd2_ref, up_ref, down_ref, low, wide, sem,
        ) = refs[4 * count - 2 :]
        copy = pltpu.make_async_copy(flat_ref.at[pl.ds(G1_AT, FLAT_ROWS - G1_AT), :], low, sem)
        copy.start()
        core, lane = where_ref[0], where_ref[1]
        for pieces, whole in ((ups, up_ref), (downs, down_ref)):
            half = whole.shape[1] // CORES
            whole[lane] = pieces[0][...]
            for k in range(1, count):
                at = lax.rem(lane + k, count)
                near = pl.multiple_of(core * half, 8)
                far = pl.multiple_of((1 - core) * half, 8)
                whole[at, pl.ds(near, half), :] = pieces[2 * k - 1][...]
                whole[at, pl.ds(far, half), :] = pieces[2 * k][...]
        copy.wait()
        wide[...] = low[...].astype(f32)
        widen(wide, WEMB_AT - G1_AT, wemb_ref, 4)
        widen(wide, WDQKV_AT - G1_AT, wdqkv_ref, 12)
        widen(wide, WDPROJ_AT - G1_AT, wdproj_ref, 4)
        mask_ref[...] = vector(wide, MASK_AT - G1_AT, 4)
        gd1_ref[...] = vector(wide, GD1_AT - G1_AT, 4)
        gd2_ref[...] = vector(wide, GD1_AT - G1_AT + 4, 4)

    return body


def dec_prep(ring, flat, ups, downs, later):
    hbm = pl.BlockSpec(memory_space=pl.ANY)
    whole = lambda block: ((ring.group,) + block.shape, bf16)
    return call(
        dec_prep_kernel(ring.group),
        [
            ((D, DD), bf16), ((1, DD), f32), ((DD, 3 * DD), bf16), ((DD, DD), bf16), ((1, DD), f32), ((1, DD), f32),
            whole(ups[0]), whole(downs[0]),
        ],
        jnp.stack([ring.core, ring.lane]).astype(jnp.int32), flat, later, *ups, *downs,
        in_specs=[SMEM, hbm, hbm] + [VMEM] * (len(ups) + len(downs)),
        scratch_shapes=[
            pltpu.VMEM((FLAT_ROWS - G1_AT, 128), bf16), pltpu.VMEM((FLAT_ROWS - G1_AT, 128), f32),
            pltpu.SemaphoreType.DMA,
        ],
    )


def enc_attend_kernel(
    patches_ref, visible_ref, ids_ref, wqkv_ref, wproj_ref, g1_ref, g2_ref,
    x_ref, vis_ref, qkv_ref, probs_ref, mix_ref, first_ref, in2_ref, wide_vis,
):
    x_ref[...] = jnp.concatenate(
        [patches_ref[...].astype(f32), jnp.zeros((PAD - VIS, D), f32)], axis=0
    ).astype(bf16)
    wide_vis[...] = jnp.full(wide_vis.shape, -1, jnp.int32)
    wide_vis[:, :VIS] = visible_ref[...]
    vis = wide_vis[:, :PAD]
    vis_ref[...] = vis
    last = jnp.max(ids_ref[...].astype(f32))
    clip = jnp.where(vis < 0, -1.0, jnp.minimum((vis // SHORT_PATCHES).astype(f32), last))
    square = (PAD, PAD)
    across = jnp.broadcast_to(clip, square)
    diagonal = lax.broadcasted_iota(jnp.int32, square, 0) == lax.broadcasted_iota(jnp.int32, square, 1)
    allowed = across == jnp.sum(jnp.where(diagonal, across, 0.0), axis=1, keepdims=True)
    x = x_ref[...].astype(f32)
    normed, _ = normalize(x)
    qkv_ref[...] = mm((normed * g1_ref[...]).astype(bf16), wqkv_ref[...]).astype(bf16)
    low_lanes = lax.broadcasted_iota(jnp.int32, (PAD, 128), 1) < 64
    for pair in range(HEADS // 2):
        at = slice(pair * 128, pair * 128 + 128)
        query = qkv_ref[:, at]
        key = qkv_ref[:, D + pair * 128 : D + pair * 128 + 128]
        value = qkv_ref[:, 2 * D + pair * 128 : 2 * D + pair * 128 + 128]
        mixed = []
        for side in range(2):
            mine = low_lanes if side == 0 else jnp.logical_not(low_lanes)
            own = jnp.where(mine, query.astype(f32), 0.0).astype(bf16)
            scores = jnp.where(allowed, mm_nt(own, key) * ENC_SCALE, LOWEST)
            top = jnp.max(scores, axis=-1, keepdims=True)
            raised = jnp.exp(scores - top)
            probs = (raised / jnp.sum(raised, axis=-1, keepdims=True)).astype(bf16)
            probs_ref[2 * pair + side] = probs
            mixed.append(mm(probs, value))
        mix_ref[:, at] = jnp.where(low_lanes, mixed[0], mixed[1]).astype(bf16)
    first = x + mm(mix_ref[...], wproj_ref[...])
    first_ref[...] = first
    normed2, _ = normalize(first)
    in2_ref[...] = (normed2 * g2_ref[...]).astype(bf16)


def enc_ffn_kernel(in2_ref, fc1_ref, fc2_ref, part_ref, hidden_ref, slope_ref):
    act, slope = gelu_parts(mm(in2_ref[...], fc1_ref[...]))
    hidden = act.astype(bf16)
    hidden_ref[...] = hidden
    slope_ref[...] = slope.astype(bf16)
    part_ref[...] = mm(hidden, fc2_ref[...]).astype(part_ref.dtype)


def enc_ffn_back_kernel(out_grad_ref, slope_ref, fc1_ref, fc2_ref, pre_grad_ref, part_ref):
    grad = mm_nt(out_grad_ref[...], fc2_ref[...]) * slope_ref[...].astype(f32)
    pre_grad = grad.astype(bf16)
    pre_grad_ref[...] = pre_grad
    part_ref[...] = mm_nt(pre_grad, fc1_ref[...]).astype(part_ref.dtype)


def slabs(rows):
    return jnp.concatenate([rows[:, t * 128 : t * 128 + 128] for t in range(rows.shape[1] // 128)], axis=0)


def enc_weights_kernel(count, chips):
    def body(core_ref, *refs):
        in2s, pre_grads, hiddens, out_grads = (refs[i * count : (i + 1) * count] for i in range(4))
        keep_ref, send_ref = refs[4 * count : 4 * count + 2]
        at = 0
        for lefts, rights in ((in2s, pre_grads), (hiddens, out_grads)):
            total = mm_tn(lefts[0][...], rights[0][...])
            for i in range(1, count):
                total = total + mm_tn(lefts[i][...], rights[i][...])
            height = total.shape[0] // (CORES * 2 * chips)
            rows = height * total.shape[1] // 128

            def split(target, half, total=total, height=height, rows=rows, at=at):
                for way in range(2):
                    for chip in range(chips):
                        first = ((half * 2 + way) * chips + chip) * height
                        target[way, chip, at : at + rows, :] = slabs(total[first : first + height].astype(bf16))

            for half in range(CORES):
                @pl.when(core_ref[0] == half)
                def _(half=half, split=split):
                    split(keep_ref, half)
                    split(send_ref, 1 - half)

            at += rows

    return body


def embed_kernel(count):
    def body(first_ref, own_ref, *refs):
        parts = refs[: count - 1]
        wemb_ref, mask_ref, gd1_ref, wdqkv_ref, second_ref, table_ref, norm_ref = refs[count - 1 :]
        second = first_ref[...] + own_ref[...]
        for part in parts:
            second += part[...].astype(f32)
        low = second.astype(bf16)
        second_ref[...] = low
        embedded = mm(low, wemb_ref[...]).astype(bf16).astype(f32)
        row = lax.broadcasted_iota(jnp.int32, (PAD, DD), 0)
        start = jnp.where(row == VIS, mask_ref[...], embedded)
        normed, _ = normalize(start)
        dec_norm = (normed * gd1_ref[...]).astype(bf16)
        norm_ref[...] = dec_norm
        table_ref[:, : 3 * DD] = mm(dec_norm, wdqkv_ref[...]).astype(bf16)
        table_ref[:, 3 * DD :] = start.astype(bf16)

    return body


def spread(rows, same):
    left = jnp.concatenate([rows[:, :128]] * 4, axis=0) * same
    right = jnp.concatenate([rows[:, 128:]] * 4, axis=0) * same
    none = jnp.zeros_like(left)
    return jnp.concatenate(
        [jnp.concatenate([left, none], axis=1), jnp.concatenate([none, right], axis=1)], axis=0
    )


def diagonal(full):
    head = lax.broadcasted_iota(jnp.int32, (GROUP, 128), 1) // GROUP
    tiles = []
    for t in range(2):
        first = t * 128
        tile = full[first : first + GROUP, first : first + 128]
        for h in range(1, 4):
            tile = jnp.where(head == h, full[first + h * GROUP : first + (h + 1) * GROUP, first : first + 128], tile)
        tiles.append(tile)
    return jnp.concatenate(tiles, axis=1)


def segment_max(rows):
    tiles = []
    lane = lax.broadcasted_iota(jnp.int32, (rows.shape[0], 128), 1)
    for t in range(rows.shape[1] // 128):
        tile = rows[:, t * 128 : t * 128 + 128]
        for step in (1, 2, 8, 16):
            other = jnp.where(
                lane & step == 0, pltpu.roll(tile, 128 - step, 1), pltpu.roll(tile, step, 1)
            )
            tile = jnp.maximum(tile, other)
        tiles.append(tile)
    return jnp.concatenate(tiles, axis=1)


def decoder_kernel(chunks, ring):
    def body(
        vis_ref, table_ref, cot_ref, wdproj_ref, gd2_ref, up_ref, down_ref,
        decoded_ref, ends_ref, proj_grad_ref, gd2_grad_ref, packed_ref,
        qkv_ref, mix_ref, s_ref, p_ref, dmix_ref, ds_ref, back_ref, same_ref, ones_ref,
        up_acc, down_acc, proj_acc, gd2_acc, packed_acc,
    ):
        step = pl.program_id(0)

        @pl.when(step == 0)
        def _():
            up_acc[...] = jnp.zeros_like(up_acc)
            down_acc[...] = jnp.zeros_like(down_acc)
            proj_acc[...] = jnp.zeros_like(proj_acc)
            gd2_acc[...] = jnp.zeros_like(gd2_acc)
            packed_acc[...] = jnp.zeros_like(packed_acc)
            head_row = lax.broadcasted_iota(jnp.int32, (HALF, HALF), 0) // GROUP
            head_lane = lax.broadcasted_iota(jnp.int32, (HALF, HALF), 1) // GROUP
            ones = (head_row == head_lane).astype(f32).astype(bf16)
            ones_ref[...] = ones
            same_ref[...] = ones[:128, :128]

        row = lax.broadcasted_iota(jnp.int32, (BLOCK, PAD), 0) + step * BLOCK
        named = row == vis_ref[...]
        col = lax.broadcasted_iota(jnp.int32, (BLOCK, PAD), 1)
        hit = jnp.max(jnp.where(named, 1.0, 0.0), axis=1, keepdims=True)
        one_hot = jnp.where(named, 1.0, jnp.where(col == VIS, 1.0 - hit, 0.0)).astype(bf16)
        qkv_ref[...] = mm(one_hot, table_ref[:, : 3 * DD]).astype(bf16)
        start = mm(one_hot, table_ref[:, 3 * DD :])

        lane = lax.broadcasted_iota(jnp.int32, (BLOCK, DD), 1)
        line = lax.broadcasted_iota(jnp.int32, (BLOCK, DD), 0)
        window = (lane % FREQ) // WIN == (line % FREQ) // WIN
        n_groups = BLOCK // GROUP

        def parts(group, half):
            at = pl.ds(pl.multiple_of(group * GROUP, GROUP), GROUP)
            return at, slice(half * HALF, (half + 1) * HALF)

        def scores(group, _):
            same = same_ref[...]
            for half in range(2):
                at, cols = parts(group, half)
                key = qkv_ref[at, DD + half * HALF : DD + (half + 1) * HALF]
                s_ref[at, cols] = mm_nt(qkv_ref[at, cols], spread(key, same))
            return 0

        lax.fori_loop(0, n_groups, scores, 0, unroll=8)
        raw = s_ref[...] * DEC_SCALE
        top = segment_max(raw)
        raised = jnp.where(window, jnp.exp(raw - top), 0.0)
        p_low = raised.astype(bf16)
        total = jnp.concatenate(
            [mm(p_low[:, :HALF], ones_ref[...]), mm(p_low[:, HALF:], ones_ref[...])], axis=1
        )
        p_ref[...] = (raised / total).astype(bf16)

        def mixes(group, _):
            same = same_ref[...]
            for half in range(2):
                at, cols = parts(group, half)
                value = qkv_ref[at, 2 * DD + half * HALF : 2 * DD + (half + 1) * HALF]
                mix_ref[at, cols] = mm(p_ref[at, cols], spread(value, same)).astype(bf16)
            return 0

        lax.fori_loop(0, n_groups, mixes, 0, unroll=8)

        middle = start + mm(mix_ref[...], wdproj_ref[...])
        normed, scale = normalize(middle)
        in2 = (normed * gd2_ref[...]).astype(bf16)
        cot = cot_ref[...]
        out = jnp.zeros_like(middle)
        in2_grad = jnp.zeros_like(middle)
        for c in range(chunks):
            act, slope = gelu_parts(mm(in2, up_ref[c]))
            hidden = act.astype(bf16)
            out += mm(hidden, down_ref[c])
            pre_grad = (mm_nt(cot, down_ref[c]) * slope).astype(bf16)
            in2_grad += mm_nt(pre_grad, up_ref[c])
            down_acc[c] += mm_tn(hidden, cot)
            up_acc[c] += mm_tn(in2, pre_grad)
        decoded_ref[...] = (middle + out).astype(bf16)

        gd2_acc[...] += gained(in2_grad, normed)
        middle_grad = cot.astype(f32) + norm_back(in2_grad, normed, scale, gd2_ref[...])
        branch = middle_grad.astype(bf16)
        back_ref[:, 3 * DD :] = branch
        proj_acc[...] += mm_tn(mix_ref[...], branch)
        dmix_ref[...] = mm_nt(branch, wdproj_ref[...]).astype(bf16)

        def prob_grads(group, _):
            same = same_ref[...]
            for half in range(2):
                at, cols = parts(group, half)
                value = qkv_ref[at, 2 * DD + half * HALF : 2 * DD + (half + 1) * HALF]
                s_ref[at, cols] = mm_nt(dmix_ref[at, cols], spread(value, same))
            return 0

        lax.fori_loop(0, n_groups, prob_grads, 0, unroll=8)
        probs = p_ref[...].astype(f32)
        prob_grad = s_ref[...]
        weighed = (probs * prob_grad).astype(bf16)
        row_sum = jnp.concatenate(
            [mm(weighed[:, :HALF], ones_ref[...]), mm(weighed[:, HALF:], ones_ref[...])], axis=1
        )
        ds_ref[...] = (probs * (prob_grad - row_sum)).astype(bf16)

        def qkv_grads(group, _):
            same = same_ref[...]
            for half in range(2):
                at, cols = parts(group, half)
                key_cols = slice(DD + half * HALF, DD + (half + 1) * HALF)
                value_cols = slice(2 * DD + half * HALF, 2 * DD + (half + 1) * HALF)
                key = qkv_ref[at, key_cols]
                back_ref[at, cols] = (mm(ds_ref[at, cols], spread(key, same)) * DEC_SCALE).astype(bf16)
                key_grad = diagonal(mm_tn(ds_ref[at, cols], qkv_ref[at, cols]))
                back_ref[at, key_cols] = (key_grad * DEC_SCALE).astype(bf16)
                back_ref[at, value_cols] = diagonal(mm_tn(p_ref[at, cols], dmix_ref[at, cols])).astype(bf16)
            return 0

        lax.fori_loop(0, n_groups, qkv_grads, 0, unroll=8)
        packed_acc[...] += mm_tn(one_hot, back_ref[...])

        @pl.when(step == pl.num_programs(0) - 1)
        def _():
            tall, low = DD // (CORES * 2 * ring.chips), up_acc.shape[2] // (CORES * 2 * ring.chips)
            cut = tall * up_acc.shape[2] // 128
            for clip in range(ring.clips):
                for way in range(2):
                    block = ring.ahead(clip, way)
                    for y in range(chunks):
                        ends_ref[clip, y, way, :cut] = slabs(up_acc[y, block * tall : (block + 1) * tall].astype(bf16))
                        ends_ref[clip, y, way, cut:] = slabs(down_acc[y, block * low : (block + 1) * low].astype(bf16))
            proj_grad_ref[...] = proj_acc[...].astype(bf16)
            gd2_grad_ref[...] = gd2_acc[...]
            packed_ref[...] = packed_acc[...]

    return body


def decoder(ring, vis_row, table, cotangent, w_dproj, gd_two, up, down):
    chunks, _, width = up.shape
    rows = cotangent.shape[0]
    kept = lambda *shape: pl.BlockSpec(shape, lambda i: (0,) * len(shape), pipeline_mode=pl.Buffered(1))
    by_rows = pl.BlockSpec((BLOCK, DD), lambda i: (i, 0))
    ends = (ring.clips, chunks, 2, DD * width // (128 * ring.clips), 128)
    outs = [
        ((rows, DD), bf16, by_rows),
        (ends, bf16, kept(*ends)),
        ((DD, DD), bf16, kept(DD, DD)),
        ((1, DD), f32, kept(1, DD)),
        ((PAD, 4 * DD), f32, kept(PAD, 4 * DD)),
    ]
    return pl.pallas_call(
        decoder_kernel(chunks, ring),
        cost_estimate=hint(80),
        grid=(rows // BLOCK,),
        in_specs=[
            kept(1, PAD), kept(PAD, 4 * DD), by_rows, kept(DD, DD), kept(1, DD),
            kept(chunks, DD, width), kept(chunks, width, DD),
        ],
        out_specs=[spec for _, _, spec in outs],
        out_shape=[jax.ShapeDtypeStruct(shape, dtype) for shape, dtype, _ in outs],
        scratch_shapes=[
            pltpu.VMEM((BLOCK, 3 * DD), bf16),
            pltpu.VMEM((BLOCK, DD), bf16),
            pltpu.VMEM((BLOCK, DD), f32),
            pltpu.VMEM((BLOCK, DD), bf16),
            pltpu.VMEM((BLOCK, DD), bf16),
            pltpu.VMEM((BLOCK, DD), bf16),
            pltpu.VMEM((BLOCK, 4 * DD), bf16),
            pltpu.VMEM((128, 128), bf16),
            pltpu.VMEM((HALF, HALF), bf16),
            pltpu.VMEM((chunks, DD, width), f32),
            pltpu.VMEM((chunks, width, DD), f32),
            pltpu.VMEM((DD, DD), f32),
            pltpu.VMEM((1, DD), f32),
            pltpu.VMEM((PAD, 4 * DD), f32),
        ],
        compiler_params=pltpu.CompilerParams(vmem_limit_bytes=56 * 2**20),
    )(vis_row, table, cotangent, w_dproj, gd_two, up, down)


def embed_back_kernel(
    packed_ref, table_ref, norm_ref, second_ref, gd1_ref, wdqkv_ref, wemb_ref,
    second_grad_ref, out_grad_ref, qkv_grad_ref, embed_grad_ref, gd1_grad_ref, mask_grad_ref,
):
    qkv_grad = packed_ref[:, : 3 * DD].astype(bf16)
    qkv_grad_ref[...] = qkv_grad
    grad = mm_nt(qkv_grad, wdqkv_ref[...])
    normed, scale = normalize(table_ref[:, 3 * DD :].astype(f32))
    gd1_grad_ref[...] = gained(grad, normed)
    start_grad = packed_ref[:, 3 * DD :] + norm_back(grad, normed, scale, gd1_ref[...])
    mask_grad_ref[...] = start_grad[VIS : VIS + 1]
    row = lax.broadcasted_iota(jnp.int32, (PAD, DD), 0)
    embed_grad = jnp.where(row < VIS, start_grad, 0.0).astype(bf16)
    embed_grad_ref[...] = embed_grad
    second_grad = mm_nt(embed_grad, wemb_ref[...])
    second_grad_ref[...] = second_grad
    out_grad_ref[...] = second_grad.astype(bf16)


def dec_flat_kernel(ring):
    def body(
        norm_ref, qkv_grad_ref, second_ref, embed_grad_ref, proj_grad_ref, mask_grad_ref, gd1_grad_ref, gd2_grad_ref,
        flat_ref, wide,
    ):
        flatten(wide, 0, mm_tn(second_ref[...], embed_grad_ref[...]), 4)
        flatten(wide, MASK_AT - WEMB_AT, mask_grad_ref[...], 4)
        flatten(wide, WDQKV_AT - WEMB_AT, mm_tn(norm_ref[...], qkv_grad_ref[...]), 12)
        flatten(wide, WDPROJ_AT - WEMB_AT, proj_grad_ref[...].astype(f32), 4)
        flatten(wide, GD1_AT - WEMB_AT, gd1_grad_ref[...], 4)
        flatten(wide, GD1_AT + 4 - WEMB_AT, gd2_grad_ref[...], 4)
        if not ring.apart:
            flat_ref[...] = wide[...].astype(bf16)
            return
        wide[DEC_ROWS:, :] = jnp.zeros((wide.shape[0] - DEC_ROWS, 128), f32)
        for clip in range(ring.clips):
            for way in range(2):
                block = ring.ahead(clip, way)
                flat_ref[clip, way] = wide[block * ring.dec_rows : (block + 1) * ring.dec_rows, :].astype(bf16)

    return body


def enc_back_kernel(count, ring):
    def body(core_ref, own_ref, *refs):
        parts = refs[: count - 1]
        (
            second_grad_ref, first_ref, x_ref, qkv_ref, probs_ref, mix_ref, wqkv_ref, wproj_ref, g1_ref, g2_ref,
        ) = refs[count - 1 : count + 9]
        input_grad_ref, keep_ref, send_ref, qkv_grad_ref, wide = refs[-5:]
        in2_grad = own_ref[...]
        for part in parts:
            in2_grad += part[...].astype(f32)
        normed2, scale2 = normalize(first_ref[...])
        flatten(wide, G1_AT + 6, gained(in2_grad, normed2), 6)
        first_grad = second_grad_ref[...] + norm_back(in2_grad, normed2, scale2, g2_ref[...])
        branch = first_grad.astype(bf16)
        flatten(wide, D * 18, mm_tn(mix_ref[...], branch), 6)
        if not ring.apart:
            wide[WEMB_AT:FLAT_ROWS, :] = refs[-6][...].astype(f32)
        mix_grad = mm_nt(branch, wproj_ref[...]).astype(bf16)
        low_lanes = lax.broadcasted_iota(jnp.int32, (PAD, 128), 1) < 64
        for pair in range(HEADS // 2):
            at = slice(pair * 128, pair * 128 + 128)
            query = qkv_ref[:, at]
            key = qkv_ref[:, D + pair * 128 : D + pair * 128 + 128]
            value = qkv_ref[:, 2 * D + pair * 128 : 2 * D + pair * 128 + 128]
            upstream = mix_grad[:, at]
            found = []
            for side in range(2):
                mine = low_lanes if side == 0 else jnp.logical_not(low_lanes)
                own = jnp.where(mine, upstream.astype(f32), 0.0).astype(bf16)
                low_probs = probs_ref[2 * pair + side]
                probs = low_probs.astype(f32)
                prob_grad = mm_nt(own, value)
                row_sum = jnp.sum(probs * prob_grad, axis=-1, keepdims=True)
                score_grad = (probs * (prob_grad - row_sum)).astype(bf16)
                found.append((mm(score_grad, key), mm_tn(score_grad, query), mm_tn(low_probs, upstream)))
            for part, factor in enumerate((ENC_SCALE, ENC_SCALE, 1.0)):
                merged = jnp.where(low_lanes, found[0][part], found[1][part]) * factor
                qkv_grad_ref[:, part * D + pair * 128 : part * D + pair * 128 + 128] = merged.astype(bf16)
        normed, scale = normalize(x_ref[...].astype(f32))
        flatten(wide, 0, mm_tn((normed * g1_ref[...]).astype(bf16), qkv_grad_ref[...]), 18)
        grad = mm_nt(qkv_grad_ref[...], wqkv_ref[...])
        flatten(wide, G1_AT, gained(grad, normed), 6)
        input_grad_ref[...] = (first_grad + norm_back(grad, normed, scale, g1_ref[...]))[:VIS]

        def split(target, half):
            for way in range(2):
                for chip in range(ring.chips):
                    block = (half * 2 + way) * ring.chips + chip
                    at = 0
                    for y in range(ring.group):
                        height = ring.rows[y]
                        first = y * ring.part + block * height
                        count = max(0, min(height, ring.counts[y] - block * height))
                        if count > 0:
                            target[way, chip, at : at + count] = wide[first : first + count, :].astype(bf16)
                        if count < height:
                            target[way, chip, at + count : at + height] = jnp.zeros((height - count, 128), bf16)
                        at += height

        for half in range(CORES):
            @pl.when(core_ref[0] == half)
            def _(half=half):
                split(keep_ref, half)
                split(send_ref, 1 - half)

    return body


class Ring:
    def __init__(self, clips, group):
        self.chips = clips // CORES
        self.group = group
        chips = self.chips
        if chips == 8:
            order = [4 * z // 2 for z in range(4)] + [4 * z // 2 + 1 for z in reversed(range(4))]
        else:
            order = list(range(chips))
        place = [0] * chips
        for at, chip in enumerate(order):
            place[chip] = at
        clip = lax.axis_index("clips")
        self.places = place
        self.core = clip % CORES
        chip = clip // CORES
        if chips == 8:
            self.at = jnp.where(chip % 2 == 0, chip // 2, 7 - chip // 2)
        else:
            self.at = chip
        self.lane = lax.axis_index("mlp")
        step = lambda way: [
            (order[i] * CORES + c, order[(i + way) % chips] * CORES + c) for i in range(chips) for c in range(CORES)
        ]
        self.ways = (step(1), step(-1))
        self.swap = [(i, i ^ 1) for i in range(clips)]
        self.clips = clips
        self.cut = max(1, chips - 3)
        blocks = CORES * 2 * chips
        self.part = FLAT_ROWS // group
        whole = -(-(-(-self.part // blocks)) // 8) * 8
        self.apart = False
        if self.apart:
            self.counts = [self.part, WEMB_AT - self.part]
            second = -(-(-(-self.counts[1] // blocks)) // 8) * 8
            self.rows = [whole, second]
            self.dec_rows = whole - second
        else:
            self.counts = [self.part] * group
            self.rows = [whole] * group
            self.dec_rows = 0

    def ahead(self, clip, way):
        chip = (self.places[clip // CORES] + (1 if way == 0 else -1)) % self.chips
        return (clip % CORES * 2 + way) * self.chips + chip

    def fetch(self, block):
        half = block.shape[0] // CORES
        mine = lax.dynamic_slice_in_dim(block, self.core * half, half, 0)
        pieces = [block]
        for k in range(1, self.group):
            near = lax.ppermute(mine, "mlp", [(j, (j - k) % self.group) for j in range(self.group)])
            pieces += [near, self.swapped(near)]
        return pieces

    def swapped(self, value):
        return lax.ppermute(value, "clips", self.swap)

    def block(self, half, way, back):
        sign = 1 if way == 0 else -1
        return lax.dynamic_index_in_dim(half[way], (self.at - sign * back) % self.chips, 0, False)

    def start(self, keep, send):
        return keep + self.swapped(send)

    def round_trip(self, half, early, ends=None):
        held = [self.block(half, way, 0) for way in range(2)]
        for step in range(1, self.chips):
            came = [lax.ppermute(held[way], "clips", self.ways[way]) for way in range(2)]
            held = [came[way] + self.block(half, way, step) for way in range(2)]
            if ends is not None and step == 2:
                held, ends[0] = lax.optimization_barrier((held, ends[0]))
            if ends is not None and step == 5:
                held, ends[1:] = lax.optimization_barrier((held, ends[1:]))
            held = yield held
        if ends is not None:
            both = []
            for way in range(2):
                parts = []
                at = 0
                for y in range(self.group):
                    rows = [held[way][at : at + self.rows[y]]]
                    at += self.rows[y]
                    if self.apart and y == 1:
                        rows.append(ends[1][way])
                    parts.append(jnp.concatenate(rows + [ends[0][y, way]]))
                both.append(jnp.stack(parts))
            held = self.over_group(both)
        return (yield from self.spread(held, early))

    def over_group(self, held):
        both = jnp.stack(held, axis=1)
        total = lax.dynamic_index_in_dim(both, self.lane, 0, False)
        for k in range(1, self.group):
            away = lax.dynamic_index_in_dim(both, (self.lane + k) % self.group, 0, False)
            total = total + lax.ppermute(away, "mlp", [(j, (j + k) % self.group) for j in range(self.group)])
        return [total[0], total[1]]

    def spread(self, held, early):
        found = [[held[0]], [held[1]]]
        cut = self.cut
        placed = None
        for step in range(1, self.chips):
            came = [lax.ppermute(found[way][-1], "clips", self.ways[way]) for way in range(2)]
            if step == self.chips - 2:
                came, placed = lax.optimization_barrier((came, placed))
            came = yield came
            for way in range(2):
                found[way].append(came[way])
            if step == cut - 1:
                first = found[0] + found[1]
                placed = early(first, self.swapped(jnp.stack(first)))
        last = found[0][cut:] + found[1][cut:]
        return placed, last, self.swapped(jnp.stack(last))


def side_by_side(one, two, lead):
    trips, done = (one, two), [None, None]
    kept = [None, None]

    def advance(i):
        try:
            value = next(trips[i]) if kept[i] is None else trips[i].send(kept[i])
        except StopIteration as end:
            done[i] = end.value
            return
        other = kept[1 - i]
        kept[i] = value if other is None else lax.optimization_barrier((value, other))[0]

    for _ in range(lead):
        advance(0)
    while done[0] is None or done[1] is None:
        for i in range(2):
            if done[i] is None:
                advance(i)
    return done


def place_kernel(ring, shares, steps, aliased):
    n_outs = len(shares)
    count = len(steps)
    last_block = CORES * 2 * ring.chips - 1

    def body(where_ref, *refs):
        mine, other = refs[: 2 * count], refs[2 * count]
        rest = refs[2 * count + 1 + (n_outs if aliased else 0) :]
        outs, buffers, sems = rest[:n_outs], rest[n_outs : 2 * n_outs], rest[2 * n_outs]
        core, at, lane = where_ref[0], where_ref[1], where_ref[2]
        copies = []
        for way in range(2):
            sign = 1 if way == 0 else -1
            for i, step in enumerate(steps):
                slot = lax.rem(at + sign * (1 - step) + ring.chips, ring.chips)
                for near in (True, False):
                    value = mine[way * count + i][...] if near else other[way * count + i]
                    value = value.astype(f32)
                    side = core if near else 1 - core
                    block = (side * 2 + way) * ring.chips + slot
                    index = (way * count + i) * 2 + (0 if near else 1)
                    first = 0
                    for out, buffer, (total, columns, pieces) in zip(outs, buffers, shares):
                        tiles = columns // 128
                        high = sum(height for height, _, _ in pieces)
                        wide = [value[first + t * high : first + (t + 1) * high] for t in range(tiles)]
                        buffer[index] = jnp.concatenate(wide, axis=1) if tiles > 1 else wide[0]
                        first += tiles * high
                        start = 0
                        for height, row_of, short in pieces:
                            row = pl.multiple_of(row_of(block, lane), 8)
                            cases = [(height, None)] if short == height else [(height, False), (short, True)]
                            for rows, at_end in cases:
                                if rows == 0:
                                    continue
                                copy = pltpu.make_async_copy(
                                    buffer.at[index, pl.ds(start, rows), :], out.at[pl.ds(row, rows), :], sems.at[len(copies)]
                                )
                                copies.append((copy, None if at_end is None else (block == last_block) == at_end))
                                run(copy.start, copies[-1][1])
                            start += height
        for copy, condition in copies:
            run(copy.wait, condition)

    return body


def run(action, condition):
    if condition is None:
        action()
    else:
        pl.when(condition)(action)


def place(ring, where, shares, steps, mine, other, earlier=()):
    hbm = pl.BlockSpec(memory_space=pl.ANY)
    count = len(steps)
    copies = 4 * count * sum(1 if s == h else 2 for _, _, pieces in shares for h, _, s in pieces)
    return call(
        place_kernel(ring, shares, steps, bool(earlier)),
        [((total, columns), f32) for total, columns, _ in shares],
        where, *mine, other, *earlier,
        in_specs=[SMEM] + [VMEM] * (len(mine) + 1) + [hbm] * len(earlier),
        out_specs=[hbm] * len(shares),
        input_output_aliases={len(mine) + 2 + i: i for i in range(len(earlier))},
        scratch_shapes=[
            pltpu.VMEM((4 * count, sum(h for h, _, _ in pieces), columns), f32) for _, columns, pieces in shares
        ] + [pltpu.SemaphoreType.DMA((copies,))],
        us=6,
    )


def place_rows(ring, shares, steps, mine, other, earlier):
    count = len(steps)
    outs = list(earlier)
    first = 0
    for k, (total, columns, pieces) in enumerate(shares):
        tiles = columns // 128
        (height, _, _) = pieces[0]
        padded = CORES * 2 * ring.chips * height
        out = outs[k] if earlier else jnp.zeros((padded, columns), f32)
        for way in range(2):
            for i, step in enumerate(steps):
                slot = (ring.at + (1 if way == 0 else -1) * (1 - step)) % ring.chips
                for side, value in ((ring.core, mine[way * count + i]), (1 - ring.core, other[way * count + i])):
                    value = value[first : first + tiles * height].reshape(tiles, height, 128)
                    value = value.transpose(1, 0, 2).reshape(height, columns).astype(f32)
                    row = ((side * 2 + way) * ring.chips + slot) * height
                    out = lax.dynamic_update_slice_in_dim(out, value, row, 0)
        if earlier:
            outs[k] = out
        else:
            outs.append(out)
        first += tiles * height
    return outs


class Placer:
    def __init__(self, ring, where, totals):
        self.ring, self.where = ring, where
        blocks = CORES * 2 * ring.chips
        self.shares = []
        for total, columns in totals:
            flat = columns == 128
            if flat and ring.apart:
                whole, second = ring.rows
                cut = max(0, total - (blocks - 1) * whole)
                pieces = [
                    (second, lambda b, lane: jnp.where(lane == 0, b * whole, b * second), min(second, cut)),
                    (
                        whole - second,
                        lambda b, lane: jnp.where(
                            lane == 0, b * whole + second, ring.counts[1] + b * (whole - second)
                        ),
                        max(0, cut - second),
                    ),
                ]
            else:
                height = ring.rows[0] if flat else total // blocks
                pieces = [(height, lambda b, lane, height=height: b * height, total - (blocks - 1) * height)]
            self.shares.append((total, columns, pieces))
        self.plain = any(h % 8 for _, _, pieces in self.shares for h, _, _ in pieces)

    def early(self, mine, other):
        return self.put(range(self.ring.cut), mine, other, [])

    def late(self, found):
        placed, mine, other = found
        outs = self.put(range(self.ring.cut, self.ring.chips), mine, other, placed)
        return [out[:total] for out, (total, _, _) in zip(outs, self.shares)]

    def put(self, steps, mine, other, earlier):
        steps = list(steps)
        if self.plain:
            return place_rows(self.ring, self.shares, steps, mine, other, earlier)
        return place(self.ring, self.where, self.shares, steps, mine, other, earlier)


def after(value, *others):
    return lax.optimization_barrier((value,) + others)[0]


def shards(clips, group, flat_params, w_fc1, w_fc2, w_up, w_down, patches, clip_ids, visible_index, cotangent):
    width = w_fc1.shape[1]
    ring = Ring(clips, group)
    core = ring.core.astype(jnp.int32).reshape(1)
    turns = [[(i, (i + k) % group) for i in range(group)] for k in range(1, group)]
    back_turns = [[(i, (i - k) % group) for i in range(group)] for k in range(1, group)]

    ups = ring.fetch(w_up)
    downs = ring.fetch(w_down)

    flat = flat_params.reshape(FLAT_ROWS, 128)
    w_qkv, w_proj, g_one, g_two = enc_prep(flat)
    x, vis, qkv, probs, mix, first, in2 = call(
        enc_attend_kernel,
        [
            ((PAD, D), bf16), ((1, PAD), jnp.int32), ((PAD, 3 * D), bf16), ((HEADS, PAD, PAD), bf16), ((PAD, D), bf16),
            ((PAD, D), f32), ((PAD, D), bf16),
        ],
        patches, visible_index[None, :], clip_ids.reshape(-1, 128), w_qkv, w_proj, g_one, g_two,
        scratch_shapes=[pltpu.VMEM((1, 384), jnp.int32)],
        us=11,
    )

    in2s, hiddens, slopes, parts = [in2], [], [], []
    for i in range(group):
        if i > 0:
            in2s.append(after(lax.ppermute(in2, "mlp", turns[i - 1]), parts[0]))
        part, hidden, slope = call(
            enc_ffn_kernel,
            [((PAD, D), f32 if i == 0 else bf16), ((PAD, width), bf16), ((PAD, width), bf16)],
            in2s[i], w_fc1, w_fc2,
        )
        hiddens.append(hidden)
        slopes.append(slope)
        parts.append(part if i == 0 else lax.ppermute(part, "mlp", back_turns[i - 1]))
    w_embed, mask_token, w_dqkv, w_dproj, gd_one, gd_two, up_all, down_all = dec_prep(ring, flat, ups, downs, part)

    second_low, table, dec_norm = call(
        embed_kernel(group),
        [((PAD, D), bf16), ((PAD, 4 * DD), bf16), ((PAD, DD), bf16)],
        first, *parts, w_embed, mask_token, gd_one, w_dqkv,
    )
    decoded, ends, wdproj_grad, gd_two_grad, packed = decoder(
        ring, vis, table, cotangent, w_dproj, gd_two, up_all, down_all
    )
    ends = lax.psum_scatter(ends.reshape(-1, 128), "clips", scatter_dimension=0, tiled=True)
    ends = ends.reshape(group, 2, -1, 128)
    second_grad, out_grad, dec_qkv_grad, embed_grad, gd_one_grad, mask_grad = call(
        embed_back_kernel,
        [
            ((PAD, D), f32), ((PAD, D), bf16), ((PAD, 3 * DD), bf16), ((PAD, DD), bf16), ((1, DD), f32), ((1, DD), f32),
        ],
        packed, table, dec_norm, second_low, gd_one, w_dqkv, w_embed,
    )
    dec_wide = CORES * 2 * ring.chips * ring.dec_rows if ring.apart else DEC_ROWS
    dec_flat = call(
        dec_flat_kernel(ring),
        [((clips, 2, ring.dec_rows, 128) if ring.apart else (DEC_ROWS, 128), bf16)],
        dec_norm, dec_qkv_grad, second_low, embed_grad, wdproj_grad, mask_grad, gd_one_grad, gd_two_grad,
        scratch_shapes=[pltpu.VMEM((dec_wide, 128), f32)],
    )[0]
    dec_ends = []
    if ring.apart:
        dec_ends = lax.psum_scatter(dec_flat.reshape(-1, 128), "clips", scatter_dimension=0, tiled=True)
        dec_ends = [dec_ends.reshape(2, -1, 128)]

    out_grads, pre_grads, parts = [out_grad], [], []
    for i in range(group):
        if i > 0:
            out_grads.append(after(lax.ppermute(out_grad, "mlp", turns[i - 1]), parts[0], dec_flat))
        pre_grad, part = call(
            enc_ffn_back_kernel,
            [((PAD, width), bf16), ((PAD, D), f32 if i == 0 else bf16)],
            out_grads[i], slopes[i], w_fc1, w_fc2,
        )
        pre_grads.append(pre_grad)
        parts.append(part if i == 0 else lax.ppermute(part, "mlp", back_turns[i - 1]))
    fc_halves = ((2, ring.chips, 2 * D * width // (CORES * 2 * ring.chips * 128), 128), bf16)
    fc_keep, fc_send = call(
        enc_weights_kernel(group, ring.chips), [fc_halves, fc_halves],
        core, *in2s, *pre_grads, *hiddens, *out_grads,
        in_specs=[SMEM] + [VMEM] * (4 * group),
        us=10,
    )
    parts[1:] = [after(part, fc_keep) for part in parts[1:]]
    flat_halves = ((2, ring.chips, sum(ring.rows), 128), bf16)
    input_grad, flat_keep, flat_send = call(
        enc_back_kernel(group, ring),
        [((VIS, D), f32), flat_halves, flat_halves],
        core, *parts, second_grad, first, x, qkv, probs, mix, w_qkv, w_proj, g_one, g_two, *([] if ring.apart else [dec_flat]),
        in_specs=[SMEM] + [VMEM] * (group + (10 if ring.apart else 11)),
        scratch_shapes=[
            pltpu.VMEM((PAD, 3 * D), bf16), pltpu.VMEM((WEMB_AT + 4 if ring.apart else FLAT_ROWS, 128), f32),
        ],
        us=20,
    )
    where = jnp.stack([ring.core, ring.at, ring.lane]).astype(jnp.int32)
    fc_placer = Placer(ring, where, [(D, width), (width, D)])
    flat_placer = Placer(ring, where, [(ring.part, 128), (DD, w_up.shape[1]), (w_up.shape[1], DD)])
    fc_found, flat_found = side_by_side(
        ring.round_trip(ring.start(fc_keep, fc_send), fc_placer.early),
        ring.round_trip(ring.start(flat_keep, flat_send), flat_placer.early, [ends] + dec_ends),
        0,
    )
    fc1_grad, fc2_grad = fc_placer.late(fc_found)
    param_grad, up_grad, down_grad = flat_placer.late(flat_found)
    return decoded, input_grad, param_grad.reshape(-1), fc1_grad, fc2_grad, up_grad, down_grad


def solution(mesh):
    placed = (
        P(),
        P(None, "mlp"),
        P("mlp", None),
        P(None, "mlp"),
        P("mlp", None),
        P(("clips", "mlp"), None),
        P(("clips", "mlp")),
        P(("clips", "mlp")),
        P(("clips", "mlp"), None),
    )
    group = mesh.shape["mlp"]

    def body(*args):
        return shards(mesh.shape["clips"], group, *args)

    return jax.shard_map(
        body,
        mesh=mesh,
        in_specs=placed,
        out_specs=(
            P(("clips", "mlp"), None),
            P(("clips", "mlp"), None),
            P("mlp"),
            P(None, "mlp"),
            P("mlp", None),
            P(None, "mlp"),
            P("mlp", None),
        ),
        check_vma=False,
    )
```

```python
import math

import jax
import jax.numpy as jnp
from jax import lax
from jax.experimental import pallas as pl
from jax.experimental.pallas import tpu as pltpu
from jax.sharding import PartitionSpec as P

D = 768
HEADS = 12
DD = 512
DHEADS = 16
FREQ = 8
WIN = 4
ROWS = 1536
VIS = 312
PAD = 320
SHORT_PATCHES = 512
PARAMS = 3804160
EPSILON = 1e-06
BLOCK = 512
GROUP = WIN * FREQ
HALF = DD // 2
ENC_SCALE = 1.0 / math.sqrt(D // HEADS)
DEC_SCALE = 1.0 / math.sqrt(DD // DHEADS)
LOWEST = -1e30
CORES = 2
bf16 = jnp.bfloat16
f32 = jnp.float32


def mm(left, right):
    return jnp.dot(left, right, preferred_element_type=f32)


def mm_nt(left, right):
    return lax.dot_general(left, right, (((1,), (1,)), ((), ())), preferred_element_type=f32)


def mm_tn(left, right):
    return lax.dot_general(left, right, (((0,), (0,)), ((), ())), preferred_element_type=f32)


def normalize(rows):
    centred = rows - jnp.mean(rows, axis=-1, keepdims=True)
    scale = lax.rsqrt(jnp.mean(centred * centred, axis=-1, keepdims=True) + EPSILON)
    return centred * scale, scale


def norm_back(grad, normed, scale, gain):
    weighted = grad * gain
    return scale * (
        weighted
        - jnp.mean(weighted, axis=-1, keepdims=True)
        - normed * jnp.mean(weighted * normed, axis=-1, keepdims=True)
    )


def gelu_parts(pre):
    cdf = 0.5 * (1.0 + lax.erf(pre * math.sqrt(0.5)))
    return pre * cdf, cdf + pre * jnp.exp(-0.5 * pre * pre) * (1.0 / math.sqrt(2.0 * math.pi))


def gained(grad, normed):
    return jnp.sum(grad * normed, axis=0, keepdims=True)


SMEM = pl.BlockSpec(memory_space=pltpu.SMEM)
VMEM = pl.BlockSpec(memory_space=pltpu.VMEM)


def hint(us):
    return pl.CostEstimate(flops=int(us * 8e8), transcendentals=0, bytes_accessed=int(us * 1e6))


def call(body, outs, *args, us=5, **more):
    return pl.pallas_call(
        body,
        cost_estimate=hint(us),
        out_shape=[jax.ShapeDtypeStruct(shape, dtype) for shape, dtype in outs],
        compiler_params=pltpu.CompilerParams(vmem_limit_bytes=56 * 2**20),
        **more,
    )(*args)


TILES = {"wqkv": 18, "wproj": 6, "wemb": 4, "wdqkv": 12, "wdproj": 4}
G1_AT = (D * 3 * D + D * D) // 128
WEMB_AT = G1_AT + 12
MASK_AT = WEMB_AT + D * 4
WDQKV_AT = MASK_AT + 4
WDPROJ_AT = WDQKV_AT + DD * 12
GD1_AT = WDPROJ_AT + DD * 4
FLAT_ROWS = PARAMS // 128
DEC_ROWS = FLAT_ROWS - WEMB_AT
PREP = 64


def widen(flat_ref, first, out_ref, tiles):
    for t in range(tiles):
        out_ref[:, t * 128 : t * 128 + 128] = flat_ref[
            pl.ds(first + t, out_ref.shape[0], stride=tiles), :
        ].astype(bf16)


def vector(flat_ref, first, count):
    return jnp.concatenate([flat_ref[first + i : first + i + 1, :] for i in range(count)], axis=1)


def flatten(flat_ref, first, value, tiles):
    for t in range(tiles):
        flat_ref[pl.ds(first + t, value.shape[0], stride=tiles), :] = value[:, t * 128 : t * 128 + 128]


def enc_prep_kernel(qkv_ref, proj_ref, gains_ref, wqkv_ref, wproj_ref, g1_ref, g2_ref, qkv_flat, proj_flat, gains_flat):
    qkv_flat[...] = qkv_ref[...].astype(f32)
    proj_flat[...] = proj_ref[...].astype(f32)
    widen(qkv_flat, 0, wqkv_ref, 18)
    widen(proj_flat, 0, wproj_ref, 6)

    @pl.when(pl.program_id(0) == 0)
    def _():
        gains_flat[...] = gains_ref[...].astype(f32)
        g1_ref[...] = vector(gains_flat, 0, 6)
        g2_ref[...] = vector(gains_flat, 6, 6)


def enc_prep(flat):
    whole = lambda *shape: pl.BlockSpec(shape, lambda i: (0,) * len(shape))
    return pl.pallas_call(
        enc_prep_kernel,
        grid=(D // PREP,),
        in_specs=[
            pl.BlockSpec((PREP * 18, 128), lambda i: (i, 0)),
            pl.BlockSpec((PREP * 6, 128), lambda i: (D * 18 // (PREP * 6) + i, 0)),
            pl.BlockSpec((16, 128), lambda i: (G1_AT // 16, 0)),
        ],
        out_specs=[
            pl.BlockSpec((PREP, 3 * D), lambda i: (i, 0)),
            pl.BlockSpec((PREP, D), lambda i: (i, 0)),
            whole(1, D),
            whole(1, D),
        ],
        out_shape=[
            jax.ShapeDtypeStruct((D, 3 * D), bf16),
            jax.ShapeDtypeStruct((D, D), bf16),
            jax.ShapeDtypeStruct((1, D), f32),
            jax.ShapeDtypeStruct((1, D), f32),
        ],
        scratch_shapes=[
            pltpu.VMEM((PREP * 18, 128), f32), pltpu.VMEM((PREP * 6, 128), f32), pltpu.VMEM((16, 128), f32),
        ],
    )(flat, flat, flat)


def dec_prep_kernel(count):
    def body(where_ref, flat_ref, _, *refs):
        ups, downs = refs[: 2 * count - 1], refs[2 * count - 1 : 4 * count - 2]
        (
            wemb_ref, mask_ref, wdqkv_ref, wdproj_ref, gd1_ref, gd2_ref, up_ref, down_ref, low, wide, sem,
        ) = refs[4 * count - 2 :]
        copy = pltpu.make_async_copy(flat_ref.at[pl.ds(G1_AT, FLAT_ROWS - G1_AT), :], low, sem)
        copy.start()
        core, lane = where_ref[0], where_ref[1]
        for pieces, whole in ((ups, up_ref), (downs, down_ref)):
            half = whole.shape[1] // CORES
            whole[lane] = pieces[0][...]
            for k in range(1, count):
                at = lax.rem(lane + k, count)
                near = pl.multiple_of(core * half, 8)
                far = pl.multiple_of((1 - core) * half, 8)
                whole[at, pl.ds(near, half), :] = pieces[2 * k - 1][...]
                whole[at, pl.ds(far, half), :] = pieces[2 * k][...]
        copy.wait()
        wide[...] = low[...].astype(f32)
        widen(wide, WEMB_AT - G1_AT, wemb_ref, 4)
        widen(wide, WDQKV_AT - G1_AT, wdqkv_ref, 12)
        widen(wide, WDPROJ_AT - G1_AT, wdproj_ref, 4)
        mask_ref[...] = vector(wide, MASK_AT - G1_AT, 4)
        gd1_ref[...] = vector(wide, GD1_AT - G1_AT, 4)
        gd2_ref[...] = vector(wide, GD1_AT - G1_AT + 4, 4)

    return body


def dec_prep(ring, flat, ups, downs, later):
    hbm = pl.BlockSpec(memory_space=pl.ANY)
    whole = lambda block: ((ring.group,) + block.shape, bf16)
    return call(
        dec_prep_kernel(ring.group),
        [
            ((D, DD), bf16), ((1, DD), f32), ((DD, 3 * DD), bf16), ((DD, DD), bf16), ((1, DD), f32), ((1, DD), f32),
            whole(ups[0]), whole(downs[0]),
        ],
        jnp.stack([ring.core, ring.lane]).astype(jnp.int32), flat, later, *ups, *downs,
        in_specs=[SMEM, hbm, hbm] + [VMEM] * (len(ups) + len(downs)),
        scratch_shapes=[
            pltpu.VMEM((FLAT_ROWS - G1_AT, 128), bf16), pltpu.VMEM((FLAT_ROWS - G1_AT, 128), f32),
            pltpu.SemaphoreType.DMA,
        ],
    )


def enc_attend_kernel(
    patches_ref, visible_ref, ids_ref, wqkv_ref, wproj_ref, g1_ref, g2_ref,
    x_ref, vis_ref, qkv_ref, probs_ref, mix_ref, first_ref, in2_ref, wide_vis,
):
    x_ref[...] = jnp.concatenate(
        [patches_ref[...].astype(f32), jnp.zeros((PAD - VIS, D), f32)], axis=0
    ).astype(bf16)
    wide_vis[...] = jnp.full(wide_vis.shape, -1, jnp.int32)
    wide_vis[:, :VIS] = visible_ref[...]
    vis = wide_vis[:, :PAD]
    vis_ref[...] = vis
    last = jnp.max(ids_ref[...].astype(f32))
    clip = jnp.where(vis < 0, -1.0, jnp.minimum((vis // SHORT_PATCHES).astype(f32), last))
    square = (PAD, PAD)
    across = jnp.broadcast_to(clip, square)
    diagonal = lax.broadcasted_iota(jnp.int32, square, 0) == lax.broadcasted_iota(jnp.int32, square, 1)
    allowed = across == jnp.sum(jnp.where(diagonal, across, 0.0), axis=1, keepdims=True)
    x = x_ref[...].astype(f32)
    normed, _ = normalize(x)
    qkv_ref[...] = mm((normed * g1_ref[...]).astype(bf16), wqkv_ref[...]).astype(bf16)
    low_lanes = lax.broadcasted_iota(jnp.int32, (PAD, 128), 1) < 64
    for pair in range(HEADS // 2):
        at = slice(pair * 128, pair * 128 + 128)
        query = qkv_ref[:, at]
        key = qkv_ref[:, D + pair * 128 : D + pair * 128 + 128]
        value = qkv_ref[:, 2 * D + pair * 128 : 2 * D + pair * 128 + 128]
        mixed = []
        for side in range(2):
            mine = low_lanes if side == 0 else jnp.logical_not(low_lanes)
            own = jnp.where(mine, query.astype(f32), 0.0).astype(bf16)
            scores = jnp.where(allowed, mm_nt(own, key) * ENC_SCALE, LOWEST)
            top = jnp.max(scores, axis=-1, keepdims=True)
            raised = jnp.exp(scores - top)
            probs = (raised / jnp.sum(raised, axis=-1, keepdims=True)).astype(bf16)
            probs_ref[2 * pair + side] = probs
            mixed.append(mm(probs, value))
        mix_ref[:, at] = jnp.where(low_lanes, mixed[0], mixed[1]).astype(bf16)
    first = x + mm(mix_ref[...], wproj_ref[...])
    first_ref[...] = first
    normed2, _ = normalize(first)
    in2_ref[...] = (normed2 * g2_ref[...]).astype(bf16)


def enc_ffn_kernel(in2_ref, fc1_ref, fc2_ref, part_ref, hidden_ref, slope_ref):
    act, slope = gelu_parts(mm(in2_ref[...], fc1_ref[...]))
    hidden = act.astype(bf16)
    hidden_ref[...] = hidden
    slope_ref[...] = slope.astype(bf16)
    part_ref[...] = mm(hidden, fc2_ref[...]).astype(part_ref.dtype)


def enc_ffn_back_kernel(out_grad_ref, slope_ref, fc1_ref, fc2_ref, pre_grad_ref, part_ref):
    grad = mm_nt(out_grad_ref[...], fc2_ref[...]) * slope_ref[...].astype(f32)
    pre_grad = grad.astype(bf16)
    pre_grad_ref[...] = pre_grad
    part_ref[...] = mm_nt(pre_grad, fc1_ref[...]).astype(part_ref.dtype)


def slabs(rows):
    return jnp.concatenate([rows[:, t * 128 : t * 128 + 128] for t in range(rows.shape[1] // 128)], axis=0)


def enc_weights_kernel(count, chips):
    def body(core_ref, *refs):
        in2s, pre_grads, hiddens, out_grads = (refs[i * count : (i + 1) * count] for i in range(4))
        keep_ref, send_ref = refs[4 * count : 4 * count + 2]
        at = 0
        for lefts, rights in ((in2s, pre_grads), (hiddens, out_grads)):
            total = mm_tn(lefts[0][...], rights[0][...])
            for i in range(1, count):
                total = total + mm_tn(lefts[i][...], rights[i][...])
            height = total.shape[0] // (CORES * 2 * chips)
            rows = height * total.shape[1] // 128

            def split(target, half, total=total, height=height, rows=rows, at=at):
                for way in range(2):
                    for chip in range(chips):
                        first = ((half * 2 + way) * chips + chip) * height
                        target[way, chip, at : at + rows, :] = slabs(total[first : first + height].astype(bf16))

            for half in range(CORES):
                @pl.when(core_ref[0] == half)
                def _(half=half, split=split):
                    split(keep_ref, half)
                    split(send_ref, 1 - half)

            at += rows

    return body


def embed_kernel(count):
    def body(first_ref, own_ref, *refs):
        parts = refs[: count - 1]
        wemb_ref, mask_ref, gd1_ref, wdqkv_ref, second_ref, table_ref, norm_ref = refs[count - 1 :]
        second = first_ref[...] + own_ref[...]
        for part in parts:
            second += part[...].astype(f32)
        low = second.astype(bf16)
        second_ref[...] = low
        embedded = mm(low, wemb_ref[...]).astype(bf16).astype(f32)
        row = lax.broadcasted_iota(jnp.int32, (PAD, DD), 0)
        start = jnp.where(row == VIS, mask_ref[...], embedded)
        normed, _ = normalize(start)
        dec_norm = (normed * gd1_ref[...]).astype(bf16)
        norm_ref[...] = dec_norm
        table_ref[:, : 3 * DD] = mm(dec_norm, wdqkv_ref[...]).astype(bf16)
        table_ref[:, 3 * DD :] = start.astype(bf16)

    return body


def spread(rows, same):
    left = jnp.concatenate([rows[:, :128]] * 4, axis=0) * same
    right = jnp.concatenate([rows[:, 128:]] * 4, axis=0) * same
    none = jnp.zeros_like(left)
    return jnp.concatenate(
        [jnp.concatenate([left, none], axis=1), jnp.concatenate([none, right], axis=1)], axis=0
    )


def diagonal(full):
    head = lax.broadcasted_iota(jnp.int32, (GROUP, 128), 1) // GROUP
    tiles = []
    for t in range(2):
        first = t * 128
        tile = full[first : first + GROUP, first : first + 128]
        for h in range(1, 4):
            tile = jnp.where(head == h, full[first + h * GROUP : first + (h + 1) * GROUP, first : first + 128], tile)
        tiles.append(tile)
    return jnp.concatenate(tiles, axis=1)


def segment_max(rows):
    tiles = []
    lane = lax.broadcasted_iota(jnp.int32, (rows.shape[0], 128), 1)
    for t in range(rows.shape[1] // 128):
        tile = rows[:, t * 128 : t * 128 + 128]
        for step in (1, 2, 8, 16):
            other = jnp.where(
                lane & step == 0, pltpu.roll(tile, 128 - step, 1), pltpu.roll(tile, step, 1)
            )
            tile = jnp.maximum(tile, other)
        tiles.append(tile)
    return jnp.concatenate(tiles, axis=1)


def decoder_kernel(chunks, ring):
    def body(
        vis_ref, table_ref, cot_ref, wdproj_ref, gd2_ref, up_ref, down_ref,
        decoded_ref, ends_ref, proj_grad_ref, gd2_grad_ref, packed_ref,
        qkv_ref, mix_ref, s_ref, p_ref, dmix_ref, ds_ref, back_ref, same_ref, ones_ref,
        up_acc, down_acc, proj_acc, gd2_acc, packed_acc,
    ):
        step = pl.program_id(0)

        @pl.when(step == 0)
        def _():
            up_acc[...] = jnp.zeros_like(up_acc)
            down_acc[...] = jnp.zeros_like(down_acc)
            proj_acc[...] = jnp.zeros_like(proj_acc)
            gd2_acc[...] = jnp.zeros_like(gd2_acc)
            packed_acc[...] = jnp.zeros_like(packed_acc)
            head_row = lax.broadcasted_iota(jnp.int32, (HALF, HALF), 0) // GROUP
            head_lane = lax.broadcasted_iota(jnp.int32, (HALF, HALF), 1) // GROUP
            ones = (head_row == head_lane).astype(f32).astype(bf16)
            ones_ref[...] = ones
            same_ref[...] = ones[:128, :128]

        row = lax.broadcasted_iota(jnp.int32, (BLOCK, PAD), 0) + step * BLOCK
        named = row == vis_ref[...]
        col = lax.broadcasted_iota(jnp.int32, (BLOCK, PAD), 1)
        hit = jnp.max(jnp.where(named, 1.0, 0.0), axis=1, keepdims=True)
        one_hot = jnp.where(named, 1.0, jnp.where(col == VIS, 1.0 - hit, 0.0)).astype(bf16)
        qkv_ref[...] = mm(one_hot, table_ref[:, : 3 * DD]).astype(bf16)
        start = mm(one_hot, table_ref[:, 3 * DD :])

        lane = lax.broadcasted_iota(jnp.int32, (BLOCK, DD), 1)
        line = lax.broadcasted_iota(jnp.int32, (BLOCK, DD), 0)
        window = (lane % FREQ) // WIN == (line % FREQ) // WIN
        n_groups = BLOCK // GROUP

        def parts(group, half):
            at = pl.ds(pl.multiple_of(group * GROUP, GROUP), GROUP)
            return at, slice(half * HALF, (half + 1) * HALF)

        def scores(group, _):
            same = same_ref[...]
            for half in range(2):
                at, cols = parts(group, half)
                key = qkv_ref[at, DD + half * HALF : DD + (half + 1) * HALF]
                s_ref[at, cols] = mm_nt(qkv_ref[at, cols], spread(key, same))
            return 0

        lax.fori_loop(0, n_groups, scores, 0, unroll=16)
        raw = s_ref[...] * DEC_SCALE
        top = segment_max(raw)
        raised = jnp.where(window, jnp.exp(raw - top), 0.0)
        p_low = raised.astype(bf16)
        total = jnp.concatenate(
            [mm(p_low[:, :HALF], ones_ref[...]), mm(p_low[:, HALF:], ones_ref[...])], axis=1
        )
        p_ref[...] = (raised / total).astype(bf16)

        def mixes(group, _):
            same = same_ref[...]
            for half in range(2):
                at, cols = parts(group, half)
                value = qkv_ref[at, 2 * DD + half * HALF : 2 * DD + (half + 1) * HALF]
                mix_ref[at, cols] = mm(p_ref[at, cols], spread(value, same)).astype(bf16)
            return 0

        lax.fori_loop(0, n_groups, mixes, 0, unroll=16)

        middle = start + mm(mix_ref[...], wdproj_ref[...])
        normed, scale = normalize(middle)
        in2 = (normed * gd2_ref[...]).astype(bf16)
        cot = cot_ref[...]
        out = jnp.zeros_like(middle)
        in2_grad = jnp.zeros_like(middle)
        for c in range(chunks):
            act, slope = gelu_parts(mm(in2, up_ref[c]))
            hidden = act.astype(bf16)
            out += mm(hidden, down_ref[c])
            pre_grad = (mm_nt(cot, down_ref[c]) * slope).astype(bf16)
            in2_grad += mm_nt(pre_grad, up_ref[c])
            down_acc[c] += mm_tn(hidden, cot)
            up_acc[c] += mm_tn(in2, pre_grad)
        decoded_ref[...] = (middle + out).astype(bf16)

        gd2_acc[...] += gained(in2_grad, normed)
        middle_grad = cot.astype(f32) + norm_back(in2_grad, normed, scale, gd2_ref[...])
        branch = middle_grad.astype(bf16)
        back_ref[:, 3 * DD :] = branch
        proj_acc[...] += mm_tn(mix_ref[...], branch)
        dmix_ref[...] = mm_nt(branch, wdproj_ref[...]).astype(bf16)

        def prob_grads(group, _):
            same = same_ref[...]
            for half in range(2):
                at, cols = parts(group, half)
                value = qkv_ref[at, 2 * DD + half * HALF : 2 * DD + (half + 1) * HALF]
                s_ref[at, cols] = mm_nt(dmix_ref[at, cols], spread(value, same))
            return 0

        lax.fori_loop(0, n_groups, prob_grads, 0, unroll=16)
        probs = p_ref[...].astype(f32)
        prob_grad = s_ref[...]
        weighed = (probs * prob_grad).astype(bf16)
        row_sum = jnp.concatenate(
            [mm(weighed[:, :HALF], ones_ref[...]), mm(weighed[:, HALF:], ones_ref[...])], axis=1
        )
        ds_ref[...] = (probs * (prob_grad - row_sum)).astype(bf16)

        def qkv_grads(group, _):
            same = same_ref[...]
            for half in range(2):
                at, cols = parts(group, half)
                key_cols = slice(DD + half * HALF, DD + (half + 1) * HALF)
                value_cols = slice(2 * DD + half * HALF, 2 * DD + (half + 1) * HALF)
                key = qkv_ref[at, key_cols]
                back_ref[at, cols] = (mm(ds_ref[at, cols], spread(key, same)) * DEC_SCALE).astype(bf16)
                key_grad = diagonal(mm_tn(ds_ref[at, cols], qkv_ref[at, cols]))
                back_ref[at, key_cols] = (key_grad * DEC_SCALE).astype(bf16)
                back_ref[at, value_cols] = diagonal(mm_tn(p_ref[at, cols], dmix_ref[at, cols])).astype(bf16)
            return 0

        lax.fori_loop(0, n_groups, qkv_grads, 0, unroll=16)
        packed_acc[...] += mm_tn(one_hot, back_ref[...])

        @pl.when(step == pl.num_programs(0) - 1)
        def _():
            tall, low = DD // (CORES * 2 * ring.chips), up_acc.shape[2] // (CORES * 2 * ring.chips)
            cut = tall * up_acc.shape[2] // 128
            for clip in range(ring.clips):
                for way in range(2):
                    block = ring.ahead(clip, way)
                    for y in range(chunks):
                        ends_ref[clip, y, way, :cut] = slabs(up_acc[y, block * tall : (block + 1) * tall].astype(bf16))
                        ends_ref[clip, y, way, cut:] = slabs(down_acc[y, block * low : (block + 1) * low].astype(bf16))
            proj_grad_ref[...] = proj_acc[...].astype(bf16)
            gd2_grad_ref[...] = gd2_acc[...]
            packed_ref[...] = packed_acc[...]

    return body


def decoder(ring, vis_row, table, cotangent, w_dproj, gd_two, up, down):
    chunks, _, width = up.shape
    rows = cotangent.shape[0]
    kept = lambda *shape: pl.BlockSpec(shape, lambda i: (0,) * len(shape), pipeline_mode=pl.Buffered(1))
    by_rows = pl.BlockSpec((BLOCK, DD), lambda i: (i, 0))
    ends = (ring.clips, chunks, 2, DD * width // (128 * ring.clips), 128)
    outs = [
        ((rows, DD), bf16, by_rows),
        (ends, bf16, kept(*ends)),
        ((DD, DD), bf16, kept(DD, DD)),
        ((1, DD), f32, kept(1, DD)),
        ((PAD, 4 * DD), f32, kept(PAD, 4 * DD)),
    ]
    return pl.pallas_call(
        decoder_kernel(chunks, ring),
        cost_estimate=hint(80),
        grid=(rows // BLOCK,),
        in_specs=[
            kept(1, PAD), kept(PAD, 4 * DD), by_rows, kept(DD, DD), kept(1, DD),
            kept(chunks, DD, width), kept(chunks, width, DD),
        ],
        out_specs=[spec for _, _, spec in outs],
        out_shape=[jax.ShapeDtypeStruct(shape, dtype) for shape, dtype, _ in outs],
        scratch_shapes=[
            pltpu.VMEM((BLOCK, 3 * DD), bf16),
            pltpu.VMEM((BLOCK, DD), bf16),
            pltpu.VMEM((BLOCK, DD), f32),
            pltpu.VMEM((BLOCK, DD), bf16),
            pltpu.VMEM((BLOCK, DD), bf16),
            pltpu.VMEM((BLOCK, DD), bf16),
            pltpu.VMEM((BLOCK, 4 * DD), bf16),
            pltpu.VMEM((128, 128), bf16),
            pltpu.VMEM((HALF, HALF), bf16),
            pltpu.VMEM((chunks, DD, width), f32),
            pltpu.VMEM((chunks, width, DD), f32),
            pltpu.VMEM((DD, DD), f32),
            pltpu.VMEM((1, DD), f32),
            pltpu.VMEM((PAD, 4 * DD), f32),
        ],
        compiler_params=pltpu.CompilerParams(vmem_limit_bytes=56 * 2**20),
    )(vis_row, table, cotangent, w_dproj, gd_two, up, down)


def embed_back_kernel(
    packed_ref, table_ref, norm_ref, second_ref, gd1_ref, wdqkv_ref, wemb_ref,
    second_grad_ref, out_grad_ref, qkv_grad_ref, embed_grad_ref, gd1_grad_ref, mask_grad_ref,
):
    qkv_grad = packed_ref[:, : 3 * DD].astype(bf16)
    qkv_grad_ref[...] = qkv_grad
    grad = mm_nt(qkv_grad, wdqkv_ref[...])
    normed, scale = normalize(table_ref[:, 3 * DD :].astype(f32))
    gd1_grad_ref[...] = gained(grad, normed)
    start_grad = packed_ref[:, 3 * DD :] + norm_back(grad, normed, scale, gd1_ref[...])
    mask_grad_ref[...] = start_grad[VIS : VIS + 1]
    row = lax.broadcasted_iota(jnp.int32, (PAD, DD), 0)
    embed_grad = jnp.where(row < VIS, start_grad, 0.0).astype(bf16)
    embed_grad_ref[...] = embed_grad
    second_grad = mm_nt(embed_grad, wemb_ref[...])
    second_grad_ref[...] = second_grad
    out_grad_ref[...] = second_grad.astype(bf16)


def dec_flat_kernel(ring):
    def body(
        norm_ref, qkv_grad_ref, second_ref, embed_grad_ref, proj_grad_ref, mask_grad_ref, gd1_grad_ref, gd2_grad_ref,
        flat_ref, wide,
    ):
        flatten(wide, 0, mm_tn(second_ref[...], embed_grad_ref[...]), 4)
        flatten(wide, MASK_AT - WEMB_AT, mask_grad_ref[...], 4)
        flatten(wide, WDQKV_AT - WEMB_AT, mm_tn(norm_ref[...], qkv_grad_ref[...]), 12)
        flatten(wide, WDPROJ_AT - WEMB_AT, proj_grad_ref[...].astype(f32), 4)
        flatten(wide, GD1_AT - WEMB_AT, gd1_grad_ref[...], 4)
        flatten(wide, GD1_AT + 4 - WEMB_AT, gd2_grad_ref[...], 4)
        if not ring.apart:
            flat_ref[...] = wide[...].astype(bf16)
            return
        wide[DEC_ROWS:, :] = jnp.zeros((wide.shape[0] - DEC_ROWS, 128), f32)
        for clip in range(ring.clips):
            for way in range(2):
                block = ring.ahead(clip, way)
                flat_ref[clip, way] = wide[block * ring.dec_rows : (block + 1) * ring.dec_rows, :].astype(bf16)

    return body


def enc_back_kernel(count, ring):
    def body(core_ref, own_ref, *refs):
        parts = refs[: count - 1]
        (
            second_grad_ref, first_ref, x_ref, qkv_ref, probs_ref, mix_ref, wqkv_ref, wproj_ref, g1_ref, g2_ref,
        ) = refs[count - 1 : count + 9]
        input_grad_ref, keep_ref, send_ref, qkv_grad_ref, wide = refs[-5:]
        in2_grad = own_ref[...]
        for part in parts:
            in2_grad += part[...].astype(f32)
        normed2, scale2 = normalize(first_ref[...])
        flatten(wide, G1_AT + 6, gained(in2_grad, normed2), 6)
        first_grad = second_grad_ref[...] + norm_back(in2_grad, normed2, scale2, g2_ref[...])
        branch = first_grad.astype(bf16)
        flatten(wide, D * 18, mm_tn(mix_ref[...], branch), 6)
        if not ring.apart:
            wide[WEMB_AT:FLAT_ROWS, :] = refs[-6][...].astype(f32)
        mix_grad = mm_nt(branch, wproj_ref[...]).astype(bf16)
        low_lanes = lax.broadcasted_iota(jnp.int32, (PAD, 128), 1) < 64
        for pair in range(HEADS // 2):
            at = slice(pair * 128, pair * 128 + 128)
            query = qkv_ref[:, at]
            key = qkv_ref[:, D + pair * 128 : D + pair * 128 + 128]
            value = qkv_ref[:, 2 * D + pair * 128 : 2 * D + pair * 128 + 128]
            upstream = mix_grad[:, at]
            found = []
            for side in range(2):
                mine = low_lanes if side == 0 else jnp.logical_not(low_lanes)
                own = jnp.where(mine, upstream.astype(f32), 0.0).astype(bf16)
                low_probs = probs_ref[2 * pair + side]
                probs = low_probs.astype(f32)
                prob_grad = mm_nt(own, value)
                row_sum = jnp.sum(probs * prob_grad, axis=-1, keepdims=True)
                score_grad = (probs * (prob_grad - row_sum)).astype(bf16)
                found.append((mm(score_grad, key), mm_tn(score_grad, query), mm_tn(low_probs, upstream)))
            for part, factor in enumerate((ENC_SCALE, ENC_SCALE, 1.0)):
                merged = jnp.where(low_lanes, found[0][part], found[1][part]) * factor
                qkv_grad_ref[:, part * D + pair * 128 : part * D + pair * 128 + 128] = merged.astype(bf16)
        normed, scale = normalize(x_ref[...].astype(f32))
        flatten(wide, 0, mm_tn((normed * g1_ref[...]).astype(bf16), qkv_grad_ref[...]), 18)
        grad = mm_nt(qkv_grad_ref[...], wqkv_ref[...])
        flatten(wide, G1_AT, gained(grad, normed), 6)
        input_grad_ref[...] = (first_grad + norm_back(grad, normed, scale, g1_ref[...]))[:VIS]

        def split(target, half):
            for way in range(2):
                for chip in range(ring.chips):
                    block = (half * 2 + way) * ring.chips + chip
                    at = 0
                    for y in range(ring.group):
                        height = ring.rows[y]
                        first = y * ring.part + block * height
                        count = max(0, min(height, ring.counts[y] - block * height))
                        if count > 0:
                            target[way, chip, at : at + count] = wide[first : first + count, :].astype(bf16)
                        if count < height:
                            target[way, chip, at + count : at + height] = jnp.zeros((height - count, 128), bf16)
                        at += height

        for half in range(CORES):
            @pl.when(core_ref[0] == half)
            def _(half=half):
                split(keep_ref, half)
                split(send_ref, 1 - half)

    return body


class Ring:
    def __init__(self, clips, group):
        self.chips = clips // CORES
        self.group = group
        chips = self.chips
        if chips == 8:
            order = [4 * z // 2 for z in range(4)] + [4 * z // 2 + 1 for z in reversed(range(4))]
        else:
            order = list(range(chips))
        place = [0] * chips
        for at, chip in enumerate(order):
            place[chip] = at
        clip = lax.axis_index("clips")
        self.places = place
        self.core = clip % CORES
        chip = clip // CORES
        if chips == 8:
            self.at = jnp.where(chip % 2 == 0, chip // 2, 7 - chip // 2)
        else:
            self.at = chip
        self.lane = lax.axis_index("mlp")
        step = lambda way: [
            (order[i] * CORES + c, order[(i + way) % chips] * CORES + c) for i in range(chips) for c in range(CORES)
        ]
        self.ways = (step(1), step(-1))
        self.swap = [(i, i ^ 1) for i in range(clips)]
        self.clips = clips
        self.cut = max(2, chips - 2)
        blocks = CORES * 2 * chips
        self.part = FLAT_ROWS // group
        whole = -(-(-(-self.part // blocks)) // 8) * 8
        self.apart = False
        if self.apart:
            self.counts = [self.part, WEMB_AT - self.part]
            second = -(-(-(-self.counts[1] // blocks)) // 8) * 8
            self.rows = [whole, second]
            self.dec_rows = whole - second
        else:
            self.counts = [self.part] * group
            self.rows = [whole] * group
            self.dec_rows = 0

    def ahead(self, clip, way):
        chip = (self.places[clip // CORES] + (1 if way == 0 else -1)) % self.chips
        return (clip % CORES * 2 + way) * self.chips + chip

    def fetch(self, block):
        half = block.shape[0] // CORES
        mine = lax.dynamic_slice_in_dim(block, self.core * half, half, 0)
        pieces = [block]
        for k in range(1, self.group):
            near = lax.ppermute(mine, "mlp", [(j, (j - k) % self.group) for j in range(self.group)])
            pieces += [near, self.swapped(near)]
        return pieces

    def swapped(self, value):
        return lax.ppermute(value, "clips", self.swap)

    def block(self, halves, way, back):
        sign = 1 if way == 0 else -1
        at = (self.at - sign * back) % self.chips
        one, two = (lax.dynamic_index_in_dim(half[way], at, 0, False).astype(f32) for half in halves)
        return one + two

    def start(self, keep, send):
        return keep, self.swapped(send)

    def round_trip(self, halves, ends=None):
        held = [self.block(halves, way, 0).astype(bf16) for way in range(2)]
        for step in range(1, self.chips):
            came = [lax.ppermute(held[way], "clips", self.ways[way]) for way in range(2)]
            held = [(came[way].astype(f32) + self.block(halves, way, step)).astype(bf16) for way in range(2)]
            if ends is not None and step == 2:
                held, ends[0] = lax.optimization_barrier((held, ends[0]))
            if ends is not None and step == 5:
                held, ends[1:] = lax.optimization_barrier((held, ends[1:]))
            held = yield held
        if ends is not None:
            both = []
            for way in range(2):
                parts = []
                at = 0
                for y in range(self.group):
                    rows = [held[way][at : at + self.rows[y]]]
                    at += self.rows[y]
                    if self.apart and y == 1:
                        rows.append(ends[1][way])
                    parts.append(jnp.concatenate(rows + [ends[0][y, way]]))
                both.append(jnp.stack(parts))
            held = self.over_group(both)
        return (yield from self.spread(held))

    def over_group(self, held):
        both = jnp.stack(held, axis=1)
        total = lax.dynamic_index_in_dim(both, self.lane, 0, False)
        for k in range(1, self.group):
            away = lax.dynamic_index_in_dim(both, (self.lane + k) % self.group, 0, False)
            total = total + lax.ppermute(away, "mlp", [(j, (j + k) % self.group) for j in range(self.group)])
        return [total[0], total[1]]

    def spread(self, held):
        found = [[held[0]], [held[1]]]
        early = None
        for step in range(1, self.chips):
            came = yield [lax.ppermute(found[way][-1], "clips", self.ways[way]) for way in range(2)]
            for way in range(2):
                found[way].append(came[way])
            if step == self.cut - 1:
                early = self.swapped(jnp.stack(found[0] + found[1]))
        late = self.swapped(jnp.stack(found[0][self.cut :] + found[1][self.cut :]))
        return found[0] + found[1], early, late


def side_by_side(one, two, lead):
    trips, done = (one, two), [None, None]
    kept = [None, None]

    def advance(i):
        try:
            value = next(trips[i]) if kept[i] is None else trips[i].send(kept[i])
        except StopIteration as end:
            done[i] = end.value
            return
        other = kept[1 - i]
        kept[i] = value if other is None else lax.optimization_barrier((value, other))[0]

    for _ in range(lead):
        advance(0)
    while done[0] is None or done[1] is None:
        for i in range(2):
            if done[i] is None:
                advance(i)
    return done


def place_kernel(ring, streams):
    chips, cut = ring.chips, ring.cut
    each = 2 * chips + 2
    n_outs = sum(len(shares) for shares in streams)
    last_block = CORES * 2 * chips - 1

    def body(where_ref, *refs):
        sources, rest = refs[: each * len(streams)], refs[each * len(streams) :]
        outs, buffers, sems = rest[:n_outs], rest[n_outs : 2 * n_outs], rest[2 * n_outs]
        core, at, lane = where_ref[0], where_ref[1], where_ref[2]
        copies = []

        def put(shares, first_out, index, block, value):
            first = 0
            for i, (total, columns, pieces) in enumerate(shares):
                out, buffer = outs[first_out + i], buffers[first_out + i]
                tiles = columns // 128
                high = sum(height for height, _, _ in pieces)
                wide = [value[first + t * high : first + (t + 1) * high] for t in range(tiles)]
                buffer[index] = jnp.concatenate(wide, axis=1) if tiles > 1 else wide[0]
                first += tiles * high
                start = 0
                for height, row_of, short in pieces:
                    row = pl.multiple_of(row_of(block, lane), 8)
                    cases = [(height, None)] if short == height else [(height, False), (short, True)]
                    for rows, at_end in cases:
                        if rows == 0:
                            continue
                        copy = pltpu.make_async_copy(
                            buffer.at[index, pl.ds(start, rows), :], out.at[pl.ds(row, rows), :], sems.at[len(copies)]
                        )
                        copies.append((copy, None if at_end is None else (block == last_block) == at_end))
                        run(copy.start, copies[-1][1])
                    start += height

        for n, shares in enumerate(streams):
            mine = sources[n * each : n * each + 2 * chips]
            early, late = sources[n * each + 2 * chips : (n + 1) * each]
            first_out = sum(len(other) for other in streams[:n])
            for step in range(chips):
                for way in range(2):
                    slot = lax.rem(at + (1 if way == 0 else -1) * (1 - step) + chips, chips)
                    other = early[way * cut + step] if step < cut else late[way * (chips - cut) + step - cut]
                    for side, near, value in ((core, 0, mine[way * chips + step][...]), (1 - core, 1, other)):
                        block = (side * 2 + way) * chips + slot
                        put(shares, first_out, (step * 2 + way) * 2 + near, block, value.astype(f32))
        for copy, condition in copies:
            run(copy.wait, condition)

    return body


def run(action, condition):
    if condition is None:
        action()
    else:
        pl.when(condition)(action)


def shares_of(ring, totals):
    blocks = CORES * 2 * ring.chips
    shares = []
    for total, columns in totals:
        flat = columns == 128
        if flat and ring.apart:
            whole, second = ring.rows
            cut = max(0, total - (blocks - 1) * whole)
            pieces = [
                (second, lambda b, lane: jnp.where(lane == 0, b * whole, b * second), min(second, cut)),
                (
                    whole - second,
                    lambda b, lane: jnp.where(lane == 0, b * whole + second, ring.counts[1] + b * (whole - second)),
                    max(0, cut - second),
                ),
            ]
        else:
            height = ring.rows[0] if flat else total // blocks
            pieces = [(height, lambda b, lane, height=height: b * height, total - (blocks - 1) * height)]
        shares.append((total, columns, pieces))
    return shares


def place(ring, founds, totals):
    streams = [shares_of(ring, shapes) for shapes in totals]
    if any(height % 8 for shares in streams for _, _, pieces in shares for height, _, _ in pieces):
        return [out for found, shares in zip(founds, streams) for out in place_rows(ring, found, shares)]
    hbm = pl.BlockSpec(memory_space=pl.ANY)
    blocks = CORES * 2 * ring.chips
    flat_shares = [share for shares in streams for share in shares]
    copies = blocks * sum(1 if s == h else 2 for _, _, pieces in flat_shares for h, _, s in pieces)
    sources = [ref for mine, early, late in founds for ref in (*mine, early, late)]
    return call(
        place_kernel(ring, streams),
        [((total, columns), f32) for total, columns, _ in flat_shares],
        jnp.stack([ring.core, ring.at, ring.lane]).astype(jnp.int32), *sources,
        in_specs=[SMEM] + [VMEM] * len(sources),
        out_specs=[hbm] * len(flat_shares),
        scratch_shapes=[
            pltpu.VMEM((blocks, sum(h for h, _, _ in pieces), columns), f32) for _, columns, pieces in flat_shares
        ] + [pltpu.SemaphoreType.DMA((copies,))],
        us=9,
    )


def place_rows(ring, found, shares):
    mine, early, late = found
    chips, cut = ring.chips, ring.cut
    outs = []
    first = 0
    for total, columns, pieces in shares:
        tiles = columns // 128
        height = pieces[0][0]
        out = jnp.zeros((CORES * 2 * chips * height, columns), f32)
        for way in range(2):
            for step in range(chips):
                slot = (ring.at + (1 if way == 0 else -1) * (1 - step)) % chips
                other = early[way * cut + step] if step < cut else late[way * (chips - cut) + step - cut]
                for side, value in ((ring.core, mine[way * chips + step]), (1 - ring.core, other)):
                    value = value[first : first + tiles * height].reshape(tiles, height, 128)
                    value = value.transpose(1, 0, 2).reshape(height, columns).astype(f32)
                    row = ((side * 2 + way) * chips + slot) * height
                    out = lax.dynamic_update_slice_in_dim(out, value, row, 0)
        outs.append(out[:total])
        first += tiles * height
    return outs


def after(value, *others):
    return lax.optimization_barrier((value,) + others)[0]


def shards(clips, group, flat_params, w_fc1, w_fc2, w_up, w_down, patches, clip_ids, visible_index, cotangent):
    width = w_fc1.shape[1]
    ring = Ring(clips, group)
    core = ring.core.astype(jnp.int32).reshape(1)
    turns = [[(i, (i + k) % group) for i in range(group)] for k in range(1, group)]
    back_turns = [[(i, (i - k) % group) for i in range(group)] for k in range(1, group)]

    ups = ring.fetch(w_up)
    downs = ring.fetch(w_down)

    flat = flat_params.reshape(FLAT_ROWS, 128)
    w_qkv, w_proj, g_one, g_two = enc_prep(flat)
    x, vis, qkv, probs, mix, first, in2 = call(
        enc_attend_kernel,
        [
            ((PAD, D), bf16), ((1, PAD), jnp.int32), ((PAD, 3 * D), bf16), ((HEADS, PAD, PAD), bf16), ((PAD, D), bf16),
            ((PAD, D), f32), ((PAD, D), bf16),
        ],
        patches, visible_index[None, :], clip_ids.reshape(-1, 128), w_qkv, w_proj, g_one, g_two,
        scratch_shapes=[pltpu.VMEM((1, 384), jnp.int32)],
        us=11,
    )

    in2s, hiddens, slopes, parts = [in2], [], [], []
    for i in range(group):
        if i > 0:
            in2s.append(after(lax.ppermute(in2, "mlp", turns[i - 1]), parts[0]))
        part, hidden, slope = call(
            enc_ffn_kernel,
            [((PAD, D), f32 if i == 0 else bf16), ((PAD, width), bf16), ((PAD, width), bf16)],
            in2s[i], w_fc1, w_fc2,
        )
        hiddens.append(hidden)
        slopes.append(slope)
        parts.append(part if i == 0 else lax.ppermute(part, "mlp", back_turns[i - 1]))
    w_embed, mask_token, w_dqkv, w_dproj, gd_one, gd_two, up_all, down_all = dec_prep(ring, flat, ups, downs, part)

    second_low, table, dec_norm = call(
        embed_kernel(group),
        [((PAD, D), bf16), ((PAD, 4 * DD), bf16), ((PAD, DD), bf16)],
        first, *parts, w_embed, mask_token, gd_one, w_dqkv,
    )
    decoded, ends, wdproj_grad, gd_two_grad, packed = decoder(
        ring, vis, table, cotangent, w_dproj, gd_two, up_all, down_all
    )
    ends = lax.psum_scatter(ends.reshape(-1, 128), "clips", scatter_dimension=0, tiled=True)
    ends = ends.reshape(group, 2, -1, 128)
    second_grad, out_grad, dec_qkv_grad, embed_grad, gd_one_grad, mask_grad = call(
        embed_back_kernel,
        [
            ((PAD, D), f32), ((PAD, D), bf16), ((PAD, 3 * DD), bf16), ((PAD, DD), bf16), ((1, DD), f32), ((1, DD), f32),
        ],
        packed, table, dec_norm, second_low, gd_one, w_dqkv, w_embed,
    )
    dec_wide = CORES * 2 * ring.chips * ring.dec_rows if ring.apart else DEC_ROWS
    dec_flat = call(
        dec_flat_kernel(ring),
        [((clips, 2, ring.dec_rows, 128) if ring.apart else (DEC_ROWS, 128), bf16)],
        dec_norm, dec_qkv_grad, second_low, embed_grad, wdproj_grad, mask_grad, gd_one_grad, gd_two_grad,
        scratch_shapes=[pltpu.VMEM((dec_wide, 128), f32)],
    )[0]
    dec_ends = []
    if ring.apart:
        dec_ends = lax.psum_scatter(dec_flat.reshape(-1, 128), "clips", scatter_dimension=0, tiled=True)
        dec_ends = [dec_ends.reshape(2, -1, 128)]

    out_grads, pre_grads, parts = [out_grad], [], []
    for i in range(group):
        if i > 0:
            out_grads.append(after(lax.ppermute(out_grad, "mlp", turns[i - 1]), parts[0], dec_flat))
        pre_grad, part = call(
            enc_ffn_back_kernel,
            [((PAD, width), bf16), ((PAD, D), f32 if i == 0 else bf16)],
            out_grads[i], slopes[i], w_fc1, w_fc2,
        )
        pre_grads.append(pre_grad)
        parts.append(part if i == 0 else lax.ppermute(part, "mlp", back_turns[i - 1]))
    fc_halves = ((2, ring.chips, 2 * D * width // (CORES * 2 * ring.chips * 128), 128), bf16)
    fc_keep, fc_send = call(
        enc_weights_kernel(group, ring.chips), [fc_halves, fc_halves],
        core, *in2s, *pre_grads, *hiddens, *out_grads,
        in_specs=[SMEM] + [VMEM] * (4 * group),
        us=10,
    )
    parts[1:] = [after(part, fc_keep) for part in parts[1:]]
    flat_halves = ((2, ring.chips, sum(ring.rows), 128), bf16)
    input_grad, flat_keep, flat_send = call(
        enc_back_kernel(group, ring),
        [((VIS, D), f32), flat_halves, flat_halves],
        core, *parts, second_grad, first, x, qkv, probs, mix, w_qkv, w_proj, g_one, g_two, *([] if ring.apart else [dec_flat]),
        in_specs=[SMEM] + [VMEM] * (group + (10 if ring.apart else 11)),
        scratch_shapes=[
            pltpu.VMEM((PAD, 3 * D), bf16), pltpu.VMEM((WEMB_AT + 4 if ring.apart else FLAT_ROWS, 128), f32),
        ],
        us=20,
    )
    found = side_by_side(
        ring.round_trip(ring.start(fc_keep, fc_send)),
        ring.round_trip(ring.start(flat_keep, flat_send), [ends] + dec_ends),
        1,
    )
    fc1_grad, fc2_grad, param_grad, up_grad, down_grad = place(
        ring, found,
        [[(D, width), (width, D)], [(ring.part, 128), (DD, w_up.shape[1]), (w_up.shape[1], DD)]],
    )
    return decoded, input_grad, param_grad.reshape(-1), fc1_grad, fc2_grad, up_grad, down_grad


def solution(mesh):
    placed = (
        P(),
        P(None, "mlp"),
        P("mlp", None),
        P(None, "mlp"),
        P("mlp", None),
        P(("clips", "mlp"), None),
        P(("clips", "mlp")),
        P(("clips", "mlp")),
        P(("clips", "mlp"), None),
    )
    group = mesh.shape["mlp"]

    def body(*args):
        return shards(mesh.shape["clips"], group, *args)

    return jax.shard_map(
        body,
        mesh=mesh,
        in_specs=placed,
        out_specs=(
            P(("clips", "mlp"), None),
            P(("clips", "mlp"), None),
            P("mlp"),
            P(None, "mlp"),
            P("mlp", None),
            P(None, "mlp"),
            P("mlp", None),
        ),
        check_vma=False,
    )
```

```python
import math

import jax
import jax.numpy as jnp
from jax import lax
from jax.experimental import pallas as pl
from jax.experimental.pallas import tpu as pltpu
from jax.sharding import PartitionSpec as P

D = 768
HEADS = 12
DD = 512
DHEADS = 16
FREQ = 8
WIN = 4
ROWS = 1536
VIS = 312
PAD = 320
SHORT_PATCHES = 512
PARAMS = 3804160
EPSILON = 1e-06
BLOCK = 512
GROUP = WIN * FREQ
HALF = DD // 2
ENC_SCALE = 1.0 / math.sqrt(D // HEADS)
DEC_SCALE = 1.0 / math.sqrt(DD // DHEADS)
LOWEST = -1e30
CORES = 2
bf16 = jnp.bfloat16
f32 = jnp.float32


def mm(left, right):
    return jnp.dot(left, right, preferred_element_type=f32)


def mm_nt(left, right):
    return lax.dot_general(left, right, (((1,), (1,)), ((), ())), preferred_element_type=f32)


def mm_tn(left, right):
    return lax.dot_general(left, right, (((0,), (0,)), ((), ())), preferred_element_type=f32)


def normalize(rows):
    centred = rows - jnp.mean(rows, axis=-1, keepdims=True)
    scale = lax.rsqrt(jnp.mean(centred * centred, axis=-1, keepdims=True) + EPSILON)
    return centred * scale, scale


def norm_back(grad, normed, scale, gain):
    weighted = grad * gain
    return scale * (
        weighted
        - jnp.mean(weighted, axis=-1, keepdims=True)
        - normed * jnp.mean(weighted * normed, axis=-1, keepdims=True)
    )


def gelu_parts(pre):
    cdf = 0.5 * (1.0 + lax.erf(pre * math.sqrt(0.5)))
    return pre * cdf, cdf + pre * jnp.exp(-0.5 * pre * pre) * (1.0 / math.sqrt(2.0 * math.pi))


def gained(grad, normed):
    return jnp.sum(grad * normed, axis=0, keepdims=True)


SMEM = pl.BlockSpec(memory_space=pltpu.SMEM)
VMEM = pl.BlockSpec(memory_space=pltpu.VMEM)


def hint(us):
    return pl.CostEstimate(flops=int(us * 8e8), transcendentals=0, bytes_accessed=int(us * 1e6))


def call(body, outs, *args, us=5, **more):
    return pl.pallas_call(
        body,
        cost_estimate=hint(us),
        out_shape=[jax.ShapeDtypeStruct(shape, dtype) for shape, dtype in outs],
        compiler_params=pltpu.CompilerParams(vmem_limit_bytes=56 * 2**20),
        **more,
    )(*args)


TILES = {"wqkv": 18, "wproj": 6, "wemb": 4, "wdqkv": 12, "wdproj": 4}
G1_AT = (D * 3 * D + D * D) // 128
WEMB_AT = G1_AT + 12
MASK_AT = WEMB_AT + D * 4
WDQKV_AT = MASK_AT + 4
WDPROJ_AT = WDQKV_AT + DD * 12
GD1_AT = WDPROJ_AT + DD * 4
FLAT_ROWS = PARAMS // 128
DEC_ROWS = FLAT_ROWS - WEMB_AT
PREP = 64


def widen(flat_ref, first, out_ref, tiles):
    for t in range(tiles):
        out_ref[:, t * 128 : t * 128 + 128] = flat_ref[
            pl.ds(first + t, out_ref.shape[0], stride=tiles), :
        ].astype(bf16)


def vector(flat_ref, first, count):
    return jnp.concatenate([flat_ref[first + i : first + i + 1, :] for i in range(count)], axis=1)


def flatten(flat_ref, first, value, tiles):
    for t in range(tiles):
        flat_ref[pl.ds(first + t, value.shape[0], stride=tiles), :] = value[:, t * 128 : t * 128 + 128]


def enc_prep_kernel(qkv_ref, proj_ref, gains_ref, wqkv_ref, wproj_ref, g1_ref, g2_ref, qkv_flat, proj_flat, gains_flat):
    qkv_flat[...] = qkv_ref[...].astype(f32)
    proj_flat[...] = proj_ref[...].astype(f32)
    widen(qkv_flat, 0, wqkv_ref, 18)
    widen(proj_flat, 0, wproj_ref, 6)

    @pl.when(pl.program_id(0) == 0)
    def _():
        gains_flat[...] = gains_ref[...].astype(f32)
        g1_ref[...] = vector(gains_flat, 0, 6)
        g2_ref[...] = vector(gains_flat, 6, 6)


def enc_prep(flat):
    whole = lambda *shape: pl.BlockSpec(shape, lambda i: (0,) * len(shape))
    return pl.pallas_call(
        enc_prep_kernel,
        grid=(D // PREP,),
        in_specs=[
            pl.BlockSpec((PREP * 18, 128), lambda i: (i, 0)),
            pl.BlockSpec((PREP * 6, 128), lambda i: (D * 18 // (PREP * 6) + i, 0)),
            pl.BlockSpec((16, 128), lambda i: (G1_AT // 16, 0)),
        ],
        out_specs=[
            pl.BlockSpec((PREP, 3 * D), lambda i: (i, 0)),
            pl.BlockSpec((PREP, D), lambda i: (i, 0)),
            whole(1, D),
            whole(1, D),
        ],
        out_shape=[
            jax.ShapeDtypeStruct((D, 3 * D), bf16),
            jax.ShapeDtypeStruct((D, D), bf16),
            jax.ShapeDtypeStruct((1, D), f32),
            jax.ShapeDtypeStruct((1, D), f32),
        ],
        scratch_shapes=[
            pltpu.VMEM((PREP * 18, 128), f32), pltpu.VMEM((PREP * 6, 128), f32), pltpu.VMEM((16, 128), f32),
        ],
    )(flat, flat, flat)


def dec_prep_kernel(count):
    def body(where_ref, flat_ref, _, *refs):
        ups, downs = refs[: 2 * count - 1], refs[2 * count - 1 : 4 * count - 2]
        (
            wemb_ref, mask_ref, wdqkv_ref, wdproj_ref, gd1_ref, gd2_ref, up_ref, down_ref, low, wide, sem,
        ) = refs[4 * count - 2 :]
        copy = pltpu.make_async_copy(flat_ref.at[pl.ds(G1_AT, FLAT_ROWS - G1_AT), :], low, sem)
        copy.start()
        core, lane = where_ref[0], where_ref[1]
        for pieces, whole in ((ups, up_ref), (downs, down_ref)):
            half = whole.shape[1] // CORES
            whole[lane] = pieces[0][...]
            for k in range(1, count):
                at = lax.rem(lane + k, count)
                near = pl.multiple_of(core * half, 8)
                far = pl.multiple_of((1 - core) * half, 8)
                whole[at, pl.ds(near, half), :] = pieces[2 * k - 1][...]
                whole[at, pl.ds(far, half), :] = pieces[2 * k][...]
        copy.wait()
        wide[...] = low[...].astype(f32)
        widen(wide, WEMB_AT - G1_AT, wemb_ref, 4)
        widen(wide, WDQKV_AT - G1_AT, wdqkv_ref, 12)
        widen(wide, WDPROJ_AT - G1_AT, wdproj_ref, 4)
        mask_ref[...] = vector(wide, MASK_AT - G1_AT, 4)
        gd1_ref[...] = vector(wide, GD1_AT - G1_AT, 4)
        gd2_ref[...] = vector(wide, GD1_AT - G1_AT + 4, 4)

    return body


def dec_prep(ring, flat, ups, downs, later):
    hbm = pl.BlockSpec(memory_space=pl.ANY)
    whole = lambda block: ((ring.group,) + block.shape, bf16)
    return call(
        dec_prep_kernel(ring.group),
        [
            ((D, DD), bf16), ((1, DD), f32), ((DD, 3 * DD), bf16), ((DD, DD), bf16), ((1, DD), f32), ((1, DD), f32),
            whole(ups[0]), whole(downs[0]),
        ],
        jnp.stack([ring.core, ring.lane]).astype(jnp.int32), flat, later, *ups, *downs,
        in_specs=[SMEM, hbm, hbm] + [VMEM] * (len(ups) + len(downs)),
        scratch_shapes=[
            pltpu.VMEM((FLAT_ROWS - G1_AT, 128), bf16), pltpu.VMEM((FLAT_ROWS - G1_AT, 128), f32),
            pltpu.SemaphoreType.DMA,
        ],
    )


def enc_attend_kernel(
    patches_ref, visible_ref, ids_ref, wqkv_ref, wproj_ref, g1_ref, g2_ref,
    x_ref, vis_ref, qkv_ref, probs_ref, mix_ref, first_ref, in2_ref, wide_vis,
):
    x_ref[...] = jnp.concatenate(
        [patches_ref[...].astype(f32), jnp.zeros((PAD - VIS, D), f32)], axis=0
    ).astype(bf16)
    wide_vis[...] = jnp.full(wide_vis.shape, -1, jnp.int32)
    wide_vis[:, :VIS] = visible_ref[...]
    vis = wide_vis[:, :PAD]
    vis_ref[...] = vis
    last = jnp.max(ids_ref[...].astype(f32))
    clip = jnp.where(vis < 0, -1.0, jnp.minimum((vis // SHORT_PATCHES).astype(f32), last))
    square = (PAD, PAD)
    across = jnp.broadcast_to(clip, square)
    diagonal = lax.broadcasted_iota(jnp.int32, square, 0) == lax.broadcasted_iota(jnp.int32, square, 1)
    allowed = across == jnp.sum(jnp.where(diagonal, across, 0.0), axis=1, keepdims=True)
    x = x_ref[...].astype(f32)
    normed, _ = normalize(x)
    qkv_ref[...] = mm((normed * g1_ref[...]).astype(bf16), wqkv_ref[...]).astype(bf16)
    low_lanes = lax.broadcasted_iota(jnp.int32, (PAD, 128), 1) < 64
    for pair in range(HEADS // 2):
        at = slice(pair * 128, pair * 128 + 128)
        query = qkv_ref[:, at]
        key = qkv_ref[:, D + pair * 128 : D + pair * 128 + 128]
        value = qkv_ref[:, 2 * D + pair * 128 : 2 * D + pair * 128 + 128]
        mixed = []
        for side in range(2):
            mine = low_lanes if side == 0 else jnp.logical_not(low_lanes)
            own = jnp.where(mine, query.astype(f32), 0.0).astype(bf16)
            scores = jnp.where(allowed, mm_nt(own, key) * ENC_SCALE, LOWEST)
            top = jnp.max(scores, axis=-1, keepdims=True)
            raised = jnp.exp(scores - top)
            probs = (raised / jnp.sum(raised, axis=-1, keepdims=True)).astype(bf16)
            probs_ref[2 * pair + side] = probs
            mixed.append(mm(probs, value))
        mix_ref[:, at] = jnp.where(low_lanes, mixed[0], mixed[1]).astype(bf16)
    first = x + mm(mix_ref[...], wproj_ref[...])
    first_ref[...] = first
    normed2, _ = normalize(first)
    in2_ref[...] = (normed2 * g2_ref[...]).astype(bf16)


def enc_ffn_kernel(in2_ref, fc1_ref, fc2_ref, part_ref, hidden_ref, slope_ref, total):
    step = pl.program_id(0)
    act, slope = gelu_parts(mm(in2_ref[...], fc1_ref[...]))
    hidden = act.astype(bf16)
    hidden_ref[...] = hidden
    slope_ref[...] = slope.astype(bf16)
    found = mm(hidden, fc2_ref[...])

    @pl.when(step == 0)
    def _():
        total[...] = found

    @pl.when(step > 0)
    def _():
        total[...] += found

    @pl.when(step == pl.num_programs(0) - 1)
    def _():
        part_ref[...] = total[...].astype(part_ref.dtype)


def enc_ffn_back_kernel(out_grad_ref, slope_ref, fc1_ref, fc2_ref, pre_grad_ref, part_ref, total):
    step = pl.program_id(0)
    grad = mm_nt(out_grad_ref[...], fc2_ref[...]) * slope_ref[...].astype(f32)
    pre_grad = grad.astype(bf16)
    pre_grad_ref[...] = pre_grad
    found = mm_nt(pre_grad, fc1_ref[...])

    @pl.when(step == 0)
    def _():
        total[...] = found

    @pl.when(step > 0)
    def _():
        total[...] += found

    @pl.when(step == pl.num_programs(0) - 1)
    def _():
        part_ref[...] = total[...].astype(part_ref.dtype)


def by_hidden_units(kernel, rows, slope, fc1, fc2, dtype, n_wide):
    width = fc1.shape[1]
    chunk = width // 3
    whole = pl.BlockSpec((PAD, D), lambda i: (0, 0))
    wide = pl.BlockSpec((PAD, chunk), lambda i: (0, i))
    weights = [pl.BlockSpec((D, chunk), lambda i: (0, i)), pl.BlockSpec((chunk, D), lambda i: (i, 0))]
    part = (whole, jax.ShapeDtypeStruct((PAD, D), dtype))
    grown = [(wide, jax.ShapeDtypeStruct((PAD, width), bf16))] * n_wide
    outs = [part] + grown if slope is None else grown + [part]
    return pl.pallas_call(
        kernel,
        grid=(3,),
        in_specs=[whole] + ([] if slope is None else [wide]) + weights,
        out_specs=[spec for spec, _ in outs],
        out_shape=[shape for _, shape in outs],
        scratch_shapes=[pltpu.VMEM((PAD, D), f32)],
        cost_estimate=hint(5),
        compiler_params=pltpu.CompilerParams(vmem_limit_bytes=56 * 2**20),
    )(*([rows] if slope is None else [rows, slope]), fc1, fc2)


def slabs(rows):
    return jnp.concatenate([rows[:, t * 128 : t * 128 + 128] for t in range(rows.shape[1] // 128)], axis=0)


def enc_weights_kernel(count, chips):
    def body(core_ref, *refs):
        in2s, pre_grads, hiddens, out_grads = (refs[i * count : (i + 1) * count] for i in range(4))
        keep_ref, send_ref = refs[4 * count : 4 * count + 2]
        at = 0
        for lefts, rights in ((in2s, pre_grads), (hiddens, out_grads)):
            total = mm_tn(lefts[0][...], rights[0][...])
            for i in range(1, count):
                total = total + mm_tn(lefts[i][...], rights[i][...])
            height = total.shape[0] // (CORES * 2 * chips)
            rows = height * total.shape[1] // 128

            def split(target, half, total=total, height=height, rows=rows, at=at):
                for way in range(2):
                    for chip in range(chips):
                        first = ((half * 2 + way) * chips + chip) * height
                        target[way, chip, at : at + rows, :] = slabs(total[first : first + height].astype(bf16))

            for half in range(CORES):
                @pl.when(core_ref[0] == half)
                def _(half=half, split=split):
                    split(keep_ref, half)
                    split(send_ref, 1 - half)

            at += rows

    return body


def embed_kernel(count):
    def body(first_ref, own_ref, *refs):
        parts = refs[: count - 1]
        wemb_ref, mask_ref, gd1_ref, wdqkv_ref, second_ref, table_ref, norm_ref = refs[count - 1 :]
        second = first_ref[...] + own_ref[...]
        for part in parts:
            second += part[...].astype(f32)
        low = second.astype(bf16)
        second_ref[...] = low
        embedded = mm(low, wemb_ref[...]).astype(bf16).astype(f32)
        row = lax.broadcasted_iota(jnp.int32, (PAD, DD), 0)
        start = jnp.where(row == VIS, mask_ref[...], embedded)
        normed, _ = normalize(start)
        dec_norm = (normed * gd1_ref[...]).astype(bf16)
        norm_ref[...] = dec_norm
        table_ref[:, : 3 * DD] = mm(dec_norm, wdqkv_ref[...]).astype(bf16)
        table_ref[:, 3 * DD :] = start.astype(bf16)

    return body


def spread(rows, same):
    left = jnp.concatenate([rows[:, :128]] * 4, axis=0) * same
    right = jnp.concatenate([rows[:, 128:]] * 4, axis=0) * same
    none = jnp.zeros_like(left)
    return jnp.concatenate(
        [jnp.concatenate([left, none], axis=1), jnp.concatenate([none, right], axis=1)], axis=0
    )


def diagonal(full):
    head = lax.broadcasted_iota(jnp.int32, (GROUP, 128), 1) // GROUP
    tiles = []
    for t in range(2):
        first = t * 128
        tile = full[first : first + GROUP, first : first + 128]
        for h in range(1, 4):
            tile = jnp.where(head == h, full[first + h * GROUP : first + (h + 1) * GROUP, first : first + 128], tile)
        tiles.append(tile)
    return jnp.concatenate(tiles, axis=1)


def segment_max(rows):
    tiles = []
    lane = lax.broadcasted_iota(jnp.int32, (rows.shape[0], 128), 1)
    for t in range(rows.shape[1] // 128):
        tile = rows[:, t * 128 : t * 128 + 128]
        for step in (1, 2, 8, 16):
            other = jnp.where(
                lane & step == 0, pltpu.roll(tile, 128 - step, 1), pltpu.roll(tile, step, 1)
            )
            tile = jnp.maximum(tile, other)
        tiles.append(tile)
    return jnp.concatenate(tiles, axis=1)


def decoder_kernel(chunks, ring):
    def body(
        vis_ref, table_ref, cot_ref, wdproj_ref, gd2_ref, up_ref, down_ref,
        decoded_ref, ends_ref, proj_grad_ref, gd2_grad_ref, packed_ref,
        qkv_ref, mix_ref, s_ref, p_ref, dmix_ref, ds_ref, back_ref, same_ref, ones_ref,
        up_acc, down_acc, proj_acc, gd2_acc, packed_acc,
    ):
        step = pl.program_id(0)

        @pl.when(step == 0)
        def _():
            up_acc[...] = jnp.zeros_like(up_acc)
            down_acc[...] = jnp.zeros_like(down_acc)
            proj_acc[...] = jnp.zeros_like(proj_acc)
            gd2_acc[...] = jnp.zeros_like(gd2_acc)
            packed_acc[...] = jnp.zeros_like(packed_acc)
            head_row = lax.broadcasted_iota(jnp.int32, (HALF, HALF), 0) // GROUP
            head_lane = lax.broadcasted_iota(jnp.int32, (HALF, HALF), 1) // GROUP
            ones = (head_row == head_lane).astype(f32).astype(bf16)
            ones_ref[...] = ones
            same_ref[...] = ones[:128, :128]

        row = lax.broadcasted_iota(jnp.int32, (BLOCK, PAD), 0) + step * BLOCK
        named = row == vis_ref[...]
        col = lax.broadcasted_iota(jnp.int32, (BLOCK, PAD), 1)
        hit = jnp.max(jnp.where(named, 1.0, 0.0), axis=1, keepdims=True)
        one_hot = jnp.where(named, 1.0, jnp.where(col == VIS, 1.0 - hit, 0.0)).astype(bf16)
        qkv_ref[...] = mm(one_hot, table_ref[:, : 3 * DD]).astype(bf16)
        start = mm(one_hot, table_ref[:, 3 * DD :])

        lane = lax.broadcasted_iota(jnp.int32, (BLOCK, DD), 1)
        line = lax.broadcasted_iota(jnp.int32, (BLOCK, DD), 0)
        window = (lane % FREQ) // WIN == (line % FREQ) // WIN
        n_groups = BLOCK // GROUP

        def parts(group, half):
            at = pl.ds(pl.multiple_of(group * GROUP, GROUP), GROUP)
            return at, slice(half * HALF, (half + 1) * HALF)

        def scores(group, _):
            same = same_ref[...]
            for half in range(2):
                at, cols = parts(group, half)
                key = qkv_ref[at, DD + half * HALF : DD + (half + 1) * HALF]
                s_ref[at, cols] = mm_nt(qkv_ref[at, cols], spread(key, same))
            return 0

        lax.fori_loop(0, n_groups, scores, 0, unroll=16)
        raw = s_ref[...] * DEC_SCALE
        top = segment_max(raw)
        raised = jnp.where(window, jnp.exp(raw - top), 0.0)
        p_low = raised.astype(bf16)
        total = jnp.concatenate(
            [mm(p_low[:, :HALF], ones_ref[...]), mm(p_low[:, HALF:], ones_ref[...])], axis=1
        )
        p_ref[...] = (raised / total).astype(bf16)

        def mixes(group, _):
            same = same_ref[...]
            for half in range(2):
                at, cols = parts(group, half)
                value = qkv_ref[at, 2 * DD + half * HALF : 2 * DD + (half + 1) * HALF]
                mix_ref[at, cols] = mm(p_ref[at, cols], spread(value, same)).astype(bf16)
            return 0

        lax.fori_loop(0, n_groups, mixes, 0, unroll=16)

        middle = start + mm(mix_ref[...], wdproj_ref[...])
        normed, scale = normalize(middle)
        in2 = (normed * gd2_ref[...]).astype(bf16)
        cot = cot_ref[...]
        out = jnp.zeros_like(middle)
        in2_grad = jnp.zeros_like(middle)
        for c in range(chunks):
            act, slope = gelu_parts(mm(in2, up_ref[c]))
            hidden = act.astype(bf16)
            out += mm(hidden, down_ref[c])
            pre_grad = (mm_nt(cot, down_ref[c]) * slope).astype(bf16)
            in2_grad += mm_nt(pre_grad, up_ref[c])
            down_acc[c] += mm_tn(hidden, cot)
            up_acc[c] += mm_tn(in2, pre_grad)
        decoded_ref[...] = (middle + out).astype(bf16)

        gd2_acc[...] += gained(in2_grad, normed)
        middle_grad = cot.astype(f32) + norm_back(in2_grad, normed, scale, gd2_ref[...])
        branch = middle_grad.astype(bf16)
        back_ref[:, 3 * DD :] = branch
        proj_acc[...] += mm_tn(mix_ref[...], branch)
        dmix_ref[...] = mm_nt(branch, wdproj_ref[...]).astype(bf16)

        def prob_grads(group, _):
            same = same_ref[...]
            for half in range(2):
                at, cols = parts(group, half)
                value = qkv_ref[at, 2 * DD + half * HALF : 2 * DD + (half + 1) * HALF]
                s_ref[at, cols] = mm_nt(dmix_ref[at, cols], spread(value, same))
            return 0

        lax.fori_loop(0, n_groups, prob_grads, 0, unroll=16)
        probs = p_ref[...].astype(f32)
        prob_grad = s_ref[...]
        weighed = (probs * prob_grad).astype(bf16)
        row_sum = jnp.concatenate(
            [mm(weighed[:, :HALF], ones_ref[...]), mm(weighed[:, HALF:], ones_ref[...])], axis=1
        )
        ds_ref[...] = (probs * (prob_grad - row_sum)).astype(bf16)

        def qkv_grads(group, _):
            same = same_ref[...]
            for half in range(2):
                at, cols = parts(group, half)
                key_cols = slice(DD + half * HALF, DD + (half + 1) * HALF)
                value_cols = slice(2 * DD + half * HALF, 2 * DD + (half + 1) * HALF)
                key = qkv_ref[at, key_cols]
                back_ref[at, cols] = (mm(ds_ref[at, cols], spread(key, same)) * DEC_SCALE).astype(bf16)
                key_grad = diagonal(mm_tn(ds_ref[at, cols], qkv_ref[at, cols]))
                back_ref[at, key_cols] = (key_grad * DEC_SCALE).astype(bf16)
                back_ref[at, value_cols] = diagonal(mm_tn(p_ref[at, cols], dmix_ref[at, cols])).astype(bf16)
            return 0

        lax.fori_loop(0, n_groups, qkv_grads, 0, unroll=16)
        packed_acc[...] += mm_tn(one_hot, back_ref[...])

        @pl.when(step == pl.num_programs(0) - 1)
        def _():
            tall, low = DD // (CORES * 2 * ring.chips), up_acc.shape[2] // (CORES * 2 * ring.chips)
            cut = tall * up_acc.shape[2] // 128
            for clip in range(ring.clips):
                for way in range(2):
                    block = ring.ahead(clip, way)
                    for y in range(chunks):
                        ends_ref[clip, y, way, :cut] = slabs(up_acc[y, block * tall : (block + 1) * tall].astype(bf16))
                        ends_ref[clip, y, way, cut:] = slabs(down_acc[y, block * low : (block + 1) * low].astype(bf16))
            proj_grad_ref[...] = proj_acc[...].astype(bf16)
            gd2_grad_ref[...] = gd2_acc[...]
            packed_ref[...] = packed_acc[...]

    return body


def decoder(ring, vis_row, table, cotangent, w_dproj, gd_two, up, down):
    chunks, _, width = up.shape
    rows = cotangent.shape[0]
    kept = lambda *shape: pl.BlockSpec(shape, lambda i: (0,) * len(shape), pipeline_mode=pl.Buffered(1))
    by_rows = pl.BlockSpec((BLOCK, DD), lambda i: (i, 0))
    ends = (ring.clips, chunks, 2, DD * width // (128 * ring.clips), 128)
    outs = [
        ((rows, DD), bf16, by_rows),
        (ends, bf16, kept(*ends)),
        ((DD, DD), bf16, kept(DD, DD)),
        ((1, DD), f32, kept(1, DD)),
        ((PAD, 4 * DD), f32, kept(PAD, 4 * DD)),
    ]
    return pl.pallas_call(
        decoder_kernel(chunks, ring),
        cost_estimate=hint(80),
        grid=(rows // BLOCK,),
        in_specs=[
            kept(1, PAD), kept(PAD, 4 * DD), by_rows, kept(DD, DD), kept(1, DD),
            kept(chunks, DD, width), kept(chunks, width, DD),
        ],
        out_specs=[spec for _, _, spec in outs],
        out_shape=[jax.ShapeDtypeStruct(shape, dtype) for shape, dtype, _ in outs],
        scratch_shapes=[
            pltpu.VMEM((BLOCK, 3 * DD), bf16),
            pltpu.VMEM((BLOCK, DD), bf16),
            pltpu.VMEM((BLOCK, DD), f32),
            pltpu.VMEM((BLOCK, DD), bf16),
            pltpu.VMEM((BLOCK, DD), bf16),
            pltpu.VMEM((BLOCK, DD), bf16),
            pltpu.VMEM((BLOCK, 4 * DD), bf16),
            pltpu.VMEM((128, 128), bf16),
            pltpu.VMEM((HALF, HALF), bf16),
            pltpu.VMEM((chunks, DD, width), f32),
            pltpu.VMEM((chunks, width, DD), f32),
            pltpu.VMEM((DD, DD), f32),
            pltpu.VMEM((1, DD), f32),
            pltpu.VMEM((PAD, 4 * DD), f32),
        ],
        compiler_params=pltpu.CompilerParams(vmem_limit_bytes=56 * 2**20),
    )(vis_row, table, cotangent, w_dproj, gd_two, up, down)


def embed_back_kernel(
    packed_ref, table_ref, norm_ref, second_ref, gd1_ref, wdqkv_ref, wemb_ref,
    second_grad_ref, out_grad_ref, qkv_grad_ref, embed_grad_ref, gd1_grad_ref, mask_grad_ref,
):
    qkv_grad = packed_ref[:, : 3 * DD].astype(bf16)
    qkv_grad_ref[...] = qkv_grad
    grad = mm_nt(qkv_grad, wdqkv_ref[...])
    normed, scale = normalize(table_ref[:, 3 * DD :].astype(f32))
    gd1_grad_ref[...] = gained(grad, normed)
    start_grad = packed_ref[:, 3 * DD :] + norm_back(grad, normed, scale, gd1_ref[...])
    mask_grad_ref[...] = start_grad[VIS : VIS + 1]
    row = lax.broadcasted_iota(jnp.int32, (PAD, DD), 0)
    embed_grad = jnp.where(row < VIS, start_grad, 0.0).astype(bf16)
    embed_grad_ref[...] = embed_grad
    second_grad = mm_nt(embed_grad, wemb_ref[...])
    second_grad_ref[...] = second_grad
    out_grad_ref[...] = second_grad.astype(bf16)


def dec_flat_kernel(ring):
    def body(
        norm_ref, qkv_grad_ref, second_ref, embed_grad_ref, proj_grad_ref, mask_grad_ref, gd1_grad_ref, gd2_grad_ref,
        flat_ref, wide,
    ):
        flatten(wide, 0, mm_tn(second_ref[...], embed_grad_ref[...]), 4)
        flatten(wide, MASK_AT - WEMB_AT, mask_grad_ref[...], 4)
        flatten(wide, WDQKV_AT - WEMB_AT, mm_tn(norm_ref[...], qkv_grad_ref[...]), 12)
        flatten(wide, WDPROJ_AT - WEMB_AT, proj_grad_ref[...].astype(f32), 4)
        flatten(wide, GD1_AT - WEMB_AT, gd1_grad_ref[...], 4)
        flatten(wide, GD1_AT + 4 - WEMB_AT, gd2_grad_ref[...], 4)
        if not ring.apart:
            flat_ref[...] = wide[...].astype(bf16)
            return
        wide[DEC_ROWS:, :] = jnp.zeros((wide.shape[0] - DEC_ROWS, 128), f32)
        for clip in range(ring.clips):
            for way in range(2):
                block = ring.ahead(clip, way)
                flat_ref[clip, way] = wide[block * ring.dec_rows : (block + 1) * ring.dec_rows, :].astype(bf16)

    return body


def enc_back_kernel(count, ring):
    def body(core_ref, own_ref, *refs):
        parts = refs[: count - 1]
        (
            second_grad_ref, first_ref, x_ref, qkv_ref, probs_ref, mix_ref, wqkv_ref, wproj_ref, g1_ref, g2_ref,
        ) = refs[count - 1 : count + 9]
        input_grad_ref, keep_ref, send_ref, qkv_grad_ref, wide = refs[-5:]
        in2_grad = own_ref[...]
        for part in parts:
            in2_grad += part[...].astype(f32)
        normed2, scale2 = normalize(first_ref[...])
        flatten(wide, G1_AT + 6, gained(in2_grad, normed2), 6)
        first_grad = second_grad_ref[...] + norm_back(in2_grad, normed2, scale2, g2_ref[...])
        branch = first_grad.astype(bf16)
        flatten(wide, D * 18, mm_tn(mix_ref[...], branch), 6)
        if not ring.apart:
            wide[WEMB_AT:FLAT_ROWS, :] = refs[-6][...].astype(f32)
        mix_grad = mm_nt(branch, wproj_ref[...]).astype(bf16)
        low_lanes = lax.broadcasted_iota(jnp.int32, (PAD, 128), 1) < 64
        for pair in range(HEADS // 2):
            at = slice(pair * 128, pair * 128 + 128)
            query = qkv_ref[:, at]
            key = qkv_ref[:, D + pair * 128 : D + pair * 128 + 128]
            value = qkv_ref[:, 2 * D + pair * 128 : 2 * D + pair * 128 + 128]
            upstream = mix_grad[:, at]
            found = []
            for side in range(2):
                mine = low_lanes if side == 0 else jnp.logical_not(low_lanes)
                own = jnp.where(mine, upstream.astype(f32), 0.0).astype(bf16)
                low_probs = probs_ref[2 * pair + side]
                probs = low_probs.astype(f32)
                prob_grad = mm_nt(own, value)
                row_sum = jnp.sum(probs * prob_grad, axis=-1, keepdims=True)
                score_grad = (probs * (prob_grad - row_sum)).astype(bf16)
                found.append((mm(score_grad, key), mm_tn(score_grad, query), mm_tn(low_probs, upstream)))
            for part, factor in enumerate((ENC_SCALE, ENC_SCALE, 1.0)):
                merged = jnp.where(low_lanes, found[0][part], found[1][part]) * factor
                qkv_grad_ref[:, part * D + pair * 128 : part * D + pair * 128 + 128] = merged.astype(bf16)
        normed, scale = normalize(x_ref[...].astype(f32))
        flatten(wide, 0, mm_tn((normed * g1_ref[...]).astype(bf16), qkv_grad_ref[...]), 18)
        grad = mm_nt(qkv_grad_ref[...], wqkv_ref[...])
        flatten(wide, G1_AT, gained(grad, normed), 6)
        input_grad_ref[...] = (first_grad + norm_back(grad, normed, scale, g1_ref[...]))[:VIS]

        def split(target, half):
            for way in range(2):
                for chip in range(ring.chips):
                    block = (half * 2 + way) * ring.chips + chip
                    at = 0
                    for y in range(ring.group):
                        height = ring.rows[y]
                        first = y * ring.part + block * height
                        count = max(0, min(height, ring.counts[y] - block * height))
                        if count > 0:
                            target[way, chip, at : at + count] = wide[first : first + count, :].astype(bf16)
                        if count < height:
                            target[way, chip, at + count : at + height] = jnp.zeros((height - count, 128), bf16)
                        at += height

        for half in range(CORES):
            @pl.when(core_ref[0] == half)
            def _(half=half):
                split(keep_ref, half)
                split(send_ref, 1 - half)

    return body


class Ring:
    def __init__(self, clips, group):
        self.chips = clips // CORES
        self.group = group
        chips = self.chips
        if chips == 8:
            order = [4 * z // 2 for z in range(4)] + [4 * z // 2 + 1 for z in reversed(range(4))]
        else:
            order = list(range(chips))
        place = [0] * chips
        for at, chip in enumerate(order):
            place[chip] = at
        clip = lax.axis_index("clips")
        self.places = place
        self.core = clip % CORES
        chip = clip // CORES
        if chips == 8:
            self.at = jnp.where(chip % 2 == 0, chip // 2, 7 - chip // 2)
        else:
            self.at = chip
        self.lane = lax.axis_index("mlp")
        step = lambda way: [
            (order[i] * CORES + c, order[(i + way) % chips] * CORES + c) for i in range(chips) for c in range(CORES)
        ]
        self.ways = (step(1), step(-1))
        self.swap = [(i, i ^ 1) for i in range(clips)]
        self.clips = clips
        self.cut = max(2, chips - 2)
        blocks = CORES * 2 * chips
        self.part = FLAT_ROWS // group
        whole = -(-(-(-self.part // blocks)) // 8) * 8
        self.apart = False
        if self.apart:
            self.counts = [self.part, WEMB_AT - self.part]
            second = -(-(-(-self.counts[1] // blocks)) // 8) * 8
            self.rows = [whole, second]
            self.dec_rows = whole - second
        else:
            self.counts = [self.part] * group
            self.rows = [whole] * group
            self.dec_rows = 0

    def ahead(self, clip, way):
        chip = (self.places[clip // CORES] + (1 if way == 0 else -1)) % self.chips
        return (clip % CORES * 2 + way) * self.chips + chip

    def fetch(self, block):
        half = block.shape[0] // CORES
        mine = lax.dynamic_slice_in_dim(block, self.core * half, half, 0)
        pieces = [block]
        for k in range(1, self.group):
            near = lax.ppermute(mine, "mlp", [(j, (j - k) % self.group) for j in range(self.group)])
            pieces += [near, self.swapped(near)]
        return pieces

    def swapped(self, value):
        return lax.ppermute(value, "clips", self.swap)

    def block(self, halves, way, back):
        sign = 1 if way == 0 else -1
        at = (self.at - sign * back) % self.chips
        one, two = (lax.dynamic_index_in_dim(half[way], at, 0, False).astype(f32) for half in halves)
        return one + two

    def start(self, keep, send, hurry=False):
        if not hurry:
            halves = keep, self.swapped(send)
            return halves, [self.block(halves, way, 0).astype(bf16) for way in range(2)]
        pick = lambda half: jnp.stack([lax.dynamic_index_in_dim(half[way], self.at, 0, False) for way in range(2)])
        piece = self.swapped(pick(send))
        first = (pick(keep).astype(f32) + piece.astype(f32)).astype(bf16)
        return (keep, self.swapped(after(send, piece))), [first[0], first[1]]

    def round_trip(self, started, ends=None):
        halves, held = started
        for step in range(1, self.chips):
            came = [lax.ppermute(held[way], "clips", self.ways[way]) for way in range(2)]
            held = [(came[way].astype(f32) + self.block(halves, way, step)).astype(bf16) for way in range(2)]
            if ends is not None and step == 2:
                held, ends[0] = lax.optimization_barrier((held, ends[0]))
            if ends is not None and step == 5:
                held, ends[1:] = lax.optimization_barrier((held, ends[1:]))
            held = yield held
        if ends is not None:
            both = []
            for way in range(2):
                parts = []
                at = 0
                for y in range(self.group):
                    rows = [held[way][at : at + self.rows[y]]]
                    at += self.rows[y]
                    if self.apart and y == 1:
                        rows.append(ends[1][way])
                    parts.append(jnp.concatenate(rows + [ends[0][y, way]]))
                both.append(jnp.stack(parts))
            held = self.over_group(both)
        return (yield from self.spread(held))

    def over_group(self, held):
        both = jnp.stack(held, axis=1)
        total = lax.dynamic_index_in_dim(both, self.lane, 0, False)
        for k in range(1, self.group):
            away = lax.dynamic_index_in_dim(both, (self.lane + k) % self.group, 0, False)
            total = total + lax.ppermute(away, "mlp", [(j, (j + k) % self.group) for j in range(self.group)])
        return [total[0], total[1]]

    def spread(self, held):
        found = [[held[0]], [held[1]]]
        early = None
        for step in range(1, self.chips):
            came = yield [lax.ppermute(found[way][-1], "clips", self.ways[way]) for way in range(2)]
            for way in range(2):
                found[way].append(came[way])
            if step == self.cut - 1:
                early = self.swapped(jnp.stack(found[0] + found[1]))
        late = self.swapped(jnp.stack(found[0][self.cut :] + found[1][self.cut :]))
        return found[0] + found[1], early, late


def side_by_side(one, two, lead):
    trips, done = (one, two), [None, None]
    kept = [None, None]

    def advance(i):
        try:
            value = next(trips[i]) if kept[i] is None else trips[i].send(kept[i])
        except StopIteration as end:
            done[i] = end.value
            return
        other = kept[1 - i]
        kept[i] = value if other is None else lax.optimization_barrier((value, other))[0]

    for _ in range(lead):
        advance(0)
    while done[0] is None or done[1] is None:
        for i in range(2):
            if done[i] is None:
                advance(i)
    return done


def place_kernel(ring, streams):
    chips, cut = ring.chips, ring.cut
    each = 2 * chips + 2
    n_outs = sum(len(shares) for shares in streams)
    last_block = CORES * 2 * chips - 1

    def body(where_ref, *refs):
        sources, rest = refs[: each * len(streams)], refs[each * len(streams) :]
        outs, buffers, sems = rest[:n_outs], rest[n_outs : 2 * n_outs], rest[2 * n_outs]
        core, at, lane = where_ref[0], where_ref[1], where_ref[2]
        copies = []

        def put(shares, first_out, index, block, value):
            first = 0
            for i, (total, columns, pieces) in enumerate(shares):
                out, buffer = outs[first_out + i], buffers[first_out + i]
                tiles = columns // 128
                high = sum(height for height, _, _ in pieces)
                wide = [value[first + t * high : first + (t + 1) * high] for t in range(tiles)]
                buffer[index] = jnp.concatenate(wide, axis=1) if tiles > 1 else wide[0]
                first += tiles * high
                start = 0
                for height, row_of, short in pieces:
                    row = pl.multiple_of(row_of(block, lane), 8)
                    cases = [(height, None)] if short == height else [(height, False), (short, True)]
                    for rows, at_end in cases:
                        if rows == 0:
                            continue
                        copy = pltpu.make_async_copy(
                            buffer.at[index, pl.ds(start, rows), :], out.at[pl.ds(row, rows), :], sems.at[len(copies)]
                        )
                        copies.append((copy, None if at_end is None else (block == last_block) == at_end))
                        run(copy.start, copies[-1][1])
                    start += height

        for n, shares in enumerate(streams):
            mine = sources[n * each : n * each + 2 * chips]
            early, late = sources[n * each + 2 * chips : (n + 1) * each]
            first_out = sum(len(other) for other in streams[:n])
            for step in range(chips):
                for way in range(2):
                    slot = lax.rem(at + (1 if way == 0 else -1) * (1 - step) + chips, chips)
                    other = early[way * cut + step] if step < cut else late[way * (chips - cut) + step - cut]
                    for side, near, value in ((core, 0, mine[way * chips + step][...]), (1 - core, 1, other)):
                        block = (side * 2 + way) * chips + slot
                        put(shares, first_out, (step * 2 + way) * 2 + near, block, value.astype(f32))
        for copy, condition in copies:
            run(copy.wait, condition)

    return body


def run(action, condition):
    if condition is None:
        action()
    else:
        pl.when(condition)(action)


def shares_of(ring, totals):
    blocks = CORES * 2 * ring.chips
    shares = []
    for total, columns in totals:
        flat = columns == 128
        if flat and ring.apart:
            whole, second = ring.rows
            cut = max(0, total - (blocks - 1) * whole)
            pieces = [
                (second, lambda b, lane: jnp.where(lane == 0, b * whole, b * second), min(second, cut)),
                (
                    whole - second,
                    lambda b, lane: jnp.where(lane == 0, b * whole + second, ring.counts[1] + b * (whole - second)),
                    max(0, cut - second),
                ),
            ]
        else:
            height = ring.rows[0] if flat else total // blocks
            pieces = [(height, lambda b, lane, height=height: b * height, total - (blocks - 1) * height)]
        shares.append((total, columns, pieces))
    return shares


def place(ring, founds, totals):
    streams = [shares_of(ring, shapes) for shapes in totals]
    if any(height % 8 for shares in streams for _, _, pieces in shares for height, _, _ in pieces):
        return [out for found, shares in zip(founds, streams) for out in place_rows(ring, found, shares)]
    hbm = pl.BlockSpec(memory_space=pl.ANY)
    blocks = CORES * 2 * ring.chips
    flat_shares = [share for shares in streams for share in shares]
    copies = blocks * sum(1 if s == h else 2 for _, _, pieces in flat_shares for h, _, s in pieces)
    sources = [ref for mine, early, late in founds for ref in (*mine, early, late)]
    return call(
        place_kernel(ring, streams),
        [((total, columns), f32) for total, columns, _ in flat_shares],
        jnp.stack([ring.core, ring.at, ring.lane]).astype(jnp.int32), *sources,
        in_specs=[SMEM] + [VMEM] * len(sources),
        out_specs=[hbm] * len(flat_shares),
        scratch_shapes=[
            pltpu.VMEM((blocks, sum(h for h, _, _ in pieces), columns), f32) for _, columns, pieces in flat_shares
        ] + [pltpu.SemaphoreType.DMA((copies,))],
        us=9,
    )


def place_rows(ring, found, shares):
    mine, early, late = found
    chips, cut = ring.chips, ring.cut
    outs = []
    first = 0
    for total, columns, pieces in shares:
        tiles = columns // 128
        height = pieces[0][0]
        out = jnp.zeros((CORES * 2 * chips * height, columns), f32)
        for way in range(2):
            for step in range(chips):
                slot = (ring.at + (1 if way == 0 else -1) * (1 - step)) % chips
                other = early[way * cut + step] if step < cut else late[way * (chips - cut) + step - cut]
                for side, value in ((ring.core, mine[way * chips + step]), (1 - ring.core, other)):
                    value = value[first : first + tiles * height].reshape(tiles, height, 128)
                    value = value.transpose(1, 0, 2).reshape(height, columns).astype(f32)
                    row = ((side * 2 + way) * chips + slot) * height
                    out = lax.dynamic_update_slice_in_dim(out, value, row, 0)
        outs.append(out[:total])
        first += tiles * height
    return outs


def after(value, *others):
    return lax.optimization_barrier((value,) + others)[0]


def shards(clips, group, flat_params, w_fc1, w_fc2, w_up, w_down, patches, clip_ids, visible_index, cotangent):
    width = w_fc1.shape[1]
    ring = Ring(clips, group)
    core = ring.core.astype(jnp.int32).reshape(1)
    turns = [[(i, (i + k) % group) for i in range(group)] for k in range(1, group)]
    back_turns = [[(i, (i - k) % group) for i in range(group)] for k in range(1, group)]

    ups = ring.fetch(w_up)
    downs = ring.fetch(w_down)

    flat = flat_params.reshape(FLAT_ROWS, 128)
    w_qkv, w_proj, g_one, g_two = enc_prep(flat)
    x, vis, qkv, probs, mix, first, in2 = call(
        enc_attend_kernel,
        [
            ((PAD, D), bf16), ((1, PAD), jnp.int32), ((PAD, 3 * D), bf16), ((HEADS, PAD, PAD), bf16), ((PAD, D), bf16),
            ((PAD, D), f32), ((PAD, D), bf16),
        ],
        patches, visible_index[None, :], clip_ids.reshape(-1, 128), w_qkv, w_proj, g_one, g_two,
        scratch_shapes=[pltpu.VMEM((1, 384), jnp.int32)],
        us=11,
    )

    in2s, hiddens, slopes, parts = [in2], [], [], []
    for i in range(group):
        if i > 0:
            in2s.append(after(lax.ppermute(in2, "mlp", turns[i - 1]), parts[0]))
        part, hidden, slope = by_hidden_units(
            enc_ffn_kernel, in2s[i], None, w_fc1, w_fc2, f32 if i == 0 else bf16, 2
        )
        hiddens.append(hidden)
        slopes.append(slope)
        parts.append(part if i == 0 else lax.ppermute(part, "mlp", back_turns[i - 1]))
    w_embed, mask_token, w_dqkv, w_dproj, gd_one, gd_two, up_all, down_all = dec_prep(ring, flat, ups, downs, part)

    second_low, table, dec_norm = call(
        embed_kernel(group),
        [((PAD, D), bf16), ((PAD, 4 * DD), bf16), ((PAD, DD), bf16)],
        first, *parts, w_embed, mask_token, gd_one, w_dqkv,
    )
    decoded, ends, wdproj_grad, gd_two_grad, packed = decoder(
        ring, vis, table, cotangent, w_dproj, gd_two, up_all, down_all
    )
    ends = lax.psum_scatter(ends.reshape(-1, 128), "clips", scatter_dimension=0, tiled=True)
    ends = ends.reshape(group, 2, -1, 128)
    second_grad, out_grad, dec_qkv_grad, embed_grad, gd_one_grad, mask_grad = call(
        embed_back_kernel,
        [
            ((PAD, D), f32), ((PAD, D), bf16), ((PAD, 3 * DD), bf16), ((PAD, DD), bf16), ((1, DD), f32), ((1, DD), f32),
        ],
        packed, table, dec_norm, second_low, gd_one, w_dqkv, w_embed,
    )
    dec_wide = CORES * 2 * ring.chips * ring.dec_rows if ring.apart else DEC_ROWS
    dec_flat = call(
        dec_flat_kernel(ring),
        [((clips, 2, ring.dec_rows, 128) if ring.apart else (DEC_ROWS, 128), bf16)],
        dec_norm, dec_qkv_grad, second_low, embed_grad, wdproj_grad, mask_grad, gd_one_grad, gd_two_grad,
        scratch_shapes=[pltpu.VMEM((dec_wide, 128), f32)],
    )[0]
    dec_ends = []
    if ring.apart:
        dec_ends = lax.psum_scatter(dec_flat.reshape(-1, 128), "clips", scatter_dimension=0, tiled=True)
        dec_ends = [dec_ends.reshape(2, -1, 128)]

    out_grads, pre_grads, parts = [out_grad], [], []
    for i in range(group):
        if i > 0:
            out_grads.append(after(lax.ppermute(out_grad, "mlp", turns[i - 1]), parts[0], dec_flat))
        pre_grad, part = by_hidden_units(
            enc_ffn_back_kernel, out_grads[i], slopes[i], w_fc1, w_fc2, f32 if i == 0 else bf16, 1
        )
        pre_grads.append(pre_grad)
        parts.append(part if i == 0 else lax.ppermute(part, "mlp", back_turns[i - 1]))
    fc_halves = ((2, ring.chips, 2 * D * width // (CORES * 2 * ring.chips * 128), 128), bf16)
    fc_keep, fc_send = call(
        enc_weights_kernel(group, ring.chips), [fc_halves, fc_halves],
        core, *in2s, *pre_grads, *hiddens, *out_grads,
        in_specs=[SMEM] + [VMEM] * (4 * group),
        us=10,
    )
    parts[1:] = [after(part, fc_keep) for part in parts[1:]]
    flat_halves = ((2, ring.chips, sum(ring.rows), 128), bf16)
    input_grad, flat_keep, flat_send = call(
        enc_back_kernel(group, ring),
        [((VIS, D), f32), flat_halves, flat_halves],
        core, *parts, second_grad, first, x, qkv, probs, mix, w_qkv, w_proj, g_one, g_two, *([] if ring.apart else [dec_flat]),
        in_specs=[SMEM] + [VMEM] * (group + (10 if ring.apart else 11)),
        scratch_shapes=[
            pltpu.VMEM((PAD, 3 * D), bf16), pltpu.VMEM((WEMB_AT + 4 if ring.apart else FLAT_ROWS, 128), f32),
        ],
        us=20,
    )
    found = side_by_side(
        ring.round_trip(ring.start(fc_keep, fc_send)),
        ring.round_trip(ring.start(flat_keep, flat_send, True), [ends] + dec_ends),
        2,
    )
    fc1_grad, fc2_grad, param_grad, up_grad, down_grad = place(
        ring, found,
        [[(D, width), (width, D)], [(ring.part, 128), (DD, w_up.shape[1]), (w_up.shape[1], DD)]],
    )
    return decoded, input_grad, param_grad.reshape(-1), fc1_grad, fc2_grad, up_grad, down_grad


def solution(mesh):
    placed = (
        P(),
        P(None, "mlp"),
        P("mlp", None),
        P(None, "mlp"),
        P("mlp", None),
        P(("clips", "mlp"), None),
        P(("clips", "mlp")),
        P(("clips", "mlp")),
        P(("clips", "mlp"), None),
    )
    group = mesh.shape["mlp"]

    def body(*args):
        return shards(mesh.shape["clips"], group, *args)

    return jax.shard_map(
        body,
        mesh=mesh,
        in_specs=placed,
        out_specs=(
            P(("clips", "mlp"), None),
            P(("clips", "mlp"), None),
            P("mlp"),
            P(None, "mlp"),
            P("mlp", None),
            P(None, "mlp"),
            P("mlp", None),
        ),
        check_vma=False,
    )
```

```python
import math

import jax
import jax.numpy as jnp
from jax import lax
from jax.experimental import pallas as pl
from jax.experimental.pallas import tpu as pltpu
from jax.sharding import PartitionSpec as P

D = 768
HEADS = 12
DD = 512
DHEADS = 16
FREQ = 8
WIN = 4
ROWS = 1536
VIS = 312
PAD = 320
SHORT_PATCHES = 512
PARAMS = 3804160
EPSILON = 1e-06
BLOCK = 512
GROUP = WIN * FREQ
HALF = DD // 2
ENC_SCALE = 1.0 / math.sqrt(D // HEADS)
DEC_SCALE = 1.0 / math.sqrt(DD // DHEADS)
LOWEST = -1e30
CORES = 2
bf16 = jnp.bfloat16
f32 = jnp.float32


def mm(left, right):
    return jnp.dot(left, right, preferred_element_type=f32)


def mm_nt(left, right):
    return lax.dot_general(left, right, (((1,), (1,)), ((), ())), preferred_element_type=f32)


def mm_tn(left, right):
    return lax.dot_general(left, right, (((0,), (0,)), ((), ())), preferred_element_type=f32)


def normalize(rows):
    centred = rows - jnp.mean(rows, axis=-1, keepdims=True)
    scale = lax.rsqrt(jnp.mean(centred * centred, axis=-1, keepdims=True) + EPSILON)
    return centred * scale, scale


def norm_back(grad, normed, scale, gain):
    weighted = grad * gain
    return scale * (
        weighted
        - jnp.mean(weighted, axis=-1, keepdims=True)
        - normed * jnp.mean(weighted * normed, axis=-1, keepdims=True)
    )


def gelu_parts(pre):
    cdf = 0.5 * (1.0 + lax.erf(pre * math.sqrt(0.5)))
    return pre * cdf, cdf + pre * jnp.exp(-0.5 * pre * pre) * (1.0 / math.sqrt(2.0 * math.pi))


def gained(grad, normed):
    return jnp.sum(grad * normed, axis=0, keepdims=True)


SMEM = pl.BlockSpec(memory_space=pltpu.SMEM)
VMEM = pl.BlockSpec(memory_space=pltpu.VMEM)


def hint(us):
    return pl.CostEstimate(flops=int(us * 8e8), transcendentals=0, bytes_accessed=int(us * 1e6))


def call(body, outs, *args, us=5, **more):
    return pl.pallas_call(
        body,
        cost_estimate=hint(us),
        out_shape=[jax.ShapeDtypeStruct(shape, dtype) for shape, dtype in outs],
        compiler_params=pltpu.CompilerParams(vmem_limit_bytes=56 * 2**20),
        **more,
    )(*args)


TILES = {"wqkv": 18, "wproj": 6, "wemb": 4, "wdqkv": 12, "wdproj": 4}
G1_AT = (D * 3 * D + D * D) // 128
WEMB_AT = G1_AT + 12
MASK_AT = WEMB_AT + D * 4
WDQKV_AT = MASK_AT + 4
WDPROJ_AT = WDQKV_AT + DD * 12
GD1_AT = WDPROJ_AT + DD * 4
FLAT_ROWS = PARAMS // 128
DEC_ROWS = FLAT_ROWS - WEMB_AT
PREP = 64


def widen(flat_ref, first, out_ref, tiles):
    for t in range(tiles):
        out_ref[:, t * 128 : t * 128 + 128] = flat_ref[
            pl.ds(first + t, out_ref.shape[0], stride=tiles), :
        ].astype(bf16)


def vector(flat_ref, first, count):
    return jnp.concatenate([flat_ref[first + i : first + i + 1, :] for i in range(count)], axis=1)


def flatten(flat_ref, first, value, tiles):
    for t in range(tiles):
        flat_ref[pl.ds(first + t, value.shape[0], stride=tiles), :] = value[:, t * 128 : t * 128 + 128]


def enc_prep_kernel(qkv_ref, proj_ref, gains_ref, wqkv_ref, wproj_ref, g1_ref, g2_ref, qkv_flat, proj_flat, gains_flat):
    qkv_flat[...] = qkv_ref[...].astype(f32)
    proj_flat[...] = proj_ref[...].astype(f32)
    widen(qkv_flat, 0, wqkv_ref, 18)
    widen(proj_flat, 0, wproj_ref, 6)

    @pl.when(pl.program_id(0) == 0)
    def _():
        gains_flat[...] = gains_ref[...].astype(f32)
        g1_ref[...] = vector(gains_flat, 0, 6)
        g2_ref[...] = vector(gains_flat, 6, 6)


def enc_prep(flat):
    whole = lambda *shape: pl.BlockSpec(shape, lambda i: (0,) * len(shape))
    return pl.pallas_call(
        enc_prep_kernel,
        grid=(D // PREP,),
        in_specs=[
            pl.BlockSpec((PREP * 18, 128), lambda i: (i, 0)),
            pl.BlockSpec((PREP * 6, 128), lambda i: (D * 18 // (PREP * 6) + i, 0)),
            pl.BlockSpec((16, 128), lambda i: (G1_AT // 16, 0)),
        ],
        out_specs=[
            pl.BlockSpec((PREP, 3 * D), lambda i: (i, 0)),
            pl.BlockSpec((PREP, D), lambda i: (i, 0)),
            whole(1, D),
            whole(1, D),
        ],
        out_shape=[
            jax.ShapeDtypeStruct((D, 3 * D), bf16),
            jax.ShapeDtypeStruct((D, D), bf16),
            jax.ShapeDtypeStruct((1, D), f32),
            jax.ShapeDtypeStruct((1, D), f32),
        ],
        scratch_shapes=[
            pltpu.VMEM((PREP * 18, 128), f32), pltpu.VMEM((PREP * 6, 128), f32), pltpu.VMEM((16, 128), f32),
        ],
    )(flat, flat, flat)


def dec_prep_kernel(count):
    def body(where_ref, flat_ref, _, *refs):
        ups, downs = refs[: 2 * count - 1], refs[2 * count - 1 : 4 * count - 2]
        (
            wemb_ref, mask_ref, wdqkv_ref, wdproj_ref, gd1_ref, gd2_ref, up_ref, down_ref, low, wide, sem,
        ) = refs[4 * count - 2 :]
        copy = pltpu.make_async_copy(flat_ref.at[pl.ds(G1_AT, FLAT_ROWS - G1_AT), :], low, sem)
        copy.start()
        core, lane = where_ref[0], where_ref[1]
        for pieces, whole in ((ups, up_ref), (downs, down_ref)):
            half = whole.shape[1] // CORES
            whole[lane] = pieces[0][...]
            for k in range(1, count):
                at = lax.rem(lane + k, count)
                near = pl.multiple_of(core * half, 8)
                far = pl.multiple_of((1 - core) * half, 8)
                whole[at, pl.ds(near, half), :] = pieces[2 * k - 1][...]
                whole[at, pl.ds(far, half), :] = pieces[2 * k][...]
        copy.wait()
        wide[...] = low[...].astype(f32)
        widen(wide, WEMB_AT - G1_AT, wemb_ref, 4)
        widen(wide, WDQKV_AT - G1_AT, wdqkv_ref, 12)
        widen(wide, WDPROJ_AT - G1_AT, wdproj_ref, 4)
        mask_ref[...] = vector(wide, MASK_AT - G1_AT, 4)
        gd1_ref[...] = vector(wide, GD1_AT - G1_AT, 4)
        gd2_ref[...] = vector(wide, GD1_AT - G1_AT + 4, 4)

    return body


def dec_prep(ring, flat, ups, downs, later):
    hbm = pl.BlockSpec(memory_space=pl.ANY)
    whole = lambda block: ((ring.group,) + block.shape, bf16)
    return call(
        dec_prep_kernel(ring.group),
        [
            ((D, DD), bf16), ((1, DD), f32), ((DD, 3 * DD), bf16), ((DD, DD), bf16), ((1, DD), f32), ((1, DD), f32),
            whole(ups[0]), whole(downs[0]),
        ],
        jnp.stack([ring.core, ring.lane]).astype(jnp.int32), flat, later, *ups, *downs,
        in_specs=[SMEM, hbm, hbm] + [VMEM] * (len(ups) + len(downs)),
        scratch_shapes=[
            pltpu.VMEM((FLAT_ROWS - G1_AT, 128), bf16), pltpu.VMEM((FLAT_ROWS - G1_AT, 128), f32),
            pltpu.SemaphoreType.DMA,
        ],
    )


def enc_attend_kernel(
    patches_ref, visible_ref, ids_ref, wqkv_ref, wproj_ref, g1_ref, g2_ref,
    x_ref, vis_ref, qkv_ref, probs_ref, mix_ref, first_ref, in2_ref, wide_vis,
):
    x_ref[...] = jnp.concatenate(
        [patches_ref[...].astype(f32), jnp.zeros((PAD - VIS, D), f32)], axis=0
    ).astype(bf16)
    wide_vis[...] = jnp.full(wide_vis.shape, -1, jnp.int32)
    wide_vis[:, :VIS] = visible_ref[...]
    vis = wide_vis[:, :PAD]
    vis_ref[...] = vis
    last = jnp.max(ids_ref[...].astype(f32))
    clip = jnp.where(vis < 0, -1.0, jnp.minimum((vis // SHORT_PATCHES).astype(f32), last))
    square = (PAD, PAD)
    across = jnp.broadcast_to(clip, square)
    diagonal = lax.broadcasted_iota(jnp.int32, square, 0) == lax.broadcasted_iota(jnp.int32, square, 1)
    allowed = across == jnp.sum(jnp.where(diagonal, across, 0.0), axis=1, keepdims=True)
    x = x_ref[...].astype(f32)
    normed, _ = normalize(x)
    qkv_ref[...] = mm((normed * g1_ref[...]).astype(bf16), wqkv_ref[...]).astype(bf16)
    low_lanes = lax.broadcasted_iota(jnp.int32, (PAD, 128), 1) < 64
    for pair in range(HEADS // 2):
        at = slice(pair * 128, pair * 128 + 128)
        query = qkv_ref[:, at]
        key = qkv_ref[:, D + pair * 128 : D + pair * 128 + 128]
        value = qkv_ref[:, 2 * D + pair * 128 : 2 * D + pair * 128 + 128]
        mixed = []
        for side in range(2):
            mine = low_lanes if side == 0 else jnp.logical_not(low_lanes)
            own = jnp.where(mine, query.astype(f32), 0.0).astype(bf16)
            scores = jnp.where(allowed, mm_nt(own, key) * ENC_SCALE, LOWEST)
            top = jnp.max(scores, axis=-1, keepdims=True)
            raised = jnp.exp(scores - top)
            probs = (raised / jnp.sum(raised, axis=-1, keepdims=True)).astype(bf16)
            probs_ref[2 * pair + side] = probs
            mixed.append(mm(probs, value))
        mix_ref[:, at] = jnp.where(low_lanes, mixed[0], mixed[1]).astype(bf16)
    first = x + mm(mix_ref[...], wproj_ref[...])
    first_ref[...] = first
    normed2, _ = normalize(first)
    in2_ref[...] = (normed2 * g2_ref[...]).astype(bf16)


def enc_ffn_kernel(in2_ref, fc1_ref, fc2_ref, part_ref, hidden_ref, slope_ref):
    act, slope = gelu_parts(mm(in2_ref[...], fc1_ref[...]))
    hidden = act.astype(bf16)
    hidden_ref[...] = hidden
    slope_ref[...] = slope.astype(bf16)
    part_ref[...] = mm(hidden, fc2_ref[...]).astype(part_ref.dtype)


def enc_ffn_back_kernel(out_grad_ref, slope_ref, fc1_ref, fc2_ref, pre_grad_ref, part_ref):
    grad = mm_nt(out_grad_ref[...], fc2_ref[...]) * slope_ref[...].astype(f32)
    pre_grad = grad.astype(bf16)
    pre_grad_ref[...] = pre_grad
    part_ref[...] = mm_nt(pre_grad, fc1_ref[...]).astype(part_ref.dtype)


def slabs(rows):
    return jnp.concatenate([rows[:, t * 128 : t * 128 + 128] for t in range(rows.shape[1] // 128)], axis=0)


def enc_weights_kernel(count, chips):
    def body(core_ref, *refs):
        in2s, pre_grads, hiddens, out_grads = (refs[i * count : (i + 1) * count] for i in range(4))
        keep_ref, send_ref = refs[4 * count : 4 * count + 2]
        at = 0
        for lefts, rights in ((in2s, pre_grads), (hiddens, out_grads)):
            total = mm_tn(lefts[0][...], rights[0][...])
            for i in range(1, count):
                total = total + mm_tn(lefts[i][...], rights[i][...])
            height = total.shape[0] // (CORES * 2 * chips)
            rows = height * total.shape[1] // 128

            def split(target, half, total=total, height=height, rows=rows, at=at):
                for way in range(2):
                    for chip in range(chips):
                        first = ((half * 2 + way) * chips + chip) * height
                        target[way, chip, at : at + rows, :] = slabs(total[first : first + height].astype(bf16))

            for half in range(CORES):
                @pl.when(core_ref[0] == half)
                def _(half=half, split=split):
                    split(keep_ref, half)
                    split(send_ref, 1 - half)

            at += rows

    return body


def embed_kernel(count):
    def body(first_ref, own_ref, *refs):
        parts = refs[: count - 1]
        wemb_ref, mask_ref, gd1_ref, wdqkv_ref, second_ref, table_ref, norm_ref = refs[count - 1 :]
        second = first_ref[...] + own_ref[...]
        for part in parts:
            second += part[...].astype(f32)
        low = second.astype(bf16)
        second_ref[...] = low
        embedded = mm(low, wemb_ref[...]).astype(bf16).astype(f32)
        row = lax.broadcasted_iota(jnp.int32, (PAD, DD), 0)
        start = jnp.where(row == VIS, mask_ref[...], embedded)
        normed, _ = normalize(start)
        dec_norm = (normed * gd1_ref[...]).astype(bf16)
        norm_ref[...] = dec_norm
        table_ref[:, : 3 * DD] = mm(dec_norm, wdqkv_ref[...]).astype(bf16)
        table_ref[:, 3 * DD :] = start.astype(bf16)

    return body


def spread(rows, same):
    left = jnp.concatenate([rows[:, :128]] * 4, axis=0) * same
    right = jnp.concatenate([rows[:, 128:]] * 4, axis=0) * same
    none = jnp.zeros_like(left)
    return jnp.concatenate(
        [jnp.concatenate([left, none], axis=1), jnp.concatenate([none, right], axis=1)], axis=0
    )


def diagonal(full):
    head = lax.broadcasted_iota(jnp.int32, (GROUP, 128), 1) // GROUP
    tiles = []
    for t in range(2):
        first = t * 128
        tile = full[first : first + GROUP, first : first + 128]
        for h in range(1, 4):
            tile = jnp.where(head == h, full[first + h * GROUP : first + (h + 1) * GROUP, first : first + 128], tile)
        tiles.append(tile)
    return jnp.concatenate(tiles, axis=1)


def segment_max(rows):
    tiles = []
    lane = lax.broadcasted_iota(jnp.int32, (rows.shape[0], 128), 1)
    for t in range(rows.shape[1] // 128):
        tile = rows[:, t * 128 : t * 128 + 128]
        for step in (1, 2, 8, 16):
            other = jnp.where(
                lane & step == 0, pltpu.roll(tile, 128 - step, 1), pltpu.roll(tile, step, 1)
            )
            tile = jnp.maximum(tile, other)
        tiles.append(tile)
    return jnp.concatenate(tiles, axis=1)


def decoder_kernel(chunks, ring):
    def body(
        vis_ref, table_ref, cot_ref, wdproj_ref, gd2_ref, up_ref, down_ref,
        decoded_ref, ends_ref, proj_grad_ref, gd2_grad_ref, packed_ref,
        qkv_ref, mix_ref, s_ref, p_ref, dmix_ref, ds_ref, back_ref, same_ref, ones_ref,
        up_acc, down_acc, proj_acc, gd2_acc, packed_acc,
    ):
        step = pl.program_id(0)

        @pl.when(step == 0)
        def _():
            up_acc[...] = jnp.zeros_like(up_acc)
            down_acc[...] = jnp.zeros_like(down_acc)
            proj_acc[...] = jnp.zeros_like(proj_acc)
            gd2_acc[...] = jnp.zeros_like(gd2_acc)
            packed_acc[...] = jnp.zeros_like(packed_acc)
            head_row = lax.broadcasted_iota(jnp.int32, (HALF, HALF), 0) // GROUP
            head_lane = lax.broadcasted_iota(jnp.int32, (HALF, HALF), 1) // GROUP
            ones = (head_row == head_lane).astype(f32).astype(bf16)
            ones_ref[...] = ones
            same_ref[...] = ones[:128, :128]

        row = lax.broadcasted_iota(jnp.int32, (BLOCK, PAD), 0) + step * BLOCK
        named = row == vis_ref[...]
        col = lax.broadcasted_iota(jnp.int32, (BLOCK, PAD), 1)
        hit = jnp.max(jnp.where(named, 1.0, 0.0), axis=1, keepdims=True)
        one_hot = jnp.where(named, 1.0, jnp.where(col == VIS, 1.0 - hit, 0.0)).astype(bf16)
        qkv_ref[...] = mm(one_hot, table_ref[:, : 3 * DD]).astype(bf16)
        start = mm(one_hot, table_ref[:, 3 * DD :])

        lane = lax.broadcasted_iota(jnp.int32, (BLOCK, DD), 1)
        line = lax.broadcasted_iota(jnp.int32, (BLOCK, DD), 0)
        window = (lane % FREQ) // WIN == (line % FREQ) // WIN
        n_groups = BLOCK // GROUP

        def parts(group, half):
            at = pl.ds(pl.multiple_of(group * GROUP, GROUP), GROUP)
            return at, slice(half * HALF, (half + 1) * HALF)

        def scores(group, _):
            same = same_ref[...]
            for half in range(2):
                at, cols = parts(group, half)
                key = qkv_ref[at, DD + half * HALF : DD + (half + 1) * HALF]
                s_ref[at, cols] = mm_nt(qkv_ref[at, cols], spread(key, same))
            return 0

        lax.fori_loop(0, n_groups, scores, 0, unroll=16)
        raw = s_ref[...] * DEC_SCALE
        top = segment_max(raw)
        raised = jnp.where(window, jnp.exp(raw - top), 0.0)
        p_low = raised.astype(bf16)
        total = jnp.concatenate(
            [mm(p_low[:, :HALF], ones_ref[...]), mm(p_low[:, HALF:], ones_ref[...])], axis=1
        )
        p_ref[...] = (raised / total).astype(bf16)

        def mixes(group, _):
            same = same_ref[...]
            for half in range(2):
                at, cols = parts(group, half)
                value = qkv_ref[at, 2 * DD + half * HALF : 2 * DD + (half + 1) * HALF]
                mix_ref[at, cols] = mm(p_ref[at, cols], spread(value, same)).astype(bf16)
            return 0

        lax.fori_loop(0, n_groups, mixes, 0, unroll=16)

        middle = start + mm(mix_ref[...], wdproj_ref[...])
        normed, scale = normalize(middle)
        in2 = (normed * gd2_ref[...]).astype(bf16)
        cot = cot_ref[...]
        out = jnp.zeros_like(middle)
        in2_grad = jnp.zeros_like(middle)
        for c in range(chunks):
            act, slope = gelu_parts(mm(in2, up_ref[c]))
            hidden = act.astype(bf16)
            out += mm(hidden, down_ref[c])
            pre_grad = (mm_nt(cot, down_ref[c]) * slope).astype(bf16)
            in2_grad += mm_nt(pre_grad, up_ref[c])
            down_acc[c] += mm_tn(hidden, cot)
            up_acc[c] += mm_tn(in2, pre_grad)
        decoded_ref[...] = (middle + out).astype(bf16)

        gd2_acc[...] += gained(in2_grad, normed)
        middle_grad = cot.astype(f32) + norm_back(in2_grad, normed, scale, gd2_ref[...])
        branch = middle_grad.astype(bf16)
        back_ref[:, 3 * DD :] = branch
        proj_acc[...] += mm_tn(mix_ref[...], branch)
        dmix_ref[...] = mm_nt(branch, wdproj_ref[...]).astype(bf16)

        def prob_grads(group, _):
            same = same_ref[...]
            for half in range(2):
                at, cols = parts(group, half)
                value = qkv_ref[at, 2 * DD + half * HALF : 2 * DD + (half + 1) * HALF]
                s_ref[at, cols] = mm_nt(dmix_ref[at, cols], spread(value, same))
            return 0

        lax.fori_loop(0, n_groups, prob_grads, 0, unroll=16)
        probs = p_ref[...].astype(f32)
        prob_grad = s_ref[...]
        weighed = (probs * prob_grad).astype(bf16)
        row_sum = jnp.concatenate(
            [mm(weighed[:, :HALF], ones_ref[...]), mm(weighed[:, HALF:], ones_ref[...])], axis=1
        )
        ds_ref[...] = (probs * (prob_grad - row_sum)).astype(bf16)

        def qkv_grads(group, _):
            same = same_ref[...]
            for half in range(2):
                at, cols = parts(group, half)
                key_cols = slice(DD + half * HALF, DD + (half + 1) * HALF)
                value_cols = slice(2 * DD + half * HALF, 2 * DD + (half + 1) * HALF)
                key = qkv_ref[at, key_cols]
                back_ref[at, cols] = (mm(ds_ref[at, cols], spread(key, same)) * DEC_SCALE).astype(bf16)
                key_grad = diagonal(mm_tn(ds_ref[at, cols], qkv_ref[at, cols]))
                back_ref[at, key_cols] = (key_grad * DEC_SCALE).astype(bf16)
                back_ref[at, value_cols] = diagonal(mm_tn(p_ref[at, cols], dmix_ref[at, cols])).astype(bf16)
            return 0

        lax.fori_loop(0, n_groups, qkv_grads, 0, unroll=16)
        packed_acc[...] += mm_tn(one_hot, back_ref[...])

        @pl.when(step == pl.num_programs(0) - 1)
        def _():
            tall, low = DD // (CORES * 2 * ring.chips), up_acc.shape[2] // (CORES * 2 * ring.chips)
            cut = tall * up_acc.shape[2] // 128
            for clip in range(ring.clips):
                for way in range(2):
                    block = ring.ahead(clip, way)
                    for y in range(chunks):
                        ends_ref[clip, y, way, :cut] = slabs(up_acc[y, block * tall : (block + 1) * tall].astype(bf16))
                        ends_ref[clip, y, way, cut:] = slabs(down_acc[y, block * low : (block + 1) * low].astype(bf16))
            proj_grad_ref[...] = proj_acc[...].astype(bf16)
            gd2_grad_ref[...] = gd2_acc[...]
            packed_ref[...] = packed_acc[...]

    return body


def decoder(ring, vis_row, table, cotangent, w_dproj, gd_two, up, down):
    chunks, _, width = up.shape
    rows = cotangent.shape[0]
    kept = lambda *shape: pl.BlockSpec(shape, lambda i: (0,) * len(shape), pipeline_mode=pl.Buffered(1))
    by_rows = pl.BlockSpec((BLOCK, DD), lambda i: (i, 0))
    ends = (ring.clips, chunks, 2, DD * width // (128 * ring.clips), 128)
    outs = [
        ((rows, DD), bf16, by_rows),
        (ends, bf16, kept(*ends)),
        ((DD, DD), bf16, kept(DD, DD)),
        ((1, DD), f32, kept(1, DD)),
        ((PAD, 4 * DD), f32, kept(PAD, 4 * DD)),
    ]
    return pl.pallas_call(
        decoder_kernel(chunks, ring),
        cost_estimate=hint(80),
        grid=(rows // BLOCK,),
        in_specs=[
            kept(1, PAD), kept(PAD, 4 * DD), by_rows, kept(DD, DD), kept(1, DD),
            kept(chunks, DD, width), kept(chunks, width, DD),
        ],
        out_specs=[spec for _, _, spec in outs],
        out_shape=[jax.ShapeDtypeStruct(shape, dtype) for shape, dtype, _ in outs],
        scratch_shapes=[
            pltpu.VMEM((BLOCK, 3 * DD), bf16),
            pltpu.VMEM((BLOCK, DD), bf16),
            pltpu.VMEM((BLOCK, DD), f32),
            pltpu.VMEM((BLOCK, DD), bf16),
            pltpu.VMEM((BLOCK, DD), bf16),
            pltpu.VMEM((BLOCK, DD), bf16),
            pltpu.VMEM((BLOCK, 4 * DD), bf16),
            pltpu.VMEM((128, 128), bf16),
            pltpu.VMEM((HALF, HALF), bf16),
            pltpu.VMEM((chunks, DD, width), f32),
            pltpu.VMEM((chunks, width, DD), f32),
            pltpu.VMEM((DD, DD), f32),
            pltpu.VMEM((1, DD), f32),
            pltpu.VMEM((PAD, 4 * DD), f32),
        ],
        compiler_params=pltpu.CompilerParams(vmem_limit_bytes=56 * 2**20),
    )(vis_row, table, cotangent, w_dproj, gd_two, up, down)


def embed_back_kernel(
    packed_ref, table_ref, norm_ref, second_ref, gd1_ref, wdqkv_ref, wemb_ref,
    second_grad_ref, out_grad_ref, qkv_grad_ref, embed_grad_ref, gd1_grad_ref, mask_grad_ref,
):
    qkv_grad = packed_ref[:, : 3 * DD].astype(bf16)
    qkv_grad_ref[...] = qkv_grad
    grad = mm_nt(qkv_grad, wdqkv_ref[...])
    normed, scale = normalize(table_ref[:, 3 * DD :].astype(f32))
    gd1_grad_ref[...] = gained(grad, normed)
    start_grad = packed_ref[:, 3 * DD :] + norm_back(grad, normed, scale, gd1_ref[...])
    mask_grad_ref[...] = start_grad[VIS : VIS + 1]
    row = lax.broadcasted_iota(jnp.int32, (PAD, DD), 0)
    embed_grad = jnp.where(row < VIS, start_grad, 0.0).astype(bf16)
    embed_grad_ref[...] = embed_grad
    second_grad = mm_nt(embed_grad, wemb_ref[...])
    second_grad_ref[...] = second_grad
    out_grad_ref[...] = second_grad.astype(bf16)


def dec_flat_kernel(ring):
    def body(
        norm_ref, qkv_grad_ref, second_ref, embed_grad_ref, proj_grad_ref, mask_grad_ref, gd1_grad_ref, gd2_grad_ref,
        flat_ref, wide,
    ):
        flatten(wide, 0, mm_tn(second_ref[...], embed_grad_ref[...]), 4)
        flatten(wide, MASK_AT - WEMB_AT, mask_grad_ref[...], 4)
        flatten(wide, WDQKV_AT - WEMB_AT, mm_tn(norm_ref[...], qkv_grad_ref[...]), 12)
        flatten(wide, WDPROJ_AT - WEMB_AT, proj_grad_ref[...].astype(f32), 4)
        flatten(wide, GD1_AT - WEMB_AT, gd1_grad_ref[...], 4)
        flatten(wide, GD1_AT + 4 - WEMB_AT, gd2_grad_ref[...], 4)
        if not ring.apart:
            flat_ref[...] = wide[...].astype(bf16)
            return
        wide[DEC_ROWS:, :] = jnp.zeros((wide.shape[0] - DEC_ROWS, 128), f32)
        for clip in range(ring.clips):
            for way in range(2):
                block = ring.ahead(clip, way)
                flat_ref[clip, way] = wide[block * ring.dec_rows : (block + 1) * ring.dec_rows, :].astype(bf16)

    return body


def enc_back_kernel(count, ring):
    def body(core_ref, own_ref, *refs):
        parts = refs[: count - 1]
        (
            second_grad_ref, first_ref, x_ref, qkv_ref, probs_ref, mix_ref, wqkv_ref, wproj_ref, g1_ref, g2_ref,
        ) = refs[count - 1 : count + 9]
        input_grad_ref, keep_ref, send_ref, qkv_grad_ref, wide = refs[-5:]
        in2_grad = own_ref[...]
        for part in parts:
            in2_grad += part[...].astype(f32)
        normed2, scale2 = normalize(first_ref[...])
        flatten(wide, G1_AT + 6, gained(in2_grad, normed2), 6)
        first_grad = second_grad_ref[...] + norm_back(in2_grad, normed2, scale2, g2_ref[...])
        branch = first_grad.astype(bf16)
        flatten(wide, D * 18, mm_tn(mix_ref[...], branch), 6)
        if not ring.apart:
            wide[WEMB_AT:FLAT_ROWS, :] = refs[-6][...].astype(f32)
        mix_grad = mm_nt(branch, wproj_ref[...]).astype(bf16)
        low_lanes = lax.broadcasted_iota(jnp.int32, (PAD, 128), 1) < 64
        for pair in range(HEADS // 2):
            at = slice(pair * 128, pair * 128 + 128)
            query = qkv_ref[:, at]
            key = qkv_ref[:, D + pair * 128 : D + pair * 128 + 128]
            value = qkv_ref[:, 2 * D + pair * 128 : 2 * D + pair * 128 + 128]
            upstream = mix_grad[:, at]
            found = []
            for side in range(2):
                mine = low_lanes if side == 0 else jnp.logical_not(low_lanes)
                own = jnp.where(mine, upstream.astype(f32), 0.0).astype(bf16)
                low_probs = probs_ref[2 * pair + side]
                probs = low_probs.astype(f32)
                prob_grad = mm_nt(own, value)
                row_sum = jnp.sum(probs * prob_grad, axis=-1, keepdims=True)
                score_grad = (probs * (prob_grad - row_sum)).astype(bf16)
                found.append((mm(score_grad, key), mm_tn(score_grad, query), mm_tn(low_probs, upstream)))
            for part, factor in enumerate((ENC_SCALE, ENC_SCALE, 1.0)):
                merged = jnp.where(low_lanes, found[0][part], found[1][part]) * factor
                qkv_grad_ref[:, part * D + pair * 128 : part * D + pair * 128 + 128] = merged.astype(bf16)
        normed, scale = normalize(x_ref[...].astype(f32))
        flatten(wide, 0, mm_tn((normed * g1_ref[...]).astype(bf16), qkv_grad_ref[...]), 18)
        grad = mm_nt(qkv_grad_ref[...], wqkv_ref[...])
        flatten(wide, G1_AT, gained(grad, normed), 6)
        input_grad_ref[...] = (first_grad + norm_back(grad, normed, scale, g1_ref[...]))[:VIS]

        def split(target, half):
            for way in range(2):
                for chip in range(ring.chips):
                    block = (half * 2 + way) * ring.chips + chip
                    at = 0
                    for y in range(ring.group):
                        height = ring.rows[y]
                        first = y * ring.part + block * height
                        count = max(0, min(height, ring.counts[y] - block * height))
                        if count > 0:
                            target[way, chip, at : at + count] = wide[first : first + count, :].astype(bf16)
                        if count < height:
                            target[way, chip, at + count : at + height] = jnp.zeros((height - count, 128), bf16)
                        at += height

        for half in range(CORES):
            @pl.when(core_ref[0] == half)
            def _(half=half):
                split(keep_ref, half)
                split(send_ref, 1 - half)

    return body


class Ring:
    def __init__(self, clips, group):
        self.chips = clips // CORES
        self.group = group
        chips = self.chips
        if chips == 8:
            order = [4 * z // 2 for z in range(4)] + [4 * z // 2 + 1 for z in reversed(range(4))]
        else:
            order = list(range(chips))
        place = [0] * chips
        for at, chip in enumerate(order):
            place[chip] = at
        clip = lax.axis_index("clips")
        self.places = place
        self.core = clip % CORES
        chip = clip // CORES
        if chips == 8:
            self.at = jnp.where(chip % 2 == 0, chip // 2, 7 - chip // 2)
        else:
            self.at = chip
        self.lane = lax.axis_index("mlp")
        step = lambda way: [
            (order[i] * CORES + c, order[(i + way) % chips] * CORES + c) for i in range(chips) for c in range(CORES)
        ]
        self.ways = (step(1), step(-1))
        self.swap = [(i, i ^ 1) for i in range(clips)]
        self.clips = clips
        self.cut = max(2, chips - 2)
        blocks = CORES * 2 * chips
        self.part = FLAT_ROWS // group
        whole = -(-(-(-self.part // blocks)) // 8) * 8
        self.apart = False
        if self.apart:
            self.counts = [self.part, WEMB_AT - self.part]
            second = -(-(-(-self.counts[1] // blocks)) // 8) * 8
            self.rows = [whole, second]
            self.dec_rows = whole - second
        else:
            self.counts = [self.part] * group
            self.rows = [whole] * group
            self.dec_rows = 0

    def ahead(self, clip, way):
        chip = (self.places[clip // CORES] + (1 if way == 0 else -1)) % self.chips
        return (clip % CORES * 2 + way) * self.chips + chip

    def fetch(self, block):
        half = block.shape[0] // CORES
        mine = lax.dynamic_slice_in_dim(block, self.core * half, half, 0)
        pieces = [block]
        for k in range(1, self.group):
            near = lax.ppermute(mine, "mlp", [(j, (j - k) % self.group) for j in range(self.group)])
            pieces += [near, self.swapped(near)]
        return pieces

    def swapped(self, value):
        return lax.ppermute(value, "clips", self.swap)

    def block(self, halves, way, back):
        sign = 1 if way == 0 else -1
        at = (self.at - sign * back) % self.chips
        one, two = (lax.dynamic_index_in_dim(half[way], at, 0, False).astype(f32) for half in halves)
        return one + two

    def start(self, keep, send, hurry=False):
        if not hurry:
            halves = keep, self.swapped(send)
            return halves, [self.block(halves, way, 0).astype(bf16) for way in range(2)]
        pick = lambda half: jnp.stack([lax.dynamic_index_in_dim(half[way], self.at, 0, False) for way in range(2)])
        piece = self.swapped(pick(send))
        first = (pick(keep).astype(f32) + piece.astype(f32)).astype(bf16)
        return (keep, self.swapped(after(send, piece))), [first[0], first[1]]

    def round_trip(self, started, ends=None):
        halves, held = started
        for step in range(1, self.chips):
            came = [lax.ppermute(held[way], "clips", self.ways[way]) for way in range(2)]
            held = [(came[way].astype(f32) + self.block(halves, way, step)).astype(bf16) for way in range(2)]
            if ends is not None and step == 2:
                held, ends[0] = lax.optimization_barrier((held, ends[0]))
            if ends is not None and step == 5:
                held, ends[1:] = lax.optimization_barrier((held, ends[1:]))
            held = yield held
        if ends is not None:
            both = []
            for way in range(2):
                parts = []
                at = 0
                for y in range(self.group):
                    rows = [held[way][at : at + self.rows[y]]]
                    at += self.rows[y]
                    if self.apart and y == 1:
                        rows.append(ends[1][way])
                    parts.append(jnp.concatenate(rows + [ends[0][y, way]]))
                both.append(jnp.stack(parts))
            held = self.over_group(both)
        return (yield from self.spread(held))

    def over_group(self, held):
        both = jnp.stack(held, axis=1)
        total = lax.dynamic_index_in_dim(both, self.lane, 0, False)
        for k in range(1, self.group):
            away = lax.dynamic_index_in_dim(both, (self.lane + k) % self.group, 0, False)
            total = total + lax.ppermute(away, "mlp", [(j, (j + k) % self.group) for j in range(self.group)])
        return [total[0], total[1]]

    def spread(self, held):
        found = [[held[0]], [held[1]]]
        early = None
        for step in range(1, self.chips):
            came = yield [lax.ppermute(found[way][-1], "clips", self.ways[way]) for way in range(2)]
            for way in range(2):
                found[way].append(came[way])
            if step == self.cut - 1:
                early = self.swapped(jnp.stack(found[0] + found[1]))
        late = self.swapped(jnp.stack(found[0][self.cut :] + found[1][self.cut :]))
        return found[0] + found[1], early, late


def side_by_side(one, two, lead):
    trips, done = (one, two), [None, None]
    kept = [None, None]

    def advance(i):
        try:
            value = next(trips[i]) if kept[i] is None else trips[i].send(kept[i])
        except StopIteration as end:
            done[i] = end.value
            return
        other = kept[1 - i]
        kept[i] = value if other is None else lax.optimization_barrier((value, other))[0]

    for _ in range(lead):
        advance(0)
    while done[0] is None or done[1] is None:
        for i in range(2):
            if done[i] is None:
                advance(i)
    return done


def place_kernel(ring, streams):
    chips, cut = ring.chips, ring.cut
    each = 2 * chips + 2
    n_outs = sum(len(shares) for shares in streams)
    last_block = CORES * 2 * chips - 1

    def body(where_ref, *refs):
        sources, rest = refs[: each * len(streams)], refs[each * len(streams) :]
        outs, buffers, sems = rest[:n_outs], rest[n_outs : 2 * n_outs], rest[2 * n_outs]
        core, at, lane = where_ref[0], where_ref[1], where_ref[2]
        copies = []

        def put(shares, first_out, index, block, value):
            first = 0
            for i, (total, columns, pieces) in enumerate(shares):
                out, buffer = outs[first_out + i], buffers[first_out + i]
                tiles = columns // 128
                high = sum(height for height, _, _ in pieces)
                wide = [value[first + t * high : first + (t + 1) * high] for t in range(tiles)]
                buffer[index] = jnp.concatenate(wide, axis=1) if tiles > 1 else wide[0]
                first += tiles * high
                start = 0
                for height, row_of, short in pieces:
                    row = pl.multiple_of(row_of(block, lane), 8)
                    cases = [(height, None)] if short == height else [(height, False), (short, True)]
                    for rows, at_end in cases:
                        if rows == 0:
                            continue
                        copy = pltpu.make_async_copy(
                            buffer.at[index, pl.ds(start, rows), :], out.at[pl.ds(row, rows), :], sems.at[len(copies)]
                        )
                        copies.append((copy, None if at_end is None else (block == last_block) == at_end))
                        run(copy.start, copies[-1][1])
                    start += height

        for n, shares in enumerate(streams):
            mine = sources[n * each : n * each + 2 * chips]
            early, late = sources[n * each + 2 * chips : (n + 1) * each]
            first_out = sum(len(other) for other in streams[:n])
            for step in range(chips):
                for way in range(2):
                    slot = lax.rem(at + (1 if way == 0 else -1) * (1 - step) + chips, chips)
                    other = early[way * cut + step] if step < cut else late[way * (chips - cut) + step - cut]
                    for side, near, value in ((core, 0, mine[way * chips + step][...]), (1 - core, 1, other)):
                        block = (side * 2 + way) * chips + slot
                        put(shares, first_out, (step * 2 + way) * 2 + near, block, value.astype(f32))
        for copy, condition in copies:
            run(copy.wait, condition)

    return body


def run(action, condition):
    if condition is None:
        action()
    else:
        pl.when(condition)(action)


def shares_of(ring, totals):
    blocks = CORES * 2 * ring.chips
    shares = []
    for total, columns in totals:
        flat = columns == 128
        if flat and ring.apart:
            whole, second = ring.rows
            cut = max(0, total - (blocks - 1) * whole)
            pieces = [
                (second, lambda b, lane: jnp.where(lane == 0, b * whole, b * second), min(second, cut)),
                (
                    whole - second,
                    lambda b, lane: jnp.where(lane == 0, b * whole + second, ring.counts[1] + b * (whole - second)),
                    max(0, cut - second),
                ),
            ]
        else:
            height = ring.rows[0] if flat else total // blocks
            pieces = [(height, lambda b, lane, height=height: b * height, total - (blocks - 1) * height)]
        shares.append((total, columns, pieces))
    return shares


def place(ring, founds, totals):
    streams = [shares_of(ring, shapes) for shapes in totals]
    if any(height % 8 for shares in streams for _, _, pieces in shares for height, _, _ in pieces):
        return [out for found, shares in zip(founds, streams) for out in place_rows(ring, found, shares)]
    hbm = pl.BlockSpec(memory_space=pl.ANY)
    blocks = CORES * 2 * ring.chips
    flat_shares = [share for shares in streams for share in shares]
    copies = blocks * sum(1 if s == h else 2 for _, _, pieces in flat_shares for h, _, s in pieces)
    sources = [ref for mine, early, late in founds for ref in (*mine, early, late)]
    return call(
        place_kernel(ring, streams),
        [((total, columns), f32) for total, columns, _ in flat_shares],
        jnp.stack([ring.core, ring.at, ring.lane]).astype(jnp.int32), *sources,
        in_specs=[SMEM] + [VMEM] * len(sources),
        out_specs=[hbm] * len(flat_shares),
        scratch_shapes=[
            pltpu.VMEM((blocks, sum(h for h, _, _ in pieces), columns), f32) for _, columns, pieces in flat_shares
        ] + [pltpu.SemaphoreType.DMA((copies,))],
        us=9,
    )


def place_rows(ring, found, shares):
    mine, early, late = found
    chips, cut = ring.chips, ring.cut
    outs = []
    first = 0
    for total, columns, pieces in shares:
        tiles = columns // 128
        height = pieces[0][0]
        out = jnp.zeros((CORES * 2 * chips * height, columns), f32)
        for way in range(2):
            for step in range(chips):
                slot = (ring.at + (1 if way == 0 else -1) * (1 - step)) % chips
                other = early[way * cut + step] if step < cut else late[way * (chips - cut) + step - cut]
                for side, value in ((ring.core, mine[way * chips + step]), (1 - ring.core, other)):
                    value = value[first : first + tiles * height].reshape(tiles, height, 128)
                    value = value.transpose(1, 0, 2).reshape(height, columns).astype(f32)
                    row = ((side * 2 + way) * chips + slot) * height
                    out = lax.dynamic_update_slice_in_dim(out, value, row, 0)
        outs.append(out[:total])
        first += tiles * height
    return outs


def after(value, *others):
    return lax.optimization_barrier((value,) + others)[0]


def shards(clips, group, flat_params, w_fc1, w_fc2, w_up, w_down, patches, clip_ids, visible_index, cotangent):
    width = w_fc1.shape[1]
    ring = Ring(clips, group)
    core = ring.core.astype(jnp.int32).reshape(1)
    turns = [[(i, (i + k) % group) for i in range(group)] for k in range(1, group)]
    back_turns = [[(i, (i - k) % group) for i in range(group)] for k in range(1, group)]

    ups = ring.fetch(w_up)
    downs = ring.fetch(w_down)

    flat = flat_params.reshape(FLAT_ROWS, 128)
    w_qkv, w_proj, g_one, g_two = enc_prep(flat)
    x, vis, qkv, probs, mix, first, in2 = call(
        enc_attend_kernel,
        [
            ((PAD, D), bf16), ((1, PAD), jnp.int32), ((PAD, 3 * D), bf16), ((HEADS, PAD, PAD), bf16), ((PAD, D), bf16),
            ((PAD, D), f32), ((PAD, D), bf16),
        ],
        patches, visible_index[None, :], clip_ids.reshape(-1, 128), w_qkv, w_proj, g_one, g_two,
        scratch_shapes=[pltpu.VMEM((1, 384), jnp.int32)],
        us=11,
    )

    in2s, hiddens, slopes, parts = [in2], [], [], []
    for i in range(group):
        if i > 0:
            in2s.append(after(lax.ppermute(in2, "mlp", turns[i - 1]), parts[0]))
        part, hidden, slope = call(
            enc_ffn_kernel,
            [((PAD, D), f32 if i == 0 else bf16), ((PAD, width), bf16), ((PAD, width), bf16)],
            in2s[i], w_fc1, w_fc2,
        )
        hiddens.append(hidden)
        slopes.append(slope)
        parts.append(part if i == 0 else lax.ppermute(part, "mlp", back_turns[i - 1]))
    w_embed, mask_token, w_dqkv, w_dproj, gd_one, gd_two, up_all, down_all = dec_prep(ring, flat, ups, downs, part)

    second_low, table, dec_norm = call(
        embed_kernel(group),
        [((PAD, D), bf16), ((PAD, 4 * DD), bf16), ((PAD, DD), bf16)],
        first, *parts, w_embed, mask_token, gd_one, w_dqkv,
    )
    decoded, ends, wdproj_grad, gd_two_grad, packed = decoder(
        ring, vis, table, cotangent, w_dproj, gd_two, up_all, down_all
    )
    ends = lax.psum_scatter(ends.reshape(-1, 128), "clips", scatter_dimension=0, tiled=True)
    ends = ends.reshape(group, 2, -1, 128)
    second_grad, out_grad, dec_qkv_grad, embed_grad, gd_one_grad, mask_grad = call(
        embed_back_kernel,
        [
            ((PAD, D), f32), ((PAD, D), bf16), ((PAD, 3 * DD), bf16), ((PAD, DD), bf16), ((1, DD), f32), ((1, DD), f32),
        ],
        packed, table, dec_norm, second_low, gd_one, w_dqkv, w_embed,
    )
    dec_wide = CORES * 2 * ring.chips * ring.dec_rows if ring.apart else DEC_ROWS
    dec_flat = call(
        dec_flat_kernel(ring),
        [((clips, 2, ring.dec_rows, 128) if ring.apart else (DEC_ROWS, 128), bf16)],
        dec_norm, dec_qkv_grad, second_low, embed_grad, wdproj_grad, mask_grad, gd_one_grad, gd_two_grad,
        scratch_shapes=[pltpu.VMEM((dec_wide, 128), f32)],
    )[0]
    dec_ends = []
    if ring.apart:
        dec_ends = lax.psum_scatter(dec_flat.reshape(-1, 128), "clips", scatter_dimension=0, tiled=True)
        dec_ends = [dec_ends.reshape(2, -1, 128)]

    out_grads, pre_grads, parts = [out_grad], [], []
    for i in range(group):
        if i > 0:
            out_grads.append(after(lax.ppermute(out_grad, "mlp", turns[i - 1]), parts[0], dec_flat))
        pre_grad, part = call(
            enc_ffn_back_kernel,
            [((PAD, width), bf16), ((PAD, D), f32 if i == 0 else bf16)],
            out_grads[i], slopes[i], w_fc1, w_fc2,
        )
        pre_grads.append(pre_grad)
        parts.append(part if i == 0 else lax.ppermute(part, "mlp", back_turns[i - 1]))
    fc_halves = ((2, ring.chips, 2 * D * width // (CORES * 2 * ring.chips * 128), 128), bf16)
    fc_keep, fc_send = call(
        enc_weights_kernel(group, ring.chips), [fc_halves, fc_halves],
        core, *in2s, *pre_grads, *hiddens, *out_grads,
        in_specs=[SMEM] + [VMEM] * (4 * group),
        us=10,
    )
    parts[1:] = [after(part, fc_keep) for part in parts[1:]]
    flat_halves = ((2, ring.chips, sum(ring.rows), 128), bf16)
    input_grad, flat_keep, flat_send = call(
        enc_back_kernel(group, ring),
        [((VIS, D), f32), flat_halves, flat_halves],
        core, *parts, second_grad, first, x, qkv, probs, mix, w_qkv, w_proj, g_one, g_two, *([] if ring.apart else [dec_flat]),
        in_specs=[SMEM] + [VMEM] * (group + (10 if ring.apart else 11)),
        scratch_shapes=[
            pltpu.VMEM((PAD, 3 * D), bf16), pltpu.VMEM((WEMB_AT + 4 if ring.apart else FLAT_ROWS, 128), f32),
        ],
        us=20,
    )
    found = side_by_side(
        ring.round_trip(ring.start(fc_keep, fc_send, True)),
        ring.round_trip(ring.start(flat_keep, flat_send, True), [ends] + dec_ends),
        0,
    )
    fc1_grad, fc2_grad, param_grad, up_grad, down_grad = place(
        ring, found,
        [[(D, width), (width, D)], [(ring.part, 128), (DD, w_up.shape[1]), (w_up.shape[1], DD)]],
    )
    return decoded, input_grad, param_grad.reshape(-1), fc1_grad, fc2_grad, up_grad, down_grad


def solution(mesh):
    placed = (
        P(),
        P(None, "mlp"),
        P("mlp", None),
        P(None, "mlp"),
        P("mlp", None),
        P(("clips", "mlp"), None),
        P(("clips", "mlp")),
        P(("clips", "mlp")),
        P(("clips", "mlp"), None),
    )
    group = mesh.shape["mlp"]

    def body(*args):
        return shards(mesh.shape["clips"], group, *args)

    return jax.shard_map(
        body,
        mesh=mesh,
        in_specs=placed,
        out_specs=(
            P(("clips", "mlp"), None),
            P(("clips", "mlp"), None),
            P("mlp"),
            P(None, "mlp"),
            P("mlp", None),
            P(None, "mlp"),
            P("mlp", None),
        ),
        check_vma=False,
    )
```

```python
import math

import jax
import jax.numpy as jnp
from jax import lax
from jax.experimental import pallas as pl
from jax.experimental.pallas import tpu as pltpu
from jax.sharding import PartitionSpec as P

D = 768
HEADS = 12
DD = 512
DHEADS = 16
FREQ = 8
WIN = 4
ROWS = 1536
VIS = 312
PAD = 320
SHORT_PATCHES = 512
PARAMS = 3804160
EPSILON = 1e-06
BLOCK = 512
GROUP = WIN * FREQ
HALF = DD // 2
ENC_SCALE = 1.0 / math.sqrt(D // HEADS)
DEC_SCALE = 1.0 / math.sqrt(DD // DHEADS)
LOWEST = -1e30
CORES = 2
bf16 = jnp.bfloat16
f32 = jnp.float32


def mm(left, right):
    return jnp.dot(left, right, preferred_element_type=f32)


def mm_nt(left, right):
    return lax.dot_general(left, right, (((1,), (1,)), ((), ())), preferred_element_type=f32)


def mm_tn(left, right):
    return lax.dot_general(left, right, (((0,), (0,)), ((), ())), preferred_element_type=f32)


def normalize(rows):
    centred = rows - jnp.mean(rows, axis=-1, keepdims=True)
    scale = lax.rsqrt(jnp.mean(centred * centred, axis=-1, keepdims=True) + EPSILON)
    return centred * scale, scale


def norm_back(grad, normed, scale, gain):
    weighted = grad * gain
    return scale * (
        weighted
        - jnp.mean(weighted, axis=-1, keepdims=True)
        - normed * jnp.mean(weighted * normed, axis=-1, keepdims=True)
    )


def gelu_parts(pre):
    cdf = 0.5 * (1.0 + lax.erf(pre * math.sqrt(0.5)))
    return pre * cdf, cdf + pre * jnp.exp(-0.5 * pre * pre) * (1.0 / math.sqrt(2.0 * math.pi))


def gained(grad, normed):
    return jnp.sum(grad * normed, axis=0, keepdims=True)


SMEM = pl.BlockSpec(memory_space=pltpu.SMEM)
VMEM = pl.BlockSpec(memory_space=pltpu.VMEM)


def hint(us):
    return pl.CostEstimate(flops=int(us * 8e8), transcendentals=0, bytes_accessed=int(us * 1e6))


def call(body, outs, *args, us=5, room=28, **more):
    return pl.pallas_call(
        body,
        cost_estimate=hint(us),
        out_shape=[jax.ShapeDtypeStruct(shape, dtype) for shape, dtype in outs],
        compiler_params=pltpu.CompilerParams(vmem_limit_bytes=room * 2**20),
        **more,
    )(*args)


TILES = {"wqkv": 18, "wproj": 6, "wemb": 4, "wdqkv": 12, "wdproj": 4}
G1_AT = (D * 3 * D + D * D) // 128
WEMB_AT = G1_AT + 12
MASK_AT = WEMB_AT + D * 4
WDQKV_AT = MASK_AT + 4
WDPROJ_AT = WDQKV_AT + DD * 12
GD1_AT = WDPROJ_AT + DD * 4
FLAT_ROWS = PARAMS // 128
DEC_ROWS = FLAT_ROWS - WEMB_AT
PREP = 192


def widen(flat_ref, first, out_ref, tiles):
    for t in range(tiles):
        out_ref[:, t * 128 : t * 128 + 128] = flat_ref[
            pl.ds(first + t, out_ref.shape[0], stride=tiles), :
        ].astype(bf16)


def vector(flat_ref, first, count):
    return jnp.concatenate([flat_ref[first + i : first + i + 1, :] for i in range(count)], axis=1)


def flatten(flat_ref, first, value, tiles):
    for t in range(tiles):
        flat_ref[pl.ds(first + t, value.shape[0], stride=tiles), :] = value[:, t * 128 : t * 128 + 128]


def enc_prep_kernel(qkv_ref, proj_ref, gains_ref, wqkv_ref, wproj_ref, g1_ref, g2_ref, qkv_flat, proj_flat, gains_flat):
    qkv_flat[...] = qkv_ref[...].astype(f32)
    proj_flat[...] = proj_ref[...].astype(f32)
    widen(qkv_flat, 0, wqkv_ref, 18)
    widen(proj_flat, 0, wproj_ref, 6)

    @pl.when(pl.program_id(0) == 0)
    def _():
        gains_flat[...] = gains_ref[...].astype(f32)
        g1_ref[...] = vector(gains_flat, 0, 6)
        g2_ref[...] = vector(gains_flat, 6, 6)


def enc_prep(flat):
    whole = lambda *shape: pl.BlockSpec(shape, lambda i: (0,) * len(shape))
    return pl.pallas_call(
        enc_prep_kernel,
        grid=(D // PREP,),
        in_specs=[
            pl.BlockSpec((PREP * 18, 128), lambda i: (i, 0)),
            pl.BlockSpec((PREP * 6, 128), lambda i: (D * 18 // (PREP * 6) + i, 0)),
            pl.BlockSpec((16, 128), lambda i: (G1_AT // 16, 0)),
        ],
        out_specs=[
            pl.BlockSpec((PREP, 3 * D), lambda i: (i, 0)),
            pl.BlockSpec((PREP, D), lambda i: (i, 0)),
            whole(1, D),
            whole(1, D),
        ],
        out_shape=[
            jax.ShapeDtypeStruct((D, 3 * D), bf16),
            jax.ShapeDtypeStruct((D, D), bf16),
            jax.ShapeDtypeStruct((1, D), f32),
            jax.ShapeDtypeStruct((1, D), f32),
        ],
        scratch_shapes=[
            pltpu.VMEM((PREP * 18, 128), f32), pltpu.VMEM((PREP * 6, 128), f32), pltpu.VMEM((16, 128), f32),
        ],
    )(flat, flat, flat)


def dec_prep_kernel(count):
    def body(where_ref, flat_ref, _, *refs):
        ups, downs = refs[: 2 * count - 1], refs[2 * count - 1 : 4 * count - 2]
        (
            wemb_ref, mask_ref, wdqkv_ref, wdproj_ref, gd1_ref, gd2_ref, up_ref, down_ref, low, wide, sem,
        ) = refs[4 * count - 2 :]
        copy = pltpu.make_async_copy(flat_ref.at[pl.ds(G1_AT, FLAT_ROWS - G1_AT), :], low, sem)
        copy.start()
        core, lane = where_ref[0], where_ref[1]
        for pieces, whole in ((ups, up_ref), (downs, down_ref)):
            half = whole.shape[1] // CORES
            whole[lane] = pieces[0][...]
            for k in range(1, count):
                at = lax.rem(lane + k, count)
                near = pl.multiple_of(core * half, 8)
                far = pl.multiple_of((1 - core) * half, 8)
                whole[at, pl.ds(near, half), :] = pieces[2 * k - 1][...]
                whole[at, pl.ds(far, half), :] = pieces[2 * k][...]
        copy.wait()
        wide[...] = low[...].astype(f32)
        widen(wide, WEMB_AT - G1_AT, wemb_ref, 4)
        widen(wide, WDQKV_AT - G1_AT, wdqkv_ref, 12)
        widen(wide, WDPROJ_AT - G1_AT, wdproj_ref, 4)
        mask_ref[...] = vector(wide, MASK_AT - G1_AT, 4)
        gd1_ref[...] = vector(wide, GD1_AT - G1_AT, 4)
        gd2_ref[...] = vector(wide, GD1_AT - G1_AT + 4, 4)

    return body


def dec_prep(ring, flat, ups, downs, later):
    hbm = pl.BlockSpec(memory_space=pl.ANY)
    whole = lambda block: ((ring.group,) + block.shape, bf16)
    return call(
        dec_prep_kernel(ring.group),
        [
            ((D, DD), bf16), ((1, DD), f32), ((DD, 3 * DD), bf16), ((DD, DD), bf16), ((1, DD), f32), ((1, DD), f32),
            whole(ups[0]), whole(downs[0]),
        ],
        jnp.stack([ring.core, ring.lane]).astype(jnp.int32), flat, later, *ups, *downs,
        in_specs=[SMEM, hbm, hbm] + [VMEM] * (len(ups) + len(downs)),
        scratch_shapes=[
            pltpu.VMEM((FLAT_ROWS - G1_AT, 128), bf16), pltpu.VMEM((FLAT_ROWS - G1_AT, 128), f32),
            pltpu.SemaphoreType.DMA,
        ],
    )


def enc_attend_kernel(
    patches_ref, visible_ref, ids_ref, wqkv_ref, wproj_ref, g1_ref, g2_ref,
    x_ref, vis_ref, qkv_ref, probs_ref, mix_ref, first_ref, in2_ref, wide_vis,
):
    x_ref[...] = jnp.concatenate(
        [patches_ref[...].astype(f32), jnp.zeros((PAD - VIS, D), f32)], axis=0
    ).astype(bf16)
    wide_vis[...] = jnp.full(wide_vis.shape, -1, jnp.int32)
    wide_vis[:, :VIS] = visible_ref[...]
    vis = wide_vis[:, :PAD]
    vis_ref[...] = vis
    last = jnp.max(ids_ref[...].astype(f32))
    clip = jnp.where(vis < 0, -1.0, jnp.minimum((vis // SHORT_PATCHES).astype(f32), last))
    square = (PAD, PAD)
    across = jnp.broadcast_to(clip, square)
    diagonal = lax.broadcasted_iota(jnp.int32, square, 0) == lax.broadcasted_iota(jnp.int32, square, 1)
    allowed = across == jnp.sum(jnp.where(diagonal, across, 0.0), axis=1, keepdims=True)
    x = x_ref[...].astype(f32)
    normed, _ = normalize(x)
    qkv_ref[...] = mm((normed * g1_ref[...]).astype(bf16), wqkv_ref[...]).astype(bf16)
    low_lanes = lax.broadcasted_iota(jnp.int32, (PAD, 128), 1) < 64
    for pair in range(HEADS // 2):
        at = slice(pair * 128, pair * 128 + 128)
        query = qkv_ref[:, at]
        key = qkv_ref[:, D + pair * 128 : D + pair * 128 + 128]
        value = qkv_ref[:, 2 * D + pair * 128 : 2 * D + pair * 128 + 128]
        mixed = []
        for side in range(2):
            mine = low_lanes if side == 0 else jnp.logical_not(low_lanes)
            own = jnp.where(mine, query.astype(f32) * ENC_SCALE, 0.0).astype(bf16)
            scores = jnp.where(allowed, mm_nt(own, key), LOWEST)
            top = jnp.max(scores, axis=-1, keepdims=True)
            raised = jnp.exp(scores - top)
            probs = (raised * (1.0 / jnp.sum(raised, axis=-1, keepdims=True))).astype(bf16)
            probs_ref[2 * pair + side] = probs
            mixed.append(mm(probs, value))
        mix_ref[:, at] = jnp.where(low_lanes, mixed[0], mixed[1]).astype(bf16)
    first = x + mm(mix_ref[...], wproj_ref[...])
    first_ref[...] = first
    normed2, _ = normalize(first)
    in2_ref[...] = (normed2 * g2_ref[...]).astype(bf16)


def enc_ffn_kernel(in2_ref, fc1_ref, fc2_ref, part_ref, hidden_ref, slope_ref):
    act, slope = gelu_parts(mm(in2_ref[...], fc1_ref[...]))
    hidden = act.astype(bf16)
    hidden_ref[...] = hidden
    slope_ref[...] = slope.astype(bf16)
    part_ref[...] = mm(hidden, fc2_ref[...]).astype(part_ref.dtype)


def enc_ffn_back_kernel(out_grad_ref, slope_ref, fc1_ref, fc2_ref, pre_grad_ref, part_ref):
    grad = mm_nt(out_grad_ref[...], fc2_ref[...]) * slope_ref[...].astype(f32)
    pre_grad = grad.astype(bf16)
    pre_grad_ref[...] = pre_grad
    part_ref[...] = mm_nt(pre_grad, fc1_ref[...]).astype(part_ref.dtype)


def slabs(rows):
    return jnp.concatenate([rows[:, t * 128 : t * 128 + 128] for t in range(rows.shape[1] // 128)], axis=0)


def enc_weights_kernel(count, chips):
    def body(core_ref, *refs):
        in2s, pre_grads, hiddens, out_grads = (refs[i * count : (i + 1) * count] for i in range(4))
        keep_ref, send_ref = refs[4 * count : 4 * count + 2]
        at = 0
        for lefts, rights in ((in2s, pre_grads), (hiddens, out_grads)):
            total = mm_tn(lefts[0][...], rights[0][...])
            for i in range(1, count):
                total = total + mm_tn(lefts[i][...], rights[i][...])
            height = total.shape[0] // (CORES * 2 * chips)
            rows = height * total.shape[1] // 128

            def split(target, half, total=total, height=height, rows=rows, at=at):
                for way in range(2):
                    for chip in range(chips):
                        first = ((half * 2 + way) * chips + chip) * height
                        target[way, chip, at : at + rows, :] = slabs(total[first : first + height].astype(bf16))

            for half in range(CORES):
                @pl.when(core_ref[0] == half)
                def _(half=half, split=split):
                    split(keep_ref, half)
                    split(send_ref, 1 - half)

            at += rows

    return body


def embed_kernel(count):
    def body(first_ref, own_ref, *refs):
        parts = refs[: count - 1]
        wemb_ref, mask_ref, gd1_ref, wdqkv_ref, second_ref, table_ref, norm_ref = refs[count - 1 :]
        second = first_ref[...] + own_ref[...]
        for part in parts:
            second += part[...].astype(f32)
        low = second.astype(bf16)
        second_ref[...] = low
        embedded = mm(low, wemb_ref[...]).astype(bf16).astype(f32)
        row = lax.broadcasted_iota(jnp.int32, (PAD, DD), 0)
        start = jnp.where(row == VIS, mask_ref[...], embedded)
        normed, _ = normalize(start)
        dec_norm = (normed * gd1_ref[...]).astype(bf16)
        norm_ref[...] = dec_norm
        table_ref[:, : 3 * DD] = mm(dec_norm, wdqkv_ref[...]).astype(bf16)
        table_ref[:, 3 * DD :] = start.astype(bf16)

    return body


def spread(rows, same):
    left = jnp.concatenate([rows[:, :128]] * 4, axis=0) * same
    right = jnp.concatenate([rows[:, 128:]] * 4, axis=0) * same
    none = jnp.zeros_like(left)
    return jnp.concatenate(
        [jnp.concatenate([left, none], axis=1), jnp.concatenate([none, right], axis=1)], axis=0
    )


def diagonal(full):
    head = lax.broadcasted_iota(jnp.int32, (GROUP, 128), 1) // GROUP
    tiles = []
    for t in range(2):
        first = t * 128
        tile = full[first : first + GROUP, first : first + 128]
        for h in range(1, 4):
            tile = jnp.where(head == h, full[first + h * GROUP : first + (h + 1) * GROUP, first : first + 128], tile)
        tiles.append(tile)
    return jnp.concatenate(tiles, axis=1)


def segment_max(rows):
    tiles = []
    lane = lax.broadcasted_iota(jnp.int32, (rows.shape[0], 128), 1)
    for t in range(rows.shape[1] // 128):
        tile = rows[:, t * 128 : t * 128 + 128]
        for step in (1, 2, 8, 16):
            other = jnp.where(
                lane & step == 0, pltpu.roll(tile, 128 - step, 1), pltpu.roll(tile, step, 1)
            )
            tile = jnp.maximum(tile, other)
        tiles.append(tile)
    return jnp.concatenate(tiles, axis=1)


def decoder_kernel(chunks, ring):
    def body(
        vis_ref, table_ref, cot_ref, wdproj_ref, gd2_ref, up_ref, down_ref,
        decoded_ref, ends_ref, proj_grad_ref, gd2_grad_ref, packed_ref,
        qkv_ref, mix_ref, s_ref, p_ref, dmix_ref, ds_ref, back_ref, same_ref, ones_ref,
        up_acc, down_acc, proj_acc, gd2_acc, packed_acc,
    ):
        step = pl.program_id(0)

        @pl.when(step == 0)
        def _():
            up_acc[...] = jnp.zeros_like(up_acc)
            down_acc[...] = jnp.zeros_like(down_acc)
            proj_acc[...] = jnp.zeros_like(proj_acc)
            gd2_acc[...] = jnp.zeros_like(gd2_acc)
            packed_acc[...] = jnp.zeros_like(packed_acc)
            head_row = lax.broadcasted_iota(jnp.int32, (HALF, HALF), 0) // GROUP
            head_lane = lax.broadcasted_iota(jnp.int32, (HALF, HALF), 1) // GROUP
            ones = (head_row == head_lane).astype(f32).astype(bf16)
            ones_ref[...] = ones
            same_ref[...] = ones[:128, :128]

        row = lax.broadcasted_iota(jnp.int32, (BLOCK, PAD), 0) + step * BLOCK
        named = row == vis_ref[...]
        col = lax.broadcasted_iota(jnp.int32, (BLOCK, PAD), 1)
        hit = jnp.max(jnp.where(named, 1.0, 0.0), axis=1, keepdims=True)
        one_hot = jnp.where(named, 1.0, jnp.where(col == VIS, 1.0 - hit, 0.0)).astype(bf16)
        qkv_ref[...] = mm(one_hot, table_ref[:, : 3 * DD]).astype(bf16)
        start = mm(one_hot, table_ref[:, 3 * DD :])

        lane = lax.broadcasted_iota(jnp.int32, (BLOCK, DD), 1)
        line = lax.broadcasted_iota(jnp.int32, (BLOCK, DD), 0)
        window = (lane % FREQ) // WIN == (line % FREQ) // WIN
        n_groups = BLOCK // GROUP

        def parts(group, half):
            at = pl.ds(pl.multiple_of(group * GROUP, GROUP), GROUP)
            return at, slice(half * HALF, (half + 1) * HALF)

        def scores(group, _):
            same = same_ref[...]
            for half in range(2):
                at, cols = parts(group, half)
                key = qkv_ref[at, DD + half * HALF : DD + (half + 1) * HALF]
                s_ref[at, cols] = mm_nt(qkv_ref[at, cols], spread(key, same))
            return 0

        lax.fori_loop(0, n_groups, scores, 0, unroll=16)
        raw = s_ref[...] * DEC_SCALE
        top = segment_max(raw)
        raised = jnp.where(window, jnp.exp(raw - top), 0.0)
        p_low = raised.astype(bf16)
        total = jnp.concatenate(
            [mm(p_low[:, :HALF], ones_ref[...]), mm(p_low[:, HALF:], ones_ref[...])], axis=1
        )
        p_ref[...] = (raised / total).astype(bf16)

        def mixes(group, _):
            same = same_ref[...]
            for half in range(2):
                at, cols = parts(group, half)
                value = qkv_ref[at, 2 * DD + half * HALF : 2 * DD + (half + 1) * HALF]
                mix_ref[at, cols] = mm(p_ref[at, cols], spread(value, same)).astype(bf16)
            return 0

        lax.fori_loop(0, n_groups, mixes, 0, unroll=16)

        middle = start + mm(mix_ref[...], wdproj_ref[...])
        normed, scale = normalize(middle)
        in2 = (normed * gd2_ref[...]).astype(bf16)
        cot = cot_ref[...]
        out = jnp.zeros_like(middle)
        in2_grad = jnp.zeros_like(middle)
        for c in range(chunks):
            act, slope = gelu_parts(mm(in2, up_ref[c]))
            hidden = act.astype(bf16)
            out += mm(hidden, down_ref[c])
            pre_grad = (mm_nt(cot, down_ref[c]) * slope).astype(bf16)
            in2_grad += mm_nt(pre_grad, up_ref[c])
            down_acc[c] += mm_tn(hidden, cot)
            up_acc[c] += mm_tn(in2, pre_grad)
        decoded_ref[...] = (middle + out).astype(bf16)

        gd2_acc[...] += gained(in2_grad, normed)
        middle_grad = cot.astype(f32) + norm_back(in2_grad, normed, scale, gd2_ref[...])
        branch = middle_grad.astype(bf16)
        back_ref[:, 3 * DD :] = branch
        proj_acc[...] += mm_tn(mix_ref[...], branch)
        dmix_ref[...] = mm_nt(branch, wdproj_ref[...]).astype(bf16)

        def prob_grads(group, _):
            same = same_ref[...]
            for half in range(2):
                at, cols = parts(group, half)
                value = qkv_ref[at, 2 * DD + half * HALF : 2 * DD + (half + 1) * HALF]
                s_ref[at, cols] = mm_nt(dmix_ref[at, cols], spread(value, same))
            return 0

        lax.fori_loop(0, n_groups, prob_grads, 0, unroll=16)
        probs = p_ref[...].astype(f32)
        prob_grad = s_ref[...]
        weighed = (probs * prob_grad).astype(bf16)
        row_sum = jnp.concatenate(
            [mm(weighed[:, :HALF], ones_ref[...]), mm(weighed[:, HALF:], ones_ref[...])], axis=1
        )
        ds_ref[...] = (probs * (prob_grad - row_sum)).astype(bf16)

        def qkv_grads(group, _):
            same = same_ref[...]
            for half in range(2):
                at, cols = parts(group, half)
                key_cols = slice(DD + half * HALF, DD + (half + 1) * HALF)
                value_cols = slice(2 * DD + half * HALF, 2 * DD + (half + 1) * HALF)
                key = qkv_ref[at, key_cols]
                back_ref[at, cols] = (mm(ds_ref[at, cols], spread(key, same)) * DEC_SCALE).astype(bf16)
                key_grad = diagonal(mm_tn(ds_ref[at, cols], qkv_ref[at, cols]))
                back_ref[at, key_cols] = (key_grad * DEC_SCALE).astype(bf16)
                back_ref[at, value_cols] = diagonal(mm_tn(p_ref[at, cols], dmix_ref[at, cols])).astype(bf16)
            return 0

        lax.fori_loop(0, n_groups, qkv_grads, 0, unroll=16)
        packed_acc[...] += mm_tn(one_hot, back_ref[...])

        @pl.when(step == pl.num_programs(0) - 1)
        def _():
            tall, low = DD // (CORES * 2 * ring.chips), up_acc.shape[2] // (CORES * 2 * ring.chips)
            cut = tall * up_acc.shape[2] // 128
            for clip in range(ring.clips):
                for way in range(2):
                    block = ring.ahead(clip, way)
                    for y in range(chunks):
                        ends_ref[clip, y, way, :cut] = slabs(up_acc[y, block * tall : (block + 1) * tall].astype(bf16))
                        ends_ref[clip, y, way, cut:] = slabs(down_acc[y, block * low : (block + 1) * low].astype(bf16))
            proj_grad_ref[...] = proj_acc[...].astype(bf16)
            gd2_grad_ref[...] = gd2_acc[...]
            packed_ref[...] = packed_acc[...]

    return body


def decoder(ring, vis_row, table, cotangent, w_dproj, gd_two, up, down):
    chunks, _, width = up.shape
    rows = cotangent.shape[0]
    kept = lambda *shape: pl.BlockSpec(shape, lambda i: (0,) * len(shape), pipeline_mode=pl.Buffered(1))
    by_rows = pl.BlockSpec((BLOCK, DD), lambda i: (i, 0))
    ends = (ring.clips, chunks, 2, DD * width // (128 * ring.clips), 128)
    outs = [
        ((rows, DD), bf16, by_rows),
        (ends, bf16, kept(*ends)),
        ((DD, DD), bf16, kept(DD, DD)),
        ((1, DD), f32, kept(1, DD)),
        ((PAD, 4 * DD), f32, kept(PAD, 4 * DD)),
    ]
    return pl.pallas_call(
        decoder_kernel(chunks, ring),
        cost_estimate=hint(80),
        grid=(rows // BLOCK,),
        in_specs=[
            kept(1, PAD), kept(PAD, 4 * DD), by_rows, kept(DD, DD), kept(1, DD),
            kept(chunks, DD, width), kept(chunks, width, DD),
        ],
        out_specs=[spec for _, _, spec in outs],
        out_shape=[jax.ShapeDtypeStruct(shape, dtype) for shape, dtype, _ in outs],
        scratch_shapes=[
            pltpu.VMEM((BLOCK, 3 * DD), bf16),
            pltpu.VMEM((BLOCK, DD), bf16),
            pltpu.VMEM((BLOCK, DD), f32),
            pltpu.VMEM((BLOCK, DD), bf16),
            pltpu.VMEM((BLOCK, DD), bf16),
            pltpu.VMEM((BLOCK, DD), bf16),
            pltpu.VMEM((BLOCK, 4 * DD), bf16),
            pltpu.VMEM((128, 128), bf16),
            pltpu.VMEM((HALF, HALF), bf16),
            pltpu.VMEM((chunks, DD, width), f32),
            pltpu.VMEM((chunks, width, DD), f32),
            pltpu.VMEM((DD, DD), f32),
            pltpu.VMEM((1, DD), f32),
            pltpu.VMEM((PAD, 4 * DD), f32),
        ],
        compiler_params=pltpu.CompilerParams(vmem_limit_bytes=56 * 2**20),
    )(vis_row, table, cotangent, w_dproj, gd_two, up, down)


def embed_back_kernel(
    packed_ref, table_ref, norm_ref, second_ref, gd1_ref, wdqkv_ref, wemb_ref,
    second_grad_ref, out_grad_ref, qkv_grad_ref, embed_grad_ref, gd1_grad_ref, mask_grad_ref,
):
    qkv_grad = packed_ref[:, : 3 * DD].astype(bf16)
    qkv_grad_ref[...] = qkv_grad
    grad = mm_nt(qkv_grad, wdqkv_ref[...])
    normed, scale = normalize(table_ref[:, 3 * DD :].astype(f32))
    gd1_grad_ref[...] = gained(grad, normed)
    start_grad = packed_ref[:, 3 * DD :] + norm_back(grad, normed, scale, gd1_ref[...])
    mask_grad_ref[...] = start_grad[VIS : VIS + 1]
    row = lax.broadcasted_iota(jnp.int32, (PAD, DD), 0)
    embed_grad = jnp.where(row < VIS, start_grad, 0.0).astype(bf16)
    embed_grad_ref[...] = embed_grad
    second_grad = mm_nt(embed_grad, wemb_ref[...])
    second_grad_ref[...] = second_grad
    out_grad_ref[...] = second_grad.astype(bf16)


def dec_flat_kernel(ring):
    def body(
        norm_ref, qkv_grad_ref, second_ref, embed_grad_ref, proj_grad_ref, mask_grad_ref, gd1_grad_ref, gd2_grad_ref,
        flat_ref, wide,
    ):
        flatten(wide, 0, mm_tn(second_ref[...], embed_grad_ref[...]), 4)
        flatten(wide, MASK_AT - WEMB_AT, mask_grad_ref[...], 4)
        flatten(wide, WDQKV_AT - WEMB_AT, mm_tn(norm_ref[...], qkv_grad_ref[...]), 12)
        flatten(wide, WDPROJ_AT - WEMB_AT, proj_grad_ref[...].astype(f32), 4)
        flatten(wide, GD1_AT - WEMB_AT, gd1_grad_ref[...], 4)
        flatten(wide, GD1_AT + 4 - WEMB_AT, gd2_grad_ref[...], 4)
        if not ring.apart:
            flat_ref[...] = wide[...].astype(bf16)
            return
        wide[DEC_ROWS:, :] = jnp.zeros((wide.shape[0] - DEC_ROWS, 128), f32)
        for clip in range(ring.clips):
            for way in range(2):
                block = ring.ahead(clip, way)
                flat_ref[clip, way] = wide[block * ring.dec_rows : (block + 1) * ring.dec_rows, :].astype(bf16)

    return body


def enc_back_kernel(count, ring):
    def body(core_ref, own_ref, *refs):
        parts = refs[: count - 1]
        (
            second_grad_ref, first_ref, x_ref, qkv_ref, probs_ref, mix_ref, wqkv_ref, wproj_ref, g1_ref, g2_ref,
        ) = refs[count - 1 : count + 9]
        input_grad_ref, keep_ref, send_ref, qkv_grad_ref, wide = refs[-5:]
        in2_grad = own_ref[...]
        for part in parts:
            in2_grad += part[...].astype(f32)
        normed2, scale2 = normalize(first_ref[...])
        flatten(wide, G1_AT + 6, gained(in2_grad, normed2), 6)
        first_grad = second_grad_ref[...] + norm_back(in2_grad, normed2, scale2, g2_ref[...])
        branch = first_grad.astype(bf16)
        flatten(wide, D * 18, mm_tn(mix_ref[...], branch), 6)
        if not ring.apart:
            wide[WEMB_AT:FLAT_ROWS, :] = refs[-6][...].astype(f32)
        mix_grad = mm_nt(branch, wproj_ref[...]).astype(bf16)
        low_lanes = lax.broadcasted_iota(jnp.int32, (PAD, 128), 1) < 64
        for pair in range(HEADS // 2):
            at = slice(pair * 128, pair * 128 + 128)
            query = qkv_ref[:, at]
            key = qkv_ref[:, D + pair * 128 : D + pair * 128 + 128]
            value = qkv_ref[:, 2 * D + pair * 128 : 2 * D + pair * 128 + 128]
            upstream = mix_grad[:, at]
            found = []
            for side in range(2):
                mine = low_lanes if side == 0 else jnp.logical_not(low_lanes)
                own = jnp.where(mine, upstream.astype(f32), 0.0).astype(bf16)
                low_probs = probs_ref[2 * pair + side]
                probs = low_probs.astype(f32)
                prob_grad = mm_nt(own, value)
                row_sum = jnp.sum(probs * prob_grad, axis=-1, keepdims=True)
                score_grad = (probs * (prob_grad - row_sum)).astype(bf16)
                found.append((mm(score_grad, key), mm_tn(score_grad, query), mm_tn(low_probs, upstream)))
            for part, factor in enumerate((ENC_SCALE, ENC_SCALE, 1.0)):
                merged = jnp.where(low_lanes, found[0][part], found[1][part]) * factor
                qkv_grad_ref[:, part * D + pair * 128 : part * D + pair * 128 + 128] = merged.astype(bf16)
        normed, scale = normalize(x_ref[...].astype(f32))
        flatten(wide, 0, mm_tn((normed * g1_ref[...]).astype(bf16), qkv_grad_ref[...]), 18)
        grad = mm_nt(qkv_grad_ref[...], wqkv_ref[...])
        flatten(wide, G1_AT, gained(grad, normed), 6)
        input_grad_ref[...] = (first_grad + norm_back(grad, normed, scale, g1_ref[...]))[:VIS]

        def split(target, half):
            for way in range(2):
                for chip in range(ring.chips):
                    block = (half * 2 + way) * ring.chips + chip
                    at = 0
                    for y in range(ring.group):
                        height = ring.rows[y]
                        first = y * ring.part + block * height
                        count = max(0, min(height, ring.counts[y] - block * height))
                        if count > 0:
                            target[way, chip, at : at + count] = wide[first : first + count, :].astype(bf16)
                        if count < height:
                            target[way, chip, at + count : at + height] = jnp.zeros((height - count, 128), bf16)
                        at += height

        for half in range(CORES):
            @pl.when(core_ref[0] == half)
            def _(half=half):
                split(keep_ref, half)
                split(send_ref, 1 - half)

    return body


class Ring:
    def __init__(self, clips, group):
        self.chips = clips // CORES
        self.group = group
        chips = self.chips
        if chips == 8:
            order = [4 * z // 2 for z in range(4)] + [4 * z // 2 + 1 for z in reversed(range(4))]
        else:
            order = list(range(chips))
        place = [0] * chips
        for at, chip in enumerate(order):
            place[chip] = at
        clip = lax.axis_index("clips")
        self.places = place
        self.core = clip % CORES
        chip = clip // CORES
        if chips == 8:
            self.at = jnp.where(chip % 2 == 0, chip // 2, 7 - chip // 2)
        else:
            self.at = chip
        self.lane = lax.axis_index("mlp")
        step = lambda way: [
            (order[i] * CORES + c, order[(i + way) % chips] * CORES + c) for i in range(chips) for c in range(CORES)
        ]
        self.ways = (step(1), step(-1))
        self.swap = [(i, i ^ 1) for i in range(clips)]
        self.clips = clips
        self.cut = max(2, chips - 2)
        blocks = CORES * 2 * chips
        self.part = FLAT_ROWS // group
        whole = -(-(-(-self.part // blocks)) // 8) * 8
        self.apart = False
        if self.apart:
            self.counts = [self.part, WEMB_AT - self.part]
            second = -(-(-(-self.counts[1] // blocks)) // 8) * 8
            self.rows = [whole, second]
            self.dec_rows = whole - second
        else:
            self.counts = [self.part] * group
            self.rows = [whole] * group
            self.dec_rows = 0

    def ahead(self, clip, way):
        chip = (self.places[clip // CORES] + (1 if way == 0 else -1)) % self.chips
        return (clip % CORES * 2 + way) * self.chips + chip

    def fetch(self, block):
        half = block.shape[0] // CORES
        mine = lax.dynamic_slice_in_dim(block, self.core * half, half, 0)
        pieces = [block]
        for k in range(1, self.group):
            near = lax.ppermute(mine, "mlp", [(j, (j - k) % self.group) for j in range(self.group)])
            pieces += [near, self.swapped(near)]
        return pieces

    def swapped(self, value):
        return lax.ppermute(value, "clips", self.swap)

    def block(self, halves, way, back):
        sign = 1 if way == 0 else -1
        at = (self.at - sign * back) % self.chips
        one, two = (lax.dynamic_index_in_dim(half[way], at, 0, False).astype(f32) for half in halves)
        return one + two

    def start(self, keep, send, hurry=False):
        if not hurry:
            halves = keep, self.swapped(send)
            return halves, [self.block(halves, way, 0).astype(bf16) for way in range(2)]
        pick = lambda half: jnp.stack([lax.dynamic_index_in_dim(half[way], self.at, 0, False) for way in range(2)])
        piece = self.swapped(pick(send))
        first = (pick(keep).astype(f32) + piece.astype(f32)).astype(bf16)
        return (keep, self.swapped(after(send, piece))), [first[0], first[1]]

    def round_trip(self, started, ends=None):
        halves, held = started
        for step in range(1, self.chips):
            came = [lax.ppermute(held[way], "clips", self.ways[way]) for way in range(2)]
            held = [(came[way].astype(f32) + self.block(halves, way, step)).astype(bf16) for way in range(2)]
            if ends is not None and step == 2:
                held, ends[0] = lax.optimization_barrier((held, ends[0]))
                ridden = self.over_group([ends[0][:, 0], ends[0][:, 1]])
            if ends is not None and step == 5:
                held, ends[1:] = lax.optimization_barrier((held, ends[1:]))
            held = yield held
        if ends is not None:
            both = []
            for way in range(2):
                parts = []
                at = 0
                for y in range(self.group):
                    rows = [held[way][at : at + self.rows[y]]]
                    at += self.rows[y]
                    if self.apart and y == 1:
                        rows.append(ends[1][way])
                    parts.append(jnp.concatenate(rows) if len(rows) > 1 else rows[0])
                both.append(jnp.stack(parts))
            held = [jnp.concatenate(rows) for rows in zip(self.over_group(both), ridden)]
        return (yield from self.spread(held))

    def over_group(self, held):
        both = jnp.stack(held, axis=1)
        total = lax.dynamic_index_in_dim(both, self.lane, 0, False)
        for k in range(1, self.group):
            away = lax.dynamic_index_in_dim(both, (self.lane + k) % self.group, 0, False)
            total = total + lax.ppermute(away, "mlp", [(j, (j + k) % self.group) for j in range(self.group)])
        return [total[0], total[1]]

    def spread(self, held):
        found = [[held[0]], [held[1]]]
        early = None
        for step in range(1, self.chips):
            came = yield [lax.ppermute(found[way][-1], "clips", self.ways[way]) for way in range(2)]
            for way in range(2):
                found[way].append(came[way])
            if step == self.cut - 1:
                early = self.swapped(jnp.stack(found[0] + found[1]))
        late = self.swapped(jnp.stack(found[0][self.cut :] + found[1][self.cut :]))
        return found[0] + found[1], early, late


def side_by_side(one, two, lead):
    trips, done = (one, two), [None, None]
    kept = [None, None]

    def advance(i):
        try:
            value = next(trips[i]) if kept[i] is None else trips[i].send(kept[i])
        except StopIteration as end:
            done[i] = end.value
            return
        other = kept[1 - i]
        kept[i] = value if other is None else lax.optimization_barrier((value, other))[0]

    for _ in range(lead):
        advance(0)
    while done[0] is None or done[1] is None:
        for i in range(2):
            if done[i] is None:
                advance(i)
    return done


def place_kernel(ring, streams):
    chips, cut = ring.chips, ring.cut
    each = 2 * chips + 2
    n_outs = sum(len(shares) for shares in streams)
    last_block = CORES * 2 * chips - 1

    def body(where_ref, *refs):
        sources, rest = refs[: each * len(streams)], refs[each * len(streams) :]
        outs, buffers, sems = rest[:n_outs], rest[n_outs : 2 * n_outs], rest[2 * n_outs]
        core, at, lane = where_ref[0], where_ref[1], where_ref[2]
        copies = []

        def put(shares, first_out, index, block, value):
            first = 0
            for i, (total, columns, pieces) in enumerate(shares):
                out, buffer = outs[first_out + i], buffers[first_out + i]
                tiles = columns // 128
                high = sum(height for height, _, _ in pieces)
                wide = [value[first + t * high : first + (t + 1) * high] for t in range(tiles)]
                buffer[index] = jnp.concatenate(wide, axis=1) if tiles > 1 else wide[0]
                first += tiles * high
                start = 0
                for height, row_of, short in pieces:
                    row = pl.multiple_of(row_of(block, lane), 8)
                    cases = [(height, None)] if short == height else [(height, False), (short, True)]
                    for rows, at_end in cases:
                        if rows == 0:
                            continue
                        copy = pltpu.make_async_copy(
                            buffer.at[index, pl.ds(start, rows), :], out.at[pl.ds(row, rows), :], sems.at[len(copies)]
                        )
                        copies.append((copy, None if at_end is None else (block == last_block) == at_end))
                        run(copy.start, copies[-1][1])
                    start += height

        for n, shares in enumerate(streams):
            mine = sources[n * each : n * each + 2 * chips]
            early, late = sources[n * each + 2 * chips : (n + 1) * each]
            first_out = sum(len(other) for other in streams[:n])
            for step in range(chips):
                for way in range(2):
                    slot = lax.rem(at + (1 if way == 0 else -1) * (1 - step) + chips, chips)
                    other = early[way * cut + step] if step < cut else late[way * (chips - cut) + step - cut]
                    for side, near, value in ((core, 0, mine[way * chips + step][...]), (1 - core, 1, other)):
                        block = (side * 2 + way) * chips + slot
                        put(shares, first_out, (step * 2 + way) * 2 + near, block, value.astype(f32))
        for copy, condition in copies:
            run(copy.wait, condition)

    return body


def run(action, condition):
    if condition is None:
        action()
    else:
        pl.when(condition)(action)


def shares_of(ring, totals):
    blocks = CORES * 2 * ring.chips
    shares = []
    for total, columns in totals:
        flat = columns == 128
        if flat and ring.apart:
            whole, second = ring.rows
            cut = max(0, total - (blocks - 1) * whole)
            pieces = [
                (second, lambda b, lane: jnp.where(lane == 0, b * whole, b * second), min(second, cut)),
                (
                    whole - second,
                    lambda b, lane: jnp.where(lane == 0, b * whole + second, ring.counts[1] + b * (whole - second)),
                    max(0, cut - second),
                ),
            ]
        else:
            height = ring.rows[0] if flat else total // blocks
            pieces = [(height, lambda b, lane, height=height: b * height, total - (blocks - 1) * height)]
        shares.append((total, columns, pieces))
    return shares


def place(ring, founds, totals):
    streams = [shares_of(ring, shapes) for shapes in totals]
    if any(height % 8 for shares in streams for _, _, pieces in shares for height, _, _ in pieces):
        return [out for found, shares in zip(founds, streams) for out in place_rows(ring, found, shares)]
    hbm = pl.BlockSpec(memory_space=pl.ANY)
    blocks = CORES * 2 * ring.chips
    flat_shares = [share for shares in streams for share in shares]
    copies = blocks * sum(1 if s == h else 2 for _, _, pieces in flat_shares for h, _, s in pieces)
    sources = [ref for mine, early, late in founds for ref in (*mine, early, late)]
    return call(
        place_kernel(ring, streams),
        [((total, columns), f32) for total, columns, _ in flat_shares],
        jnp.stack([ring.core, ring.at, ring.lane]).astype(jnp.int32), *sources,
        in_specs=[SMEM] + [VMEM] * len(sources),
        out_specs=[hbm] * len(flat_shares),
        scratch_shapes=[
            pltpu.VMEM((blocks, sum(h for h, _, _ in pieces), columns), f32) for _, columns, pieces in flat_shares
        ] + [pltpu.SemaphoreType.DMA((copies,))],
        us=9,
        room=32,
    )


def place_rows(ring, found, shares):
    mine, early, late = found
    chips, cut = ring.chips, ring.cut
    outs = []
    first = 0
    for total, columns, pieces in shares:
        tiles = columns // 128
        height = pieces[0][0]
        out = jnp.zeros((CORES * 2 * chips * height, columns), f32)
        for way in range(2):
            for step in range(chips):
                slot = (ring.at + (1 if way == 0 else -1) * (1 - step)) % chips
                other = early[way * cut + step] if step < cut else late[way * (chips - cut) + step - cut]
                for side, value in ((ring.core, mine[way * chips + step]), (1 - ring.core, other)):
                    value = value[first : first + tiles * height].reshape(tiles, height, 128)
                    value = value.transpose(1, 0, 2).reshape(height, columns).astype(f32)
                    row = ((side * 2 + way) * chips + slot) * height
                    out = lax.dynamic_update_slice_in_dim(out, value, row, 0)
        outs.append(out[:total])
        first += tiles * height
    return outs


def after(value, *others):
    return lax.optimization_barrier((value,) + others)[0]


def shards(clips, group, flat_params, w_fc1, w_fc2, w_up, w_down, patches, clip_ids, visible_index, cotangent):
    width = w_fc1.shape[1]
    ring = Ring(clips, group)
    core = ring.core.astype(jnp.int32).reshape(1)
    turns = [[(i, (i + k) % group) for i in range(group)] for k in range(1, group)]
    back_turns = [[(i, (i - k) % group) for i in range(group)] for k in range(1, group)]

    ups = ring.fetch(w_up)
    downs = ring.fetch(w_down)

    flat = flat_params.reshape(FLAT_ROWS, 128)
    w_qkv, w_proj, g_one, g_two = enc_prep(flat)
    x, vis, qkv, probs, mix, first, in2 = call(
        enc_attend_kernel,
        [
            ((PAD, D), bf16), ((1, PAD), jnp.int32), ((PAD, 3 * D), bf16), ((HEADS, PAD, PAD), bf16), ((PAD, D), bf16),
            ((PAD, D), f32), ((PAD, D), bf16),
        ],
        patches, visible_index[None, :], clip_ids.reshape(-1, 128), w_qkv, w_proj, g_one, g_two,
        scratch_shapes=[pltpu.VMEM((1, 384), jnp.int32)],
        us=11,
    )

    in2s, hiddens, slopes, parts = [in2], [], [], []
    for i in range(group):
        if i > 0:
            in2s.append(after(lax.ppermute(in2, "mlp", turns[i - 1]), parts[0]))
        part, hidden, slope = call(
            enc_ffn_kernel,
            [((PAD, D), f32 if i == 0 else bf16), ((PAD, width), bf16), ((PAD, width), bf16)],
            in2s[i], w_fc1, w_fc2,
        )
        hiddens.append(hidden)
        slopes.append(slope)
        parts.append(part if i == 0 else lax.ppermute(part, "mlp", back_turns[i - 1]))
    w_embed, mask_token, w_dqkv, w_dproj, gd_one, gd_two, up_all, down_all = dec_prep(ring, flat, ups, downs, part)

    second_low, table, dec_norm = call(
        embed_kernel(group),
        [((PAD, D), bf16), ((PAD, 4 * DD), bf16), ((PAD, DD), bf16)],
        first, *parts, w_embed, mask_token, gd_one, w_dqkv,
    )
    decoded, ends, wdproj_grad, gd_two_grad, packed = decoder(
        ring, vis, table, cotangent, w_dproj, gd_two, up_all, down_all
    )
    ends = lax.psum_scatter(ends.reshape(-1, 128), "clips", scatter_dimension=0, tiled=True)
    ends = ends.reshape(group, 2, -1, 128)
    second_grad, out_grad, dec_qkv_grad, embed_grad, gd_one_grad, mask_grad = call(
        embed_back_kernel,
        [
            ((PAD, D), f32), ((PAD, D), bf16), ((PAD, 3 * DD), bf16), ((PAD, DD), bf16), ((1, DD), f32), ((1, DD), f32),
        ],
        packed, table, dec_norm, second_low, gd_one, w_dqkv, w_embed,
    )
    dec_wide = CORES * 2 * ring.chips * ring.dec_rows if ring.apart else DEC_ROWS
    dec_flat = call(
        dec_flat_kernel(ring),
        [((clips, 2, ring.dec_rows, 128) if ring.apart else (DEC_ROWS, 128), bf16)],
        dec_norm, dec_qkv_grad, second_low, embed_grad, wdproj_grad, mask_grad, gd_one_grad, gd_two_grad,
        scratch_shapes=[pltpu.VMEM((dec_wide, 128), f32)],
    )[0]
    dec_ends = []
    if ring.apart:
        dec_ends = lax.psum_scatter(dec_flat.reshape(-1, 128), "clips", scatter_dimension=0, tiled=True)
        dec_ends = [dec_ends.reshape(2, -1, 128)]

    out_grads, pre_grads, parts = [out_grad], [], []
    for i in range(group):
        if i > 0:
            out_grads.append(after(lax.ppermute(out_grad, "mlp", turns[i - 1]), parts[0], dec_flat))
        pre_grad, part = call(
            enc_ffn_back_kernel,
            [((PAD, width), bf16), ((PAD, D), f32 if i == 0 else bf16)],
            out_grads[i], slopes[i], w_fc1, w_fc2,
        )
        pre_grads.append(pre_grad)
        parts.append(part if i == 0 else lax.ppermute(part, "mlp", back_turns[i - 1]))
    fc_halves = ((2, ring.chips, 2 * D * width // (CORES * 2 * ring.chips * 128), 128), bf16)
    fc_keep, fc_send = call(
        enc_weights_kernel(group, ring.chips), [fc_halves, fc_halves],
        core, *in2s, *pre_grads, *hiddens, *out_grads,
        in_specs=[SMEM] + [VMEM] * (4 * group),
        us=10,
    )
    parts[1:] = [after(part, fc_keep) for part in parts[1:]]
    flat_halves = ((2, ring.chips, sum(ring.rows), 128), bf16)
    input_grad, flat_keep, flat_send = call(
        enc_back_kernel(group, ring),
        [((VIS, D), f32), flat_halves, flat_halves],
        core, *parts, second_grad, first, x, qkv, probs, mix, w_qkv, w_proj, g_one, g_two, *([] if ring.apart else [dec_flat]),
        in_specs=[SMEM] + [VMEM] * (group + (10 if ring.apart else 11)),
        scratch_shapes=[
            pltpu.VMEM((PAD, 3 * D), bf16), pltpu.VMEM((WEMB_AT + 4 if ring.apart else FLAT_ROWS, 128), f32),
        ],
        us=20,
        room=48,
    )
    flat_found, fc_found = side_by_side(
        ring.round_trip(ring.start(flat_keep, flat_send, True), [ends] + dec_ends),
        ring.round_trip(ring.start(fc_keep, fc_send, True)),
        0,
    )
    fc1_grad, fc2_grad = place(ring, [fc_found], [[(D, width), (width, D)]])
    param_grad, up_grad, down_grad = place(
        ring, [flat_found], [[(ring.part, 128), (DD, w_up.shape[1]), (w_up.shape[1], DD)]]
    )
    return decoded, input_grad, param_grad.reshape(-1), fc1_grad, fc2_grad, up_grad, down_grad


def solution(mesh):
    placed = (
        P(),
        P(None, "mlp"),
        P("mlp", None),
        P(None, "mlp"),
        P("mlp", None),
        P(("clips", "mlp"), None),
        P(("clips", "mlp")),
        P(("clips", "mlp")),
        P(("clips", "mlp"), None),
    )
    group = mesh.shape["mlp"]

    def body(*args):
        return shards(mesh.shape["clips"], group, *args)

    return jax.shard_map(
        body,
        mesh=mesh,
        in_specs=placed,
        out_specs=(
            P(("clips", "mlp"), None),
            P(("clips", "mlp"), None),
            P("mlp"),
            P(None, "mlp"),
            P("mlp", None),
            P(None, "mlp"),
            P("mlp", None),
        ),
        check_vma=False,
    )
```

```python
import math

import jax
import jax.numpy as jnp
from jax import lax
from jax.experimental import pallas as pl
from jax.experimental.pallas import tpu as pltpu
from jax.sharding import PartitionSpec as P

D = 768
HEADS = 12
DD = 512
DHEADS = 16
FREQ = 8
WIN = 4
ROWS = 1536
VIS = 312
PAD = 320
SHORT_PATCHES = 512
PARAMS = 3804160
EPSILON = 1e-06
BLOCK = 512
GROUP = WIN * FREQ
HALF = DD // 2
ENC_SCALE = 1.0 / math.sqrt(D // HEADS)
DEC_SCALE = 1.0 / math.sqrt(DD // DHEADS)
LOWEST = -1e30
CORES = 2
bf16 = jnp.bfloat16
f32 = jnp.float32


def mm(left, right):
    return jnp.dot(left, right, preferred_element_type=f32)


def mm_nt(left, right):
    return lax.dot_general(left, right, (((1,), (1,)), ((), ())), preferred_element_type=f32)


def mm_tn(left, right):
    return lax.dot_general(left, right, (((0,), (0,)), ((), ())), preferred_element_type=f32)


def normalize(rows):
    centred = rows - jnp.mean(rows, axis=-1, keepdims=True)
    scale = lax.rsqrt(jnp.mean(centred * centred, axis=-1, keepdims=True) + EPSILON)
    return centred * scale, scale


def norm_back(grad, normed, scale, gain):
    weighted = grad * gain
    return scale * (
        weighted
        - jnp.mean(weighted, axis=-1, keepdims=True)
        - normed * jnp.mean(weighted * normed, axis=-1, keepdims=True)
    )


def gelu_parts(pre):
    cdf = 0.5 * (1.0 + lax.erf(pre * math.sqrt(0.5)))
    return pre * cdf, cdf + pre * jnp.exp(-0.5 * pre * pre) * (1.0 / math.sqrt(2.0 * math.pi))


def gained(grad, normed):
    return jnp.sum(grad * normed, axis=0, keepdims=True)


SMEM = pl.BlockSpec(memory_space=pltpu.SMEM)
VMEM = pl.BlockSpec(memory_space=pltpu.VMEM)


def hint(us):
    return pl.CostEstimate(flops=int(us * 8e8), transcendentals=0, bytes_accessed=int(us * 1e6))


def call(body, outs, *args, us=5, room=20, **more):
    return pl.pallas_call(
        body,
        cost_estimate=hint(us),
        out_shape=[jax.ShapeDtypeStruct(shape, dtype) for shape, dtype in outs],
        compiler_params=pltpu.CompilerParams(vmem_limit_bytes=room * 2**20),
        **more,
    )(*args)


TILES = {"wqkv": 18, "wproj": 6, "wemb": 4, "wdqkv": 12, "wdproj": 4}
G1_AT = (D * 3 * D + D * D) // 128
WEMB_AT = G1_AT + 12
MASK_AT = WEMB_AT + D * 4
WDQKV_AT = MASK_AT + 4
WDPROJ_AT = WDQKV_AT + DD * 12
GD1_AT = WDPROJ_AT + DD * 4
FLAT_ROWS = PARAMS // 128
DEC_ROWS = FLAT_ROWS - WEMB_AT
PREP = 192


def widen(flat_ref, first, out_ref, tiles):
    for t in range(tiles):
        out_ref[:, t * 128 : t * 128 + 128] = flat_ref[
            pl.ds(first + t, out_ref.shape[0], stride=tiles), :
        ].astype(bf16)


def vector(flat_ref, first, count):
    return jnp.concatenate([flat_ref[first + i : first + i + 1, :] for i in range(count)], axis=1)


def flatten(flat_ref, first, value, tiles):
    for t in range(tiles):
        flat_ref[pl.ds(first + t, value.shape[0], stride=tiles), :] = value[:, t * 128 : t * 128 + 128]


def enc_prep_kernel(qkv_ref, proj_ref, gains_ref, wqkv_ref, wproj_ref, g1_ref, g2_ref, qkv_flat, proj_flat, gains_flat):
    qkv_flat[...] = qkv_ref[...].astype(f32)
    proj_flat[...] = proj_ref[...].astype(f32)
    widen(qkv_flat, 0, wqkv_ref, 18)
    widen(proj_flat, 0, wproj_ref, 6)

    @pl.when(pl.program_id(0) == 0)
    def _():
        gains_flat[...] = gains_ref[...].astype(f32)
        g1_ref[...] = vector(gains_flat, 0, 6)
        g2_ref[...] = vector(gains_flat, 6, 6)


def enc_prep(flat):
    whole = lambda *shape: pl.BlockSpec(shape, lambda i: (0,) * len(shape))
    return pl.pallas_call(
        enc_prep_kernel,
        grid=(D // PREP,),
        in_specs=[
            pl.BlockSpec((PREP * 18, 128), lambda i: (i, 0)),
            pl.BlockSpec((PREP * 6, 128), lambda i: (D * 18 // (PREP * 6) + i, 0)),
            pl.BlockSpec((16, 128), lambda i: (G1_AT // 16, 0)),
        ],
        out_specs=[
            pl.BlockSpec((PREP, 3 * D), lambda i: (i, 0)),
            pl.BlockSpec((PREP, D), lambda i: (i, 0)),
            whole(1, D),
            whole(1, D),
        ],
        out_shape=[
            jax.ShapeDtypeStruct((D, 3 * D), bf16),
            jax.ShapeDtypeStruct((D, D), bf16),
            jax.ShapeDtypeStruct((1, D), f32),
            jax.ShapeDtypeStruct((1, D), f32),
        ],
        scratch_shapes=[
            pltpu.VMEM((PREP * 18, 128), f32), pltpu.VMEM((PREP * 6, 128), f32), pltpu.VMEM((16, 128), f32),
        ],
    )(flat, flat, flat)


def dec_prep_kernel(count):
    def body(where_ref, flat_ref, _, *refs):
        ups, downs = refs[: 2 * count - 1], refs[2 * count - 1 : 4 * count - 2]
        (
            wemb_ref, mask_ref, wdqkv_ref, wdproj_ref, gd1_ref, gd2_ref, up_ref, down_ref, low, wide, sem,
        ) = refs[4 * count - 2 :]
        copy = pltpu.make_async_copy(flat_ref.at[pl.ds(G1_AT, FLAT_ROWS - G1_AT), :], low, sem)
        copy.start()
        core, lane = where_ref[0], where_ref[1]
        for pieces, whole in ((ups, up_ref), (downs, down_ref)):
            half = whole.shape[1] // CORES
            whole[lane] = pieces[0][...]
            for k in range(1, count):
                at = lax.rem(lane + k, count)
                near = pl.multiple_of(core * half, 8)
                far = pl.multiple_of((1 - core) * half, 8)
                whole[at, pl.ds(near, half), :] = pieces[2 * k - 1][...]
                whole[at, pl.ds(far, half), :] = pieces[2 * k][...]
        copy.wait()
        wide[...] = low[...].astype(f32)
        widen(wide, WEMB_AT - G1_AT, wemb_ref, 4)
        widen(wide, WDQKV_AT - G1_AT, wdqkv_ref, 12)
        widen(wide, WDPROJ_AT - G1_AT, wdproj_ref, 4)
        mask_ref[...] = vector(wide, MASK_AT - G1_AT, 4)
        gd1_ref[...] = vector(wide, GD1_AT - G1_AT, 4)
        gd2_ref[...] = vector(wide, GD1_AT - G1_AT + 4, 4)

    return body


def dec_prep(ring, flat, ups, downs, later):
    hbm = pl.BlockSpec(memory_space=pl.ANY)
    whole = lambda block: ((ring.group,) + block.shape, bf16)
    return call(
        dec_prep_kernel(ring.group),
        [
            ((D, DD), bf16), ((1, DD), f32), ((DD, 3 * DD), bf16), ((DD, DD), bf16), ((1, DD), f32), ((1, DD), f32),
            whole(ups[0]), whole(downs[0]),
        ],
        jnp.stack([ring.core, ring.lane]).astype(jnp.int32), flat, later, *ups, *downs,
        in_specs=[SMEM, hbm, hbm] + [VMEM] * (len(ups) + len(downs)),
        scratch_shapes=[
            pltpu.VMEM((FLAT_ROWS - G1_AT, 128), bf16), pltpu.VMEM((FLAT_ROWS - G1_AT, 128), f32),
            pltpu.SemaphoreType.DMA,
        ],
    )


def enc_attend_kernel(
    patches_ref, visible_ref, ids_ref, wqkv_ref, wproj_ref, g1_ref, g2_ref,
    x_ref, vis_ref, qkv_ref, probs_ref, mix_ref, first_ref, in2_ref, wide_vis,
):
    x_ref[...] = jnp.concatenate(
        [patches_ref[...].astype(f32), jnp.zeros((PAD - VIS, D), f32)], axis=0
    ).astype(bf16)
    wide_vis[...] = jnp.full(wide_vis.shape, -1, jnp.int32)
    wide_vis[:, :VIS] = visible_ref[...]
    vis = wide_vis[:, :PAD]
    vis_ref[...] = vis
    last = jnp.max(ids_ref[...].astype(f32))
    clip = jnp.where(vis < 0, -1.0, jnp.minimum((vis // SHORT_PATCHES).astype(f32), last))
    square = (PAD, PAD)
    across = jnp.broadcast_to(clip, square)
    diagonal = lax.broadcasted_iota(jnp.int32, square, 0) == lax.broadcasted_iota(jnp.int32, square, 1)
    allowed = across == jnp.sum(jnp.where(diagonal, across, 0.0), axis=1, keepdims=True)
    x = x_ref[...].astype(f32)
    normed, _ = normalize(x)
    qkv_ref[...] = mm((normed * g1_ref[...]).astype(bf16), wqkv_ref[...]).astype(bf16)
    low_lanes = lax.broadcasted_iota(jnp.int32, (PAD, 128), 1) < 64
    for pair in range(HEADS // 2):
        at = slice(pair * 128, pair * 128 + 128)
        query = qkv_ref[:, at]
        key = qkv_ref[:, D + pair * 128 : D + pair * 128 + 128]
        value = qkv_ref[:, 2 * D + pair * 128 : 2 * D + pair * 128 + 128]
        mixed = []
        for side in range(2):
            mine = low_lanes if side == 0 else jnp.logical_not(low_lanes)
            own = jnp.where(mine, query.astype(f32) * ENC_SCALE, 0.0).astype(bf16)
            scores = jnp.where(allowed, mm_nt(own, key), LOWEST)
            top = jnp.max(scores, axis=-1, keepdims=True)
            raised = jnp.exp(scores - top)
            probs = (raised * (1.0 / jnp.sum(raised, axis=-1, keepdims=True))).astype(bf16)
            probs_ref[2 * pair + side] = probs
            mixed.append(mm(probs, value))
        mix_ref[:, at] = jnp.where(low_lanes, mixed[0], mixed[1]).astype(bf16)
    first = x + mm(mix_ref[...], wproj_ref[...])
    first_ref[...] = first
    normed2, _ = normalize(first)
    in2_ref[...] = (normed2 * g2_ref[...]).astype(bf16)


def enc_ffn_kernel(in2_ref, fc1_ref, fc2_ref, part_ref, hidden_ref, slope_ref):
    act, slope = gelu_parts(mm(in2_ref[...], fc1_ref[...]))
    hidden = act.astype(bf16)
    hidden_ref[...] = hidden
    slope_ref[...] = slope.astype(bf16)
    part_ref[...] = mm(hidden, fc2_ref[...]).astype(part_ref.dtype)


def enc_ffn_back_kernel(out_grad_ref, slope_ref, fc1_ref, fc2_ref, pre_grad_ref, part_ref):
    grad = mm_nt(out_grad_ref[...], fc2_ref[...]) * slope_ref[...].astype(f32)
    pre_grad = grad.astype(bf16)
    pre_grad_ref[...] = pre_grad
    part_ref[...] = mm_nt(pre_grad, fc1_ref[...]).astype(part_ref.dtype)


def slabs(rows):
    return jnp.concatenate([rows[:, t * 128 : t * 128 + 128] for t in range(rows.shape[1] // 128)], axis=0)


def enc_weights_kernel(count, chips):
    def body(core_ref, *refs):
        in2s, pre_grads, hiddens, out_grads = (refs[i * count : (i + 1) * count] for i in range(4))
        keep_ref, send_ref = refs[4 * count : 4 * count + 2]
        at = 0
        for lefts, rights in ((in2s, pre_grads), (hiddens, out_grads)):
            total = mm_tn(lefts[0][...], rights[0][...])
            for i in range(1, count):
                total = total + mm_tn(lefts[i][...], rights[i][...])
            height = total.shape[0] // (CORES * 2 * chips)
            rows = height * total.shape[1] // 128

            def split(target, half, total=total, height=height, rows=rows, at=at):
                for way in range(2):
                    for chip in range(chips):
                        first = ((half * 2 + way) * chips + chip) * height
                        target[way, chip, at : at + rows, :] = slabs(total[first : first + height].astype(bf16))

            for half in range(CORES):
                @pl.when(core_ref[0] == half)
                def _(half=half, split=split):
                    split(keep_ref, half)
                    split(send_ref, 1 - half)

            at += rows

    return body


def embed_kernel(count):
    def body(first_ref, own_ref, *refs):
        parts = refs[: count - 1]
        wemb_ref, mask_ref, gd1_ref, wdqkv_ref, second_ref, table_ref, norm_ref = refs[count - 1 :]
        second = first_ref[...] + own_ref[...]
        for part in parts:
            second += part[...].astype(f32)
        low = second.astype(bf16)
        second_ref[...] = low
        embedded = mm(low, wemb_ref[...]).astype(bf16).astype(f32)
        row = lax.broadcasted_iota(jnp.int32, (PAD, DD), 0)
        start = jnp.where(row == VIS, mask_ref[...], embedded)
        normed, _ = normalize(start)
        dec_norm = (normed * gd1_ref[...]).astype(bf16)
        norm_ref[...] = dec_norm
        table_ref[:, : 3 * DD] = mm(dec_norm, wdqkv_ref[...]).astype(bf16)
        table_ref[:, 3 * DD :] = start.astype(bf16)

    return body


def spread(rows, same):
    left = jnp.concatenate([rows[:, :128]] * 4, axis=0) * same
    right = jnp.concatenate([rows[:, 128:]] * 4, axis=0) * same
    none = jnp.zeros_like(left)
    return jnp.concatenate(
        [jnp.concatenate([left, none], axis=1), jnp.concatenate([none, right], axis=1)], axis=0
    )


def diagonal(full):
    head = lax.broadcasted_iota(jnp.int32, (GROUP, 128), 1) // GROUP
    tiles = []
    for t in range(2):
        first = t * 128
        tile = full[first : first + GROUP, first : first + 128]
        for h in range(1, 4):
            tile = jnp.where(head == h, full[first + h * GROUP : first + (h + 1) * GROUP, first : first + 128], tile)
        tiles.append(tile)
    return jnp.concatenate(tiles, axis=1)


def segment_max(rows):
    tiles = []
    lane = lax.broadcasted_iota(jnp.int32, (rows.shape[0], 128), 1)
    for t in range(rows.shape[1] // 128):
        tile = rows[:, t * 128 : t * 128 + 128]
        for step in (1, 2, 8, 16):
            other = jnp.where(
                lane & step == 0, pltpu.roll(tile, 128 - step, 1), pltpu.roll(tile, step, 1)
            )
            tile = jnp.maximum(tile, other)
        tiles.append(tile)
    return jnp.concatenate(tiles, axis=1)


def decoder_kernel(chunks, ring):
    def body(
        vis_ref, table_ref, cot_ref, wdproj_ref, gd2_ref, up_ref, down_ref,
        decoded_ref, ends_ref, proj_grad_ref, gd2_grad_ref, packed_ref,
        qkv_ref, mix_ref, s_ref, p_ref, dmix_ref, ds_ref, back_ref, same_ref, ones_ref,
        up_acc, down_acc, proj_acc, gd2_acc, packed_acc,
    ):
        step = pl.program_id(0)

        @pl.when(step == 0)
        def _():
            up_acc[...] = jnp.zeros_like(up_acc)
            down_acc[...] = jnp.zeros_like(down_acc)
            proj_acc[...] = jnp.zeros_like(proj_acc)
            gd2_acc[...] = jnp.zeros_like(gd2_acc)
            packed_acc[...] = jnp.zeros_like(packed_acc)
            head_row = lax.broadcasted_iota(jnp.int32, (HALF, HALF), 0) // GROUP
            head_lane = lax.broadcasted_iota(jnp.int32, (HALF, HALF), 1) // GROUP
            ones = (head_row == head_lane).astype(f32).astype(bf16)
            ones_ref[...] = ones
            same_ref[...] = ones[:128, :128]

        row = lax.broadcasted_iota(jnp.int32, (BLOCK, PAD), 0) + step * BLOCK
        named = row == vis_ref[...]
        col = lax.broadcasted_iota(jnp.int32, (BLOCK, PAD), 1)
        hit = jnp.max(jnp.where(named, 1.0, 0.0), axis=1, keepdims=True)
        one_hot = jnp.where(named, 1.0, jnp.where(col == VIS, 1.0 - hit, 0.0)).astype(bf16)
        qkv_ref[...] = mm(one_hot, table_ref[:, : 3 * DD]).astype(bf16)
        start = mm(one_hot, table_ref[:, 3 * DD :])

        lane = lax.broadcasted_iota(jnp.int32, (BLOCK, DD), 1)
        line = lax.broadcasted_iota(jnp.int32, (BLOCK, DD), 0)
        window = (lane % FREQ) // WIN == (line % FREQ) // WIN
        n_groups = BLOCK // GROUP

        def parts(group, half):
            at = pl.ds(pl.multiple_of(group * GROUP, GROUP), GROUP)
            return at, slice(half * HALF, (half + 1) * HALF)

        def scores(group, _):
            same = same_ref[...]
            for half in range(2):
                at, cols = parts(group, half)
                key = qkv_ref[at, DD + half * HALF : DD + (half + 1) * HALF]
                s_ref[at, cols] = mm_nt(qkv_ref[at, cols], spread(key, same))
            return 0

        lax.fori_loop(0, n_groups, scores, 0, unroll=16)
        raw = s_ref[...] * DEC_SCALE
        top = segment_max(raw)
        raised = jnp.where(window, jnp.exp(raw - top), 0.0)
        p_low = raised.astype(bf16)
        total = jnp.concatenate(
            [mm(p_low[:, :HALF], ones_ref[...]), mm(p_low[:, HALF:], ones_ref[...])], axis=1
        )
        p_ref[...] = (raised / total).astype(bf16)

        def mixes(group, _):
            same = same_ref[...]
            for half in range(2):
                at, cols = parts(group, half)
                value = qkv_ref[at, 2 * DD + half * HALF : 2 * DD + (half + 1) * HALF]
                mix_ref[at, cols] = mm(p_ref[at, cols], spread(value, same)).astype(bf16)
            return 0

        lax.fori_loop(0, n_groups, mixes, 0, unroll=16)

        middle = start + mm(mix_ref[...], wdproj_ref[...])
        normed, scale = normalize(middle)
        in2 = (normed * gd2_ref[...]).astype(bf16)
        cot = cot_ref[...]
        out = jnp.zeros_like(middle)
        in2_grad = jnp.zeros_like(middle)
        for c in range(chunks):
            act, slope = gelu_parts(mm(in2, up_ref[c]))
            hidden = act.astype(bf16)
            out += mm(hidden, down_ref[c])
            pre_grad = (mm_nt(cot, down_ref[c]) * slope).astype(bf16)
            in2_grad += mm_nt(pre_grad, up_ref[c])
            down_acc[c] += mm_tn(hidden, cot)
            up_acc[c] += mm_tn(in2, pre_grad)
        decoded_ref[...] = (middle + out).astype(bf16)

        gd2_acc[...] += gained(in2_grad, normed)
        middle_grad = cot.astype(f32) + norm_back(in2_grad, normed, scale, gd2_ref[...])
        branch = middle_grad.astype(bf16)
        back_ref[:, 3 * DD :] = branch
        proj_acc[...] += mm_tn(mix_ref[...], branch)
        dmix_ref[...] = mm_nt(branch, wdproj_ref[...]).astype(bf16)

        def prob_grads(group, _):
            same = same_ref[...]
            for half in range(2):
                at, cols = parts(group, half)
                value = qkv_ref[at, 2 * DD + half * HALF : 2 * DD + (half + 1) * HALF]
                s_ref[at, cols] = mm_nt(dmix_ref[at, cols], spread(value, same))
            return 0

        lax.fori_loop(0, n_groups, prob_grads, 0, unroll=16)
        probs = p_ref[...].astype(f32)
        prob_grad = s_ref[...]
        weighed = (probs * prob_grad).astype(bf16)
        row_sum = jnp.concatenate(
            [mm(weighed[:, :HALF], ones_ref[...]), mm(weighed[:, HALF:], ones_ref[...])], axis=1
        )
        ds_ref[...] = (probs * (prob_grad - row_sum)).astype(bf16)

        def qkv_grads(group, _):
            same = same_ref[...]
            for half in range(2):
                at, cols = parts(group, half)
                key_cols = slice(DD + half * HALF, DD + (half + 1) * HALF)
                value_cols = slice(2 * DD + half * HALF, 2 * DD + (half + 1) * HALF)
                key = qkv_ref[at, key_cols]
                back_ref[at, cols] = (mm(ds_ref[at, cols], spread(key, same)) * DEC_SCALE).astype(bf16)
                key_grad = diagonal(mm_tn(ds_ref[at, cols], qkv_ref[at, cols]))
                back_ref[at, key_cols] = (key_grad * DEC_SCALE).astype(bf16)
                back_ref[at, value_cols] = diagonal(mm_tn(p_ref[at, cols], dmix_ref[at, cols])).astype(bf16)
            return 0

        lax.fori_loop(0, n_groups, qkv_grads, 0, unroll=16)
        packed_acc[...] += mm_tn(one_hot, back_ref[...])

        @pl.when(step == pl.num_programs(0) - 1)
        def _():
            tall, low = DD // (CORES * 2 * ring.chips), up_acc.shape[2] // (CORES * 2 * ring.chips)
            cut = tall * up_acc.shape[2] // 128
            for clip in range(ring.clips):
                for way in range(2):
                    block = ring.ahead(clip, way)
                    for y in range(chunks):
                        ends_ref[clip, y, way, :cut] = slabs(up_acc[y, block * tall : (block + 1) * tall].astype(bf16))
                        ends_ref[clip, y, way, cut:] = slabs(down_acc[y, block * low : (block + 1) * low].astype(bf16))
            proj_grad_ref[...] = proj_acc[...].astype(bf16)
            gd2_grad_ref[...] = gd2_acc[...]
            packed_ref[...] = packed_acc[...]

    return body


def decoder(ring, vis_row, table, cotangent, w_dproj, gd_two, up, down):
    chunks, _, width = up.shape
    rows = cotangent.shape[0]
    kept = lambda *shape: pl.BlockSpec(shape, lambda i: (0,) * len(shape), pipeline_mode=pl.Buffered(1))
    by_rows = pl.BlockSpec((BLOCK, DD), lambda i: (i, 0))
    ends = (ring.clips, chunks, 2, DD * width // (128 * ring.clips), 128)
    outs = [
        ((rows, DD), bf16, by_rows),
        (ends, bf16, kept(*ends)),
        ((DD, DD), bf16, kept(DD, DD)),
        ((1, DD), f32, kept(1, DD)),
        ((PAD, 4 * DD), f32, kept(PAD, 4 * DD)),
    ]
    return pl.pallas_call(
        decoder_kernel(chunks, ring),
        cost_estimate=hint(80),
        grid=(rows // BLOCK,),
        in_specs=[
            kept(1, PAD), kept(PAD, 4 * DD), by_rows, kept(DD, DD), kept(1, DD),
            kept(chunks, DD, width), kept(chunks, width, DD),
        ],
        out_specs=[spec for _, _, spec in outs],
        out_shape=[jax.ShapeDtypeStruct(shape, dtype) for shape, dtype, _ in outs],
        scratch_shapes=[
            pltpu.VMEM((BLOCK, 3 * DD), bf16),
            pltpu.VMEM((BLOCK, DD), bf16),
            pltpu.VMEM((BLOCK, DD), f32),
            pltpu.VMEM((BLOCK, DD), bf16),
            pltpu.VMEM((BLOCK, DD), bf16),
            pltpu.VMEM((BLOCK, DD), bf16),
            pltpu.VMEM((BLOCK, 4 * DD), bf16),
            pltpu.VMEM((128, 128), bf16),
            pltpu.VMEM((HALF, HALF), bf16),
            pltpu.VMEM((chunks, DD, width), f32),
            pltpu.VMEM((chunks, width, DD), f32),
            pltpu.VMEM((DD, DD), f32),
            pltpu.VMEM((1, DD), f32),
            pltpu.VMEM((PAD, 4 * DD), f32),
        ],
        compiler_params=pltpu.CompilerParams(vmem_limit_bytes=40 * 2**20),
    )(vis_row, table, cotangent, w_dproj, gd_two, up, down)


def embed_back_kernel(
    packed_ref, table_ref, norm_ref, second_ref, gd1_ref, wdqkv_ref, wemb_ref,
    second_grad_ref, out_grad_ref, qkv_grad_ref, embed_grad_ref, gd1_grad_ref, mask_grad_ref,
):
    qkv_grad = packed_ref[:, : 3 * DD].astype(bf16)
    qkv_grad_ref[...] = qkv_grad
    grad = mm_nt(qkv_grad, wdqkv_ref[...])
    normed, scale = normalize(table_ref[:, 3 * DD :].astype(f32))
    gd1_grad_ref[...] = gained(grad, normed)
    start_grad = packed_ref[:, 3 * DD :] + norm_back(grad, normed, scale, gd1_ref[...])
    mask_grad_ref[...] = start_grad[VIS : VIS + 1]
    row = lax.broadcasted_iota(jnp.int32, (PAD, DD), 0)
    embed_grad = jnp.where(row < VIS, start_grad, 0.0).astype(bf16)
    embed_grad_ref[...] = embed_grad
    second_grad = mm_nt(embed_grad, wemb_ref[...])
    second_grad_ref[...] = second_grad
    out_grad_ref[...] = second_grad.astype(bf16)


def dec_flat_kernel(ring):
    def body(
        norm_ref, qkv_grad_ref, second_ref, embed_grad_ref, proj_grad_ref, mask_grad_ref, gd1_grad_ref, gd2_grad_ref,
        flat_ref, wide,
    ):
        flatten(wide, 0, mm_tn(second_ref[...], embed_grad_ref[...]), 4)
        flatten(wide, MASK_AT - WEMB_AT, mask_grad_ref[...], 4)
        flatten(wide, WDQKV_AT - WEMB_AT, mm_tn(norm_ref[...], qkv_grad_ref[...]), 12)
        flatten(wide, WDPROJ_AT - WEMB_AT, proj_grad_ref[...].astype(f32), 4)
        flatten(wide, GD1_AT - WEMB_AT, gd1_grad_ref[...], 4)
        flatten(wide, GD1_AT + 4 - WEMB_AT, gd2_grad_ref[...], 4)
        if not ring.apart:
            flat_ref[...] = wide[...].astype(bf16)
            return
        wide[DEC_ROWS:, :] = jnp.zeros((wide.shape[0] - DEC_ROWS, 128), f32)
        for clip in range(ring.clips):
            for way in range(2):
                block = ring.ahead(clip, way)
                flat_ref[clip, way] = wide[block * ring.dec_rows : (block + 1) * ring.dec_rows, :].astype(bf16)

    return body


def enc_back_kernel(count, ring):
    def body(core_ref, own_ref, *refs):
        parts = refs[: count - 1]
        (
            second_grad_ref, first_ref, x_ref, qkv_ref, probs_ref, mix_ref, wqkv_ref, wproj_ref, g1_ref, g2_ref,
        ) = refs[count - 1 : count + 9]
        input_grad_ref, keep_ref, send_ref, qkv_grad_ref, wide = refs[-5:]
        in2_grad = own_ref[...]
        for part in parts:
            in2_grad += part[...].astype(f32)
        normed2, scale2 = normalize(first_ref[...])
        flatten(wide, G1_AT + 6, gained(in2_grad, normed2), 6)
        first_grad = second_grad_ref[...] + norm_back(in2_grad, normed2, scale2, g2_ref[...])
        branch = first_grad.astype(bf16)
        flatten(wide, D * 18, mm_tn(mix_ref[...], branch), 6)
        if not ring.apart:
            wide[WEMB_AT:FLAT_ROWS, :] = refs[-6][...].astype(f32)
        mix_grad = mm_nt(branch, wproj_ref[...]).astype(bf16)
        low_lanes = lax.broadcasted_iota(jnp.int32, (PAD, 128), 1) < 64
        for pair in range(HEADS // 2):
            at = slice(pair * 128, pair * 128 + 128)
            query = qkv_ref[:, at]
            key = qkv_ref[:, D + pair * 128 : D + pair * 128 + 128]
            value = qkv_ref[:, 2 * D + pair * 128 : 2 * D + pair * 128 + 128]
            upstream = mix_grad[:, at]
            found = []
            for side in range(2):
                mine = low_lanes if side == 0 else jnp.logical_not(low_lanes)
                own = jnp.where(mine, upstream.astype(f32), 0.0).astype(bf16)
                low_probs = probs_ref[2 * pair + side]
                probs = low_probs.astype(f32)
                prob_grad = mm_nt(own, value)
                row_sum = jnp.sum(probs * prob_grad, axis=-1, keepdims=True)
                score_grad = (probs * (prob_grad - row_sum)).astype(bf16)
                found.append((mm(score_grad, key), mm_tn(score_grad, query), mm_tn(low_probs, upstream)))
            for part, factor in enumerate((ENC_SCALE, ENC_SCALE, 1.0)):
                merged = jnp.where(low_lanes, found[0][part], found[1][part]) * factor
                qkv_grad_ref[:, part * D + pair * 128 : part * D + pair * 128 + 128] = merged.astype(bf16)
        normed, scale = normalize(x_ref[...].astype(f32))
        flatten(wide, 0, mm_tn((normed * g1_ref[...]).astype(bf16), qkv_grad_ref[...]), 18)
        grad = mm_nt(qkv_grad_ref[...], wqkv_ref[...])
        flatten(wide, G1_AT, gained(grad, normed), 6)
        input_grad_ref[...] = (first_grad + norm_back(grad, normed, scale, g1_ref[...]))[:VIS]

        def split(target, half):
            for way in range(2):
                for chip in range(ring.chips):
                    block = (half * 2 + way) * ring.chips + chip
                    at = 0
                    for y in range(ring.group):
                        height = ring.rows[y]
                        first = y * ring.part + block * height
                        count = max(0, min(height, ring.counts[y] - block * height))
                        if count > 0:
                            target[way, chip, at : at + count] = wide[first : first + count, :].astype(bf16)
                        if count < height:
                            target[way, chip, at + count : at + height] = jnp.zeros((height - count, 128), bf16)
                        at += height

        for half in range(CORES):
            @pl.when(core_ref[0] == half)
            def _(half=half):
                split(keep_ref, half)
                split(send_ref, 1 - half)

    return body


class Ring:
    def __init__(self, clips, group):
        self.chips = clips // CORES
        self.group = group
        chips = self.chips
        if chips == 8:
            order = [4 * z // 2 for z in range(4)] + [4 * z // 2 + 1 for z in reversed(range(4))]
        else:
            order = list(range(chips))
        place = [0] * chips
        for at, chip in enumerate(order):
            place[chip] = at
        clip = lax.axis_index("clips")
        self.places = place
        self.core = clip % CORES
        chip = clip // CORES
        if chips == 8:
            self.at = jnp.where(chip % 2 == 0, chip // 2, 7 - chip // 2)
        else:
            self.at = chip
        self.lane = lax.axis_index("mlp")
        step = lambda way: [
            (order[i] * CORES + c, order[(i + way) % chips] * CORES + c) for i in range(chips) for c in range(CORES)
        ]
        self.ways = (step(1), step(-1))
        self.swap = [(i, i ^ 1) for i in range(clips)]
        self.clips = clips
        self.cut = max(2, chips - 2)
        blocks = CORES * 2 * chips
        self.part = FLAT_ROWS // group
        whole = -(-(-(-self.part // blocks)) // 8) * 8
        self.apart = False
        if self.apart:
            self.counts = [self.part, WEMB_AT - self.part]
            second = -(-(-(-self.counts[1] // blocks)) // 8) * 8
            self.rows = [whole, second]
            self.dec_rows = whole - second
        else:
            self.counts = [self.part] * group
            self.rows = [whole] * group
            self.dec_rows = 0

    def ahead(self, clip, way):
        chip = (self.places[clip // CORES] + (1 if way == 0 else -1)) % self.chips
        return (clip % CORES * 2 + way) * self.chips + chip

    def fetch(self, block):
        half = block.shape[0] // CORES
        mine = lax.dynamic_slice_in_dim(block, self.core * half, half, 0)
        pieces = [block]
        for k in range(1, self.group):
            near = lax.ppermute(mine, "mlp", [(j, (j - k) % self.group) for j in range(self.group)])
            pieces += [near, self.swapped(near)]
        return pieces

    def swapped(self, value):
        return lax.ppermute(value, "clips", self.swap)

    def block(self, halves, way, back):
        sign = 1 if way == 0 else -1
        at = (self.at - sign * back) % self.chips
        one, two = (lax.dynamic_index_in_dim(half[way], at, 0, False).astype(f32) for half in halves)
        return one + two

    def start(self, keep, send, hurry=False):
        if not hurry:
            halves = keep, self.swapped(send)
            return halves, [self.block(halves, way, 0).astype(bf16) for way in range(2)]
        pick = lambda half: jnp.stack([lax.dynamic_index_in_dim(half[way], self.at, 0, False) for way in range(2)])
        piece = self.swapped(pick(send))
        first = (pick(keep).astype(f32) + piece.astype(f32)).astype(bf16)
        return (keep, self.swapped(after(send, piece))), [first[0], first[1]]

    def round_trip(self, started, ends=None):
        halves, held = started
        for step in range(1, self.chips):
            came = [lax.ppermute(held[way], "clips", self.ways[way]) for way in range(2)]
            held = [(came[way].astype(f32) + self.block(halves, way, step)).astype(bf16) for way in range(2)]
            if ends is not None and step == 2:
                held, ends[0] = lax.optimization_barrier((held, ends[0]))
                ridden = self.over_group([ends[0][:, 0], ends[0][:, 1]])
            if ends is not None and step == 5:
                held, ends[1:] = lax.optimization_barrier((held, ends[1:]))
            held = yield held
        if ends is not None:
            both = []
            for way in range(2):
                parts = []
                at = 0
                for y in range(self.group):
                    rows = [held[way][at : at + self.rows[y]]]
                    at += self.rows[y]
                    if self.apart and y == 1:
                        rows.append(ends[1][way])
                    parts.append(jnp.concatenate(rows) if len(rows) > 1 else rows[0])
                both.append(jnp.stack(parts))
            held = [jnp.concatenate(rows) for rows in zip(self.over_group(both), ridden)]
        return (yield from self.spread(held))

    def over_group(self, held):
        both = jnp.stack(held, axis=1)
        total = lax.dynamic_index_in_dim(both, self.lane, 0, False)
        for k in range(1, self.group):
            away = lax.dynamic_index_in_dim(both, (self.lane + k) % self.group, 0, False)
            total = total + lax.ppermute(away, "mlp", [(j, (j + k) % self.group) for j in range(self.group)])
        return [total[0], total[1]]

    def spread(self, held):
        found = [[held[0]], [held[1]]]
        early = None
        for step in range(1, self.chips):
            came = yield [lax.ppermute(found[way][-1], "clips", self.ways[way]) for way in range(2)]
            for way in range(2):
                found[way].append(came[way])
            if step == self.cut - 1:
                early = self.swapped(jnp.stack(found[0] + found[1]))
        late = self.swapped(jnp.stack(found[0][self.cut :] + found[1][self.cut :]))
        return found[0] + found[1], early, late


def side_by_side(one, two, lead):
    trips, done = (one, two), [None, None]
    kept = [None, None]

    def advance(i):
        try:
            value = next(trips[i]) if kept[i] is None else trips[i].send(kept[i])
        except StopIteration as end:
            done[i] = end.value
            return
        other = kept[1 - i]
        kept[i] = value if other is None else lax.optimization_barrier((value, other))[0]

    for _ in range(lead):
        advance(0)
    while done[0] is None or done[1] is None:
        for i in range(2):
            if done[i] is None:
                advance(i)
    return done


def place_kernel(ring, streams):
    chips, cut = ring.chips, ring.cut
    each = 2 * chips + 2
    n_outs = sum(len(shares) for shares in streams)
    last_block = CORES * 2 * chips - 1

    def body(where_ref, *refs):
        sources, rest = refs[: each * len(streams)], refs[each * len(streams) :]
        outs, buffers, sems = rest[:n_outs], rest[n_outs : 2 * n_outs], rest[2 * n_outs]
        core, at, lane = where_ref[0], where_ref[1], where_ref[2]
        copies = []

        def put(shares, first_out, index, block, value):
            first = 0
            for i, (total, columns, pieces) in enumerate(shares):
                out, buffer = outs[first_out + i], buffers[first_out + i]
                tiles = columns // 128
                high = sum(height for height, _, _ in pieces)
                wide = [value[first + t * high : first + (t + 1) * high] for t in range(tiles)]
                buffer[index] = jnp.concatenate(wide, axis=1) if tiles > 1 else wide[0]
                first += tiles * high
                start = 0
                for height, row_of, short in pieces:
                    row = pl.multiple_of(row_of(block, lane), 8)
                    cases = [(height, None)] if short == height else [(height, False), (short, True)]
                    for rows, at_end in cases:
                        if rows == 0:
                            continue
                        copy = pltpu.make_async_copy(
                            buffer.at[index, pl.ds(start, rows), :], out.at[pl.ds(row, rows), :], sems.at[len(copies)]
                        )
                        copies.append((copy, None if at_end is None else (block == last_block) == at_end))
                        run(copy.start, copies[-1][1])
                    start += height

        for n, shares in enumerate(streams):
            mine = sources[n * each : n * each + 2 * chips]
            early, late = sources[n * each + 2 * chips : (n + 1) * each]
            first_out = sum(len(other) for other in streams[:n])
            for step in range(chips):
                for way in range(2):
                    slot = lax.rem(at + (1 if way == 0 else -1) * (1 - step) + chips, chips)
                    other = early[way * cut + step] if step < cut else late[way * (chips - cut) + step - cut]
                    for side, near, value in ((core, 0, mine[way * chips + step][...]), (1 - core, 1, other)):
                        block = (side * 2 + way) * chips + slot
                        put(shares, first_out, (step * 2 + way) * 2 + near, block, value.astype(f32))
        for copy, condition in copies:
            run(copy.wait, condition)

    return body


def run(action, condition):
    if condition is None:
        action()
    else:
        pl.when(condition)(action)


def shares_of(ring, totals):
    blocks = CORES * 2 * ring.chips
    shares = []
    for total, columns in totals:
        flat = columns == 128
        if flat and ring.apart:
            whole, second = ring.rows
            cut = max(0, total - (blocks - 1) * whole)
            pieces = [
                (second, lambda b, lane: jnp.where(lane == 0, b * whole, b * second), min(second, cut)),
                (
                    whole - second,
                    lambda b, lane: jnp.where(lane == 0, b * whole + second, ring.counts[1] + b * (whole - second)),
                    max(0, cut - second),
                ),
            ]
        else:
            height = ring.rows[0] if flat else total // blocks
            pieces = [(height, lambda b, lane, height=height: b * height, total - (blocks - 1) * height)]
        shares.append((total, columns, pieces))
    return shares


def place(ring, founds, totals):
    streams = [shares_of(ring, shapes) for shapes in totals]
    if any(height % 8 for shares in streams for _, _, pieces in shares for height, _, _ in pieces):
        return [out for found, shares in zip(founds, streams) for out in place_rows(ring, found, shares)]
    hbm = pl.BlockSpec(memory_space=pl.ANY)
    blocks = CORES * 2 * ring.chips
    flat_shares = [share for shares in streams for share in shares]
    copies = blocks * sum(1 if s == h else 2 for _, _, pieces in flat_shares for h, _, s in pieces)
    sources = [ref for mine, early, late in founds for ref in (*mine, early, late)]
    return call(
        place_kernel(ring, streams),
        [((total, columns), f32) for total, columns, _ in flat_shares],
        jnp.stack([ring.core, ring.at, ring.lane]).astype(jnp.int32), *sources,
        in_specs=[SMEM] + [VMEM] * len(sources),
        out_specs=[hbm] * len(flat_shares),
        scratch_shapes=[
            pltpu.VMEM((blocks, sum(h for h, _, _ in pieces), columns), f32) for _, columns, pieces in flat_shares
        ] + [pltpu.SemaphoreType.DMA((copies,))],
        us=9,
        room=32,
    )


def place_rows(ring, found, shares):
    mine, early, late = found
    chips, cut = ring.chips, ring.cut
    outs = []
    first = 0
    for total, columns, pieces in shares:
        tiles = columns // 128
        height = pieces[0][0]
        out = jnp.zeros((CORES * 2 * chips * height, columns), f32)
        for way in range(2):
            for step in range(chips):
                slot = (ring.at + (1 if way == 0 else -1) * (1 - step)) % chips
                other = early[way * cut + step] if step < cut else late[way * (chips - cut) + step - cut]
                for side, value in ((ring.core, mine[way * chips + step]), (1 - ring.core, other)):
                    value = value[first : first + tiles * height].reshape(tiles, height, 128)
                    value = value.transpose(1, 0, 2).reshape(height, columns).astype(f32)
                    row = ((side * 2 + way) * chips + slot) * height
                    out = lax.dynamic_update_slice_in_dim(out, value, row, 0)
        outs.append(out[:total])
        first += tiles * height
    return outs


def after(value, *others):
    return lax.optimization_barrier((value,) + others)[0]


def shards(clips, group, flat_params, w_fc1, w_fc2, w_up, w_down, patches, clip_ids, visible_index, cotangent):
    width = w_fc1.shape[1]
    ring = Ring(clips, group)
    core = ring.core.astype(jnp.int32).reshape(1)
    turns = [[(i, (i + k) % group) for i in range(group)] for k in range(1, group)]
    back_turns = [[(i, (i - k) % group) for i in range(group)] for k in range(1, group)]

    ups = ring.fetch(w_up)
    downs = ring.fetch(w_down)

    flat = flat_params.reshape(FLAT_ROWS, 128)
    w_qkv, w_proj, g_one, g_two = enc_prep(flat)
    x, vis, qkv, probs, mix, first, in2 = call(
        enc_attend_kernel,
        [
            ((PAD, D), bf16), ((1, PAD), jnp.int32), ((PAD, 3 * D), bf16), ((HEADS, PAD, PAD), bf16), ((PAD, D), bf16),
            ((PAD, D), f32), ((PAD, D), bf16),
        ],
        patches, visible_index[None, :], clip_ids.reshape(-1, 128), w_qkv, w_proj, g_one, g_two,
        scratch_shapes=[pltpu.VMEM((1, 384), jnp.int32)],
        us=11,
    )

    in2s, hiddens, slopes, parts = [in2], [], [], []
    for i in range(group):
        if i > 0:
            in2s.append(after(lax.ppermute(in2, "mlp", turns[i - 1]), parts[0]))
        part, hidden, slope = call(
            enc_ffn_kernel,
            [((PAD, D), f32 if i == 0 else bf16), ((PAD, width), bf16), ((PAD, width), bf16)],
            in2s[i], w_fc1, w_fc2,
        )
        hiddens.append(hidden)
        slopes.append(slope)
        parts.append(part if i == 0 else lax.ppermute(part, "mlp", back_turns[i - 1]))
    w_embed, mask_token, w_dqkv, w_dproj, gd_one, gd_two, up_all, down_all = dec_prep(ring, flat, ups, downs, part)

    second_low, table, dec_norm = call(
        embed_kernel(group),
        [((PAD, D), bf16), ((PAD, 4 * DD), bf16), ((PAD, DD), bf16)],
        first, *parts, w_embed, mask_token, gd_one, w_dqkv,
    )
    decoded, ends, wdproj_grad, gd_two_grad, packed = decoder(
        ring, vis, table, cotangent, w_dproj, gd_two, up_all, down_all
    )
    ends = lax.psum_scatter(ends.reshape(-1, 128), "clips", scatter_dimension=0, tiled=True)
    ends = ends.reshape(group, 2, -1, 128)
    second_grad, out_grad, dec_qkv_grad, embed_grad, gd_one_grad, mask_grad = call(
        embed_back_kernel,
        [
            ((PAD, D), f32), ((PAD, D), bf16), ((PAD, 3 * DD), bf16), ((PAD, DD), bf16), ((1, DD), f32), ((1, DD), f32),
        ],
        packed, table, dec_norm, second_low, gd_one, w_dqkv, w_embed,
    )
    dec_wide = CORES * 2 * ring.chips * ring.dec_rows if ring.apart else DEC_ROWS
    dec_flat = call(
        dec_flat_kernel(ring),
        [((clips, 2, ring.dec_rows, 128) if ring.apart else (DEC_ROWS, 128), bf16)],
        dec_norm, dec_qkv_grad, second_low, embed_grad, wdproj_grad, mask_grad, gd_one_grad, gd_two_grad,
        scratch_shapes=[pltpu.VMEM((dec_wide, 128), f32)],
    )[0]
    dec_ends = []
    if ring.apart:
        dec_ends = lax.psum_scatter(dec_flat.reshape(-1, 128), "clips", scatter_dimension=0, tiled=True)
        dec_ends = [dec_ends.reshape(2, -1, 128)]

    out_grads, pre_grads, parts = [out_grad], [], []
    for i in range(group):
        if i > 0:
            out_grads.append(after(lax.ppermute(out_grad, "mlp", turns[i - 1]), parts[0], dec_flat))
        pre_grad, part = call(
            enc_ffn_back_kernel,
            [((PAD, width), bf16), ((PAD, D), f32 if i == 0 else bf16)],
            out_grads[i], slopes[i], w_fc1, w_fc2,
        )
        pre_grads.append(pre_grad)
        parts.append(part if i == 0 else lax.ppermute(part, "mlp", back_turns[i - 1]))
    fc_halves = ((2, ring.chips, 2 * D * width // (CORES * 2 * ring.chips * 128), 128), bf16)
    fc_keep, fc_send = call(
        enc_weights_kernel(group, ring.chips), [fc_halves, fc_halves],
        core, *in2s, *pre_grads, *hiddens, *out_grads,
        in_specs=[SMEM] + [VMEM] * (4 * group),
        us=10,
    )
    parts[1:] = [after(part, fc_keep) for part in parts[1:]]
    flat_halves = ((2, ring.chips, sum(ring.rows), 128), bf16)
    input_grad, flat_keep, flat_send = call(
        enc_back_kernel(group, ring),
        [((VIS, D), f32), flat_halves, flat_halves],
        core, *parts, second_grad, first, x, qkv, probs, mix, w_qkv, w_proj, g_one, g_two, *([] if ring.apart else [dec_flat]),
        in_specs=[SMEM] + [VMEM] * (group + (10 if ring.apart else 11)),
        scratch_shapes=[
            pltpu.VMEM((PAD, 3 * D), bf16), pltpu.VMEM((WEMB_AT + 4 if ring.apart else FLAT_ROWS, 128), f32),
        ],
        us=20,
        room=32,
    )
    flat_found, fc_found = side_by_side(
        ring.round_trip(ring.start(flat_keep, flat_send, True), [ends] + dec_ends),
        ring.round_trip(ring.start(fc_keep, fc_send, True)),
        0,
    )
    fc1_grad, fc2_grad = place(ring, [fc_found], [[(D, width), (width, D)]])
    param_grad, up_grad, down_grad = place(
        ring, [flat_found], [[(ring.part, 128), (DD, w_up.shape[1]), (w_up.shape[1], DD)]]
    )
    return decoded, input_grad, param_grad.reshape(-1), fc1_grad, fc2_grad, up_grad, down_grad


def solution(mesh):
    placed = (
        P(),
        P(None, "mlp"),
        P("mlp", None),
        P(None, "mlp"),
        P("mlp", None),
        P(("clips", "mlp"), None),
        P(("clips", "mlp")),
        P(("clips", "mlp")),
        P(("clips", "mlp"), None),
    )
    group = mesh.shape["mlp"]

    def body(*args):
        return shards(mesh.shape["clips"], group, *args)

    return jax.shard_map(
        body,
        mesh=mesh,
        in_specs=placed,
        out_specs=(
            P(("clips", "mlp"), None),
            P(("clips", "mlp"), None),
            P("mlp"),
            P(None, "mlp"),
            P("mlp", None),
            P(None, "mlp"),
            P("mlp", None),
        ),
        check_vma=False,
    )
```

```python
import math

import jax
import jax.numpy as jnp
from jax import lax
from jax.experimental import pallas as pl
from jax.experimental.pallas import tpu as pltpu
from jax.sharding import PartitionSpec as P

D = 768
HEADS = 12
DD = 512
DHEADS = 16
FREQ = 8
WIN = 4
ROWS = 1536
VIS = 312
PAD = 320
SHORT_PATCHES = 512
PARAMS = 3804160
EPSILON = 1e-06
BLOCK = 512
GROUP = WIN * FREQ
HALF = DD // 2
ENC_SCALE = 1.0 / math.sqrt(D // HEADS)
DEC_SCALE = 1.0 / math.sqrt(DD // DHEADS)
LOWEST = -1e30
CORES = 2
bf16 = jnp.bfloat16
f32 = jnp.float32


def mm(left, right):
    return jnp.dot(left, right, preferred_element_type=f32)


def mm_nt(left, right):
    return lax.dot_general(left, right, (((1,), (1,)), ((), ())), preferred_element_type=f32)


def mm_tn(left, right):
    return lax.dot_general(left, right, (((0,), (0,)), ((), ())), preferred_element_type=f32)


def normalize(rows):
    centred = rows - jnp.mean(rows, axis=-1, keepdims=True)
    scale = lax.rsqrt(jnp.mean(centred * centred, axis=-1, keepdims=True) + EPSILON)
    return centred * scale, scale


def norm_back(grad, normed, scale, gain):
    weighted = grad * gain
    return scale * (
        weighted
        - jnp.mean(weighted, axis=-1, keepdims=True)
        - normed * jnp.mean(weighted * normed, axis=-1, keepdims=True)
    )


def gelu_parts(pre):
    cdf = 0.5 * (1.0 + lax.erf(pre * math.sqrt(0.5)))
    return pre * cdf, cdf + pre * jnp.exp(-0.5 * pre * pre) * (1.0 / math.sqrt(2.0 * math.pi))


def gained(grad, normed):
    return jnp.sum(grad * normed, axis=0, keepdims=True)


SMEM = pl.BlockSpec(memory_space=pltpu.SMEM)
VMEM = pl.BlockSpec(memory_space=pltpu.VMEM)


def hint(us):
    return pl.CostEstimate(flops=int(us * 8e8), transcendentals=0, bytes_accessed=int(us * 1e6))


def call(body, outs, *args, us=5, room=20, **more):
    return pl.pallas_call(
        body,
        cost_estimate=hint(us),
        out_shape=[jax.ShapeDtypeStruct(shape, dtype) for shape, dtype in outs],
        compiler_params=pltpu.CompilerParams(vmem_limit_bytes=room * 2**20),
        **more,
    )(*args)


TILES = {"wqkv": 18, "wproj": 6, "wemb": 4, "wdqkv": 12, "wdproj": 4}
G1_AT = (D * 3 * D + D * D) // 128
WEMB_AT = G1_AT + 12
MASK_AT = WEMB_AT + D * 4
WDQKV_AT = MASK_AT + 4
WDPROJ_AT = WDQKV_AT + DD * 12
GD1_AT = WDPROJ_AT + DD * 4
FLAT_ROWS = PARAMS // 128
DEC_ROWS = FLAT_ROWS - WEMB_AT
PREP = 192


def widen(flat_ref, first, out_ref, tiles):
    for t in range(tiles):
        out_ref[:, t * 128 : t * 128 + 128] = flat_ref[
            pl.ds(first + t, out_ref.shape[0], stride=tiles), :
        ].astype(bf16)


def vector(flat_ref, first, count):
    return jnp.concatenate([flat_ref[first + i : first + i + 1, :] for i in range(count)], axis=1)


def flatten(flat_ref, first, value, tiles):
    for t in range(tiles):
        flat_ref[pl.ds(first + t, value.shape[0], stride=tiles), :] = value[:, t * 128 : t * 128 + 128]


def enc_prep_kernel(qkv_ref, proj_ref, gains_ref, wqkv_ref, wproj_ref, g1_ref, g2_ref, qkv_flat, proj_flat, gains_flat):
    qkv_flat[...] = qkv_ref[...].astype(f32)
    proj_flat[...] = proj_ref[...].astype(f32)
    widen(qkv_flat, 0, wqkv_ref, 18)
    widen(proj_flat, 0, wproj_ref, 6)

    @pl.when(pl.program_id(0) == 0)
    def _():
        gains_flat[...] = gains_ref[...].astype(f32)
        g1_ref[...] = vector(gains_flat, 0, 6)
        g2_ref[...] = vector(gains_flat, 6, 6)


def enc_prep(flat):
    whole = lambda *shape: pl.BlockSpec(shape, lambda i: (0,) * len(shape))
    return pl.pallas_call(
        enc_prep_kernel,
        grid=(D // PREP,),
        in_specs=[
            pl.BlockSpec((PREP * 18, 128), lambda i: (i, 0)),
            pl.BlockSpec((PREP * 6, 128), lambda i: (D * 18 // (PREP * 6) + i, 0)),
            pl.BlockSpec((16, 128), lambda i: (G1_AT // 16, 0)),
        ],
        out_specs=[
            pl.BlockSpec((PREP, 3 * D), lambda i: (i, 0)),
            pl.BlockSpec((PREP, D), lambda i: (i, 0)),
            whole(1, D),
            whole(1, D),
        ],
        out_shape=[
            jax.ShapeDtypeStruct((D, 3 * D), bf16),
            jax.ShapeDtypeStruct((D, D), bf16),
            jax.ShapeDtypeStruct((1, D), f32),
            jax.ShapeDtypeStruct((1, D), f32),
        ],
        scratch_shapes=[
            pltpu.VMEM((PREP * 18, 128), f32), pltpu.VMEM((PREP * 6, 128), f32), pltpu.VMEM((16, 128), f32),
        ],
    )(flat, flat, flat)


def dec_prep_kernel(count):
    def body(where_ref, flat_ref, _, *refs):
        ups, downs = refs[: 2 * count - 1], refs[2 * count - 1 : 4 * count - 2]
        (
            wemb_ref, mask_ref, wdqkv_ref, wdproj_ref, gd1_ref, gd2_ref, up_ref, down_ref, low, wide, sem,
        ) = refs[4 * count - 2 :]
        copy = pltpu.make_async_copy(flat_ref.at[pl.ds(G1_AT, FLAT_ROWS - G1_AT), :], low, sem)
        copy.start()
        core, lane = where_ref[0], where_ref[1]
        for pieces, whole in ((ups, up_ref), (downs, down_ref)):
            half = whole.shape[1] // CORES
            whole[lane] = pieces[0][...]
            for k in range(1, count):
                at = lax.rem(lane + k, count)
                near = pl.multiple_of(core * half, 8)
                far = pl.multiple_of((1 - core) * half, 8)
                whole[at, pl.ds(near, half), :] = pieces[2 * k - 1][...]
                whole[at, pl.ds(far, half), :] = pieces[2 * k][...]
        copy.wait()
        wide[...] = low[...].astype(f32)
        widen(wide, WEMB_AT - G1_AT, wemb_ref, 4)
        widen(wide, WDQKV_AT - G1_AT, wdqkv_ref, 12)
        widen(wide, WDPROJ_AT - G1_AT, wdproj_ref, 4)
        mask_ref[...] = vector(wide, MASK_AT - G1_AT, 4)
        gd1_ref[...] = vector(wide, GD1_AT - G1_AT, 4)
        gd2_ref[...] = vector(wide, GD1_AT - G1_AT + 4, 4)

    return body


def dec_prep(ring, flat, ups, downs, later):
    hbm = pl.BlockSpec(memory_space=pl.ANY)
    whole = lambda block: ((ring.group,) + block.shape, bf16)
    return call(
        dec_prep_kernel(ring.group),
        [
            ((D, DD), bf16), ((1, DD), f32), ((DD, 3 * DD), bf16), ((DD, DD), bf16), ((1, DD), f32), ((1, DD), f32),
            whole(ups[0]), whole(downs[0]),
        ],
        jnp.stack([ring.core, ring.lane]).astype(jnp.int32), flat, later, *ups, *downs,
        in_specs=[SMEM, hbm, hbm] + [VMEM] * (len(ups) + len(downs)),
        scratch_shapes=[
            pltpu.VMEM((FLAT_ROWS - G1_AT, 128), bf16), pltpu.VMEM((FLAT_ROWS - G1_AT, 128), f32),
            pltpu.SemaphoreType.DMA,
        ],
    )


def enc_attend_kernel(
    patches_ref, visible_ref, ids_ref, wqkv_ref, wproj_ref, g1_ref, g2_ref,
    x_ref, vis_ref, qkv_ref, probs_ref, mix_ref, first_ref, in2_ref, wide_vis,
):
    x_ref[...] = jnp.concatenate(
        [patches_ref[...].astype(f32), jnp.zeros((PAD - VIS, D), f32)], axis=0
    ).astype(bf16)
    wide_vis[...] = jnp.full(wide_vis.shape, -1, jnp.int32)
    wide_vis[:, :VIS] = visible_ref[...]
    vis = wide_vis[:, :PAD]
    vis_ref[...] = vis
    last = jnp.max(ids_ref[...].astype(f32))
    clip = jnp.where(vis < 0, -1.0, jnp.minimum((vis // SHORT_PATCHES).astype(f32), last))
    square = (PAD, PAD)
    across = jnp.broadcast_to(clip, square)
    diagonal = lax.broadcasted_iota(jnp.int32, square, 0) == lax.broadcasted_iota(jnp.int32, square, 1)
    allowed = across == jnp.sum(jnp.where(diagonal, across, 0.0), axis=1, keepdims=True)
    x = x_ref[...].astype(f32)
    normed, _ = normalize(x)
    qkv_ref[...] = mm((normed * g1_ref[...]).astype(bf16), wqkv_ref[...]).astype(bf16)
    low_lanes = lax.broadcasted_iota(jnp.int32, (PAD, 128), 1) < 64
    for pair in range(HEADS // 2):
        at = slice(pair * 128, pair * 128 + 128)
        query = qkv_ref[:, at]
        key = qkv_ref[:, D + pair * 128 : D + pair * 128 + 128]
        value = qkv_ref[:, 2 * D + pair * 128 : 2 * D + pair * 128 + 128]
        mixed = []
        for side in range(2):
            mine = low_lanes if side == 0 else jnp.logical_not(low_lanes)
            own = jnp.where(mine, query.astype(f32) * ENC_SCALE, 0.0).astype(bf16)
            scores = jnp.where(allowed, mm_nt(own, key), LOWEST)
            top = jnp.max(scores, axis=-1, keepdims=True)
            raised = jnp.exp(scores - top)
            probs = (raised * (1.0 / jnp.sum(raised, axis=-1, keepdims=True))).astype(bf16)
            probs_ref[2 * pair + side] = probs
            mixed.append(mm(probs, value))
        mix_ref[:, at] = jnp.where(low_lanes, mixed[0], mixed[1]).astype(bf16)
    first = x + mm(mix_ref[...], wproj_ref[...])
    first_ref[...] = first
    normed2, _ = normalize(first)
    in2_ref[...] = (normed2 * g2_ref[...]).astype(bf16)


def enc_ffn_kernel(in2_ref, fc1_ref, fc2_ref, part_ref, hidden_ref, slope_ref):
    act, slope = gelu_parts(mm(in2_ref[...], fc1_ref[...]))
    hidden = act.astype(bf16)
    hidden_ref[...] = hidden
    slope_ref[...] = slope.astype(bf16)
    part_ref[...] = mm(hidden, fc2_ref[...]).astype(part_ref.dtype)


def enc_ffn_back_kernel(out_grad_ref, slope_ref, fc1_ref, fc2_ref, pre_grad_ref, part_ref):
    grad = mm_nt(out_grad_ref[...], fc2_ref[...]) * slope_ref[...].astype(f32)
    pre_grad = grad.astype(bf16)
    pre_grad_ref[...] = pre_grad
    part_ref[...] = mm_nt(pre_grad, fc1_ref[...]).astype(part_ref.dtype)


def slabs(rows):
    return jnp.concatenate([rows[:, t * 128 : t * 128 + 128] for t in range(rows.shape[1] // 128)], axis=0)


def enc_weights_kernel(count, chips):
    def body(core_ref, *refs):
        in2s, pre_grads, hiddens, out_grads = (refs[i * count : (i + 1) * count] for i in range(4))
        keep_ref, send_ref = refs[4 * count : 4 * count + 2]
        at = 0
        for lefts, rights in ((in2s, pre_grads), (hiddens, out_grads)):
            total = mm_tn(lefts[0][...], rights[0][...])
            for i in range(1, count):
                total = total + mm_tn(lefts[i][...], rights[i][...])
            height = total.shape[0] // (CORES * 2 * chips)
            rows = height * total.shape[1] // 128

            def split(target, half, total=total, height=height, rows=rows, at=at):
                for way in range(2):
                    for chip in range(chips):
                        first = ((half * 2 + way) * chips + chip) * height
                        target[way, chip, at : at + rows, :] = slabs(total[first : first + height].astype(bf16))

            for half in range(CORES):
                @pl.when(core_ref[0] == half)
                def _(half=half, split=split):
                    split(keep_ref, half)
                    split(send_ref, 1 - half)

            at += rows

    return body


def embed_kernel(count):
    def body(first_ref, own_ref, *refs):
        parts = refs[: count - 1]
        wemb_ref, mask_ref, gd1_ref, wdqkv_ref, second_ref, table_ref, norm_ref = refs[count - 1 :]
        second = first_ref[...] + own_ref[...]
        for part in parts:
            second += part[...].astype(f32)
        low = second.astype(bf16)
        second_ref[...] = low
        embedded = mm(low, wemb_ref[...]).astype(bf16).astype(f32)
        row = lax.broadcasted_iota(jnp.int32, (PAD, DD), 0)
        start = jnp.where(row == VIS, mask_ref[...], embedded)
        normed, _ = normalize(start)
        dec_norm = (normed * gd1_ref[...]).astype(bf16)
        norm_ref[...] = dec_norm
        table_ref[:, : 3 * DD] = mm(dec_norm, wdqkv_ref[...]).astype(bf16)
        table_ref[:, 3 * DD :] = start.astype(bf16)

    return body


def spread(rows, same):
    left = jnp.concatenate([rows[:, :128]] * 4, axis=0) * same
    right = jnp.concatenate([rows[:, 128:]] * 4, axis=0) * same
    none = jnp.zeros_like(left)
    return jnp.concatenate(
        [jnp.concatenate([left, none], axis=1), jnp.concatenate([none, right], axis=1)], axis=0
    )


def diagonal(full):
    head = lax.broadcasted_iota(jnp.int32, (GROUP, 128), 1) // GROUP
    tiles = []
    for t in range(2):
        first = t * 128
        tile = full[first : first + GROUP, first : first + 128]
        for h in range(1, 4):
            tile = jnp.where(head == h, full[first + h * GROUP : first + (h + 1) * GROUP, first : first + 128], tile)
        tiles.append(tile)
    return jnp.concatenate(tiles, axis=1)


def segment_max(rows):
    tiles = []
    lane = lax.broadcasted_iota(jnp.int32, (rows.shape[0], 128), 1)
    for t in range(rows.shape[1] // 128):
        tile = rows[:, t * 128 : t * 128 + 128]
        for step in (1, 2, 8, 16):
            other = jnp.where(
                lane & step == 0, pltpu.roll(tile, 128 - step, 1), pltpu.roll(tile, step, 1)
            )
            tile = jnp.maximum(tile, other)
        tiles.append(tile)
    return jnp.concatenate(tiles, axis=1)


def decoder_kernel(chunks, ring):
    def body(
        vis_ref, table_ref, cot_ref, wdproj_ref, gd2_ref, up_ref, down_ref,
        decoded_ref, ends_ref, proj_grad_ref, gd2_grad_ref, packed_ref,
        qkv_ref, mix_ref, s_ref, p_ref, dmix_ref, ds_ref, back_ref, same_ref, ones_ref,
        up_acc, down_acc, proj_acc, gd2_acc, packed_acc,
    ):
        step = pl.program_id(0)

        @pl.when(step == 0)
        def _():
            up_acc[...] = jnp.zeros_like(up_acc)
            down_acc[...] = jnp.zeros_like(down_acc)
            proj_acc[...] = jnp.zeros_like(proj_acc)
            gd2_acc[...] = jnp.zeros_like(gd2_acc)
            packed_acc[...] = jnp.zeros_like(packed_acc)
            head_row = lax.broadcasted_iota(jnp.int32, (HALF, HALF), 0) // GROUP
            head_lane = lax.broadcasted_iota(jnp.int32, (HALF, HALF), 1) // GROUP
            ones = (head_row == head_lane).astype(f32).astype(bf16)
            ones_ref[...] = ones
            same_ref[...] = ones[:128, :128]

        row = lax.broadcasted_iota(jnp.int32, (BLOCK, PAD), 0) + step * BLOCK
        named = row == vis_ref[...]
        col = lax.broadcasted_iota(jnp.int32, (BLOCK, PAD), 1)
        hit = jnp.max(jnp.where(named, 1.0, 0.0), axis=1, keepdims=True)
        one_hot = jnp.where(named, 1.0, jnp.where(col == VIS, 1.0 - hit, 0.0)).astype(bf16)
        qkv_ref[...] = mm(one_hot, table_ref[:, : 3 * DD]).astype(bf16)
        start = mm(one_hot, table_ref[:, 3 * DD :])

        lane = lax.broadcasted_iota(jnp.int32, (BLOCK, DD), 1)
        line = lax.broadcasted_iota(jnp.int32, (BLOCK, DD), 0)
        window = (lane % FREQ) // WIN == (line % FREQ) // WIN
        n_groups = BLOCK // GROUP

        def parts(group, half):
            at = pl.ds(pl.multiple_of(group * GROUP, GROUP), GROUP)
            return at, slice(half * HALF, (half + 1) * HALF)

        def scores(group, _):
            same = same_ref[...]
            for half in range(2):
                at, cols = parts(group, half)
                key = qkv_ref[at, DD + half * HALF : DD + (half + 1) * HALF]
                s_ref[at, cols] = mm_nt(qkv_ref[at, cols], spread(key, same))
            return 0

        lax.fori_loop(0, n_groups, scores, 0, unroll=16)
        raw = s_ref[...] * DEC_SCALE
        top = segment_max(raw)
        raised = jnp.where(window, jnp.exp(raw - top), 0.0)
        p_low = raised.astype(bf16)
        total = jnp.concatenate(
            [mm(p_low[:, :HALF], ones_ref[...]), mm(p_low[:, HALF:], ones_ref[...])], axis=1
        )
        p_ref[...] = (raised / total).astype(bf16)

        def mixes(group, _):
            same = same_ref[...]
            for half in range(2):
                at, cols = parts(group, half)
                value = qkv_ref[at, 2 * DD + half * HALF : 2 * DD + (half + 1) * HALF]
                mix_ref[at, cols] = mm(p_ref[at, cols], spread(value, same)).astype(bf16)
            return 0

        lax.fori_loop(0, n_groups, mixes, 0, unroll=16)

        middle = start + mm(mix_ref[...], wdproj_ref[...])
        normed, scale = normalize(middle)
        in2 = (normed * gd2_ref[...]).astype(bf16)
        cot = cot_ref[...]
        out = jnp.zeros_like(middle)
        in2_grad = jnp.zeros_like(middle)
        for c in range(chunks):
            act, slope = gelu_parts(mm(in2, up_ref[c]))
            hidden = act.astype(bf16)
            out += mm(hidden, down_ref[c])
            pre_grad = (mm_nt(cot, down_ref[c]) * slope).astype(bf16)
            in2_grad += mm_nt(pre_grad, up_ref[c])
            down_acc[c] += mm_tn(hidden, cot)
            up_acc[c] += mm_tn(in2, pre_grad)
        decoded_ref[...] = (middle + out).astype(bf16)

        gd2_acc[...] += gained(in2_grad, normed)
        middle_grad = cot.astype(f32) + norm_back(in2_grad, normed, scale, gd2_ref[...])
        branch = middle_grad.astype(bf16)
        back_ref[:, 3 * DD :] = branch
        proj_acc[...] += mm_tn(mix_ref[...], branch)
        dmix_ref[...] = mm_nt(branch, wdproj_ref[...]).astype(bf16)

        def prob_grads(group, _):
            same = same_ref[...]
            for half in range(2):
                at, cols = parts(group, half)
                value = qkv_ref[at, 2 * DD + half * HALF : 2 * DD + (half + 1) * HALF]
                s_ref[at, cols] = mm_nt(dmix_ref[at, cols], spread(value, same))
            return 0

        lax.fori_loop(0, n_groups, prob_grads, 0, unroll=16)
        probs = p_ref[...].astype(f32)
        prob_grad = s_ref[...]
        weighed = (probs * prob_grad).astype(bf16)
        row_sum = jnp.concatenate(
            [mm(weighed[:, :HALF], ones_ref[...]), mm(weighed[:, HALF:], ones_ref[...])], axis=1
        )
        ds_ref[...] = (probs * (prob_grad - row_sum)).astype(bf16)

        def qkv_grads(group, _):
            same = same_ref[...]
            for half in range(2):
                at, cols = parts(group, half)
                key_cols = slice(DD + half * HALF, DD + (half + 1) * HALF)
                value_cols = slice(2 * DD + half * HALF, 2 * DD + (half + 1) * HALF)
                key = qkv_ref[at, key_cols]
                back_ref[at, cols] = (mm(ds_ref[at, cols], spread(key, same)) * DEC_SCALE).astype(bf16)
                key_grad = diagonal(mm_tn(ds_ref[at, cols], qkv_ref[at, cols]))
                back_ref[at, key_cols] = (key_grad * DEC_SCALE).astype(bf16)
                back_ref[at, value_cols] = diagonal(mm_tn(p_ref[at, cols], dmix_ref[at, cols])).astype(bf16)
            return 0

        lax.fori_loop(0, n_groups, qkv_grads, 0, unroll=16)
        packed_acc[...] += mm_tn(one_hot, back_ref[...])

        @pl.when(step == pl.num_programs(0) - 1)
        def _():
            tall, low = DD // (CORES * 2 * ring.chips), up_acc.shape[2] // (CORES * 2 * ring.chips)
            cut = tall * up_acc.shape[2] // 128
            for clip in range(ring.clips):
                for way in range(2):
                    block = ring.ahead(clip, way)
                    for y in range(chunks):
                        ends_ref[clip, y, way, :cut] = slabs(up_acc[y, block * tall : (block + 1) * tall].astype(bf16))
                        ends_ref[clip, y, way, cut:] = slabs(down_acc[y, block * low : (block + 1) * low].astype(bf16))
            proj_grad_ref[...] = proj_acc[...].astype(bf16)
            gd2_grad_ref[...] = gd2_acc[...]
            packed_ref[...] = packed_acc[...]

    return body


def decoder(ring, vis_row, table, cotangent, w_dproj, gd_two, up, down):
    chunks, _, width = up.shape
    rows = cotangent.shape[0]
    kept = lambda *shape: pl.BlockSpec(shape, lambda i: (0,) * len(shape), pipeline_mode=pl.Buffered(1))
    by_rows = pl.BlockSpec((BLOCK, DD), lambda i: (i, 0))
    ends = (ring.clips, chunks, 2, DD * width // (128 * ring.clips), 128)
    outs = [
        ((rows, DD), bf16, by_rows),
        (ends, bf16, kept(*ends)),
        ((DD, DD), bf16, kept(DD, DD)),
        ((1, DD), f32, kept(1, DD)),
        ((PAD, 4 * DD), f32, kept(PAD, 4 * DD)),
    ]
    return pl.pallas_call(
        decoder_kernel(chunks, ring),
        cost_estimate=hint(80),
        grid=(rows // BLOCK,),
        in_specs=[
            kept(1, PAD), kept(PAD, 4 * DD), by_rows, kept(DD, DD), kept(1, DD),
            kept(chunks, DD, width), kept(chunks, width, DD),
        ],
        out_specs=[spec for _, _, spec in outs],
        out_shape=[jax.ShapeDtypeStruct(shape, dtype) for shape, dtype, _ in outs],
        scratch_shapes=[
            pltpu.VMEM((BLOCK, 3 * DD), bf16),
            pltpu.VMEM((BLOCK, DD), bf16),
            pltpu.VMEM((BLOCK, DD), f32),
            pltpu.VMEM((BLOCK, DD), bf16),
            pltpu.VMEM((BLOCK, DD), bf16),
            pltpu.VMEM((BLOCK, DD), bf16),
            pltpu.VMEM((BLOCK, 4 * DD), bf16),
            pltpu.VMEM((128, 128), bf16),
            pltpu.VMEM((HALF, HALF), bf16),
            pltpu.VMEM((chunks, DD, width), f32),
            pltpu.VMEM((chunks, width, DD), f32),
            pltpu.VMEM((DD, DD), f32),
            pltpu.VMEM((1, DD), f32),
            pltpu.VMEM((PAD, 4 * DD), f32),
        ],
        compiler_params=pltpu.CompilerParams(vmem_limit_bytes=40 * 2**20),
    )(vis_row, table, cotangent, w_dproj, gd_two, up, down)


def embed_back_kernel(
    packed_ref, table_ref, norm_ref, second_ref, gd1_ref, wdqkv_ref, wemb_ref,
    second_grad_ref, out_grad_ref, qkv_grad_ref, embed_grad_ref, gd1_grad_ref, mask_grad_ref,
):
    qkv_grad = packed_ref[:, : 3 * DD].astype(bf16)
    qkv_grad_ref[...] = qkv_grad
    grad = mm_nt(qkv_grad, wdqkv_ref[...])
    normed, scale = normalize(table_ref[:, 3 * DD :].astype(f32))
    gd1_grad_ref[...] = gained(grad, normed)
    start_grad = packed_ref[:, 3 * DD :] + norm_back(grad, normed, scale, gd1_ref[...])
    mask_grad_ref[...] = start_grad[VIS : VIS + 1]
    row = lax.broadcasted_iota(jnp.int32, (PAD, DD), 0)
    embed_grad = jnp.where(row < VIS, start_grad, 0.0).astype(bf16)
    embed_grad_ref[...] = embed_grad
    second_grad = mm_nt(embed_grad, wemb_ref[...])
    second_grad_ref[...] = second_grad
    out_grad_ref[...] = second_grad.astype(bf16)


def dec_flat_kernel(ring):
    def body(
        norm_ref, qkv_grad_ref, second_ref, embed_grad_ref, proj_grad_ref, mask_grad_ref, gd1_grad_ref, gd2_grad_ref,
        flat_ref, wide,
    ):
        flatten(wide, 0, mm_tn(second_ref[...], embed_grad_ref[...]), 4)
        flatten(wide, MASK_AT - WEMB_AT, mask_grad_ref[...], 4)
        flatten(wide, WDQKV_AT - WEMB_AT, mm_tn(norm_ref[...], qkv_grad_ref[...]), 12)
        flatten(wide, WDPROJ_AT - WEMB_AT, proj_grad_ref[...].astype(f32), 4)
        flatten(wide, GD1_AT - WEMB_AT, gd1_grad_ref[...], 4)
        flatten(wide, GD1_AT + 4 - WEMB_AT, gd2_grad_ref[...], 4)
        if not ring.apart:
            flat_ref[...] = wide[...].astype(bf16)
            return
        wide[DEC_ROWS:, :] = jnp.zeros((wide.shape[0] - DEC_ROWS, 128), f32)
        for clip in range(ring.clips):
            for way in range(2):
                block = ring.ahead(clip, way)
                flat_ref[clip, way] = wide[block * ring.dec_rows : (block + 1) * ring.dec_rows, :].astype(bf16)

    return body


def enc_back_kernel(count, ring):
    def body(core_ref, own_ref, *refs):
        parts = refs[: count - 1]
        (
            second_grad_ref, first_ref, x_ref, qkv_ref, probs_ref, mix_ref, wqkv_ref, wproj_ref, g1_ref, g2_ref,
        ) = refs[count - 1 : count + 9]
        input_grad_ref, keep_ref, send_ref, qkv_grad_ref, wide = refs[-5:]
        in2_grad = own_ref[...]
        for part in parts:
            in2_grad += part[...].astype(f32)
        normed2, scale2 = normalize(first_ref[...])
        flatten(wide, G1_AT + 6, gained(in2_grad, normed2), 6)
        first_grad = second_grad_ref[...] + norm_back(in2_grad, normed2, scale2, g2_ref[...])
        branch = first_grad.astype(bf16)
        flatten(wide, D * 18, mm_tn(mix_ref[...], branch), 6)
        if not ring.apart:
            wide[WEMB_AT:FLAT_ROWS, :] = refs[-6][...].astype(f32)
        mix_grad = mm_nt(branch, wproj_ref[...]).astype(bf16)
        low_lanes = lax.broadcasted_iota(jnp.int32, (PAD, 128), 1) < 64
        for pair in range(HEADS // 2):
            at = slice(pair * 128, pair * 128 + 128)
            query = qkv_ref[:, at]
            key = qkv_ref[:, D + pair * 128 : D + pair * 128 + 128]
            value = qkv_ref[:, 2 * D + pair * 128 : 2 * D + pair * 128 + 128]
            upstream = mix_grad[:, at]
            found = []
            for side in range(2):
                mine = low_lanes if side == 0 else jnp.logical_not(low_lanes)
                own = jnp.where(mine, upstream.astype(f32), 0.0).astype(bf16)
                low_probs = probs_ref[2 * pair + side]
                probs = low_probs.astype(f32)
                prob_grad = mm_nt(own, value)
                row_sum = jnp.sum(probs * prob_grad, axis=-1, keepdims=True)
                score_grad = (probs * (prob_grad - row_sum)).astype(bf16)
                found.append((mm(score_grad, key), mm_tn(score_grad, query), mm_tn(low_probs, upstream)))
            for part, factor in enumerate((ENC_SCALE, ENC_SCALE, 1.0)):
                merged = jnp.where(low_lanes, found[0][part], found[1][part]) * factor
                qkv_grad_ref[:, part * D + pair * 128 : part * D + pair * 128 + 128] = merged.astype(bf16)
        normed, scale = normalize(x_ref[...].astype(f32))
        flatten(wide, 0, mm_tn((normed * g1_ref[...]).astype(bf16), qkv_grad_ref[...]), 18)
        grad = mm_nt(qkv_grad_ref[...], wqkv_ref[...])
        flatten(wide, G1_AT, gained(grad, normed), 6)
        input_grad_ref[...] = (first_grad + norm_back(grad, normed, scale, g1_ref[...]))[:VIS]

        def split(target, half):
            for way in range(2):
                for chip in range(ring.chips):
                    block = (half * 2 + way) * ring.chips + chip
                    at = 0
                    for y in range(ring.group):
                        height = ring.rows[y]
                        first = y * ring.part + block * height
                        count = max(0, min(height, ring.counts[y] - block * height))
                        if count > 0:
                            target[way, chip, at : at + count] = wide[first : first + count, :].astype(bf16)
                        if count < height:
                            target[way, chip, at + count : at + height] = jnp.zeros((height - count, 128), bf16)
                        at += height

        for half in range(CORES):
            @pl.when(core_ref[0] == half)
            def _(half=half):
                split(keep_ref, half)
                split(send_ref, 1 - half)

    return body


class Ring:
    def __init__(self, clips, group):
        self.chips = clips // CORES
        self.group = group
        chips = self.chips
        if chips == 8:
            order = [4 * z // 2 for z in range(4)] + [4 * z // 2 + 1 for z in reversed(range(4))]
        else:
            order = list(range(chips))
        place = [0] * chips
        for at, chip in enumerate(order):
            place[chip] = at
        clip = lax.axis_index("clips")
        self.places = place
        self.core = clip % CORES
        chip = clip // CORES
        if chips == 8:
            self.at = jnp.where(chip % 2 == 0, chip // 2, 7 - chip // 2)
        else:
            self.at = chip
        self.lane = lax.axis_index("mlp")
        step = lambda way: [
            (order[i] * CORES + c, order[(i + way) % chips] * CORES + c) for i in range(chips) for c in range(CORES)
        ]
        self.ways = (step(1), step(-1))
        self.swap = [(i, i ^ 1) for i in range(clips)]
        self.clips = clips
        self.cut = max(2, chips - 2)
        blocks = CORES * 2 * chips
        self.part = FLAT_ROWS // group
        whole = -(-(-(-self.part // blocks)) // 8) * 8
        self.apart = False
        if self.apart:
            self.counts = [self.part, WEMB_AT - self.part]
            second = -(-(-(-self.counts[1] // blocks)) // 8) * 8
            self.rows = [whole, second]
            self.dec_rows = whole - second
        else:
            self.counts = [self.part] * group
            self.rows = [whole] * group
            self.dec_rows = 0

    def ahead(self, clip, way):
        chip = (self.places[clip // CORES] + (1 if way == 0 else -1)) % self.chips
        return (clip % CORES * 2 + way) * self.chips + chip

    def fetch(self, block):
        half = block.shape[0] // CORES
        mine = lax.dynamic_slice_in_dim(block, self.core * half, half, 0)
        pieces = [block]
        for k in range(1, self.group):
            near = lax.ppermute(mine, "mlp", [(j, (j - k) % self.group) for j in range(self.group)])
            pieces += [near, self.swapped(near)]
        return pieces

    def swapped(self, value):
        return lax.ppermute(value, "clips", self.swap)

    def block(self, halves, way, back):
        sign = 1 if way == 0 else -1
        at = (self.at - sign * back) % self.chips
        one, two = (lax.dynamic_index_in_dim(half[way], at, 0, False).astype(f32) for half in halves)
        return one + two

    def start(self, keep, send, hurry=False, behind=()):
        if not hurry:
            halves = keep, self.swapped(send)
            return halves, [self.block(halves, way, 0).astype(bf16) for way in range(2)]
        pick = lambda half: jnp.stack([lax.dynamic_index_in_dim(half[way], self.at, 0, False) for way in range(2)])
        piece = self.swapped(pick(send))
        first = (pick(keep).astype(f32) + piece.astype(f32)).astype(bf16)
        return (keep, self.swapped(after(send, piece, *behind))), [first[0], first[1]]

    def round_trip(self, started, ends=None):
        halves, held = started
        for step in range(1, self.chips):
            came = [lax.ppermute(held[way], "clips", self.ways[way]) for way in range(2)]
            held = [(came[way].astype(f32) + self.block(halves, way, step)).astype(bf16) for way in range(2)]
            if ends is not None and step == 2:
                held, ends[0] = lax.optimization_barrier((held, ends[0]))
                ridden = self.over_group([ends[0][:, 0], ends[0][:, 1]])
            if ends is not None and step == 5:
                held, ends[1:] = lax.optimization_barrier((held, ends[1:]))
            held = yield held
        if ends is not None:
            both = []
            for way in range(2):
                parts = []
                at = 0
                for y in range(self.group):
                    rows = [held[way][at : at + self.rows[y]]]
                    at += self.rows[y]
                    if self.apart and y == 1:
                        rows.append(ends[1][way])
                    parts.append(jnp.concatenate(rows) if len(rows) > 1 else rows[0])
                both.append(jnp.stack(parts))
            held = [jnp.concatenate(rows) for rows in zip(self.over_group(both), ridden)]
        return (yield from self.spread(held))

    def over_group(self, held):
        both = jnp.stack(held, axis=1)
        total = lax.dynamic_index_in_dim(both, self.lane, 0, False)
        for k in range(1, self.group):
            away = lax.dynamic_index_in_dim(both, (self.lane + k) % self.group, 0, False)
            total = total + lax.ppermute(away, "mlp", [(j, (j + k) % self.group) for j in range(self.group)])
        return [total[0], total[1]]

    def spread(self, held):
        found = [[held[0]], [held[1]]]
        early = None
        for step in range(1, self.chips):
            came = yield [lax.ppermute(found[way][-1], "clips", self.ways[way]) for way in range(2)]
            for way in range(2):
                found[way].append(came[way])
            if step == self.cut - 1:
                early = self.swapped(jnp.stack(found[0] + found[1]))
        late = self.swapped(jnp.stack(found[0][self.cut :] + found[1][self.cut :]))
        return found[0] + found[1], early, late


def side_by_side(one, two, lead):
    trips, done = (one, two), [None, None]
    kept = [None, None]

    def advance(i):
        try:
            value = next(trips[i]) if kept[i] is None else trips[i].send(kept[i])
        except StopIteration as end:
            done[i] = end.value
            return
        other = kept[1 - i]
        kept[i] = value if other is None else lax.optimization_barrier((value, other))[0]

    for _ in range(lead):
        advance(0)
    while done[0] is None or done[1] is None:
        for i in range(2):
            if done[i] is None:
                advance(i)
    return done


def place_kernel(ring, streams):
    chips, cut = ring.chips, ring.cut
    each = 2 * chips + 2
    n_outs = sum(len(shares) for shares in streams)
    last_block = CORES * 2 * chips - 1

    def body(where_ref, *refs):
        sources, rest = refs[: each * len(streams)], refs[each * len(streams) :]
        outs, buffers, sems = rest[:n_outs], rest[n_outs : 2 * n_outs], rest[2 * n_outs]
        core, at, lane = where_ref[0], where_ref[1], where_ref[2]
        copies = []

        def put(shares, first_out, index, block, value):
            first = 0
            for i, (total, columns, pieces) in enumerate(shares):
                out, buffer = outs[first_out + i], buffers[first_out + i]
                tiles = columns // 128
                high = sum(height for height, _, _ in pieces)
                wide = [value[first + t * high : first + (t + 1) * high] for t in range(tiles)]
                buffer[index] = jnp.concatenate(wide, axis=1) if tiles > 1 else wide[0]
                first += tiles * high
                start = 0
                for height, row_of, short in pieces:
                    row = pl.multiple_of(row_of(block, lane), 8)
                    cases = [(height, None)] if short == height else [(height, False), (short, True)]
                    for rows, at_end in cases:
                        if rows == 0:
                            continue
                        copy = pltpu.make_async_copy(
                            buffer.at[index, pl.ds(start, rows), :], out.at[pl.ds(row, rows), :], sems.at[len(copies)]
                        )
                        copies.append((copy, None if at_end is None else (block == last_block) == at_end))
                        run(copy.start, copies[-1][1])
                    start += height

        for n, shares in enumerate(streams):
            mine = sources[n * each : n * each + 2 * chips]
            early, late = sources[n * each + 2 * chips : (n + 1) * each]
            first_out = sum(len(other) for other in streams[:n])
            for step in range(chips):
                for way in range(2):
                    slot = lax.rem(at + (1 if way == 0 else -1) * (1 - step) + chips, chips)
                    other = early[way * cut + step] if step < cut else late[way * (chips - cut) + step - cut]
                    for side, near, value in ((core, 0, mine[way * chips + step][...]), (1 - core, 1, other)):
                        block = (side * 2 + way) * chips + slot
                        put(shares, first_out, (step * 2 + way) * 2 + near, block, value.astype(f32))
        for copy, condition in copies:
            run(copy.wait, condition)

    return body


def run(action, condition):
    if condition is None:
        action()
    else:
        pl.when(condition)(action)


def shares_of(ring, totals):
    blocks = CORES * 2 * ring.chips
    shares = []
    for total, columns in totals:
        flat = columns == 128
        if flat and ring.apart:
            whole, second = ring.rows
            cut = max(0, total - (blocks - 1) * whole)
            pieces = [
                (second, lambda b, lane: jnp.where(lane == 0, b * whole, b * second), min(second, cut)),
                (
                    whole - second,
                    lambda b, lane: jnp.where(lane == 0, b * whole + second, ring.counts[1] + b * (whole - second)),
                    max(0, cut - second),
                ),
            ]
        else:
            height = ring.rows[0] if flat else total // blocks
            pieces = [(height, lambda b, lane, height=height: b * height, total - (blocks - 1) * height)]
        shares.append((total, columns, pieces))
    return shares


def place(ring, founds, totals):
    streams = [shares_of(ring, shapes) for shapes in totals]
    if any(height % 8 for shares in streams for _, _, pieces in shares for height, _, _ in pieces):
        return [out for found, shares in zip(founds, streams) for out in place_rows(ring, found, shares)]
    hbm = pl.BlockSpec(memory_space=pl.ANY)
    blocks = CORES * 2 * ring.chips
    flat_shares = [share for shares in streams for share in shares]
    copies = blocks * sum(1 if s == h else 2 for _, _, pieces in flat_shares for h, _, s in pieces)
    sources = [ref for mine, early, late in founds for ref in (*mine, early, late)]
    return call(
        place_kernel(ring, streams),
        [((total, columns), f32) for total, columns, _ in flat_shares],
        jnp.stack([ring.core, ring.at, ring.lane]).astype(jnp.int32), *sources,
        in_specs=[SMEM] + [VMEM] * len(sources),
        out_specs=[hbm] * len(flat_shares),
        scratch_shapes=[
            pltpu.VMEM((blocks, sum(h for h, _, _ in pieces), columns), f32) for _, columns, pieces in flat_shares
        ] + [pltpu.SemaphoreType.DMA((copies,))],
        us=9,
        room=32,
    )


def place_rows(ring, found, shares):
    mine, early, late = found
    chips, cut = ring.chips, ring.cut
    outs = []
    first = 0
    for total, columns, pieces in shares:
        tiles = columns // 128
        height = pieces[0][0]
        out = jnp.zeros((CORES * 2 * chips * height, columns), f32)
        for way in range(2):
            for step in range(chips):
                slot = (ring.at + (1 if way == 0 else -1) * (1 - step)) % chips
                other = early[way * cut + step] if step < cut else late[way * (chips - cut) + step - cut]
                for side, value in ((ring.core, mine[way * chips + step]), (1 - ring.core, other)):
                    value = value[first : first + tiles * height].reshape(tiles, height, 128)
                    value = value.transpose(1, 0, 2).reshape(height, columns).astype(f32)
                    row = ((side * 2 + way) * chips + slot) * height
                    out = lax.dynamic_update_slice_in_dim(out, value, row, 0)
        outs.append(out[:total])
        first += tiles * height
    return outs


def after(value, *others):
    return lax.optimization_barrier((value,) + others)[0]


def shards(clips, group, flat_params, w_fc1, w_fc2, w_up, w_down, patches, clip_ids, visible_index, cotangent):
    width = w_fc1.shape[1]
    ring = Ring(clips, group)
    core = ring.core.astype(jnp.int32).reshape(1)
    turns = [[(i, (i + k) % group) for i in range(group)] for k in range(1, group)]
    back_turns = [[(i, (i - k) % group) for i in range(group)] for k in range(1, group)]

    ups = ring.fetch(w_up)
    downs = ring.fetch(w_down)

    flat = flat_params.reshape(FLAT_ROWS, 128)
    w_qkv, w_proj, g_one, g_two = enc_prep(flat)
    x, vis, qkv, probs, mix, first, in2 = call(
        enc_attend_kernel,
        [
            ((PAD, D), bf16), ((1, PAD), jnp.int32), ((PAD, 3 * D), bf16), ((HEADS, PAD, PAD), bf16), ((PAD, D), bf16),
            ((PAD, D), f32), ((PAD, D), bf16),
        ],
        patches, visible_index[None, :], clip_ids.reshape(-1, 128), w_qkv, w_proj, g_one, g_two,
        scratch_shapes=[pltpu.VMEM((1, 384), jnp.int32)],
        us=11,
    )

    in2s, hiddens, slopes, parts = [in2], [], [], []
    for i in range(group):
        if i > 0:
            in2s.append(after(lax.ppermute(in2, "mlp", turns[i - 1]), parts[0]))
        part, hidden, slope = call(
            enc_ffn_kernel,
            [((PAD, D), f32 if i == 0 else bf16), ((PAD, width), bf16), ((PAD, width), bf16)],
            in2s[i], w_fc1, w_fc2,
        )
        hiddens.append(hidden)
        slopes.append(slope)
        parts.append(part if i == 0 else lax.ppermute(part, "mlp", back_turns[i - 1]))
    w_embed, mask_token, w_dqkv, w_dproj, gd_one, gd_two, up_all, down_all = dec_prep(ring, flat, ups, downs, part)

    second_low, table, dec_norm = call(
        embed_kernel(group),
        [((PAD, D), bf16), ((PAD, 4 * DD), bf16), ((PAD, DD), bf16)],
        first, *parts, w_embed, mask_token, gd_one, w_dqkv,
    )
    decoded, ends, wdproj_grad, gd_two_grad, packed = decoder(
        ring, vis, table, cotangent, w_dproj, gd_two, up_all, down_all
    )
    ends = lax.psum_scatter(ends.reshape(-1, 128), "clips", scatter_dimension=0, tiled=True)
    ends = ends.reshape(group, 2, -1, 128)
    second_grad, out_grad, dec_qkv_grad, embed_grad, gd_one_grad, mask_grad = call(
        embed_back_kernel,
        [
            ((PAD, D), f32), ((PAD, D), bf16), ((PAD, 3 * DD), bf16), ((PAD, DD), bf16), ((1, DD), f32), ((1, DD), f32),
        ],
        packed, table, dec_norm, second_low, gd_one, w_dqkv, w_embed,
    )
    dec_wide = CORES * 2 * ring.chips * ring.dec_rows if ring.apart else DEC_ROWS
    dec_flat = call(
        dec_flat_kernel(ring),
        [((clips, 2, ring.dec_rows, 128) if ring.apart else (DEC_ROWS, 128), bf16)],
        dec_norm, dec_qkv_grad, second_low, embed_grad, wdproj_grad, mask_grad, gd_one_grad, gd_two_grad,
        scratch_shapes=[pltpu.VMEM((dec_wide, 128), f32)],
    )[0]
    dec_ends = []
    if ring.apart:
        dec_ends = lax.psum_scatter(dec_flat.reshape(-1, 128), "clips", scatter_dimension=0, tiled=True)
        dec_ends = [dec_ends.reshape(2, -1, 128)]

    out_grads, pre_grads, parts = [out_grad], [], []
    for i in range(group):
        if i > 0:
            out_grads.append(after(lax.ppermute(out_grad, "mlp", turns[i - 1]), parts[0], dec_flat))
        pre_grad, part = call(
            enc_ffn_back_kernel,
            [((PAD, width), bf16), ((PAD, D), f32 if i == 0 else bf16)],
            out_grads[i], slopes[i], w_fc1, w_fc2,
        )
        pre_grads.append(pre_grad)
        parts.append(part if i == 0 else lax.ppermute(part, "mlp", back_turns[i - 1]))
    fc_halves = ((2, ring.chips, 2 * D * width // (CORES * 2 * ring.chips * 128), 128), bf16)
    fc_keep, fc_send = call(
        enc_weights_kernel(group, ring.chips), [fc_halves, fc_halves],
        core, *in2s, *pre_grads, *hiddens, *out_grads,
        in_specs=[SMEM] + [VMEM] * (4 * group),
        us=10,
    )
    parts[1:] = [after(part, fc_keep) for part in parts[1:]]
    flat_halves = ((2, ring.chips, sum(ring.rows), 128), bf16)
    input_grad, flat_keep, flat_send = call(
        enc_back_kernel(group, ring),
        [((VIS, D), f32), flat_halves, flat_halves],
        core, *parts, second_grad, first, x, qkv, probs, mix, w_qkv, w_proj, g_one, g_two, *([] if ring.apart else [dec_flat]),
        in_specs=[SMEM] + [VMEM] * (group + (10 if ring.apart else 11)),
        scratch_shapes=[
            pltpu.VMEM((PAD, 3 * D), bf16), pltpu.VMEM((WEMB_AT + 4 if ring.apart else FLAT_ROWS, 128), f32),
        ],
        us=20,
        room=32,
    )
    fc_start = ring.start(fc_keep, fc_send, True)
    flat_found, fc_found = side_by_side(
        ring.round_trip(ring.start(flat_keep, flat_send, True, fc_start[1]), [ends] + dec_ends),
        ring.round_trip(fc_start),
        0,
    )
    fc1_grad, fc2_grad = place(ring, [fc_found], [[(D, width), (width, D)]])
    param_grad, up_grad, down_grad = place(
        ring, [flat_found], [[(ring.part, 128), (DD, w_up.shape[1]), (w_up.shape[1], DD)]]
    )
    return decoded, input_grad, param_grad.reshape(-1), fc1_grad, fc2_grad, up_grad, down_grad


def solution(mesh):
    placed = (
        P(),
        P(None, "mlp"),
        P("mlp", None),
        P(None, "mlp"),
        P("mlp", None),
        P(("clips", "mlp"), None),
        P(("clips", "mlp")),
        P(("clips", "mlp")),
        P(("clips", "mlp"), None),
    )
    group = mesh.shape["mlp"]

    def body(*args):
        return shards(mesh.shape["clips"], group, *args)

    return jax.shard_map(
        body,
        mesh=mesh,
        in_specs=placed,
        out_specs=(
            P(("clips", "mlp"), None),
            P(("clips", "mlp"), None),
            P("mlp"),
            P(None, "mlp"),
            P("mlp", None),
            P(None, "mlp"),
            P("mlp", None),
        ),
        check_vma=False,
    )
```
